32 devices in a mesh: grp: 2 (over y), seq: 4 (over z), fsdp: 2 (over x), chan: 2 (over core).
Axes of the slice: x: 2, y: 2, z: 4, core: 2. Of those that a mesh axis runs over, the one named last changes fastest.
Arguments:
- tokens: bfloat16 [2048, 4096], P(('grp', 'seq', 'fsdp'), 'chan'), parts along dimension 0, may hold values from -6 to 6
- proj_weight: bfloat16 [4096, 3, 512], P('fsdp', None, 'chan'), may hold values from -0.09375 to 0.09375
- short_weight: float32 [3, 3, 512], P(None, None, 'chan'), may hold values from -3 to 3
- skip_gain: float32 [512], P('chan'), may hold values from -4 to 4
- filter_taps: bfloat16 [1024, 512], P(('seq', 'fsdp'), 'chan'), may hold values from -0.1875 to 0.1875
Outputs:
- mixed_out: bfloat16 [2048, 512], P(('grp', 'seq', 'fsdp'), 'chan'), parts along dimension 0
The draws below stay inside these ranges and needn't reach their ends.
There are 2 independent parts, one for each index of `grp`. The reference program is written for one: setup_inputs(seed, part) draws one part's arguments, and reference() takes and returns one part's arrays. A program takes and returns all parts, laid end to end along the dimension named above; an argument that names none is the same for every part. Nothing has to cross between parts.
All inputs are finite; a program needn't handle non-finite values.
Results may differ from the reference program's by a relative error of at most 0.009.
Values may be sent and summed in bfloat16 or wider, within the bound.
A program may use at most 64 MiB of HBM per device.

```python
import math
import jax
import jax.numpy as jnp
from jax import lax

D = 4096
C = 512
TOK_DEV = 128
L = 1024


def block_scale(rng, dims, split, low, top_value):
    factor_of = 1.0
    for dim, parts in split:
        steps = jax.random.uniform(jax.random.fold_in(jax.random.fold_in(rng, 6), dim), (parts,), jnp.float32, low / len(split), top_value / len(split))
        factor_of = factor_of * jnp.repeat(jnp.exp(steps), dims[dim] // parts).reshape((-1,) + (1,) * (len(dims) - 1 - dim))
    return factor_of


def normal_values(own_key, dims, deviation, bound, shards=(), kind=jnp.bfloat16):
    drawn = deviation * jax.random.normal(own_key, dims, jnp.float32)
    if shards:
        drawn = drawn * block_scale(own_key, dims, shards, -0.22, 0.18)
    return jnp.clip(drawn, -bound, bound).astype(kind)


def setup_inputs(seed: int = 0, part: int = 0) -> dict:
    splits = jax.random.split(jax.random.key(seed), 6)
    own_keys = jax.random.split(jax.random.fold_in(splits[5], part), 6)
    return {
        "tokens": normal_values(own_keys[0], (L, D), 1.0, 6.0, ((0, 8), (1, 2))),
        "proj_weight": normal_values(splits[1], (D, 3, C), D ** -0.5, 0.09375, ((0, 2), (2, 2))),
        "short_weight": normal_values(splits[2], (3, 3, C), 0.6, 3.0, ((2, 2),), jnp.float32),
        "skip_gain": normal_values(splits[3], (C,), 1.0, 4.0, ((0, 2),), jnp.float32),
        "filter_taps": normal_values(splits[4], (L, C), L ** -0.5, 0.1875, ((0, 8), (1, 2))),
    }


highest = lax.Precision.HIGHEST


def rounded(value):
    return lax.optimization_barrier(value.astype(jnp.bfloat16))


def index_grid(row_count, col_count):
    return (lax.broadcasted_iota(jnp.int32, (row_count, col_count), 0),
            lax.broadcasted_iota(jnp.int32, (row_count, col_count), 1))


def phase_pair(row_ids, col_ids, period):
    wrapped = (row_ids * col_ids) % period
    phase = wrapped.astype(jnp.float32) * (2.0 * math.pi / period)
    return jnp.cos(phase), jnp.sin(phase)


def spectrum(signal, first_cos, first_sin, twist_cos, twist_sin, last_cos, last_sin):
    values = signal.astype(jnp.float32)
    real_a = jnp.einsum("qp,bpm->bqm", first_cos, values, precision=highest)
    imag_a = -jnp.einsum("qp,bpm->bqm", first_sin, values, precision=highest)
    real_b = rounded(real_a * twist_cos + imag_a * twist_sin).astype(jnp.float32)
    imag_b = rounded(imag_a * twist_cos - real_a * twist_sin).astype(jnp.float32)
    real_x = jnp.einsum("bqm,mr->bqr", real_b, last_cos, precision=highest) + jnp.einsum("bqm,mr->bqr", imag_b, last_sin, precision=highest)
    imag_x = jnp.einsum("bqm,mr->bqr", imag_b, last_cos, precision=highest) - jnp.einsum("bqm,mr->bqr", real_b, last_sin, precision=highest)
    return rounded(real_x).astype(jnp.float32), rounded(imag_x).astype(jnp.float32)


def invert(real_z, imag_z, first_cos, first_sin, twist_cos, twist_sin, last_cos, last_sin, length):
    real_v = jnp.einsum("bqr,mr->bqm", real_z, last_cos, precision=highest) - jnp.einsum("bqr,mr->bqm", imag_z, last_sin, precision=highest)
    imag_v = jnp.einsum("bqr,mr->bqm", imag_z, last_cos, precision=highest) + jnp.einsum("bqr,mr->bqm", real_z, last_sin, precision=highest)
    real_w = rounded(real_v * twist_cos - imag_v * twist_sin).astype(jnp.float32)
    imag_w = rounded(imag_v * twist_cos + real_v * twist_sin).astype(jnp.float32)
    summed = jnp.einsum("qp,bqm->bpm", first_cos, real_w, precision=highest) - jnp.einsum("qp,bqm->bpm", first_sin, imag_w, precision=highest)
    return (summed * (1.0 / length)).astype(jnp.bfloat16)


def reference(tokens, proj_weight, short_weight, skip_gain, filter_taps):
    total_rows, model_width = tokens.shape
    width = proj_weight.shape[2]
    block_rows = TOK_DEV
    weight_flat = proj_weight.reshape(model_width, 3 * width).astype(jnp.float32)

    def project(block):
        return jnp.dot(block.astype(jnp.float32), weight_flat, precision=highest).astype(jnp.bfloat16)

    projected = lax.map(project, tokens.reshape(total_rows // block_rows, block_rows, model_width))
    projected = lax.optimization_barrier(projected)
    projected = projected.reshape(total_rows, 3, width).astype(jnp.float32)
    padded = jnp.pad(projected, ((2, 0), (0, 0), (0, 0)))
    mixed = short_weight[0] * padded[2:] + short_weight[1] * padded[1:-1] + short_weight[2] * padded[:-2]
    query = mixed[:, 0]
    product = rounded(mixed[:, 1] * mixed[:, 2])

    half_rows = total_rows // block_rows
    period_rows = 2 * half_rows
    length = period_rows * block_rows
    bin_ids, tap_ids = index_grid(period_rows, half_rows)
    first_cos, first_sin = phase_pair(bin_ids, tap_ids, period_rows)
    first_cos = rounded(first_cos).astype(jnp.float32)
    first_sin = rounded(first_sin).astype(jnp.float32)
    col_ids, freq_ids = index_grid(block_rows, block_rows)
    last_cos, last_sin = phase_pair(col_ids, freq_ids, block_rows)
    last_cos = rounded(last_cos).astype(jnp.float32)
    last_sin = rounded(last_sin).astype(jnp.float32)
    row_ids, mid_ids = index_grid(period_rows, block_rows)
    twist_cos, twist_sin = phase_pair(row_ids, mid_ids, length)

    group_size = 8
    signal_blocks = jnp.transpose(product).reshape(width // group_size, group_size, half_rows, block_rows)
    filter_blocks = jnp.transpose(filter_taps).reshape(width // group_size, group_size, half_rows, block_rows)

    def convolve(pair):
        signal, taps = pair
        sig_real, sig_imag = spectrum(signal, first_cos, first_sin, twist_cos, twist_sin, last_cos, last_sin)
        tap_real, tap_imag = spectrum(taps, first_cos, first_sin, twist_cos, twist_sin, last_cos, last_sin)
        real_z = rounded(sig_real * tap_real - sig_imag * tap_imag).astype(jnp.float32)
        imag_z = rounded(sig_real * tap_imag + sig_imag * tap_real).astype(jnp.float32)
        return invert(real_z, imag_z, first_cos, first_sin, twist_cos, twist_sin, last_cos, last_sin, length)

    convolved = lax.map(convolve, (signal_blocks, filter_blocks))
    conv = jnp.transpose(convolved.reshape(width, total_rows))
    result = query * (conv.astype(jnp.float32) + skip_gain * product.astype(jnp.float32))
    return result.astype(jnp.bfloat16)
```

```python
import functools
import math

import jax
import jax.numpy as jnp
import ml_dtypes
import numpy as np
from jax import lax
from jax.experimental import pallas as pl
from jax.experimental.pallas import tpu as pltpu
from jax.sharding import PartitionSpec as P

MESH = pl.DeviceIdType.MESH
BF16 = jnp.bfloat16
F32 = jnp.float32
MOST_CHUNKS = 2
HALVES = 2
PIECES = 4


def phase_pair(rows, cols, period):
    wrapped = (np.arange(rows)[:, None] * np.arange(cols)[None, :]) % period
    phase = wrapped.astype(np.float32) * np.float32(2.0 * math.pi / period)
    return np.cos(phase), np.sin(phase)


def tables(groups, per, rows):
    bf = ml_dtypes.bfloat16
    bins = 2 * groups
    cos, sin = phase_pair(bins, groups, bins)
    eye = np.eye(per, dtype=np.float32)
    first = np.concatenate([np.kron(cos, eye), np.kron(-sin, eye)], axis=0).astype(bf)
    cos, sin = phase_pair(rows, rows, rows)
    ahead = np.block([[cos, -sin], [sin, cos]]).astype(bf)
    behind = np.block([[cos, sin], [-sin, cos]]).astype(bf)
    cos, sin = phase_pair(bins, rows, bins * rows)
    twist = np.stack([np.repeat(cos, per, axis=0), np.repeat(sin, per, axis=0)])
    last = np.ascontiguousarray(first.T)
    return first, last, ahead, behind, twist.astype(np.float32)


def kernel(
    sizes,
    tokens,
    weight,
    short_h,
    gain_h,
    taps_h,
    first_h,
    last_h,
    ahead_h,
    behind_h,
    twist_h,
    out,
    w,
    first,
    last,
    ahead,
    behind,
    twist,
    short,
    gain,
    taps,
    held,
    acc,
    psend,
    precv,
    hrecv,
    query,
    product,
    tsend,
    trecv,
    gsend,
    grecv,
    csend,
    crecv,
    tapspec,
    load_sem,
    tok_send,
    tok_recv,
    fwd_send,
    part_send,
    part_recv,
    halo_send,
    halo_recv,
    a2a_send,
    a2a_recv,
):
    seq, fsdp, chan = sizes
    groups = seq * fsdp
    rows = tokens.shape[0]
    chunks = weight.shape[1]
    lines = rows // HALVES
    depth = chunks * weight.shape[2]
    width = weight.shape[3]
    per = width // groups
    bins = 2 * groups
    step = depth // chunks
    share = fsdp // chan
    s = lax.axis_index("seq")
    f = lax.axis_index("fsdp")
    c = lax.axis_index("chan")
    me = s * fsdp + f

    loads = [
        pltpu.make_async_copy(source, target, load_sem.at[i])
        for i, (source, target) in enumerate(
            [
                (taps_h, taps),
                (weight.at[pl.ds(1, 2)], w.at[pl.ds(1, 2)]),
                (first_h, first),
                (ahead_h, ahead),
                (twist_h, twist),
                (last_h, last),
                (behind_h, behind),
                (short_h, short),
                (gain_h, gain),
                (weight.at[pl.ds(0, 1)], w.at[pl.ds(0, 1)]),
            ]
        )
    ]
    for load in loads:
        load.start()

    barrier = pltpu.get_barrier_semaphore()
    everyone = groups * chan

    def greet(k, carry):
        other = lax.rem(me * chan + c + k, everyone)
        spot = other // chan
        pl.semaphore_signal(
            barrier,
            inc=1,
            device_id={"seq": spot // fsdp, "fsdp": spot % fsdp, "chan": other % chan},
            device_id_type=MESH,
        )
        return carry

    lax.fori_loop(1, everyone, greet, 0, unroll=everyone <= 16)

    @pl.when(me == 0)
    def _():
        hrecv[...] = jnp.zeros_like(hrecv)

    loads[0].wait()
    tsend[...] = jnp.transpose(taps[...].astype(F32)).astype(BF16).reshape(groups, per, rows)
    pl.semaphore_wait(barrier, everyone - 1)

    sibling = lax.rem(c + 1, chan)

    def span(h):
        return pl.ds(h * lines, lines)

    def token_copy(i, h, k, same):
        return pltpu.make_async_remote_copy(
            src_ref=tokens.at[span(h), pl.ds(i * depth + k * step, step)],
            dst_ref=held.at[f, k, span(h)],
            send_sem=tok_send.at[i, h, k],
            recv_sem=tok_recv.at[f, h, k],
            device_id={"fsdp": c * share + i, "chan": sibling if same else k % chan},
            device_id_type=MESH,
        )

    for h, k in [(h, k) for h in range(HALVES) for k in range(chunks)]:
        for i in range(share):
            stays = c * share + i == f

            @pl.when(jnp.logical_not(stays))
            def _():
                token_copy(i, h, k, False).start()

            @pl.when(stays)
            def _():
                token_copy(i, h, k, True).start()
                pltpu.make_async_copy(
                    tokens.at[span(h), pl.ds(i * depth + k * step, step)],
                    held.at[f, k, span(h)],
                    tok_recv.at[f, h, k],
                ).start()

    def exchange_copy(which, source, target, k):
        other = lax.rem(me + k, groups)
        return pltpu.make_async_remote_copy(
            src_ref=source.at[other],
            dst_ref=target.at[me],
            send_sem=a2a_send.at[which, k],
            recv_sem=a2a_recv.at[which, k],
            device_id={"seq": other // fsdp, "fsdp": other % fsdp},
            device_id_type=MESH,
        )

    def exchange_start(which, source, target):
        def go(k, carry):
            exchange_copy(which, source, target, k).start()
            return carry

        lax.fori_loop(1, groups, go, 0, unroll=groups <= 8)
        target[me] = source[me]

    def exchange_wait(which, source, target):
        def go(k, carry):
            exchange_copy(which, source, target, k).wait_recv()
            return carry

        lax.fori_loop(1, groups, go, 0, unroll=groups <= 8)

    def exchange_sent(which, source, target):
        def go(k, carry):
            exchange_copy(which, source, target, k).wait_send()
            return carry

        lax.fori_loop(1, groups, go, 0)


    half = bins * per

    def spectrum(signal):
        a = jnp.dot(first[...], signal, preferred_element_type=F32)
        real_a, imag_a = a[:half], a[half:]
        real_b = (real_a * twist[0] + imag_a * twist[1]).astype(BF16)
        imag_b = (imag_a * twist[0] - real_a * twist[1]).astype(BF16)
        b = jnp.concatenate([real_b, imag_b], axis=1)
        return jnp.dot(b, ahead[...], preferred_element_type=F32).astype(BF16)

    def arrival(spot, h, k):
        block = held.at[spot, k, span(h)]
        pltpu.make_async_copy(block, block, tok_recv.at[spot, h, k]).wait()

    def forward_copy(d, h, t):
        k = t * chan + c
        block = held.at[lax.rem(f + d, fsdp), k, span(h)]
        return pltpu.make_async_remote_copy(
            src_ref=block,
            dst_ref=block,
            send_sem=fwd_send.at[d - 1, h, t],
            recv_sem=tok_recv.at[lax.rem(f + d, fsdp), h, k],
            device_id={"chan": sibling},
            device_id_type=MESH,
        )

    def part_copy(d, j, h):
        return pltpu.make_async_remote_copy(
            src_ref=psend.at[d - 1, j, span(h)],
            dst_ref=precv.at[d - 1, j, span(h)],
            send_sem=part_send.at[d - 1, j, h],
            recv_sem=part_recv.at[d - 1, j, h],
            device_id={"fsdp": lax.rem(f + d, fsdp)},
            device_id_type=MESH,
        )

    phases = ((1, 2), (0, 1))

    def halo_target(d):
        return s * fsdp + lax.rem(f + d, fsdp) + 1

    def halo_copy(d, phase):
        target = jnp.minimum(halo_target(d), groups - 1)
        start, count = phases[phase]
        return pltpu.make_async_remote_copy(
            src_ref=acc.at[d - 1, pl.ds(start, count), pl.ds(rows - 8, 8)],
            dst_ref=hrecv.at[f, pl.ds(start, count)],
            send_sem=halo_send.at[d - 1, phase],
            recv_sem=halo_recv.at[f, phase],
            device_id={"seq": target // fsdp, "fsdp": target % fsdp},
            device_id_type=MESH,
        )

    def halo_remote(d):
        target = halo_target(d)
        return jnp.logical_and(target < groups, target != me)

    def halo_start(d, phase):
        @pl.when(halo_remote(d))
        def _():
            halo_copy(d, phase).start()

        start, count = phases[phase]

        @pl.when(halo_target(d) == me)
        def _():
            hrecv[f, start : start + count] = acc[d - 1, start : start + count, rows - 8 :]

    def halo_wait(phase):
        start, count = phases[phase]
        for h in range(fsdp):
            local = jnp.logical_and(f > 0, f == h)

            @pl.when(jnp.logical_and(me > 0, jnp.logical_not(local)))
            def _():
                block = hrecv.at[h, pl.ds(start, count)]
                pltpu.make_async_copy(block, block, halo_recv.at[h, phase]).wait()

    loads[1].wait()
    for k in range(chunks):
        for h in range(HALVES):
            arrival(f, h, k)
        for j in (1, 2):
            term = jnp.dot(held[f, k], w[j, k], preferred_element_type=F32)
            acc[fsdp - 1, j] = term if k == 0 else acc[fsdp - 1, j] + term
    halo_start(fsdp, 0)

    for d in range(1, fsdp):
        spot = lax.rem(f + d, fsdp)
        for h, t, b in [
            (h, t, b)
            for h in range(HALVES)
            for t in range(chunks // chan)
            for b in range(chan)
        ]:
            k = t * chan + lax.rem(c + b, chan)
            arrival(spot, h, k)
            if b == 0:
                forward_copy(d, h, t).start()
            final = (t + 1) * chan == chunks and b == chan - 1
            at = slice(h * lines, (h + 1) * lines)
            for j in (1, 2):
                term = jnp.dot(held[spot, k, at], w[j, k], preferred_element_type=F32)
                if t > 0 or b > 0:
                    term = acc[d - 1, j, at] + term
                acc[d - 1, j, at] = term
                if final:
                    psend[d - 1, j, at] = term.astype(BF16)
                    part_copy(d, j, h).start()
        halo_start(d, 0)

    for load in loads[2:]:
        load.wait()
    exchange_start(0, tsend, trecv)

    row_ids = lax.broadcasted_iota(jnp.int32, (rows, width), 0)

    def branch(j):
        total = acc[fsdp - 1, j]
        edge = hrecv[0, j]
        for d in range(1, fsdp):
            for h in range(HALVES):
                part_copy(d, j, h).wait_recv()
            total = total + precv[d - 1, j].astype(F32)
            edge = edge + hrecv[d, j]
        now = total.astype(BF16).astype(F32)
        edge = edge.astype(BF16).astype(F32)
        before = edge[7:8]
        earlier = edge[6:7]
        one = jnp.where(row_ids == 0, before, pltpu.roll(now, 1, 0))
        two = jnp.where(
            row_ids == 0, earlier, jnp.where(row_ids == 1, before, pltpu.roll(now, 2, 0))
        )
        return (
            short[0, j : j + 1, :] * now
            + short[1, j : j + 1, :] * one
            + short[2, j : j + 1, :] * two
        )

    halo_wait(0)
    prod = (branch(1) * branch(2)).astype(BF16).astype(F32)
    gsend[...] = jnp.transpose(prod).astype(BF16).reshape(groups, per, rows)
    exchange_start(1, gsend, grecv)
    product[...] = prod * gain[...]

    for d in range(1, fsdp + 1):
        spot = lax.rem(f + d, fsdp)
        term = jnp.dot(held[spot, 0], w[0, 0], preferred_element_type=F32)
        for k in range(1, chunks):
            term += jnp.dot(held[spot, k], w[0, k], preferred_element_type=F32)
        acc[d - 1, 0] = term
        if d < fsdp:
            psend[d - 1, 0] = term.astype(BF16)

    exchange_wait(0, tsend, trecv)
    tapspec[...] = spectrum(trecv[...].reshape(width, rows))
    exchange_wait(1, gsend, grecv)
    for d in range(1, fsdp + 1):
        if d < fsdp:
            for h in range(HALVES):
                part_copy(d, 0, h).start()
        halo_start(d, 1)

    x = spectrum(grecv[...].reshape(width, rows)).astype(F32)
    t = tapspec[...].astype(F32)
    xr, xi = x[:, :rows], x[:, rows:]
    tr, ti = t[:, :rows], t[:, rows:]
    real_z = (xr * tr - xi * ti).astype(BF16)
    imag_z = (xr * ti + xi * tr).astype(BF16)
    z = jnp.concatenate([real_z, imag_z], axis=1)
    v = jnp.dot(z, behind[...], preferred_element_type=F32)
    vr, vi = v[:, :rows], v[:, rows:]
    real_w = (vr * twist[0] - vi * twist[1]).astype(BF16)
    imag_w = (vi * twist[0] + vr * twist[1]).astype(BF16)
    packed = jnp.concatenate([real_w, imag_w], axis=0)
    y = jnp.dot(last[...], packed, preferred_element_type=F32) * (1.0 / (bins * rows))
    csend[...] = y.astype(BF16).reshape(groups, per, rows)
    exchange_start(2, csend, crecv)
    halo_wait(1)
    query[...] = branch(0)
    exchange_wait(2, csend, crecv)
    conv = jnp.transpose(crecv[...].reshape(width, rows).astype(F32))
    out[...] = (query[...] * (conv + product[...])).astype(BF16)

    exchange_sent(0, tsend, trecv)
    exchange_sent(1, gsend, grecv)
    exchange_sent(2, csend, crecv)
    for d in range(1, fsdp + 1):
        for phase in range(2):

            @pl.when(halo_remote(d))
            def _():
                halo_copy(d, phase).wait_send()

    for d in range(1, fsdp):
        for h in range(HALVES):
            for j in range(3):
                part_copy(d, j, h).wait_send()
            for t in range(chunks // chan):
                forward_copy(d, h, t).wait_send()
    for h, k in [(h, k) for h in range(HALVES) for k in range(chunks)]:
        for i in range(share):
            token_copy(i, h, k, False).wait_send()


def per_device(sizes, tokens, proj_weight, short_weight, skip_gain, filter_taps):
    seq, fsdp, chan = sizes
    groups = seq * fsdp
    rows = tokens.shape[0]
    depth, branches, width = proj_weight.shape
    per = width // groups
    chunks = min(MOST_CHUNKS, depth // 128)
    made = tables(groups, per, rows)
    dma = pltpu.SemaphoreType.DMA
    vmem = pl.BlockSpec(memory_space=pltpu.VMEM)
    hbm = pl.BlockSpec(memory_space=pl.ANY)
    half = 2 * groups * per
    return pl.pallas_call(
        functools.partial(kernel, sizes),
        out_shape=jax.ShapeDtypeStruct((rows, width), BF16),
        in_specs=[hbm] * 10,
        out_specs=vmem,
        scratch_shapes=[
            pltpu.VMEM((branches, chunks, depth // chunks, width), BF16),
            pltpu.VMEM(made[0].shape, BF16),
            pltpu.VMEM(made[1].shape, BF16),
            pltpu.VMEM(made[2].shape, BF16),
            pltpu.VMEM(made[3].shape, BF16),
            pltpu.VMEM(made[4].shape, F32),
            pltpu.VMEM(short_weight.shape, F32),
            pltpu.VMEM((1, width), F32),
            pltpu.VMEM((rows, width), BF16),
            pltpu.VMEM((fsdp, chunks, rows, depth // chunks), BF16),
            pltpu.VMEM((fsdp, branches, rows, width), F32),
            pltpu.VMEM((fsdp - 1, branches, rows, width), BF16),
            pltpu.VMEM((fsdp - 1, branches, rows, width), BF16),
            pltpu.VMEM((fsdp, branches, 8, width), F32),
            pltpu.VMEM((rows, width), F32),
            pltpu.VMEM((rows, width), F32),
        ]
        + [pltpu.VMEM((groups, per, rows), BF16)] * 6
        + [
            pltpu.VMEM((half, 2 * rows), BF16),
            dma((10,)),
            dma((fsdp // chan, HALVES, chunks)),
            dma((fsdp, HALVES, chunks)),
            dma((fsdp - 1, HALVES, chunks // chan)),
            dma((fsdp - 1, branches, HALVES)),
            dma((fsdp - 1, branches, HALVES)),
            dma((fsdp, 2)),
            dma((fsdp, 2)),
            dma((3, groups)),
            dma((3, groups)),
        ],
        compiler_params=pltpu.CompilerParams(
            collective_id=0, has_side_effects=True, vmem_limit_bytes=60 * 1024 * 1024
        ),
        name="hyena",
    )(
        tokens,
        jnp.transpose(proj_weight, (1, 0, 2)).reshape(branches, chunks, depth // chunks, width),
        short_weight,
        skip_gain.reshape(1, width),
        filter_taps,
        *[jnp.asarray(table) for table in made],
    )


def causal_tables(rows):
    bf = ml_dtypes.bfloat16
    odd = 2 * np.arange(rows) + 1
    period = 4 * rows

    def angles(times):
        wrapped = (odd[:, None] * times[None, :]) % period
        return wrapped.astype(np.float64) * (2.0 * math.pi / period)

    ahead = angles(np.arange(rows))
    behind = angles(rows + np.arange(rows)).T
    forward = np.concatenate([np.cos(ahead), -np.sin(ahead)], axis=0)
    inverse = np.concatenate([np.cos(behind), -np.sin(behind)], axis=1) / rows
    return forward.astype(bf), inverse.astype(bf)


def causal_kernel(
    seq,
    tokens,
    weight,
    short_h,
    gain_h,
    taps_h,
    forward_h,
    inverse_h,
    out,
    w,
    forward,
    inverse,
    short,
    gain,
    own,
    far,
    part_out,
    part_in,
    edge_out,
    edge_in,
    halves,
    signal,
    taps,
    tapspec,
    response,
    total,
    query,
    query_out,
    query_in,
    query_edge_out,
    query_edge_in,
    result,
    final,
    load_sem,
    own_send,
    own_recv,
    far_send,
    far_recv,
    fwd_send,
    part_send,
    part_recv,
    edge_send,
    edge_recv,
    signal_send,
    signal_recv,
    taps_local,
    taps_x_send,
    taps_x_recv,
    taps_z_send,
    taps_z_recv,
    query_send,
    query_recv,
    query_edge_send,
    query_edge_recv,
    out_send,
    out_recv,
    out_local,
    ready,
):
    rows = tokens.shape[0]
    width = weight.shape[3]
    pieces = weight.shape[1]
    depth = weight.shape[2]
    lanes = width // 2
    s = lax.axis_index("seq")
    f = lax.axis_index("fsdp")
    c = lax.axis_index("chan")
    g = 1 - f
    sibling = 1 - c

    def half_of(value):
        return jnp.where(f == 0, value[:, :lanes], value[:, lanes:])

    def local(source, target, i):
        return pltpu.make_async_copy(source, target, load_sem.at[i])

    def remote(source, target, send, recv, device):
        return pltpu.make_async_remote_copy(
            src_ref=source,
            dst_ref=target,
            send_sem=send,
            recv_sem=recv,
            device_id=device,
            device_id_type=MESH,
        )

    def arrive(block, sem):
        pltpu.make_async_copy(block, block, sem).wait()

    own_load = pltpu.make_async_copy(tokens, own, own_recv)
    holds = c == f

    @pl.when(holds)
    def _():
        own_load.start()

    loads = [
        local(weight.at[pl.ds(1, 2)], w.at[pl.ds(1, 2)], 0),
        local(weight.at[pl.ds(0, 1)], w.at[pl.ds(0, 1)], 1),
        local(forward_h, forward, 2),
        local(inverse_h, inverse, 3),
        local(short_h, short, 4),
        local(gain_h, gain, 5),
    ]
    for load in loads:
        load.start()

    def columns(h):
        return pl.ds(pl.multiple_of(h * lanes, lanes), lanes)

    taps_load = pltpu.make_async_copy(taps_h.at[:, columns(f)], taps.at[s, f], taps_local)
    taps_load.start()

    edge_in[...] = jnp.zeros_like(edge_in)
    query_edge_in[...] = jnp.zeros_like(query_edge_in)
    barrier = pltpu.get_barrier_semaphore()
    across = {"fsdp": g}
    quad = [{"chan": sibling}, across, {"fsdp": g, "chan": sibling}]

    for device in quad:
        pl.semaphore_signal(barrier, inc=1, device_id=device, device_id_type=MESH)
    for t in range(seq):
        for h in range(2):

            @pl.when(t > s)
            def _():
                pl.semaphore_signal(
                    barrier, inc=1, device_id={"seq": t, "fsdp": h}, device_id_type=MESH
                )

    pl.semaphore_wait(barrier, 3 + 2 * s)

    def token_copy(k):
        return remote(
            tokens.at[:, pl.ds(k * depth, depth)],
            far.at[k],
            far_send.at[k],
            far_recv.at[k],
            {"fsdp": g, "chan": k % 2},
        )

    own_copy = remote(tokens, own, own_send, own_recv, {"chan": sibling})
    taps_x_copy = remote(
        taps_h.at[:, columns(g)], taps.at[s, f], taps_x_send, taps_x_recv, across
    )
    taps_x_copy.start()

    @pl.when(jnp.logical_not(holds))
    def _():
        for k in range(pieces):
            token_copy(k).start()

    @pl.when(holds)
    def _():
        own_copy.start()

    for t in range(seq):
        for h in range(2):

            @pl.when(t < s)
            def _():
                pl.semaphore_signal(
                    ready, inc=1, device_id={"seq": t, "fsdp": h}, device_id_type=MESH
                )

    def part_copy(j):
        return remote(
            part_out.at[j], part_in.at[j], part_send.at[j], part_recv.at[j], across
        )

    def query_copy(i):
        return remote(
            query_out.at[i], query_in.at[i], query_send.at[i], query_recv.at[i], across
        )

    def own_part(j):
        term = jnp.dot(own[:, :depth], w[j, 0], preferred_element_type=F32)
        for k in range(1, pieces):
            term += jnp.dot(
                own[:, k * depth : (k + 1) * depth], w[j, k], preferred_element_type=F32
            )
        return term

    with jax.named_scope("own_rows"):
        arrive(own, own_recv)
        loads[0].wait()
        for j in range(2):
            term = own_part(j + 1)
            part_out[j] = term.astype(BF16)
            part_copy(j).start()
            edge_out[0, j] = term[rows - 8 :]

        @pl.when(f == 0)
        def _():
            edge_in[0] = edge_out[0]

    last = seq - 1
    goes_up = s < last

    def edge_up(i):
        return remote(
            edge_out.at[i],
            edge_in.at[i],
            edge_send.at[i],
            edge_recv.at[i],
            {"seq": jnp.minimum(s + 1, last), "fsdp": 1},
        )

    edge_across = remote(
        edge_out.at[1], edge_in.at[1], edge_send.at[1], edge_recv.at[1], {"fsdp": 0}
    )

    with jax.named_scope("ready"):

        @pl.when(goes_up)
        def _():
            pl.semaphore_wait(ready, 2 * (last - s))


    @pl.when(jnp.logical_and(f == 1, goes_up))
    def _():
        edge_up(0).start()

    def taps_z_copy(t):
        return remote(
            taps.at[s], taps.at[s], taps_z_send.at[t], taps_z_recv.at[s], {"seq": t}
        )

    with jax.named_scope("taps_up"):
        taps_load.wait()
        arrive(taps.at[s, g], taps_x_recv)
        for t in range(1, seq):

            @pl.when(t > s)
            def _():
                taps_z_copy(t).start()

    with jax.named_scope("own_query"):
        loads[1].wait()
        term = own_part(0)
        query[f] = half_of(term)
        query_out[0] = jnp.where(f == 0, term[:, lanes:], term[:, :lanes]).astype(BF16)

    def forward_copy(k, i):
        return remote(
            far.at[k], far.at[k], fwd_send.at[i], far_recv.at[k], {"chan": sibling}
        )

    with jax.named_scope("far_rows"):
        parts = [None, None]
        for step in range(pieces):
            k = (step // 2) * 2 + (c if step % 2 == 0 else sibling)
            arrive(far.at[k], far_recv.at[k])
            if step % 2 == 0:
                forward_copy(k, step // 2).start()
            for j in range(2):
                term = jnp.dot(far[k], w[j + 1, k], preferred_element_type=F32)
                parts[j] = term if step == 0 else parts[j] + term
        for j in range(2):
            edge_out[1, j] = parts[j][rows - 8 :]
            total[j] = parts[j]

        @pl.when(f == 1)
        def _():
            edge_across.start()

        @pl.when(jnp.logical_and(f == 0, goes_up))
        def _():
            edge_up(1).start()

    bins = 2 * rows
    with jax.named_scope("taps_spectra"):
        for load in loads[2:]:
            load.wait()
        sign = 1.0 - 2.0 * (lax.broadcasted_iota(jnp.int32, (bins, lanes), 0) % 2).astype(F32)
        for d in range(seq):

            @pl.when(d <= s)
            def _():
                @pl.when(d < s)
                def _():
                    arrive(taps.at[d], taps_z_recv.at[d])

                spec = jnp.dot(
                    forward[...], taps[d].reshape(bins, lanes), preferred_element_type=F32
                )
                real, imag = spec[:bins], spec[bins:]
                tapspec[d] = spec
                if d == 0:
                    response[0, 0] = sign * imag
                    response[0, 1] = -sign * real
                else:
                    response[d, 0] = tapspec[d - 1, :bins] + sign * imag
                    response[d, 1] = tapspec[d - 1, bins:] - sign * real

    def shifted(now, edge):
        count = now.shape[0]
        ids = lax.broadcasted_iota(jnp.int32, now.shape, 0)
        before, earlier = edge[7:8], edge[6:7]
        one = jnp.where(ids == 0, before, pltpu.roll(now, 1, 0))
        two = jnp.where(
            ids == 0, earlier, jnp.where(ids == 1, before, pltpu.roll(now, 2, 0))
        )
        return one, two

    def rounded(value):
        return value.astype(BF16).astype(F32)

    def branch(j):
        part_copy(j).wait_recv()
        now = rounded(total[j] + part_in[j].astype(F32))
        one, two = shifted(now, rounded(edge_in[0, j] + edge_in[1, j]))
        return (
            short[0, j + 1 : j + 2, :] * now
            + short[1, j + 1 : j + 2, :] * one
            + short[2, j + 1 : j + 2, :] * two
        )

    def signal_copy(t, h):
        return remote(
            halves.at[h],
            signal.at[s, g],
            signal_send.at[t, h],
            signal_recv.at[s, g],
            {"seq": t, "fsdp": h},
        )

    own_signal = remote(
        halves.at[g],
        signal.at[s, g],
        signal_send.at[s, g],
        signal_recv.at[s, g],
        across,
    )

    with jax.named_scope("edges"):

        @pl.when(jnp.logical_and(f == 1, s > 0))
        def _():
            arrive(edge_in.at[0], edge_recv.at[0])

        @pl.when(jnp.logical_or(f == 0, s > 0))
        def _():
            arrive(edge_in.at[1], edge_recv.at[1])

    with jax.named_scope("product"):
        product = (branch(0) * branch(1)).astype(BF16)
        halves[0] = product[:, :lanes]
        halves[1] = product[:, lanes:]
        own_signal.start()
        for t in range(1, seq):

            @pl.when(t > s)
            def _():
                for h in range(2):
                    signal_copy(t, h).start()

        signal[s, g] = jnp.where(f == 0, product[:, :lanes], product[:, lanes:])

    with jax.named_scope("far_query"):
        query_copy(0).start()
        term = jnp.dot(far[0], w[0, 0], preferred_element_type=F32)
        for k in range(1, pieces):
            term += jnp.dot(far[k], w[0, k], preferred_element_type=F32)
        query[g] = half_of(term)
        query_out[1] = jnp.where(f == 0, term[:, lanes:], term[:, :lanes]).astype(BF16)
        query_copy(1).start()

    def spectrum(j):
        spec = jnp.dot(
            forward[...], signal[j].reshape(bins, lanes), preferred_element_type=F32
        )
        real, imag = spec[:bins], spec[bins:]
        d = s - j
        hr, hi = response[d, 0], response[d, 1]
        return real * hr - imag * hi, real * hi + imag * hr

    with jax.named_scope("earlier_slabs"):
        result[...] = jnp.zeros_like(result)
        for j in range(last):

            @pl.when(j < s)
            def _():
                for b in range(2):
                    arrive(signal.at[j, b], signal_recv.at[j, b])
                real, imag = spectrum(j)
                result[0] += real
                result[1] += imag

    with jax.named_scope("query_sum"):
        for i in range(2):
            query_copy(i).wait_recv()
        query[g] = rounded(query[g] + query_in[0].astype(F32))
        query[f] = rounded(query[f] + query_in[1].astype(F32))
        query_edge_out[...] = query[1, rows - 8 :]

        query_edge = remote(
            query_edge_out,
            query_edge_in,
            query_edge_send,
            query_edge_recv,
            {"seq": jnp.minimum(s + 1, last)},
        )

        @pl.when(goes_up)
        def _():
            query_edge.start()

    with jax.named_scope("own_slab"):
        arrive(signal.at[s, f], signal_recv.at[s, f])
        real, imag = spectrum(s)
        packed = jnp.concatenate([result[0] + real, result[1] + imag], axis=0)
        conv = jnp.dot(inverse[...], packed.astype(BF16), preferred_element_type=F32)

    with jax.named_scope("query_mix"):

        @pl.when(s > 0)
        def _():
            arrive(query_edge_in, query_edge_recv)

        now = query[...].reshape(bins, lanes)
        one, two = shifted(now, query_edge_in[...])
        mine = [half_of(short[i, 0:1, :]) for i in range(3)]
        mixed = mine[0] * now + mine[1] * one + mine[2] * two
        direct = half_of(gain[...]) * signal[s].reshape(bins, lanes).astype(F32)
        made = (mixed * (conv + direct)).astype(BF16)
        final[0] = made[:rows]
        final[1] = made[rows:]

    out_across = remote(final.at[g], out.at[:, columns(f)], out_send, out_recv, across)
    out_here = pltpu.make_async_copy(final.at[f], out.at[:, columns(f)], out_local)
    out_across.start()
    out_here.start()

    with jax.named_scope("drain"):

        @pl.when(jnp.logical_not(holds))
        def _():
            for k in range(pieces):
                token_copy(k).wait_send()

        @pl.when(holds)
        def _():
            own_copy.wait_send()

        taps_x_copy.wait_send()
        for j in range(2):
            part_copy(j).wait_send()
            query_copy(j).wait_send()
            forward_copy(j * 2 + c, j).wait_send()

        @pl.when(f == 1)
        def _():
            edge_across.wait_send()

        @pl.when(goes_up)
        def _():
            edge_up(1 - f).wait_send()
            query_edge.wait_send()

        own_signal.wait_send()
        for t in range(1, seq):

            @pl.when(t > s)
            def _():
                taps_z_copy(t).wait_send()
                for h in range(2):
                    signal_copy(t, h).wait_send()

    with jax.named_scope("out"):
        out_across.wait_send()
        out_here.wait()
        arrive(out.at[:, columns(g)], out_recv)


def causal_device(seq, tokens, proj_weight, short_weight, skip_gain, filter_taps):
    rows = tokens.shape[0]
    depth, branches, width = proj_weight.shape
    lanes = width // 2
    step = depth // PIECES
    forward, inverse = causal_tables(2 * rows)
    dma = pltpu.SemaphoreType.DMA
    hbm = pl.BlockSpec(memory_space=pl.ANY)
    scratch = [
        ((branches, PIECES, step, width), BF16),
        (forward.shape, BF16),
        (inverse.shape, BF16),
        (short_weight.shape, F32),
        ((1, width), F32),
        ((rows, depth), BF16),
        ((PIECES, rows, step), BF16),
        ((2, rows, width), BF16),
        ((2, rows, width), BF16),
        ((2, 2, 8, width), F32),
        ((2, 2, 8, width), F32),
        ((2, rows, lanes), BF16),
        ((seq, 2, rows, lanes), BF16),
        ((seq, 2, rows, lanes), BF16),
        ((seq, 4 * rows, lanes), F32),
        ((seq, 2, 2 * rows, lanes), F32),
        ((2, rows, width), F32),
        ((2, rows, lanes), F32),
        ((2, rows, lanes), BF16),
        ((2, rows, lanes), BF16),
        ((8, lanes), F32),
        ((8, lanes), F32),
        ((2, 2 * rows, lanes), F32),
        ((2, rows, lanes), BF16),
    ]
    sems = [
        (6,), (), (), (PIECES,), (PIECES,), (2,), (2,), (2,), (2,), (2,),
        (seq, 2), (seq, 2), (), (), (), (seq,), (seq,), (2,), (2,), (), (), (), (), (),
    ]
    return pl.pallas_call(
        functools.partial(causal_kernel, seq),
        out_shape=jax.ShapeDtypeStruct((rows, width), BF16),
        in_specs=[hbm] * 7,
        out_specs=hbm,
        scratch_shapes=[pltpu.VMEM(shape, kind) for shape, kind in scratch]
        + [dma(shape) for shape in sems]
        + [pltpu.SemaphoreType.REGULAR],
        compiler_params=pltpu.CompilerParams(
            collective_id=0, has_side_effects=True, vmem_limit_bytes=60 * 1024 * 1024
        ),
        name="hyena",
    )(
        tokens,
        jnp.transpose(proj_weight, (1, 0, 2)).reshape(branches, PIECES, step, width),
        short_weight,
        skip_gain.reshape(1, width),
        filter_taps,
        jnp.asarray(forward),
        jnp.asarray(inverse),
    )


def solution(mesh):
    seq = mesh.shape["seq"]
    paired = mesh.shape["fsdp"] == 2 and mesh.shape["chan"] == 2
    sizes = (mesh.shape["seq"], mesh.shape["fsdp"], mesh.shape["chan"])
    in_specs = (
        P(("grp", "seq", "fsdp"), "chan"),
        P("fsdp", None, "chan"),
        P(None, None, "chan"),
        P("chan"),
        P(("seq", "fsdp"), "chan"),
    )
    out_specs = P(("grp", "seq", "fsdp"), "chan")
    return jax.shard_map(
        functools.partial(causal_device, seq) if paired else functools.partial(per_device, sizes),
        mesh=mesh,
        in_specs=in_specs,
        out_specs=out_specs,
        check_vma=False,
    )
```

```python
import functools
import math

import jax
import jax.numpy as jnp
import ml_dtypes
import numpy as np
from jax import lax
from jax.experimental import pallas as pl
from jax.experimental.pallas import tpu as pltpu
from jax.sharding import PartitionSpec as P

MESH = pl.DeviceIdType.MESH
BF16 = jnp.bfloat16
F32 = jnp.float32
MOST_CHUNKS = 2
HALVES = 2
EDGE = 16
CHUNK = 64


def phase_pair(rows, cols, period):
    wrapped = (np.arange(rows)[:, None] * np.arange(cols)[None, :]) % period
    phase = wrapped.astype(np.float32) * np.float32(2.0 * math.pi / period)
    return np.cos(phase), np.sin(phase)


def tables(groups, per, rows):
    bf = ml_dtypes.bfloat16
    bins = 2 * groups
    cos, sin = phase_pair(bins, groups, bins)
    eye = np.eye(per, dtype=np.float32)
    first = np.concatenate([np.kron(cos, eye), np.kron(-sin, eye)], axis=0).astype(bf)
    cos, sin = phase_pair(rows, rows, rows)
    ahead = np.block([[cos, -sin], [sin, cos]]).astype(bf)
    behind = np.block([[cos, sin], [-sin, cos]]).astype(bf)
    cos, sin = phase_pair(bins, rows, bins * rows)
    twist = np.stack([np.repeat(cos, per, axis=0), np.repeat(sin, per, axis=0)])
    last = np.ascontiguousarray(first.T)
    return first, last, ahead, behind, twist.astype(np.float32)


def kernel(
    sizes,
    tokens,
    weight,
    short_h,
    gain_h,
    taps_h,
    first_h,
    last_h,
    ahead_h,
    behind_h,
    twist_h,
    out,
    w,
    first,
    last,
    ahead,
    behind,
    twist,
    short,
    gain,
    taps,
    held,
    acc,
    psend,
    precv,
    hrecv,
    query,
    product,
    tsend,
    trecv,
    gsend,
    grecv,
    csend,
    crecv,
    tapspec,
    load_sem,
    tok_send,
    tok_recv,
    fwd_send,
    part_send,
    part_recv,
    halo_send,
    halo_recv,
    a2a_send,
    a2a_recv,
):
    seq, fsdp, chan = sizes
    groups = seq * fsdp
    rows = tokens.shape[0]
    chunks = weight.shape[1]
    lines = rows // HALVES
    depth = chunks * weight.shape[2]
    width = weight.shape[3]
    per = width // groups
    bins = 2 * groups
    step = depth // chunks
    share = fsdp // chan
    s = lax.axis_index("seq")
    f = lax.axis_index("fsdp")
    c = lax.axis_index("chan")
    me = s * fsdp + f

    loads = [
        pltpu.make_async_copy(source, target, load_sem.at[i])
        for i, (source, target) in enumerate(
            [
                (taps_h, taps),
                (weight.at[pl.ds(1, 2)], w.at[pl.ds(1, 2)]),
                (first_h, first),
                (ahead_h, ahead),
                (twist_h, twist),
                (last_h, last),
                (behind_h, behind),
                (short_h, short),
                (gain_h, gain),
                (weight.at[pl.ds(0, 1)], w.at[pl.ds(0, 1)]),
            ]
        )
    ]
    for load in loads:
        load.start()

    barrier = pltpu.get_barrier_semaphore()
    everyone = groups * chan

    def greet(k, carry):
        other = lax.rem(me * chan + c + k, everyone)
        spot = other // chan
        pl.semaphore_signal(
            barrier,
            inc=1,
            device_id={"seq": spot // fsdp, "fsdp": spot % fsdp, "chan": other % chan},
            device_id_type=MESH,
        )
        return carry

    lax.fori_loop(1, everyone, greet, 0, unroll=everyone <= 16)

    @pl.when(me == 0)
    def _():
        hrecv[...] = jnp.zeros_like(hrecv)

    loads[0].wait()
    tsend[...] = jnp.transpose(taps[...].astype(F32)).astype(BF16).reshape(groups, per, rows)
    pl.semaphore_wait(barrier, everyone - 1)

    sibling = lax.rem(c + 1, chan)

    def span(h):
        return pl.ds(h * lines, lines)

    def token_copy(i, h, k, same):
        return pltpu.make_async_remote_copy(
            src_ref=tokens.at[span(h), pl.ds(i * depth + k * step, step)],
            dst_ref=held.at[f, k, span(h)],
            send_sem=tok_send.at[i, h, k],
            recv_sem=tok_recv.at[f, h, k],
            device_id={"fsdp": c * share + i, "chan": sibling if same else k % chan},
            device_id_type=MESH,
        )

    for h, k in [(h, k) for h in range(HALVES) for k in range(chunks)]:
        for i in range(share):
            stays = c * share + i == f

            @pl.when(jnp.logical_not(stays))
            def _():
                token_copy(i, h, k, False).start()

            @pl.when(stays)
            def _():
                token_copy(i, h, k, True).start()
                pltpu.make_async_copy(
                    tokens.at[span(h), pl.ds(i * depth + k * step, step)],
                    held.at[f, k, span(h)],
                    tok_recv.at[f, h, k],
                ).start()

    def exchange_copy(which, source, target, k):
        other = lax.rem(me + k, groups)
        return pltpu.make_async_remote_copy(
            src_ref=source.at[other],
            dst_ref=target.at[me],
            send_sem=a2a_send.at[which, k],
            recv_sem=a2a_recv.at[which, k],
            device_id={"seq": other // fsdp, "fsdp": other % fsdp},
            device_id_type=MESH,
        )

    def exchange_start(which, source, target):
        def go(k, carry):
            exchange_copy(which, source, target, k).start()
            return carry

        lax.fori_loop(1, groups, go, 0, unroll=groups <= 8)
        target[me] = source[me]

    def exchange_wait(which, source, target):
        def go(k, carry):
            exchange_copy(which, source, target, k).wait_recv()
            return carry

        lax.fori_loop(1, groups, go, 0, unroll=groups <= 8)

    def exchange_sent(which, source, target):
        def go(k, carry):
            exchange_copy(which, source, target, k).wait_send()
            return carry

        lax.fori_loop(1, groups, go, 0)


    half = bins * per

    def spectrum(signal):
        a = jnp.dot(first[...], signal, preferred_element_type=F32)
        real_a, imag_a = a[:half], a[half:]
        real_b = (real_a * twist[0] + imag_a * twist[1]).astype(BF16)
        imag_b = (imag_a * twist[0] - real_a * twist[1]).astype(BF16)
        b = jnp.concatenate([real_b, imag_b], axis=1)
        return jnp.dot(b, ahead[...], preferred_element_type=F32).astype(BF16)

    def arrival(spot, h, k):
        block = held.at[spot, k, span(h)]
        pltpu.make_async_copy(block, block, tok_recv.at[spot, h, k]).wait()

    def forward_copy(d, h, t):
        k = t * chan + c
        block = held.at[lax.rem(f + d, fsdp), k, span(h)]
        return pltpu.make_async_remote_copy(
            src_ref=block,
            dst_ref=block,
            send_sem=fwd_send.at[d - 1, h, t],
            recv_sem=tok_recv.at[lax.rem(f + d, fsdp), h, k],
            device_id={"chan": sibling},
            device_id_type=MESH,
        )

    def part_copy(d, j, h):
        return pltpu.make_async_remote_copy(
            src_ref=psend.at[d - 1, j, span(h)],
            dst_ref=precv.at[d - 1, j, span(h)],
            send_sem=part_send.at[d - 1, j, h],
            recv_sem=part_recv.at[d - 1, j, h],
            device_id={"fsdp": lax.rem(f + d, fsdp)},
            device_id_type=MESH,
        )

    phases = ((1, 2), (0, 1))

    def halo_target(d):
        return s * fsdp + lax.rem(f + d, fsdp) + 1

    def halo_copy(d, phase):
        target = jnp.minimum(halo_target(d), groups - 1)
        start, count = phases[phase]
        return pltpu.make_async_remote_copy(
            src_ref=acc.at[d - 1, pl.ds(start, count), pl.ds(rows - 8, 8)],
            dst_ref=hrecv.at[f, pl.ds(start, count)],
            send_sem=halo_send.at[d - 1, phase],
            recv_sem=halo_recv.at[f, phase],
            device_id={"seq": target // fsdp, "fsdp": target % fsdp},
            device_id_type=MESH,
        )

    def halo_remote(d):
        target = halo_target(d)
        return jnp.logical_and(target < groups, target != me)

    def halo_start(d, phase):
        @pl.when(halo_remote(d))
        def _():
            halo_copy(d, phase).start()

        start, count = phases[phase]

        @pl.when(halo_target(d) == me)
        def _():
            hrecv[f, start : start + count] = acc[d - 1, start : start + count, rows - 8 :]

    def halo_wait(phase):
        start, count = phases[phase]
        for h in range(fsdp):
            local = jnp.logical_and(f > 0, f == h)

            @pl.when(jnp.logical_and(me > 0, jnp.logical_not(local)))
            def _():
                block = hrecv.at[h, pl.ds(start, count)]
                pltpu.make_async_copy(block, block, halo_recv.at[h, phase]).wait()

    loads[1].wait()
    for k in range(chunks):
        for h in range(HALVES):
            arrival(f, h, k)
        for j in (1, 2):
            term = jnp.dot(held[f, k], w[j, k], preferred_element_type=F32)
            acc[fsdp - 1, j] = term if k == 0 else acc[fsdp - 1, j] + term
    halo_start(fsdp, 0)

    for d in range(1, fsdp):
        spot = lax.rem(f + d, fsdp)
        for h, t, b in [
            (h, t, b)
            for h in range(HALVES)
            for t in range(chunks // chan)
            for b in range(chan)
        ]:
            k = t * chan + lax.rem(c + b, chan)
            arrival(spot, h, k)
            if b == 0:
                forward_copy(d, h, t).start()
            final = (t + 1) * chan == chunks and b == chan - 1
            at = slice(h * lines, (h + 1) * lines)
            for j in (1, 2):
                term = jnp.dot(held[spot, k, at], w[j, k], preferred_element_type=F32)
                if t > 0 or b > 0:
                    term = acc[d - 1, j, at] + term
                acc[d - 1, j, at] = term
                if final:
                    psend[d - 1, j, at] = term.astype(BF16)
                    part_copy(d, j, h).start()
        halo_start(d, 0)

    for load in loads[2:]:
        load.wait()
    exchange_start(0, tsend, trecv)

    row_ids = lax.broadcasted_iota(jnp.int32, (rows, width), 0)

    def branch(j):
        total = acc[fsdp - 1, j]
        edge = hrecv[0, j]
        for d in range(1, fsdp):
            for h in range(HALVES):
                part_copy(d, j, h).wait_recv()
            total = total + precv[d - 1, j].astype(F32)
            edge = edge + hrecv[d, j]
        now = total.astype(BF16).astype(F32)
        edge = edge.astype(BF16).astype(F32)
        before = edge[7:8]
        earlier = edge[6:7]
        one = jnp.where(row_ids == 0, before, pltpu.roll(now, 1, 0))
        two = jnp.where(
            row_ids == 0, earlier, jnp.where(row_ids == 1, before, pltpu.roll(now, 2, 0))
        )
        return (
            short[0, j : j + 1, :] * now
            + short[1, j : j + 1, :] * one
            + short[2, j : j + 1, :] * two
        )

    halo_wait(0)
    prod = (branch(1) * branch(2)).astype(BF16).astype(F32)
    gsend[...] = jnp.transpose(prod).astype(BF16).reshape(groups, per, rows)
    exchange_start(1, gsend, grecv)
    product[...] = prod * gain[...]

    for d in range(1, fsdp + 1):
        spot = lax.rem(f + d, fsdp)
        term = jnp.dot(held[spot, 0], w[0, 0], preferred_element_type=F32)
        for k in range(1, chunks):
            term += jnp.dot(held[spot, k], w[0, k], preferred_element_type=F32)
        acc[d - 1, 0] = term
        if d < fsdp:
            psend[d - 1, 0] = term.astype(BF16)

    exchange_wait(0, tsend, trecv)
    tapspec[...] = spectrum(trecv[...].reshape(width, rows))
    exchange_wait(1, gsend, grecv)
    for d in range(1, fsdp + 1):
        if d < fsdp:
            for h in range(HALVES):
                part_copy(d, 0, h).start()
        halo_start(d, 1)

    x = spectrum(grecv[...].reshape(width, rows)).astype(F32)
    t = tapspec[...].astype(F32)
    xr, xi = x[:, :rows], x[:, rows:]
    tr, ti = t[:, :rows], t[:, rows:]
    real_z = (xr * tr - xi * ti).astype(BF16)
    imag_z = (xr * ti + xi * tr).astype(BF16)
    z = jnp.concatenate([real_z, imag_z], axis=1)
    v = jnp.dot(z, behind[...], preferred_element_type=F32)
    vr, vi = v[:, :rows], v[:, rows:]
    real_w = (vr * twist[0] - vi * twist[1]).astype(BF16)
    imag_w = (vi * twist[0] + vr * twist[1]).astype(BF16)
    packed = jnp.concatenate([real_w, imag_w], axis=0)
    y = jnp.dot(last[...], packed, preferred_element_type=F32) * (1.0 / (bins * rows))
    csend[...] = y.astype(BF16).reshape(groups, per, rows)
    exchange_start(2, csend, crecv)
    halo_wait(1)
    query[...] = branch(0)
    exchange_wait(2, csend, crecv)
    conv = jnp.transpose(crecv[...].reshape(width, rows).astype(F32))
    out[...] = (query[...] * (conv + product[...])).astype(BF16)

    exchange_sent(0, tsend, trecv)
    exchange_sent(1, gsend, grecv)
    exchange_sent(2, csend, crecv)
    for d in range(1, fsdp + 1):
        for phase in range(2):

            @pl.when(halo_remote(d))
            def _():
                halo_copy(d, phase).wait_send()

    for d in range(1, fsdp):
        for h in range(HALVES):
            for j in range(3):
                part_copy(d, j, h).wait_send()
            for t in range(chunks // chan):
                forward_copy(d, h, t).wait_send()
    for h, k in [(h, k) for h in range(HALVES) for k in range(chunks)]:
        for i in range(share):
            token_copy(i, h, k, False).wait_send()


def per_device(sizes, tokens, proj_weight, short_weight, skip_gain, filter_taps):
    seq, fsdp, chan = sizes
    groups = seq * fsdp
    rows = tokens.shape[0]
    depth, branches, width = proj_weight.shape
    per = width // groups
    chunks = min(MOST_CHUNKS, depth // 128)
    made = tables(groups, per, rows)
    dma = pltpu.SemaphoreType.DMA
    vmem = pl.BlockSpec(memory_space=pltpu.VMEM)
    hbm = pl.BlockSpec(memory_space=pl.ANY)
    half = 2 * groups * per
    return pl.pallas_call(
        functools.partial(kernel, sizes),
        out_shape=jax.ShapeDtypeStruct((rows, width), BF16),
        in_specs=[hbm] * 10,
        out_specs=vmem,
        scratch_shapes=[
            pltpu.VMEM((branches, chunks, depth // chunks, width), BF16),
            pltpu.VMEM(made[0].shape, BF16),
            pltpu.VMEM(made[1].shape, BF16),
            pltpu.VMEM(made[2].shape, BF16),
            pltpu.VMEM(made[3].shape, BF16),
            pltpu.VMEM(made[4].shape, F32),
            pltpu.VMEM(short_weight.shape, F32),
            pltpu.VMEM((1, width), F32),
            pltpu.VMEM((rows, width), BF16),
            pltpu.VMEM((fsdp, chunks, rows, depth // chunks), BF16),
            pltpu.VMEM((fsdp, branches, rows, width), F32),
            pltpu.VMEM((fsdp - 1, branches, rows, width), BF16),
            pltpu.VMEM((fsdp - 1, branches, rows, width), BF16),
            pltpu.VMEM((fsdp, branches, 8, width), F32),
            pltpu.VMEM((rows, width), F32),
            pltpu.VMEM((rows, width), F32),
        ]
        + [pltpu.VMEM((groups, per, rows), BF16)] * 6
        + [
            pltpu.VMEM((half, 2 * rows), BF16),
            dma((10,)),
            dma((fsdp // chan, HALVES, chunks)),
            dma((fsdp, HALVES, chunks)),
            dma((fsdp - 1, HALVES, chunks // chan)),
            dma((fsdp - 1, branches, HALVES)),
            dma((fsdp - 1, branches, HALVES)),
            dma((fsdp, 2)),
            dma((fsdp, 2)),
            dma((3, groups)),
            dma((3, groups)),
        ],
        compiler_params=pltpu.CompilerParams(
            collective_id=0, has_side_effects=True, vmem_limit_bytes=60 * 1024 * 1024
        ),
        name="hyena",
    )(
        tokens,
        jnp.transpose(proj_weight, (1, 0, 2)).reshape(branches, chunks, depth // chunks, width),
        short_weight,
        skip_gain.reshape(1, width),
        filter_taps,
        *[jnp.asarray(table) for table in made],
    )


def causal_tables(rows):
    bf = ml_dtypes.bfloat16
    odd = 2 * np.arange(rows) + 1
    period = 4 * rows

    def angles(times):
        wrapped = (odd[:, None] * times[None, :]) % period
        return wrapped.astype(np.float64) * (2.0 * math.pi / period)

    ahead = angles(np.arange(rows))
    behind = angles(rows + np.arange(rows)).T
    forward = np.concatenate([np.cos(ahead), -np.sin(ahead)], axis=0)
    inverse = np.concatenate([np.cos(behind), -np.sin(behind)], axis=1) / rows
    return forward.astype(bf), inverse.astype(bf)


def chunk_spans(rows):
    head = rows - EDGE
    return [(at, min(at + CHUNK, head)) for at in range(0, head, CHUNK)]


def causal_kernel(
    seq,
    tokens,
    weight,
    short_h,
    gain_h,
    taps_h,
    forward_h,
    inverse_h,
    out,
    w,
    forward,
    inverse,
    short,
    gain,
    own,
    far,
    part_out,
    part_in,
    edge_out,
    edge_in,
    projected,
    halves,
    signal,
    taps,
    tapspec,
    response,
    query,
    query_out,
    query_in,
    query_edge_out,
    query_edge_in,
    mixed,
    result,
    final,
    load_sem,
    own_send,
    own_recv,
    far_send,
    far_recv,
    fwd_send,
    part_send,
    part_recv,
    edge_send,
    edge_recv,
    across_send,
    across_recv,
    up_send,
    up_recv,
    cross_send,
    cross_recv,
    taps_local,
    taps_x_send,
    taps_x_recv,
    taps_z_send,
    taps_z_recv,
    query_send,
    query_recv,
    query_edge_send,
    query_edge_recv,
    out_send,
    out_recv,
    out_local,
    ready,
):
    rows = tokens.shape[0]
    width = weight.shape[3]
    depth = weight.shape[2]
    lanes = width // 2
    bins = 2 * rows
    last = seq - 1
    spans = chunk_spans(rows)
    count = len(spans)
    pieces = [(rows - EDGE, rows), *spans]
    made = [*spans[:-1], (spans[-1][0], rows)]
    s = lax.axis_index("seq")
    f = lax.axis_index("fsdp")
    c = lax.axis_index("chan")
    g = 1 - f
    sibling = 1 - c
    holds = c == f
    goes_up = s < last
    across = {"fsdp": g}

    def half_of(value):
        return jnp.where(f == 0, value[:, :lanes], value[:, lanes:])

    def other_half(value):
        return jnp.where(f == 0, value[:, lanes:], value[:, :lanes])

    def rounded(value):
        return value.astype(BF16).astype(F32)

    def columns(h):
        return pl.ds(pl.multiple_of(h * lanes, lanes), lanes)

    def at(span):
        return pl.ds(span[0], span[1] - span[0])

    def remote(source, target, send, recv, device):
        return pltpu.make_async_remote_copy(
            src_ref=source,
            dst_ref=target,
            send_sem=send,
            recv_sem=recv,
            device_id=device,
            device_id_type=MESH,
        )

    def arrive(block, sem):
        pltpu.make_async_copy(block, block, sem).wait()

    own_load = pltpu.make_async_copy(tokens, own, own_recv)

    @pl.when(holds)
    def _():
        own_load.start()

    loads = [
        pltpu.make_async_copy(source, target, load_sem.at[i])
        for i, (source, target) in enumerate(
            [
                (weight.at[pl.ds(1, 2)], w.at[pl.ds(1, 2)]),
                (weight.at[pl.ds(0, 1)], w.at[pl.ds(0, 1)]),
                (forward_h, forward),
                (inverse_h, inverse),
                (short_h, short),
                (gain_h, gain),
            ]
        )
    ]
    for load in loads:
        load.start()
    taps_load = pltpu.make_async_copy(taps_h.at[:, columns(f)], taps.at[s, f], taps_local)
    taps_load.start()
    edge_in[...] = jnp.zeros_like(edge_in)
    query_edge_in[...] = jnp.zeros_like(query_edge_in)

    barrier = pltpu.get_barrier_semaphore()
    for device in [{"chan": sibling}, across, {"fsdp": g, "chan": sibling}]:
        pl.semaphore_signal(barrier, inc=1, device_id=device, device_id_type=MESH)
    for t in range(seq):
        for h in range(2):

            @pl.when(t > s)
            def _():
                pl.semaphore_signal(
                    barrier, inc=1, device_id={"seq": t, "fsdp": h}, device_id_type=MESH
                )

    pl.semaphore_wait(barrier, 3 + 2 * s)

    def token_copy(i, a):
        return remote(
            tokens.at[at(pieces[i]), pl.ds(a * depth, depth)],
            far.at[a, at(pieces[i])],
            far_send.at[i, a],
            far_recv.at[i, a],
            {"fsdp": g, "chan": a},
        )

    own_copy = remote(tokens, own, own_send, own_recv, {"chan": sibling})
    taps_x_copy = remote(
        taps_h.at[:, columns(g)], taps.at[s, f], taps_x_send, taps_x_recv, across
    )

    taps_x_copy.start()

    @pl.when(jnp.logical_not(holds))
    def _():
        for i in range(2):
            for a in range(2):
                token_copy(i, a).start()

    @pl.when(holds)
    def _():
        own_copy.start()

    for t in range(seq):
        for h in range(2):

            @pl.when(t < s)
            def _():
                pl.semaphore_signal(
                    ready, inc=1, device_id={"seq": t, "fsdp": h}, device_id_type=MESH
                )

    def part_copy(i):
        return remote(
            part_out.at[:, at(made[i])],
            part_in.at[:, at(made[i])],
            part_send.at[i],
            part_recv.at[i],
            across,
        )

    def query_copy(i):
        return remote(
            query_out.at[i], query_in.at[i], query_send.at[i], query_recv.at[i], across
        )

    def own_part(j):
        return jnp.dot(own[:, :depth], w[j, 0], preferred_element_type=F32) + jnp.dot(
            own[:, depth:], w[j, 1], preferred_element_type=F32
        )

    def far_part(j, span):
        rows_at = slice(*span)
        return jnp.dot(far[0, rows_at], w[j, 0], preferred_element_type=F32) + jnp.dot(
            far[1, rows_at], w[j, 1], preferred_element_type=F32
        )

    with jax.named_scope("own_rows"):
        arrive(own, own_recv)
        loads[0].wait()
        for j in range(2):
            term = own_part(j + 1)
            part_out[j] = term.astype(BF16)
            edge_out[0, j] = term[rows - 8 :]
        part_copy(0).start()

        @pl.when(f == 0)
        def _():
            edge_in[0] = edge_out[0]

    with jax.named_scope("own_query"):
        for load in loads[1:]:
            load.wait()
        term = own_part(0)
        query[f] = half_of(term)
        query_out[0] = other_half(term).astype(BF16)

        @pl.when(f == 1)
        def _():
            query_edge_out[0] = term[rows - 8 :, :lanes]
            query_edge_out[1] = term[rows - 8 :, lanes:]

    def edge_up(i):
        return remote(
            edge_out.at[i],
            edge_in.at[i],
            edge_send.at[i],
            edge_recv.at[i],
            {"seq": jnp.minimum(s + 1, last), "fsdp": 1},
        )

    edge_across = remote(
        edge_out.at[1], edge_in.at[1], edge_send.at[1], edge_recv.at[1], {"fsdp": 0}
    )

    def query_edge(h):
        return remote(
            query_edge_out.at[h],
            query_edge_in.at[f],
            query_edge_send.at[h],
            query_edge_recv.at[f],
            {"seq": jnp.minimum(s + 1, last), "fsdp": h},
        )

    def taps_z_copy(t):
        return remote(
            taps.at[s], taps.at[s], taps_z_send.at[t], taps_z_recv.at[s], {"seq": t}
        )

    def forward_copy(i):
        block = far.at[c, at(pieces[i])]
        return remote(
            block, block, fwd_send.at[i], far_recv.at[i, c], {"chan": sibling}
        )

    def take(i):
        arrive(far.at[c, at(pieces[i])], far_recv.at[i, c])
        forward_copy(i).start()
        arrive(far.at[sibling, at(pieces[i])], far_recv.at[i, sibling])

    with jax.named_scope("edge_rows"):
        take(0)
        for j in range(2):
            term = far_part(j + 1, pieces[0])
            projected[j, 8 + rows - EDGE :] = term
            edge_out[1, j] = term[EDGE - 8 :]

        @pl.when(f == 1)
        def _():
            edge_across.start()

        @pl.when(jnp.logical_not(holds))
        def _():
            for i in range(2, count + 1):
                for a in range(2):
                    token_copy(i, a).start()

        for i in range(1, count):
            part_copy(i).start()

        @pl.when(goes_up)
        def _():
            pl.semaphore_wait(ready, 2 * (last - s))

            @pl.when(f == 1)
            def _():
                edge_up(0).start()
                for h in range(2):
                    query_edge(h).start()

        @pl.when(jnp.logical_and(f == 0, goes_up))
        def _():
            edge_up(1).start()
            term = far_part(0, pieces[0])
            query_edge_out[0] = term[EDGE - 8 :, :lanes]
            query_edge_out[1] = term[EDGE - 8 :, lanes:]
            for h in range(2):
                query_edge(h).start()

    with jax.named_scope("taps_up"):
        taps_load.wait()
        arrive(taps.at[s, g], taps_x_recv)
        for t in range(1, seq):

            @pl.when(t > s)
            def _():
                taps_z_copy(t).start()

    def across_copy(i):
        return remote(
            halves.at[g, at(made[i])],
            signal.at[s, g, at(made[i])],
            across_send.at[i],
            across_recv.at[i],
            across,
        )

    def up_copy(i, t):
        return remote(
            halves.at[f, at(made[i])],
            signal.at[s, g, at(made[i])],
            up_send.at[i, t],
            up_recv.at[s, i],
            {"seq": t},
        )

    def cross_copy(t):
        return remote(
            halves.at[g],
            signal.at[s, g],
            cross_send.at[t],
            cross_recv.at[s],
            {"seq": t, "fsdp": g},
        )

    def branch(j, span):
        low, high = span
        now = projected[j, 8 + low : 8 + high]
        one = projected[j, 7 + low : 7 + high]
        two = projected[j, 6 + low : 6 + high]
        return (
            short[0, j + 1 : j + 2, :] * now
            + short[1, j + 1 : j + 2, :] * one
            + short[2, j + 1 : j + 2, :] * two
        )

    def taps_spectrum():
        ids = lax.broadcasted_iota(jnp.int32, (bins, lanes), 0)
        sign = 1.0 - 2.0 * (ids % 2).astype(F32)
        for d in range(seq):

            @pl.when(d <= s)
            def _():
                @pl.when(d < s)
                def _():
                    arrive(taps.at[d], taps_z_recv.at[d])

                spec = jnp.dot(
                    forward[...], taps[d].reshape(bins, lanes), preferred_element_type=F32
                )
                real, imag = spec[:bins], spec[bins:]
                tapspec[d] = spec
                if d == 0:
                    response[0, 0] = sign * imag
                    response[0, 1] = -sign * real
                else:
                    response[d, 0] = tapspec[d - 1, :bins] + sign * imag
                    response[d, 1] = tapspec[d - 1, bins:] - sign * real

    for i in range(count):
        low, high = made[i]
        with jax.named_scope("tokens"):
            take(i + 1)
        with jax.named_scope("chunk"):
            for j in range(2):
                projected[j, 8 + spans[i][0] : 8 + spans[i][1]] = far_part(j + 1, spans[i])
        if i == 0:
            with jax.named_scope("edges"):

                @pl.when(jnp.logical_and(f == 1, s > 0))
                def _():
                    arrive(edge_in.at[0], edge_recv.at[0])

                @pl.when(jnp.logical_or(f == 0, s > 0))
                def _():
                    arrive(edge_in.at[1], edge_recv.at[1])

                for j in range(2):
                    projected[j, :8] = rounded(edge_in[0, j] + edge_in[1, j])
        with jax.named_scope("partial"):
            part_copy(i).wait_recv()
        with jax.named_scope("product"):
            for j in range(2):
                block = slice(8 + low, 8 + high)
                projected[j, block] = rounded(
                    projected[j, block] + part_in[j, low:high].astype(F32)
                )
            product = (branch(0, made[i]) * branch(1, made[i])).astype(BF16)
            halves[0, low:high] = product[:, :lanes]
            halves[1, low:high] = product[:, lanes:]
            across_copy(i).start()
            for t in range(1, seq):

                @pl.when(t > s)
                def _():
                    up_copy(i, t).start()

            signal[s, g, low:high] = half_of(product)
    with jax.named_scope("far_query"):
        query_copy(0).start()
        for t in range(1, seq):

            @pl.when(t > s)
            def _():
                cross_copy(t).start()

        term = far_part(0, (0, rows))
        query[g] = half_of(term)
        query_out[1] = other_half(term).astype(BF16)
        query_copy(1).start()

    def spectrum(j):
        spec = jnp.dot(
            forward[...], signal[j].reshape(bins, lanes), preferred_element_type=F32
        )
        real, imag = spec[:bins], spec[bins:]
        d = s - j
        hr, hi = response[d, 0], response[d, 1]
        return real * hr - imag * hi, real * hi + imag * hr

    with jax.named_scope("taps_spectra"):
        taps_spectrum()

    with jax.named_scope("earlier_slabs"):
        result[...] = jnp.zeros_like(result)
        for j in range(last):

            @pl.when(j < s)
            def _():
                for i in range(count):
                    arrive(signal.at[j, g, at(made[i])], up_recv.at[j, i])
                arrive(signal.at[j, f], cross_recv.at[j])
                real, imag = spectrum(j)
                result[0] += real
                result[1] += imag

    with jax.named_scope("query"):
        for i in range(2):
            query_copy(i).wait_recv()

        @pl.when(s > 0)
        def _():
            for i in range(2):
                arrive(query_edge_in.at[i], query_edge_recv.at[i])

        mixed[:8] = rounded(query_edge_in[0] + query_edge_in[1])
        other = pl.multiple_of(8 + g * rows, 8)
        mine = pl.multiple_of(8 + f * rows, 8)
        mixed[pl.ds(other, rows)] = rounded(query[g] + query_in[0].astype(F32))
        mixed[pl.ds(mine, rows)] = rounded(query[f] + query_in[1].astype(F32))
        gate = [half_of(short[i, 0:1, :]) for i in range(3)]
        gated = gate[0] * mixed[8 : 8 + bins] + gate[1] * mixed[7 : 7 + bins]
        gated += gate[2] * mixed[6 : 6 + bins]
        query[...] = gated.reshape(2, rows, lanes)

    with jax.named_scope("own_wait"):
        for i in range(count):
            arrive(signal.at[s, f, at(made[i])], across_recv.at[i])
    with jax.named_scope("own_slab"):
        real, imag = spectrum(s)
        packed = jnp.concatenate([result[0] + real, result[1] + imag], axis=0).astype(BF16)
        factor = half_of(gain[...])

        def finish(b):
            lines = pl.ds(pl.multiple_of(b * rows, rows), rows)
            conv = jnp.dot(inverse[lines, :], packed, preferred_element_type=F32)
            whole = conv + factor * signal[s, b].astype(F32)
            final[b] = (query[b] * whole).astype(BF16)

        out_across = remote(final.at[g], out.at[:, columns(f)], out_send, out_recv, across)
        out_here = pltpu.make_async_copy(final.at[f], out.at[:, columns(f)], out_local)
        finish(g)
        out_across.start()
        finish(f)
        out_here.start()

    with jax.named_scope("drain"):

        @pl.when(jnp.logical_not(holds))
        def _():
            for i in range(count + 1):
                for a in range(2):
                    token_copy(i, a).wait_send()

        @pl.when(holds)
        def _():
            own_copy.wait_send()

        taps_x_copy.wait_send()
        for i in range(count + 1):
            forward_copy(i).wait_send()
        for i in range(count):
            part_copy(i).wait_send()
            across_copy(i).wait_send()
        for i in range(2):
            query_copy(i).wait_send()

        @pl.when(f == 1)
        def _():
            edge_across.wait_send()

        @pl.when(goes_up)
        def _():
            edge_up(1 - f).wait_send()
            for h in range(2):
                query_edge(h).wait_send()

        for t in range(1, seq):

            @pl.when(t > s)
            def _():
                taps_z_copy(t).wait_send()
                cross_copy(t).wait_send()
                for i in range(count):
                    up_copy(i, t).wait_send()

    with jax.named_scope("out"):
        out_across.wait_send()
        out_here.wait()
        arrive(out.at[:, columns(g)], out_recv)


def causal_device(seq, tokens, proj_weight, short_weight, skip_gain, filter_taps):
    rows = tokens.shape[0]
    depth, branches, width = proj_weight.shape
    lanes = width // 2
    step = depth // 2
    forward, inverse = causal_tables(2 * rows)
    count = len(chunk_spans(rows))
    dma = pltpu.SemaphoreType.DMA
    hbm = pl.BlockSpec(memory_space=pl.ANY)
    scratch = [
        ((branches, 2, step, width), BF16),
        (forward.shape, BF16),
        (inverse.shape, BF16),
        (short_weight.shape, F32),
        ((1, width), F32),
        ((rows, depth), BF16),
        ((2, rows, step), BF16),
        ((2, rows, width), BF16),
        ((2, rows, width), BF16),
        ((2, 2, 8, width), F32),
        ((2, 2, 8, width), F32),
        ((2, 8 + rows, width), F32),
        ((2, rows, lanes), BF16),
        ((seq, 2, rows, lanes), BF16),
        ((seq, 2, rows, lanes), BF16),
        ((seq, 4 * rows, lanes), F32),
        ((seq, 2, 2 * rows, lanes), F32),
        ((2, rows, lanes), F32),
        ((2, rows, lanes), BF16),
        ((2, rows, lanes), BF16),
        ((2, 8, lanes), F32),
        ((2, 8, lanes), F32),
        ((8 + 2 * rows, lanes), F32),
        ((2, 2 * rows, lanes), F32),
        ((2, rows, lanes), BF16),
    ]
    sems = [
        (6,),
        (),
        (),
        (count + 1, 2),
        (count + 1, 2),
        (count + 1,),
        (count,),
        (count,),
        (2,),
        (2,),
        (count,),
        (count,),
        (count, seq),
        (seq, count),
        (seq,),
        (seq,),
        (),
        (),
        (),
        (seq,),
        (seq,),
        (2,),
        (2,),
        (2,),
        (2,),
        (),
        (),
        (),
    ]
    return pl.pallas_call(
        functools.partial(causal_kernel, seq),
        out_shape=jax.ShapeDtypeStruct((rows, width), BF16),
        in_specs=[hbm] * 7,
        out_specs=hbm,
        scratch_shapes=[pltpu.VMEM(shape, kind) for shape, kind in scratch]
        + [dma(shape) for shape in sems]
        + [pltpu.SemaphoreType.REGULAR],
        compiler_params=pltpu.CompilerParams(
            collective_id=0, has_side_effects=True, vmem_limit_bytes=60 * 1024 * 1024
        ),
        name="hyena",
    )(
        tokens,
        jnp.transpose(proj_weight, (1, 0, 2)).reshape(branches, 2, step, width),
        short_weight,
        skip_gain.reshape(1, width),
        filter_taps,
        jnp.asarray(forward),
        jnp.asarray(inverse),
    )


def solution(mesh):
    seq = mesh.shape["seq"]
    paired = mesh.shape["fsdp"] == 2 and mesh.shape["chan"] == 2
    sizes = (mesh.shape["seq"], mesh.shape["fsdp"], mesh.shape["chan"])
    in_specs = (
        P(("grp", "seq", "fsdp"), "chan"),
        P("fsdp", None, "chan"),
        P(None, None, "chan"),
        P("chan"),
        P(("seq", "fsdp"), "chan"),
    )
    out_specs = P(("grp", "seq", "fsdp"), "chan")
    return jax.shard_map(
        functools.partial(causal_device, seq)
        if paired
        else functools.partial(per_device, sizes),
        mesh=mesh,
        in_specs=in_specs,
        out_specs=out_specs,
        check_vma=False,
    )
```

```python
import functools
import math

import jax
import jax.numpy as jnp
import ml_dtypes
import numpy as np
from jax import lax
from jax.experimental import pallas as pl
from jax.experimental.pallas import tpu as pltpu
from jax.sharding import PartitionSpec as P

MESH = pl.DeviceIdType.MESH
BF16 = jnp.bfloat16
F32 = jnp.float32
MOST_CHUNKS = 2
HALVES = 2
EDGE = 16
CHUNK = 64


def phase_pair(rows, cols, period):
    wrapped = (np.arange(rows)[:, None] * np.arange(cols)[None, :]) % period
    phase = wrapped.astype(np.float32) * np.float32(2.0 * math.pi / period)
    return np.cos(phase), np.sin(phase)


def tables(groups, per, rows):
    bf = ml_dtypes.bfloat16
    bins = 2 * groups
    cos, sin = phase_pair(bins, groups, bins)
    eye = np.eye(per, dtype=np.float32)
    first = np.concatenate([np.kron(cos, eye), np.kron(-sin, eye)], axis=0).astype(bf)
    cos, sin = phase_pair(rows, rows, rows)
    ahead = np.block([[cos, -sin], [sin, cos]]).astype(bf)
    behind = np.block([[cos, sin], [-sin, cos]]).astype(bf)
    cos, sin = phase_pair(bins, rows, bins * rows)
    twist = np.stack([np.repeat(cos, per, axis=0), np.repeat(sin, per, axis=0)])
    last = np.ascontiguousarray(first.T)
    return first, last, ahead, behind, twist.astype(np.float32)


def kernel(
    sizes,
    tokens,
    weight,
    short_h,
    gain_h,
    taps_h,
    first_h,
    last_h,
    ahead_h,
    behind_h,
    twist_h,
    out,
    w,
    first,
    last,
    ahead,
    behind,
    twist,
    short,
    gain,
    taps,
    held,
    acc,
    psend,
    precv,
    hrecv,
    query,
    product,
    tsend,
    trecv,
    gsend,
    grecv,
    csend,
    crecv,
    tapspec,
    load_sem,
    tok_send,
    tok_recv,
    fwd_send,
    part_send,
    part_recv,
    halo_send,
    halo_recv,
    a2a_send,
    a2a_recv,
):
    seq, fsdp, chan = sizes
    groups = seq * fsdp
    rows = tokens.shape[0]
    chunks = weight.shape[1]
    lines = rows // HALVES
    depth = chunks * weight.shape[2]
    width = weight.shape[3]
    per = width // groups
    bins = 2 * groups
    step = depth // chunks
    share = fsdp // chan
    s = lax.axis_index("seq")
    f = lax.axis_index("fsdp")
    c = lax.axis_index("chan")
    me = s * fsdp + f

    loads = [
        pltpu.make_async_copy(source, target, load_sem.at[i])
        for i, (source, target) in enumerate(
            [
                (taps_h, taps),
                (weight.at[pl.ds(1, 2)], w.at[pl.ds(1, 2)]),
                (first_h, first),
                (ahead_h, ahead),
                (twist_h, twist),
                (last_h, last),
                (behind_h, behind),
                (short_h, short),
                (gain_h, gain),
                (weight.at[pl.ds(0, 1)], w.at[pl.ds(0, 1)]),
            ]
        )
    ]
    for load in loads:
        load.start()

    barrier = pltpu.get_barrier_semaphore()
    everyone = groups * chan

    def greet(k, carry):
        other = lax.rem(me * chan + c + k, everyone)
        spot = other // chan
        pl.semaphore_signal(
            barrier,
            inc=1,
            device_id={"seq": spot // fsdp, "fsdp": spot % fsdp, "chan": other % chan},
            device_id_type=MESH,
        )
        return carry

    lax.fori_loop(1, everyone, greet, 0, unroll=everyone <= 16)

    @pl.when(me == 0)
    def _():
        hrecv[...] = jnp.zeros_like(hrecv)

    loads[0].wait()
    tsend[...] = jnp.transpose(taps[...].astype(F32)).astype(BF16).reshape(groups, per, rows)
    pl.semaphore_wait(barrier, everyone - 1)

    sibling = lax.rem(c + 1, chan)

    def span(h):
        return pl.ds(h * lines, lines)

    def token_copy(i, h, k, same):
        return pltpu.make_async_remote_copy(
            src_ref=tokens.at[span(h), pl.ds(i * depth + k * step, step)],
            dst_ref=held.at[f, k, span(h)],
            send_sem=tok_send.at[i, h, k],
            recv_sem=tok_recv.at[f, h, k],
            device_id={"fsdp": c * share + i, "chan": sibling if same else k % chan},
            device_id_type=MESH,
        )

    for h, k in [(h, k) for h in range(HALVES) for k in range(chunks)]:
        for i in range(share):
            stays = c * share + i == f

            @pl.when(jnp.logical_not(stays))
            def _():
                token_copy(i, h, k, False).start()

            @pl.when(stays)
            def _():
                token_copy(i, h, k, True).start()
                pltpu.make_async_copy(
                    tokens.at[span(h), pl.ds(i * depth + k * step, step)],
                    held.at[f, k, span(h)],
                    tok_recv.at[f, h, k],
                ).start()

    def exchange_copy(which, source, target, k):
        other = lax.rem(me + k, groups)
        return pltpu.make_async_remote_copy(
            src_ref=source.at[other],
            dst_ref=target.at[me],
            send_sem=a2a_send.at[which, k],
            recv_sem=a2a_recv.at[which, k],
            device_id={"seq": other // fsdp, "fsdp": other % fsdp},
            device_id_type=MESH,
        )

    def exchange_start(which, source, target):
        def go(k, carry):
            exchange_copy(which, source, target, k).start()
            return carry

        lax.fori_loop(1, groups, go, 0, unroll=groups <= 8)
        target[me] = source[me]

    def exchange_wait(which, source, target):
        def go(k, carry):
            exchange_copy(which, source, target, k).wait_recv()
            return carry

        lax.fori_loop(1, groups, go, 0, unroll=groups <= 8)

    def exchange_sent(which, source, target):
        def go(k, carry):
            exchange_copy(which, source, target, k).wait_send()
            return carry

        lax.fori_loop(1, groups, go, 0)


    half = bins * per

    def spectrum(signal):
        a = jnp.dot(first[...], signal, preferred_element_type=F32)
        real_a, imag_a = a[:half], a[half:]
        real_b = (real_a * twist[0] + imag_a * twist[1]).astype(BF16)
        imag_b = (imag_a * twist[0] - real_a * twist[1]).astype(BF16)
        b = jnp.concatenate([real_b, imag_b], axis=1)
        return jnp.dot(b, ahead[...], preferred_element_type=F32).astype(BF16)

    def arrival(spot, h, k):
        block = held.at[spot, k, span(h)]
        pltpu.make_async_copy(block, block, tok_recv.at[spot, h, k]).wait()

    def forward_copy(d, h, t):
        k = t * chan + c
        block = held.at[lax.rem(f + d, fsdp), k, span(h)]
        return pltpu.make_async_remote_copy(
            src_ref=block,
            dst_ref=block,
            send_sem=fwd_send.at[d - 1, h, t],
            recv_sem=tok_recv.at[lax.rem(f + d, fsdp), h, k],
            device_id={"chan": sibling},
            device_id_type=MESH,
        )

    def part_copy(d, j, h):
        return pltpu.make_async_remote_copy(
            src_ref=psend.at[d - 1, j, span(h)],
            dst_ref=precv.at[d - 1, j, span(h)],
            send_sem=part_send.at[d - 1, j, h],
            recv_sem=part_recv.at[d - 1, j, h],
            device_id={"fsdp": lax.rem(f + d, fsdp)},
            device_id_type=MESH,
        )

    phases = ((1, 2), (0, 1))

    def halo_target(d):
        return s * fsdp + lax.rem(f + d, fsdp) + 1

    def halo_copy(d, phase):
        target = jnp.minimum(halo_target(d), groups - 1)
        start, count = phases[phase]
        return pltpu.make_async_remote_copy(
            src_ref=acc.at[d - 1, pl.ds(start, count), pl.ds(rows - 8, 8)],
            dst_ref=hrecv.at[f, pl.ds(start, count)],
            send_sem=halo_send.at[d - 1, phase],
            recv_sem=halo_recv.at[f, phase],
            device_id={"seq": target // fsdp, "fsdp": target % fsdp},
            device_id_type=MESH,
        )

    def halo_remote(d):
        target = halo_target(d)
        return jnp.logical_and(target < groups, target != me)

    def halo_start(d, phase):
        @pl.when(halo_remote(d))
        def _():
            halo_copy(d, phase).start()

        start, count = phases[phase]

        @pl.when(halo_target(d) == me)
        def _():
            hrecv[f, start : start + count] = acc[d - 1, start : start + count, rows - 8 :]

    def halo_wait(phase):
        start, count = phases[phase]
        for h in range(fsdp):
            local = jnp.logical_and(f > 0, f == h)

            @pl.when(jnp.logical_and(me > 0, jnp.logical_not(local)))
            def _():
                block = hrecv.at[h, pl.ds(start, count)]
                pltpu.make_async_copy(block, block, halo_recv.at[h, phase]).wait()

    loads[1].wait()
    for k in range(chunks):
        for h in range(HALVES):
            arrival(f, h, k)
        for j in (1, 2):
            term = jnp.dot(held[f, k], w[j, k], preferred_element_type=F32)
            acc[fsdp - 1, j] = term if k == 0 else acc[fsdp - 1, j] + term
    halo_start(fsdp, 0)

    for d in range(1, fsdp):
        spot = lax.rem(f + d, fsdp)
        for h, t, b in [
            (h, t, b)
            for h in range(HALVES)
            for t in range(chunks // chan)
            for b in range(chan)
        ]:
            k = t * chan + lax.rem(c + b, chan)
            arrival(spot, h, k)
            if b == 0:
                forward_copy(d, h, t).start()
            final = (t + 1) * chan == chunks and b == chan - 1
            at = slice(h * lines, (h + 1) * lines)
            for j in (1, 2):
                term = jnp.dot(held[spot, k, at], w[j, k], preferred_element_type=F32)
                if t > 0 or b > 0:
                    term = acc[d - 1, j, at] + term
                acc[d - 1, j, at] = term
                if final:
                    psend[d - 1, j, at] = term.astype(BF16)
                    part_copy(d, j, h).start()
        halo_start(d, 0)

    for load in loads[2:]:
        load.wait()
    exchange_start(0, tsend, trecv)

    row_ids = lax.broadcasted_iota(jnp.int32, (rows, width), 0)

    def branch(j):
        total = acc[fsdp - 1, j]
        edge = hrecv[0, j]
        for d in range(1, fsdp):
            for h in range(HALVES):
                part_copy(d, j, h).wait_recv()
            total = total + precv[d - 1, j].astype(F32)
            edge = edge + hrecv[d, j]
        now = total.astype(BF16).astype(F32)
        edge = edge.astype(BF16).astype(F32)
        before = edge[7:8]
        earlier = edge[6:7]
        one = jnp.where(row_ids == 0, before, pltpu.roll(now, 1, 0))
        two = jnp.where(
            row_ids == 0, earlier, jnp.where(row_ids == 1, before, pltpu.roll(now, 2, 0))
        )
        return (
            short[0, j : j + 1, :] * now
            + short[1, j : j + 1, :] * one
            + short[2, j : j + 1, :] * two
        )

    halo_wait(0)
    prod = (branch(1) * branch(2)).astype(BF16).astype(F32)
    gsend[...] = jnp.transpose(prod).astype(BF16).reshape(groups, per, rows)
    exchange_start(1, gsend, grecv)
    product[...] = prod * gain[...]

    for d in range(1, fsdp + 1):
        spot = lax.rem(f + d, fsdp)
        term = jnp.dot(held[spot, 0], w[0, 0], preferred_element_type=F32)
        for k in range(1, chunks):
            term += jnp.dot(held[spot, k], w[0, k], preferred_element_type=F32)
        acc[d - 1, 0] = term
        if d < fsdp:
            psend[d - 1, 0] = term.astype(BF16)

    exchange_wait(0, tsend, trecv)
    tapspec[...] = spectrum(trecv[...].reshape(width, rows))
    exchange_wait(1, gsend, grecv)
    for d in range(1, fsdp + 1):
        if d < fsdp:
            for h in range(HALVES):
                part_copy(d, 0, h).start()
        halo_start(d, 1)

    x = spectrum(grecv[...].reshape(width, rows)).astype(F32)
    t = tapspec[...].astype(F32)
    xr, xi = x[:, :rows], x[:, rows:]
    tr, ti = t[:, :rows], t[:, rows:]
    real_z = (xr * tr - xi * ti).astype(BF16)
    imag_z = (xr * ti + xi * tr).astype(BF16)
    z = jnp.concatenate([real_z, imag_z], axis=1)
    v = jnp.dot(z, behind[...], preferred_element_type=F32)
    vr, vi = v[:, :rows], v[:, rows:]
    real_w = (vr * twist[0] - vi * twist[1]).astype(BF16)
    imag_w = (vi * twist[0] + vr * twist[1]).astype(BF16)
    packed = jnp.concatenate([real_w, imag_w], axis=0)
    y = jnp.dot(last[...], packed, preferred_element_type=F32) * (1.0 / (bins * rows))
    csend[...] = y.astype(BF16).reshape(groups, per, rows)
    exchange_start(2, csend, crecv)
    halo_wait(1)
    query[...] = branch(0)
    exchange_wait(2, csend, crecv)
    conv = jnp.transpose(crecv[...].reshape(width, rows).astype(F32))
    out[...] = (query[...] * (conv + product[...])).astype(BF16)

    exchange_sent(0, tsend, trecv)
    exchange_sent(1, gsend, grecv)
    exchange_sent(2, csend, crecv)
    for d in range(1, fsdp + 1):
        for phase in range(2):

            @pl.when(halo_remote(d))
            def _():
                halo_copy(d, phase).wait_send()

    for d in range(1, fsdp):
        for h in range(HALVES):
            for j in range(3):
                part_copy(d, j, h).wait_send()
            for t in range(chunks // chan):
                forward_copy(d, h, t).wait_send()
    for h, k in [(h, k) for h in range(HALVES) for k in range(chunks)]:
        for i in range(share):
            token_copy(i, h, k, False).wait_send()


def per_device(sizes, tokens, proj_weight, short_weight, skip_gain, filter_taps):
    seq, fsdp, chan = sizes
    groups = seq * fsdp
    rows = tokens.shape[0]
    depth, branches, width = proj_weight.shape
    per = width // groups
    chunks = min(MOST_CHUNKS, depth // 128)
    made = tables(groups, per, rows)
    dma = pltpu.SemaphoreType.DMA
    vmem = pl.BlockSpec(memory_space=pltpu.VMEM)
    hbm = pl.BlockSpec(memory_space=pl.ANY)
    half = 2 * groups * per
    return pl.pallas_call(
        functools.partial(kernel, sizes),
        out_shape=jax.ShapeDtypeStruct((rows, width), BF16),
        in_specs=[hbm] * 10,
        out_specs=vmem,
        scratch_shapes=[
            pltpu.VMEM((branches, chunks, depth // chunks, width), BF16),
            pltpu.VMEM(made[0].shape, BF16),
            pltpu.VMEM(made[1].shape, BF16),
            pltpu.VMEM(made[2].shape, BF16),
            pltpu.VMEM(made[3].shape, BF16),
            pltpu.VMEM(made[4].shape, F32),
            pltpu.VMEM(short_weight.shape, F32),
            pltpu.VMEM((1, width), F32),
            pltpu.VMEM((rows, width), BF16),
            pltpu.VMEM((fsdp, chunks, rows, depth // chunks), BF16),
            pltpu.VMEM((fsdp, branches, rows, width), F32),
            pltpu.VMEM((fsdp - 1, branches, rows, width), BF16),
            pltpu.VMEM((fsdp - 1, branches, rows, width), BF16),
            pltpu.VMEM((fsdp, branches, 8, width), F32),
            pltpu.VMEM((rows, width), F32),
            pltpu.VMEM((rows, width), F32),
        ]
        + [pltpu.VMEM((groups, per, rows), BF16)] * 6
        + [
            pltpu.VMEM((half, 2 * rows), BF16),
            dma((10,)),
            dma((fsdp // chan, HALVES, chunks)),
            dma((fsdp, HALVES, chunks)),
            dma((fsdp - 1, HALVES, chunks // chan)),
            dma((fsdp - 1, branches, HALVES)),
            dma((fsdp - 1, branches, HALVES)),
            dma((fsdp, 2)),
            dma((fsdp, 2)),
            dma((3, groups)),
            dma((3, groups)),
        ],
        compiler_params=pltpu.CompilerParams(
            collective_id=0, has_side_effects=True, vmem_limit_bytes=60 * 1024 * 1024
        ),
        name="hyena",
    )(
        tokens,
        jnp.transpose(proj_weight, (1, 0, 2)).reshape(branches, chunks, depth // chunks, width),
        short_weight,
        skip_gain.reshape(1, width),
        filter_taps,
        *[jnp.asarray(table) for table in made],
    )


def causal_tables(rows):
    bf = ml_dtypes.bfloat16
    odd = 2 * np.arange(rows) + 1
    period = 4 * rows

    def angles(times):
        wrapped = (odd[:, None] * times[None, :]) % period
        return wrapped.astype(np.float64) * (2.0 * math.pi / period)

    ahead = angles(np.arange(rows))
    behind = angles(rows + np.arange(rows)).T
    forward = np.concatenate([np.cos(ahead), -np.sin(ahead)], axis=0)
    inverse = np.concatenate([np.cos(behind), -np.sin(behind)], axis=1) / rows
    return forward.astype(bf), inverse.astype(bf)


def chunk_spans(rows):
    head = rows - EDGE
    return [(at, min(at + CHUNK, head)) for at in range(0, head, CHUNK)]


def causal_kernel(
    seq,
    tokens,
    weight,
    short_h,
    gain_h,
    taps_h,
    forward_h,
    inverse_h,
    out,
    w,
    forward,
    inverse,
    short,
    gain,
    own,
    far,
    part_out,
    part_in,
    edge_out,
    edge_in,
    projected,
    halves,
    signal,
    taps,
    tapspec,
    response,
    query,
    query_out,
    query_in,
    query_edge_out,
    query_edge_in,
    mixed,
    result,
    final,
    load_sem,
    own_send,
    own_recv,
    far_send,
    far_recv,
    fwd_send,
    part_send,
    part_recv,
    edge_send,
    edge_recv,
    across_send,
    across_recv,
    up_send,
    up_recv,
    cross_send,
    cross_recv,
    taps_local,
    taps_x_send,
    taps_x_recv,
    taps_z_send,
    taps_z_recv,
    taps_y_send,
    taps_y_recv,
    query_send,
    query_recv,
    query_edge_send,
    query_edge_recv,
    out_send,
    out_recv,
    out_local,
    ready,
    near,
):
    rows = tokens.shape[0]
    width = weight.shape[3]
    depth = weight.shape[2]
    lanes = width // 2
    bins = 2 * rows
    last = seq - 1
    spans = chunk_spans(rows)
    count = len(spans)
    pieces = [(rows - EDGE, rows), *spans]
    made = [*spans[:-1], (spans[-1][0], rows)]
    group = lax.axis_index("grp")
    s = lax.axis_index("seq")
    f = lax.axis_index("fsdp")
    c = lax.axis_index("chan")
    g = 1 - f
    sibling = 1 - c
    holds = c == f
    goes_up = s < last
    across = {"fsdp": g}

    def half_of(value):
        return jnp.where(f == 0, value[:, :lanes], value[:, lanes:])

    def other_half(value):
        return jnp.where(f == 0, value[:, lanes:], value[:, :lanes])

    def rounded(value):
        return value.astype(BF16).astype(F32)

    def columns(h):
        return pl.ds(pl.multiple_of(h * lanes, lanes), lanes)

    def at(span):
        return pl.ds(span[0], span[1] - span[0])

    def remote(source, target, send, recv, device):
        return pltpu.make_async_remote_copy(
            src_ref=source,
            dst_ref=target,
            send_sem=send,
            recv_sem=recv,
            device_id=device,
            device_id_type=MESH,
        )

    def arrive(block, sem):
        pltpu.make_async_copy(block, block, sem).wait()

    own_load = pltpu.make_async_copy(tokens, own, own_recv)

    @pl.when(holds)
    def _():
        own_load.start()

    loads = [
        pltpu.make_async_copy(source, target, load_sem.at[i])
        for i, (source, target) in enumerate(
            [
                (weight.at[pl.ds(1, 2)], w.at[pl.ds(1, 2)]),
                (weight.at[pl.ds(0, 1)], w.at[pl.ds(0, 1)]),
                (forward_h, forward),
                (inverse_h, inverse),
                (short_h, short),
                (gain_h, gain),
            ]
        )
    ]
    for load in loads:
        load.start()
    taps_load = pltpu.make_async_copy(taps_h.at[:, columns(f)], taps.at[s, f], taps_local)
    taps_load.start()
    edge_in[...] = jnp.zeros_like(edge_in)
    query_edge_in[...] = jnp.zeros_like(query_edge_in)

    barrier = pltpu.get_barrier_semaphore()
    beside = {"grp": 1 - group}
    for device in [{"chan": sibling}, across, {"fsdp": g, "chan": sibling}]:
        pl.semaphore_signal(barrier, inc=1, device_id=device, device_id_type=MESH)

    @pl.when(f == 0)
    def _():
        pl.semaphore_signal(barrier, inc=1, device_id=beside, device_id_type=MESH)

    for t in range(seq):
        for h in range(2):

            @pl.when(t > s)
            def _():
                pl.semaphore_signal(
                    barrier, inc=1, device_id={"seq": t, "fsdp": h}, device_id_type=MESH
                )

    pl.semaphore_wait(barrier, 3 + g + 2 * s)

    def token_copy(i, a):
        return remote(
            tokens.at[at(pieces[i]), pl.ds(a * depth, depth)],
            far.at[a, at(pieces[i])],
            far_send.at[i, a],
            far_recv.at[i, a],
            {"fsdp": g, "chan": a},
        )

    own_copy = remote(tokens, own, own_send, own_recv, {"chan": sibling})
    share = pl.ds(pl.multiple_of(group * (rows // 2), rows // 2), rows // 2)
    rest = pl.ds(pl.multiple_of((1 - group) * (rows // 2), rows // 2), rows // 2)
    taps_x_copy = remote(
        taps_h.at[share, columns(g)],
        taps.at[s, f, share],
        taps_x_send,
        taps_x_recv,
        across,
    )

    taps_x_copy.start()

    @pl.when(jnp.logical_not(holds))
    def _():
        for i in range(2):
            for a in range(2):
                token_copy(i, a).start()

    @pl.when(holds)
    def _():
        own_copy.start()

    @pl.when(f == 0)
    def _():
        pl.semaphore_signal(near, inc=1, device_id=beside, device_id_type=MESH)

    for t in range(seq):
        for h in range(2):

            @pl.when(t < s)
            def _():
                pl.semaphore_signal(
                    ready, inc=1, device_id={"seq": t, "fsdp": h}, device_id_type=MESH
                )

    def part_copy(i):
        return remote(
            part_out.at[:, at(made[i])],
            part_in.at[:, at(made[i])],
            part_send.at[i],
            part_recv.at[i],
            across,
        )

    def query_copy(i):
        return remote(
            query_out.at[i], query_in.at[i], query_send.at[i], query_recv.at[i], across
        )

    def own_part(j):
        return jnp.dot(own[:, :depth], w[j, 0], preferred_element_type=F32) + jnp.dot(
            own[:, depth:], w[j, 1], preferred_element_type=F32
        )

    def far_part(j, span):
        rows_at = slice(*span)
        return jnp.dot(far[0, rows_at], w[j, 0], preferred_element_type=F32) + jnp.dot(
            far[1, rows_at], w[j, 1], preferred_element_type=F32
        )

    with jax.named_scope("own_rows"):
        arrive(own, own_recv)
        loads[0].wait()
        for j in range(2):
            term = own_part(j + 1)
            part_out[j] = term.astype(BF16)
            edge_out[0, j] = term[rows - 8 :]
        part_copy(0).start()

        @pl.when(f == 0)
        def _():
            edge_in[0] = edge_out[0]

    with jax.named_scope("own_query"):
        for load in loads[1:]:
            load.wait()
        term = own_part(0)
        query[f] = half_of(term)
        query_out[0] = other_half(term).astype(BF16)

        @pl.when(f == 1)
        def _():
            query_edge_out[0] = term[rows - 8 :, :lanes]
            query_edge_out[1] = term[rows - 8 :, lanes:]

    @pl.when(f == 0)
    def _():
        pl.semaphore_wait(near, 1)
        pl.semaphore_signal(near, inc=1, device_id=across, device_id_type=MESH)

    def edge_up(i):
        return remote(
            edge_out.at[i],
            edge_in.at[i],
            edge_send.at[i],
            edge_recv.at[i],
            {"seq": jnp.minimum(s + 1, last), "fsdp": 1},
        )

    edge_across = remote(
        edge_out.at[1], edge_in.at[1], edge_send.at[1], edge_recv.at[1], {"fsdp": 0}
    )

    def query_edge(h):
        return remote(
            query_edge_out.at[h],
            query_edge_in.at[f],
            query_edge_send.at[h],
            query_edge_recv.at[f],
            {"seq": jnp.minimum(s + 1, last), "fsdp": h},
        )

    def taps_z_copy(t):
        block = taps.at[s, :, share]
        return remote(block, block, taps_z_send.at[t], taps_z_recv.at[s], {"seq": t})

    def taps_y_copy(j):
        block = taps.at[j, :, share]
        return remote(block, block, taps_y_send.at[j], taps_y_recv.at[j], beside)

    own_taps_y = remote(
        taps.at[s, g, share],
        taps.at[s, g, share],
        taps_y_send.at[s],
        taps_y_recv.at[s],
        beside,
    )

    def forward_copy(i):
        block = far.at[c, at(pieces[i])]
        return remote(
            block, block, fwd_send.at[i], far_recv.at[i, c], {"chan": sibling}
        )

    def take(i):
        arrive(far.at[c, at(pieces[i])], far_recv.at[i, c])
        forward_copy(i).start()
        arrive(far.at[sibling, at(pieces[i])], far_recv.at[i, sibling])

    with jax.named_scope("edge_rows"):
        take(0)
        for j in range(2):
            term = far_part(j + 1, pieces[0])
            projected[j, 8 + rows - EDGE :] = term
            edge_out[1, j] = term[EDGE - 8 :]

        @pl.when(f == 1)
        def _():
            edge_across.start()

        @pl.when(jnp.logical_not(holds))
        def _():
            for i in range(2, count + 1):
                for a in range(2):
                    token_copy(i, a).start()

        for i in range(1, count):
            part_copy(i).start()

        @pl.when(goes_up)
        def _():
            pl.semaphore_wait(ready, 2 * (last - s))

            @pl.when(f == 1)
            def _():
                edge_up(0).start()
                for h in range(2):
                    query_edge(h).start()

        @pl.when(jnp.logical_and(f == 0, goes_up))
        def _():
            edge_up(1).start()
            term = far_part(0, pieces[0])
            query_edge_out[0] = term[EDGE - 8 :, :lanes]
            query_edge_out[1] = term[EDGE - 8 :, lanes:]
            for h in range(2):
                query_edge(h).start()

    with jax.named_scope("taps_up"):
        taps_load.wait()
        arrive(taps.at[s, g, share], taps_x_recv)
        for t in range(1, seq):

            @pl.when(t > s)
            def _():
                taps_z_copy(t).start()

        @pl.when(f == 1)
        def _():
            pl.semaphore_wait(near, 1)

        own_taps_y.start()

    def across_copy(i):
        return remote(
            halves.at[g, at(made[i])],
            signal.at[s, g, at(made[i])],
            across_send.at[i],
            across_recv.at[i],
            across,
        )

    def up_copy(i, t):
        return remote(
            halves.at[f, at(made[i])],
            signal.at[s, g, at(made[i])],
            up_send.at[i, t],
            up_recv.at[s, i],
            {"seq": t},
        )

    def cross_copy(t):
        return remote(
            halves.at[g],
            signal.at[s, g],
            cross_send.at[t],
            cross_recv.at[s],
            {"seq": t, "fsdp": g},
        )

    def branch(j, span):
        low, high = span
        now = projected[j, 8 + low : 8 + high]
        one = projected[j, 7 + low : 7 + high]
        two = projected[j, 6 + low : 6 + high]
        return (
            short[0, j + 1 : j + 2, :] * now
            + short[1, j + 1 : j + 2, :] * one
            + short[2, j + 1 : j + 2, :] * two
        )

    def taps_spectrum():
        ids = lax.broadcasted_iota(jnp.int32, (bins, lanes), 0)
        sign = 1.0 - 2.0 * (ids % 2).astype(F32)
        for d in range(seq):

            @pl.when(d <= s)
            def _():
                @pl.when(d < s)
                def _():
                    arrive(taps.at[d, :, rest], taps_y_recv.at[d])

                @pl.when(d == s)
                def _():
                    arrive(taps.at[s, g, rest], taps_y_recv.at[s])

                spec = jnp.dot(
                    forward[...], taps[d].reshape(bins, lanes), preferred_element_type=F32
                )
                real, imag = spec[:bins], spec[bins:]
                tapspec[d] = spec
                if d == 0:
                    response[0, 0] = sign * imag
                    response[0, 1] = -sign * real
                else:
                    response[d, 0] = tapspec[d - 1, :bins] + sign * imag
                    response[d, 1] = tapspec[d - 1, bins:] - sign * real

    for i in range(count):
        low, high = made[i]
        with jax.named_scope("tokens"):
            take(i + 1)
        with jax.named_scope("chunk"):
            for j in range(2):
                projected[j, 8 + spans[i][0] : 8 + spans[i][1]] = far_part(j + 1, spans[i])
        if i == 0:
            with jax.named_scope("edges"):

                @pl.when(jnp.logical_and(f == 1, s > 0))
                def _():
                    arrive(edge_in.at[0], edge_recv.at[0])

                @pl.when(jnp.logical_or(f == 0, s > 0))
                def _():
                    arrive(edge_in.at[1], edge_recv.at[1])

                for j in range(2):
                    projected[j, :8] = rounded(edge_in[0, j] + edge_in[1, j])
        with jax.named_scope("partial"):
            part_copy(i).wait_recv()
        with jax.named_scope("product"):
            for j in range(2):
                block = slice(8 + low, 8 + high)
                projected[j, block] = rounded(
                    projected[j, block] + part_in[j, low:high].astype(F32)
                )
            product = (branch(0, made[i]) * branch(1, made[i])).astype(BF16)
            halves[0, low:high] = product[:, :lanes]
            halves[1, low:high] = product[:, lanes:]
            across_copy(i).start()
            for t in range(1, seq):

                @pl.when(t > s)
                def _():
                    up_copy(i, t).start()

            signal[s, g, low:high] = half_of(product)
        if i == count - 1:
            query_copy(0).start()
            for t in range(1, seq):

                @pl.when(t > s)
                def _():
                    cross_copy(t).start()

        with jax.named_scope("far_query"):
            term = far_part(0, made[i])
            query[g, low:high] = half_of(term)
            query_out[1, low:high] = other_half(term).astype(BF16)
        if i == 0:
            with jax.named_scope("taps_side"):
                for t in range(last):

                    @pl.when(t < s)
                    def _():
                        arrive(taps.at[t, :, share], taps_z_recv.at[t])
                        taps_y_copy(t).start()

    def spectrum(j):
        spec = jnp.dot(
            forward[...], signal[j].reshape(bins, lanes), preferred_element_type=F32
        )
        real, imag = spec[:bins], spec[bins:]
        d = s - j
        hr, hi = response[d, 0], response[d, 1]
        return real * hr - imag * hi, real * hi + imag * hr

    query_copy(1).start()
    with jax.named_scope("taps_spectra"):
        taps_spectrum()

    with jax.named_scope("earlier_slabs"):
        result[...] = jnp.zeros_like(result)
        for j in range(last):

            @pl.when(j < s)
            def _():
                for i in range(count):
                    arrive(signal.at[j, g, at(made[i])], up_recv.at[j, i])
                arrive(signal.at[j, f], cross_recv.at[j])
                real, imag = spectrum(j)
                result[0] += real
                result[1] += imag

    with jax.named_scope("query"):
        for i in range(2):
            query_copy(i).wait_recv()

        @pl.when(s > 0)
        def _():
            for i in range(2):
                arrive(query_edge_in.at[i], query_edge_recv.at[i])

        mixed[:8] = rounded(query_edge_in[0] + query_edge_in[1])
        other = pl.multiple_of(8 + g * rows, 8)
        mine = pl.multiple_of(8 + f * rows, 8)
        mixed[pl.ds(other, rows)] = rounded(query[g] + query_in[0].astype(F32))
        mixed[pl.ds(mine, rows)] = rounded(query[f] + query_in[1].astype(F32))
        gate = [half_of(short[i, 0:1, :]) for i in range(3)]
        gated = gate[0] * mixed[8 : 8 + bins] + gate[1] * mixed[7 : 7 + bins]
        gated += gate[2] * mixed[6 : 6 + bins]
        query[...] = gated.reshape(2, rows, lanes)

    with jax.named_scope("own_wait"):
        for i in range(count):
            arrive(signal.at[s, f, at(made[i])], across_recv.at[i])
    with jax.named_scope("own_slab"):
        real, imag = spectrum(s)
        packed = jnp.concatenate([result[0] + real, result[1] + imag], axis=0).astype(BF16)
        factor = half_of(gain[...])

        def finish(b):
            lines = pl.ds(pl.multiple_of(b * rows, rows), rows)
            conv = jnp.dot(inverse[lines, :], packed, preferred_element_type=F32)
            whole = conv + factor * signal[s, b].astype(F32)
            final[b] = (query[b] * whole).astype(BF16)

        out_across = remote(final.at[g], out.at[:, columns(f)], out_send, out_recv, across)
        out_here = pltpu.make_async_copy(final.at[f], out.at[:, columns(f)], out_local)
        finish(g)
        out_across.start()
        finish(f)
        out_here.start()

    with jax.named_scope("drain"):

        @pl.when(jnp.logical_not(holds))
        def _():
            for i in range(count + 1):
                for a in range(2):
                    token_copy(i, a).wait_send()

        @pl.when(holds)
        def _():
            own_copy.wait_send()

        taps_x_copy.wait_send()
        for i in range(count + 1):
            forward_copy(i).wait_send()
        for i in range(count):
            part_copy(i).wait_send()
            across_copy(i).wait_send()
        own_taps_y.wait_send()
        for i in range(2):
            query_copy(i).wait_send()
        for t in range(last):

            @pl.when(t < s)
            def _():
                taps_y_copy(t).wait_send()


        @pl.when(f == 1)
        def _():
            edge_across.wait_send()

        @pl.when(goes_up)
        def _():
            edge_up(1 - f).wait_send()
            for h in range(2):
                query_edge(h).wait_send()

        for t in range(1, seq):

            @pl.when(t > s)
            def _():
                taps_z_copy(t).wait_send()
                cross_copy(t).wait_send()
                for i in range(count):
                    up_copy(i, t).wait_send()

    with jax.named_scope("out"):
        out_across.wait_send()
        out_here.wait()
        arrive(out.at[:, columns(g)], out_recv)


def causal_device(seq, tokens, proj_weight, short_weight, skip_gain, filter_taps):
    rows = tokens.shape[0]
    depth, branches, width = proj_weight.shape
    lanes = width // 2
    step = depth // 2
    forward, inverse = causal_tables(2 * rows)
    count = len(chunk_spans(rows))
    dma = pltpu.SemaphoreType.DMA
    hbm = pl.BlockSpec(memory_space=pl.ANY)
    scratch = [
        ((branches, 2, step, width), BF16),
        (forward.shape, BF16),
        (inverse.shape, BF16),
        (short_weight.shape, F32),
        ((1, width), F32),
        ((rows, depth), BF16),
        ((2, rows, step), BF16),
        ((2, rows, width), BF16),
        ((2, rows, width), BF16),
        ((2, 2, 8, width), F32),
        ((2, 2, 8, width), F32),
        ((2, 8 + rows, width), F32),
        ((2, rows, lanes), BF16),
        ((seq, 2, rows, lanes), BF16),
        ((seq, 2, rows, lanes), BF16),
        ((seq, 4 * rows, lanes), F32),
        ((seq, 2, 2 * rows, lanes), F32),
        ((2, rows, lanes), F32),
        ((2, rows, lanes), BF16),
        ((2, rows, lanes), BF16),
        ((2, 8, lanes), F32),
        ((2, 8, lanes), F32),
        ((8 + 2 * rows, lanes), F32),
        ((2, 2 * rows, lanes), F32),
        ((2, rows, lanes), BF16),
    ]
    sems = [
        (6,),
        (),
        (),
        (count + 1, 2),
        (count + 1, 2),
        (count + 1,),
        (count,),
        (count,),
        (2,),
        (2,),
        (count,),
        (count,),
        (count, seq),
        (seq, count),
        (seq,),
        (seq,),
        (),
        (),
        (),
        (seq,),
        (seq,),
        (seq,),
        (seq,),
        (2,),
        (2,),
        (2,),
        (2,),
        (),
        (),
        (),
    ]
    return pl.pallas_call(
        functools.partial(causal_kernel, seq),
        out_shape=jax.ShapeDtypeStruct((rows, width), BF16),
        in_specs=[hbm] * 7,
        out_specs=hbm,
        scratch_shapes=[pltpu.VMEM(shape, kind) for shape, kind in scratch]
        + [dma(shape) for shape in sems]
        + [pltpu.SemaphoreType.REGULAR] * 2,
        compiler_params=pltpu.CompilerParams(
            collective_id=0, has_side_effects=True, vmem_limit_bytes=60 * 1024 * 1024
        ),
        name="hyena",
    )(
        tokens,
        jnp.transpose(proj_weight, (1, 0, 2)).reshape(branches, 2, step, width),
        short_weight,
        skip_gain.reshape(1, width),
        filter_taps,
        jnp.asarray(forward),
        jnp.asarray(inverse),
    )


def solution(mesh):
    seq = mesh.shape["seq"]
    paired = all(mesh.shape[axis] == 2 for axis in ("grp", "fsdp", "chan"))
    sizes = (mesh.shape["seq"], mesh.shape["fsdp"], mesh.shape["chan"])
    in_specs = (
        P(("grp", "seq", "fsdp"), "chan"),
        P("fsdp", None, "chan"),
        P(None, None, "chan"),
        P("chan"),
        P(("seq", "fsdp"), "chan"),
    )
    out_specs = P(("grp", "seq", "fsdp"), "chan")
    return jax.shard_map(
        functools.partial(causal_device, seq)
        if paired
        else functools.partial(per_device, sizes),
        mesh=mesh,
        in_specs=in_specs,
        out_specs=out_specs,
        check_vma=False,
    )
```

```python
import functools
import math

import jax
import jax.numpy as jnp
import ml_dtypes
import numpy as np
from jax import lax
from jax.experimental import pallas as pl
from jax.experimental.pallas import tpu as pltpu
from jax.sharding import PartitionSpec as P

MESH = pl.DeviceIdType.MESH
BF16 = jnp.bfloat16
F32 = jnp.float32
MOST_CHUNKS = 2
HALVES = 2
EDGE = 16
CHUNK = 64


def phase_pair(rows, cols, period):
    wrapped = (np.arange(rows)[:, None] * np.arange(cols)[None, :]) % period
    phase = wrapped.astype(np.float32) * np.float32(2.0 * math.pi / period)
    return np.cos(phase), np.sin(phase)


def tables(groups, per, rows):
    bf = ml_dtypes.bfloat16
    bins = 2 * groups
    cos, sin = phase_pair(bins, groups, bins)
    eye = np.eye(per, dtype=np.float32)
    first = np.concatenate([np.kron(cos, eye), np.kron(-sin, eye)], axis=0).astype(bf)
    cos, sin = phase_pair(rows, rows, rows)
    ahead = np.block([[cos, -sin], [sin, cos]]).astype(bf)
    behind = np.block([[cos, sin], [-sin, cos]]).astype(bf)
    cos, sin = phase_pair(bins, rows, bins * rows)
    twist = np.stack([np.repeat(cos, per, axis=0), np.repeat(sin, per, axis=0)])
    last = np.ascontiguousarray(first.T)
    return first, last, ahead, behind, twist.astype(np.float32)


def kernel(
    sizes,
    tokens,
    weight,
    short_h,
    gain_h,
    taps_h,
    first_h,
    last_h,
    ahead_h,
    behind_h,
    twist_h,
    out,
    w,
    first,
    last,
    ahead,
    behind,
    twist,
    short,
    gain,
    taps,
    held,
    acc,
    psend,
    precv,
    hrecv,
    query,
    product,
    tsend,
    trecv,
    gsend,
    grecv,
    csend,
    crecv,
    tapspec,
    load_sem,
    tok_send,
    tok_recv,
    fwd_send,
    part_send,
    part_recv,
    halo_send,
    halo_recv,
    a2a_send,
    a2a_recv,
):
    seq, fsdp, chan = sizes
    groups = seq * fsdp
    rows = tokens.shape[0]
    chunks = weight.shape[1]
    lines = rows // HALVES
    depth = chunks * weight.shape[2]
    width = weight.shape[3]
    per = width // groups
    bins = 2 * groups
    step = depth // chunks
    share = fsdp // chan
    s = lax.axis_index("seq")
    f = lax.axis_index("fsdp")
    c = lax.axis_index("chan")
    me = s * fsdp + f

    loads = [
        pltpu.make_async_copy(source, target, load_sem.at[i])
        for i, (source, target) in enumerate(
            [
                (taps_h, taps),
                (weight.at[pl.ds(1, 2)], w.at[pl.ds(1, 2)]),
                (first_h, first),
                (ahead_h, ahead),
                (twist_h, twist),
                (last_h, last),
                (behind_h, behind),
                (short_h, short),
                (gain_h, gain),
                (weight.at[pl.ds(0, 1)], w.at[pl.ds(0, 1)]),
            ]
        )
    ]
    for load in loads:
        load.start()

    barrier = pltpu.get_barrier_semaphore()
    everyone = groups * chan

    def greet(k, carry):
        other = lax.rem(me * chan + c + k, everyone)
        spot = other // chan
        pl.semaphore_signal(
            barrier,
            inc=1,
            device_id={"seq": spot // fsdp, "fsdp": spot % fsdp, "chan": other % chan},
            device_id_type=MESH,
        )
        return carry

    lax.fori_loop(1, everyone, greet, 0, unroll=everyone <= 16)

    @pl.when(me == 0)
    def _():
        hrecv[...] = jnp.zeros_like(hrecv)

    loads[0].wait()
    tsend[...] = jnp.transpose(taps[...].astype(F32)).astype(BF16).reshape(groups, per, rows)
    pl.semaphore_wait(barrier, everyone - 1)

    sibling = lax.rem(c + 1, chan)

    def span(h):
        return pl.ds(h * lines, lines)

    def token_copy(i, h, k, same):
        return pltpu.make_async_remote_copy(
            src_ref=tokens.at[span(h), pl.ds(i * depth + k * step, step)],
            dst_ref=held.at[f, k, span(h)],
            send_sem=tok_send.at[i, h, k],
            recv_sem=tok_recv.at[f, h, k],
            device_id={"fsdp": c * share + i, "chan": sibling if same else k % chan},
            device_id_type=MESH,
        )

    for h, k in [(h, k) for h in range(HALVES) for k in range(chunks)]:
        for i in range(share):
            stays = c * share + i == f

            @pl.when(jnp.logical_not(stays))
            def _():
                token_copy(i, h, k, False).start()

            @pl.when(stays)
            def _():
                token_copy(i, h, k, True).start()
                pltpu.make_async_copy(
                    tokens.at[span(h), pl.ds(i * depth + k * step, step)],
                    held.at[f, k, span(h)],
                    tok_recv.at[f, h, k],
                ).start()

    def exchange_copy(which, source, target, k):
        other = lax.rem(me + k, groups)
        return pltpu.make_async_remote_copy(
            src_ref=source.at[other],
            dst_ref=target.at[me],
            send_sem=a2a_send.at[which, k],
            recv_sem=a2a_recv.at[which, k],
            device_id={"seq": other // fsdp, "fsdp": other % fsdp},
            device_id_type=MESH,
        )

    def exchange_start(which, source, target):
        def go(k, carry):
            exchange_copy(which, source, target, k).start()
            return carry

        lax.fori_loop(1, groups, go, 0, unroll=groups <= 8)
        target[me] = source[me]

    def exchange_wait(which, source, target):
        def go(k, carry):
            exchange_copy(which, source, target, k).wait_recv()
            return carry

        lax.fori_loop(1, groups, go, 0, unroll=groups <= 8)

    def exchange_sent(which, source, target):
        def go(k, carry):
            exchange_copy(which, source, target, k).wait_send()
            return carry

        lax.fori_loop(1, groups, go, 0)


    half = bins * per

    def spectrum(signal):
        a = jnp.dot(first[...], signal, preferred_element_type=F32)
        real_a, imag_a = a[:half], a[half:]
        real_b = (real_a * twist[0] + imag_a * twist[1]).astype(BF16)
        imag_b = (imag_a * twist[0] - real_a * twist[1]).astype(BF16)
        b = jnp.concatenate([real_b, imag_b], axis=1)
        return jnp.dot(b, ahead[...], preferred_element_type=F32).astype(BF16)

    def arrival(spot, h, k):
        block = held.at[spot, k, span(h)]
        pltpu.make_async_copy(block, block, tok_recv.at[spot, h, k]).wait()

    def forward_copy(d, h, t):
        k = t * chan + c
        block = held.at[lax.rem(f + d, fsdp), k, span(h)]
        return pltpu.make_async_remote_copy(
            src_ref=block,
            dst_ref=block,
            send_sem=fwd_send.at[d - 1, h, t],
            recv_sem=tok_recv.at[lax.rem(f + d, fsdp), h, k],
            device_id={"chan": sibling},
            device_id_type=MESH,
        )

    def part_copy(d, j, h):
        return pltpu.make_async_remote_copy(
            src_ref=psend.at[d - 1, j, span(h)],
            dst_ref=precv.at[d - 1, j, span(h)],
            send_sem=part_send.at[d - 1, j, h],
            recv_sem=part_recv.at[d - 1, j, h],
            device_id={"fsdp": lax.rem(f + d, fsdp)},
            device_id_type=MESH,
        )

    phases = ((1, 2), (0, 1))

    def halo_target(d):
        return s * fsdp + lax.rem(f + d, fsdp) + 1

    def halo_copy(d, phase):
        target = jnp.minimum(halo_target(d), groups - 1)
        start, count = phases[phase]
        return pltpu.make_async_remote_copy(
            src_ref=acc.at[d - 1, pl.ds(start, count), pl.ds(rows - 8, 8)],
            dst_ref=hrecv.at[f, pl.ds(start, count)],
            send_sem=halo_send.at[d - 1, phase],
            recv_sem=halo_recv.at[f, phase],
            device_id={"seq": target // fsdp, "fsdp": target % fsdp},
            device_id_type=MESH,
        )

    def halo_remote(d):
        target = halo_target(d)
        return jnp.logical_and(target < groups, target != me)

    def halo_start(d, phase):
        @pl.when(halo_remote(d))
        def _():
            halo_copy(d, phase).start()

        start, count = phases[phase]

        @pl.when(halo_target(d) == me)
        def _():
            hrecv[f, start : start + count] = acc[d - 1, start : start + count, rows - 8 :]

    def halo_wait(phase):
        start, count = phases[phase]
        for h in range(fsdp):
            local = jnp.logical_and(f > 0, f == h)

            @pl.when(jnp.logical_and(me > 0, jnp.logical_not(local)))
            def _():
                block = hrecv.at[h, pl.ds(start, count)]
                pltpu.make_async_copy(block, block, halo_recv.at[h, phase]).wait()

    loads[1].wait()
    for k in range(chunks):
        for h in range(HALVES):
            arrival(f, h, k)
        for j in (1, 2):
            term = jnp.dot(held[f, k], w[j, k], preferred_element_type=F32)
            acc[fsdp - 1, j] = term if k == 0 else acc[fsdp - 1, j] + term
    halo_start(fsdp, 0)

    for d in range(1, fsdp):
        spot = lax.rem(f + d, fsdp)
        for h, t, b in [
            (h, t, b)
            for h in range(HALVES)
            for t in range(chunks // chan)
            for b in range(chan)
        ]:
            k = t * chan + lax.rem(c + b, chan)
            arrival(spot, h, k)
            if b == 0:
                forward_copy(d, h, t).start()
            final = (t + 1) * chan == chunks and b == chan - 1
            at = slice(h * lines, (h + 1) * lines)
            for j in (1, 2):
                term = jnp.dot(held[spot, k, at], w[j, k], preferred_element_type=F32)
                if t > 0 or b > 0:
                    term = acc[d - 1, j, at] + term
                acc[d - 1, j, at] = term
                if final:
                    psend[d - 1, j, at] = term.astype(BF16)
                    part_copy(d, j, h).start()
        halo_start(d, 0)

    for load in loads[2:]:
        load.wait()
    exchange_start(0, tsend, trecv)

    row_ids = lax.broadcasted_iota(jnp.int32, (rows, width), 0)

    def branch(j):
        total = acc[fsdp - 1, j]
        edge = hrecv[0, j]
        for d in range(1, fsdp):
            for h in range(HALVES):
                part_copy(d, j, h).wait_recv()
            total = total + precv[d - 1, j].astype(F32)
            edge = edge + hrecv[d, j]
        now = total.astype(BF16).astype(F32)
        edge = edge.astype(BF16).astype(F32)
        before = edge[7:8]
        earlier = edge[6:7]
        one = jnp.where(row_ids == 0, before, pltpu.roll(now, 1, 0))
        two = jnp.where(
            row_ids == 0, earlier, jnp.where(row_ids == 1, before, pltpu.roll(now, 2, 0))
        )
        return (
            short[0, j : j + 1, :] * now
            + short[1, j : j + 1, :] * one
            + short[2, j : j + 1, :] * two
        )

    halo_wait(0)
    prod = (branch(1) * branch(2)).astype(BF16).astype(F32)
    gsend[...] = jnp.transpose(prod).astype(BF16).reshape(groups, per, rows)
    exchange_start(1, gsend, grecv)
    product[...] = prod * gain[...]

    for d in range(1, fsdp + 1):
        spot = lax.rem(f + d, fsdp)
        term = jnp.dot(held[spot, 0], w[0, 0], preferred_element_type=F32)
        for k in range(1, chunks):
            term += jnp.dot(held[spot, k], w[0, k], preferred_element_type=F32)
        acc[d - 1, 0] = term
        if d < fsdp:
            psend[d - 1, 0] = term.astype(BF16)

    exchange_wait(0, tsend, trecv)
    tapspec[...] = spectrum(trecv[...].reshape(width, rows))
    exchange_wait(1, gsend, grecv)
    for d in range(1, fsdp + 1):
        if d < fsdp:
            for h in range(HALVES):
                part_copy(d, 0, h).start()
        halo_start(d, 1)

    x = spectrum(grecv[...].reshape(width, rows)).astype(F32)
    t = tapspec[...].astype(F32)
    xr, xi = x[:, :rows], x[:, rows:]
    tr, ti = t[:, :rows], t[:, rows:]
    real_z = (xr * tr - xi * ti).astype(BF16)
    imag_z = (xr * ti + xi * tr).astype(BF16)
    z = jnp.concatenate([real_z, imag_z], axis=1)
    v = jnp.dot(z, behind[...], preferred_element_type=F32)
    vr, vi = v[:, :rows], v[:, rows:]
    real_w = (vr * twist[0] - vi * twist[1]).astype(BF16)
    imag_w = (vi * twist[0] + vr * twist[1]).astype(BF16)
    packed = jnp.concatenate([real_w, imag_w], axis=0)
    y = jnp.dot(last[...], packed, preferred_element_type=F32) * (1.0 / (bins * rows))
    csend[...] = y.astype(BF16).reshape(groups, per, rows)
    exchange_start(2, csend, crecv)
    halo_wait(1)
    query[...] = branch(0)
    exchange_wait(2, csend, crecv)
    conv = jnp.transpose(crecv[...].reshape(width, rows).astype(F32))
    out[...] = (query[...] * (conv + product[...])).astype(BF16)

    exchange_sent(0, tsend, trecv)
    exchange_sent(1, gsend, grecv)
    exchange_sent(2, csend, crecv)
    for d in range(1, fsdp + 1):
        for phase in range(2):

            @pl.when(halo_remote(d))
            def _():
                halo_copy(d, phase).wait_send()

    for d in range(1, fsdp):
        for h in range(HALVES):
            for j in range(3):
                part_copy(d, j, h).wait_send()
            for t in range(chunks // chan):
                forward_copy(d, h, t).wait_send()
    for h, k in [(h, k) for h in range(HALVES) for k in range(chunks)]:
        for i in range(share):
            token_copy(i, h, k, False).wait_send()


def per_device(sizes, tokens, proj_weight, short_weight, skip_gain, filter_taps):
    seq, fsdp, chan = sizes
    groups = seq * fsdp
    rows = tokens.shape[0]
    depth, branches, width = proj_weight.shape
    per = width // groups
    chunks = min(MOST_CHUNKS, depth // 128)
    made = tables(groups, per, rows)
    dma = pltpu.SemaphoreType.DMA
    vmem = pl.BlockSpec(memory_space=pltpu.VMEM)
    hbm = pl.BlockSpec(memory_space=pl.ANY)
    half = 2 * groups * per
    return pl.pallas_call(
        functools.partial(kernel, sizes),
        out_shape=jax.ShapeDtypeStruct((rows, width), BF16),
        in_specs=[hbm] * 10,
        out_specs=vmem,
        scratch_shapes=[
            pltpu.VMEM((branches, chunks, depth // chunks, width), BF16),
            pltpu.VMEM(made[0].shape, BF16),
            pltpu.VMEM(made[1].shape, BF16),
            pltpu.VMEM(made[2].shape, BF16),
            pltpu.VMEM(made[3].shape, BF16),
            pltpu.VMEM(made[4].shape, F32),
            pltpu.VMEM(short_weight.shape, F32),
            pltpu.VMEM((1, width), F32),
            pltpu.VMEM((rows, width), BF16),
            pltpu.VMEM((fsdp, chunks, rows, depth // chunks), BF16),
            pltpu.VMEM((fsdp, branches, rows, width), F32),
            pltpu.VMEM((fsdp - 1, branches, rows, width), BF16),
            pltpu.VMEM((fsdp - 1, branches, rows, width), BF16),
            pltpu.VMEM((fsdp, branches, 8, width), F32),
            pltpu.VMEM((rows, width), F32),
            pltpu.VMEM((rows, width), F32),
        ]
        + [pltpu.VMEM((groups, per, rows), BF16)] * 6
        + [
            pltpu.VMEM((half, 2 * rows), BF16),
            dma((10,)),
            dma((fsdp // chan, HALVES, chunks)),
            dma((fsdp, HALVES, chunks)),
            dma((fsdp - 1, HALVES, chunks // chan)),
            dma((fsdp - 1, branches, HALVES)),
            dma((fsdp - 1, branches, HALVES)),
            dma((fsdp, 2)),
            dma((fsdp, 2)),
            dma((3, groups)),
            dma((3, groups)),
        ],
        compiler_params=pltpu.CompilerParams(
            collective_id=0, has_side_effects=True, vmem_limit_bytes=60 * 1024 * 1024
        ),
        name="hyena",
    )(
        tokens,
        jnp.transpose(proj_weight, (1, 0, 2)).reshape(branches, chunks, depth // chunks, width),
        short_weight,
        skip_gain.reshape(1, width),
        filter_taps,
        *[jnp.asarray(table) for table in made],
    )


def causal_tables(rows):
    bf = ml_dtypes.bfloat16
    odd = 2 * np.arange(rows) + 1
    period = 4 * rows

    def angles(times):
        wrapped = (odd[:, None] * times[None, :]) % period
        return wrapped.astype(np.float64) * (2.0 * math.pi / period)

    ahead = angles(np.arange(rows))
    behind = angles(rows + np.arange(rows)).T
    forward = np.concatenate([np.cos(ahead), -np.sin(ahead)], axis=0)
    inverse = np.concatenate([np.cos(behind), -np.sin(behind)], axis=1) / rows
    return forward.astype(bf), inverse.astype(bf)


def chunk_spans(rows):
    head = rows - EDGE
    return [(at, min(at + CHUNK, head)) for at in range(0, head, CHUNK)]


def causal_kernel(
    seq,
    tokens,
    weight,
    short_h,
    gain_h,
    taps_h,
    forward_h,
    inverse_h,
    out,
    w,
    forward,
    inverse,
    short,
    gain,
    own,
    far,
    part_out,
    part_in,
    edge_out,
    edge_in,
    projected,
    halves,
    signal,
    taps,
    tapspec,
    response,
    query,
    query_out,
    query_in,
    query_edge_out,
    query_edge_in,
    mixed,
    result,
    final,
    load_sem,
    own_send,
    own_recv,
    far_send,
    far_recv,
    fwd_send,
    part_send,
    part_recv,
    edge_send,
    edge_recv,
    across_send,
    across_recv,
    up_send,
    up_recv,
    cross_send,
    cross_recv,
    taps_local,
    taps_x_send,
    taps_x_recv,
    taps_z_send,
    taps_z_recv,
    taps_y_send,
    taps_y_recv,
    query_send,
    query_recv,
    query_edge_send,
    query_edge_recv,
    out_send,
    out_recv,
    out_local,
    ready,
    near,
):
    rows = tokens.shape[0]
    width = weight.shape[3]
    depth = weight.shape[2]
    lanes = width // 2
    bins = 2 * rows
    last = seq - 1
    spans = chunk_spans(rows)
    count = len(spans)
    pieces = [(rows - EDGE, rows), *spans]
    made = [*spans[:-1], (spans[-1][0], rows)]
    group = lax.axis_index("grp")
    s = lax.axis_index("seq")
    f = lax.axis_index("fsdp")
    c = lax.axis_index("chan")
    g = 1 - f
    sibling = 1 - c
    holds = c == f
    goes_up = s < last
    across = {"fsdp": g}

    def half_of(value):
        return jnp.where(f == 0, value[:, :lanes], value[:, lanes:])

    def other_half(value):
        return jnp.where(f == 0, value[:, lanes:], value[:, :lanes])

    def rounded(value):
        return value.astype(BF16).astype(F32)

    def columns(h):
        return pl.ds(pl.multiple_of(h * lanes, lanes), lanes)

    def at(span):
        return pl.ds(span[0], span[1] - span[0])

    def remote(source, target, send, recv, device):
        return pltpu.make_async_remote_copy(
            src_ref=source,
            dst_ref=target,
            send_sem=send,
            recv_sem=recv,
            device_id=device,
            device_id_type=MESH,
        )

    def arrive(block, sem):
        pltpu.make_async_copy(block, block, sem).wait()

    own_load = pltpu.make_async_copy(tokens, own, own_recv)

    @pl.when(holds)
    def _():
        own_load.start()

    loads = [
        pltpu.make_async_copy(source, target, load_sem.at[i])
        for i, (source, target) in enumerate(
            [
                (weight.at[pl.ds(1, 2)], w.at[pl.ds(1, 2)]),
                (weight.at[pl.ds(0, 1)], w.at[pl.ds(0, 1)]),
                (forward_h, forward),
                (inverse_h, inverse),
                (short_h, short),
                (gain_h, gain),
            ]
        )
    ]
    for load in loads:
        load.start()
    taps_load = pltpu.make_async_copy(taps_h.at[:, columns(f)], taps.at[s, f], taps_local)
    taps_load.start()
    edge_in[...] = jnp.zeros_like(edge_in)
    query_edge_in[...] = jnp.zeros_like(query_edge_in)

    barrier = pltpu.get_barrier_semaphore()
    beside = {"grp": 1 - group}
    for device in [{"chan": sibling}, across, {"fsdp": g, "chan": sibling}]:
        pl.semaphore_signal(barrier, inc=1, device_id=device, device_id_type=MESH)

    @pl.when(f == 0)
    def _():
        pl.semaphore_signal(barrier, inc=1, device_id=beside, device_id_type=MESH)

    for t in range(seq):
        for h in range(2):

            @pl.when(t > s)
            def _():
                pl.semaphore_signal(
                    barrier, inc=1, device_id={"seq": t, "fsdp": h}, device_id_type=MESH
                )

    pl.semaphore_wait(barrier, 3 + g + 2 * s)

    def token_copy(i, a):
        return remote(
            tokens.at[at(pieces[i]), pl.ds(a * depth, depth)],
            far.at[a, at(pieces[i])],
            far_send.at[i, a],
            far_recv.at[i, a],
            {"fsdp": g, "chan": a},
        )

    own_copy = remote(tokens, own, own_send, own_recv, {"chan": sibling})
    share = pl.ds(pl.multiple_of(group * (rows // 2), rows // 2), rows // 2)
    rest = pl.ds(pl.multiple_of((1 - group) * (rows // 2), rows // 2), rows // 2)
    taps_x_copy = remote(
        taps_h.at[share, columns(g)],
        taps.at[s, f, share],
        taps_x_send,
        taps_x_recv,
        across,
    )

    taps_x_copy.start()

    @pl.when(jnp.logical_not(holds))
    def _():
        for i in range(2):
            for a in range(2):
                token_copy(i, a).start()

    @pl.when(holds)
    def _():
        own_copy.start()

    @pl.when(f == 0)
    def _():
        pl.semaphore_signal(near, inc=1, device_id=beside, device_id_type=MESH)

    for t in range(seq):
        for h in range(2):

            @pl.when(t < s)
            def _():
                pl.semaphore_signal(
                    ready, inc=1, device_id={"seq": t, "fsdp": h}, device_id_type=MESH
                )

    def part_copy(i):
        return remote(
            part_out.at[:, at(made[i])],
            part_in.at[:, at(made[i])],
            part_send.at[i],
            part_recv.at[i],
            across,
        )

    def query_copy(i):
        return remote(
            query_out.at[i], query_in.at[i], query_send.at[i], query_recv.at[i], across
        )

    def own_part(j):
        return jnp.dot(own[:, :depth], w[j, 0], preferred_element_type=F32) + jnp.dot(
            own[:, depth:], w[j, 1], preferred_element_type=F32
        )

    def far_part(j, span):
        rows_at = slice(*span)
        return jnp.dot(far[0, rows_at], w[j, 0], preferred_element_type=F32) + jnp.dot(
            far[1, rows_at], w[j, 1], preferred_element_type=F32
        )

    with jax.named_scope("own_rows"):
        arrive(own, own_recv)
        loads[0].wait()
        for j in range(2):
            term = own_part(j + 1)
            part_out[j] = term.astype(BF16)
            edge_out[0, j] = term[rows - 8 :]
        part_copy(0).start()

        @pl.when(f == 0)
        def _():
            edge_in[0] = edge_out[0]

    with jax.named_scope("own_query"):
        for load in loads[1:]:
            load.wait()
        term = own_part(0)
        query[f] = half_of(term)
        query_out[0] = other_half(term).astype(BF16)

        @pl.when(f == 1)
        def _():
            query_edge_out[0] = term[rows - 8 :, :lanes]
            query_edge_out[1] = term[rows - 8 :, lanes:]

    @pl.when(f == 0)
    def _():
        pl.semaphore_wait(near, 1)
        pl.semaphore_signal(near, inc=1, device_id=across, device_id_type=MESH)

    def edge_up(i):
        return remote(
            edge_out.at[i],
            edge_in.at[i],
            edge_send.at[i],
            edge_recv.at[i],
            {"seq": jnp.minimum(s + 1, last), "fsdp": 1},
        )

    edge_across = remote(
        edge_out.at[1], edge_in.at[1], edge_send.at[1], edge_recv.at[1], {"fsdp": 0}
    )

    def query_edge(h):
        return remote(
            query_edge_out.at[h],
            query_edge_in.at[f],
            query_edge_send.at[h],
            query_edge_recv.at[f],
            {"seq": jnp.minimum(s + 1, last), "fsdp": h},
        )

    def taps_z_copy(t):
        block = taps.at[s, :, share]
        return remote(block, block, taps_z_send.at[t], taps_z_recv.at[s], {"seq": t})

    def taps_y_copy(j):
        block = taps.at[j, :, share]
        return remote(block, block, taps_y_send.at[j], taps_y_recv.at[j], beside)

    own_taps_y = remote(
        taps.at[s, g, share],
        taps.at[s, g, share],
        taps_y_send.at[s],
        taps_y_recv.at[s],
        beside,
    )

    def forward_copy(i):
        block = far.at[c, at(pieces[i])]
        return remote(
            block, block, fwd_send.at[i], far_recv.at[i, c], {"chan": sibling}
        )

    def take(i):
        arrive(far.at[c, at(pieces[i])], far_recv.at[i, c])
        forward_copy(i).start()
        arrive(far.at[sibling, at(pieces[i])], far_recv.at[i, sibling])

    with jax.named_scope("edge_rows"):
        take(0)
        for j in range(2):
            term = far_part(j + 1, pieces[0])
            projected[j, 8 + rows - EDGE :] = term
            edge_out[1, j] = term[EDGE - 8 :]

        @pl.when(f == 1)
        def _():
            edge_across.start()

        @pl.when(jnp.logical_not(holds))
        def _():
            for i in range(2, count + 1):
                for a in range(2):
                    token_copy(i, a).start()

        for i in range(1, count):
            part_copy(i).start()

        @pl.when(goes_up)
        def _():
            pl.semaphore_wait(ready, 2 * (last - s))

            @pl.when(f == 1)
            def _():
                edge_up(0).start()
                for h in range(2):
                    query_edge(h).start()

        @pl.when(jnp.logical_and(f == 0, goes_up))
        def _():
            edge_up(1).start()
            term = far_part(0, pieces[0])
            query_edge_out[0] = term[EDGE - 8 :, :lanes]
            query_edge_out[1] = term[EDGE - 8 :, lanes:]
            for h in range(2):
                query_edge(h).start()

    with jax.named_scope("taps_up"):
        taps_load.wait()
        arrive(taps.at[s, g, share], taps_x_recv)
        for t in range(1, seq):

            @pl.when(t > s)
            def _():
                taps_z_copy(t).start()

        @pl.when(f == 1)
        def _():
            pl.semaphore_wait(near, 1)

        own_taps_y.start()

    def across_copy(i):
        return remote(
            halves.at[g, at(made[i])],
            signal.at[s, g, at(made[i])],
            across_send.at[i],
            across_recv.at[i],
            across,
        )

    def up_copy(i, t):
        return remote(
            halves.at[f, at(made[i])],
            signal.at[s, g, at(made[i])],
            up_send.at[i, t],
            up_recv.at[s, i],
            {"seq": t},
        )

    def cross_copy(i, t):
        return remote(
            halves.at[g, at(made[i])],
            signal.at[s, g, at(made[i])],
            cross_send.at[i, t],
            cross_recv.at[s, i],
            {"seq": t, "fsdp": g},
        )

    def cross_start(i, low):
        for t in range(1, seq):

            @pl.when(jnp.logical_and(t > s, (s == 0) if low else (s > 0)))
            def _():
                cross_copy(i, t).start()

    def branch(j, span):
        low, high = span
        now = projected[j, 8 + low : 8 + high]
        one = projected[j, 7 + low : 7 + high]
        two = projected[j, 6 + low : 6 + high]
        return (
            short[0, j + 1 : j + 2, :] * now
            + short[1, j + 1 : j + 2, :] * one
            + short[2, j + 1 : j + 2, :] * two
        )

    def taps_spectrum():
        ids = lax.broadcasted_iota(jnp.int32, (bins, lanes), 0)
        sign = 1.0 - 2.0 * (ids % 2).astype(F32)
        for d in range(seq):

            @pl.when(d <= s)
            def _():
                @pl.when(d < s)
                def _():
                    arrive(taps.at[d, :, rest], taps_y_recv.at[d])

                @pl.when(d == s)
                def _():
                    arrive(taps.at[s, g, rest], taps_y_recv.at[s])

                spec = jnp.dot(
                    forward[...], taps[d].reshape(bins, lanes), preferred_element_type=F32
                )
                real, imag = spec[:bins], spec[bins:]
                tapspec[d] = spec
                if d == 0:
                    response[0, 0] = sign * imag
                    response[0, 1] = -sign * real
                else:
                    response[d, 0] = tapspec[d - 1, :bins] + sign * imag
                    response[d, 1] = tapspec[d - 1, bins:] - sign * real

    for i in range(count):
        low, high = made[i]
        with jax.named_scope("tokens"):
            take(i + 1)
        with jax.named_scope("chunk"):
            for j in range(2):
                projected[j, 8 + spans[i][0] : 8 + spans[i][1]] = far_part(j + 1, spans[i])
        if i == 0:
            with jax.named_scope("edges"):

                @pl.when(jnp.logical_and(f == 1, s > 0))
                def _():
                    arrive(edge_in.at[0], edge_recv.at[0])

                @pl.when(jnp.logical_or(f == 0, s > 0))
                def _():
                    arrive(edge_in.at[1], edge_recv.at[1])

                for j in range(2):
                    projected[j, :8] = rounded(edge_in[0, j] + edge_in[1, j])
        with jax.named_scope("partial"):
            part_copy(i).wait_recv()
        with jax.named_scope("product"):
            for j in range(2):
                block = slice(8 + low, 8 + high)
                projected[j, block] = rounded(
                    projected[j, block] + part_in[j, low:high].astype(F32)
                )
            product = (branch(0, made[i]) * branch(1, made[i])).astype(BF16)
            halves[0, low:high] = product[:, :lanes]
            halves[1, low:high] = product[:, lanes:]
            across_copy(i).start()
            for t in range(1, seq):

                @pl.when(t > s)
                def _():
                    up_copy(i, t).start()

            signal[s, g, low:high] = half_of(product)
        cross_start(i, False)
        if i == count - 1:
            query_copy(0).start()
        with jax.named_scope("far_query"):
            term = far_part(0, made[i])
            query[g, low:high] = half_of(term)
            query_out[1, low:high] = other_half(term).astype(BF16)
        if i == 0:
            with jax.named_scope("taps_side"):
                for t in range(last):

                    @pl.when(t < s)
                    def _():
                        arrive(taps.at[t, :, share], taps_z_recv.at[t])
                        taps_y_copy(t).start()

    def spectrum(j):
        spec = jnp.dot(
            forward[...], signal[j].reshape(bins, lanes), preferred_element_type=F32
        )
        real, imag = spec[:bins], spec[bins:]
        d = s - j
        hr, hi = response[d, 0], response[d, 1]
        return real * hr - imag * hi, real * hi + imag * hr

    query_copy(1).start()
    for i in range(count):
        cross_start(i, True)

    with jax.named_scope("taps_spectra"):
        taps_spectrum()

    with jax.named_scope("earlier_slabs"):
        result[...] = jnp.zeros_like(result)
        for j in range(last):

            @pl.when(j < s)
            def _():
                for i in range(count):
                    arrive(signal.at[j, g, at(made[i])], up_recv.at[j, i])
                    arrive(signal.at[j, f, at(made[i])], cross_recv.at[j, i])
                real, imag = spectrum(j)
                result[0] += real
                result[1] += imag

    with jax.named_scope("query"):
        for i in range(2):
            query_copy(i).wait_recv()

        @pl.when(s > 0)
        def _():
            for i in range(2):
                arrive(query_edge_in.at[i], query_edge_recv.at[i])

        mixed[:8] = rounded(query_edge_in[0] + query_edge_in[1])
        other = pl.multiple_of(8 + g * rows, 8)
        mine = pl.multiple_of(8 + f * rows, 8)
        mixed[pl.ds(other, rows)] = rounded(query[g] + query_in[0].astype(F32))
        mixed[pl.ds(mine, rows)] = rounded(query[f] + query_in[1].astype(F32))
        gate = [half_of(short[i, 0:1, :]) for i in range(3)]
        gated = gate[0] * mixed[8 : 8 + bins] + gate[1] * mixed[7 : 7 + bins]
        gated += gate[2] * mixed[6 : 6 + bins]
        query[...] = gated.reshape(2, rows, lanes)

    with jax.named_scope("own_wait"):
        for i in range(count):
            arrive(signal.at[s, f, at(made[i])], across_recv.at[i])
    with jax.named_scope("own_slab"):
        real, imag = spectrum(s)
        packed = jnp.concatenate([result[0] + real, result[1] + imag], axis=0).astype(BF16)
        factor = half_of(gain[...])

        def finish(b):
            lines = pl.ds(pl.multiple_of(b * rows, rows), rows)
            conv = jnp.dot(inverse[lines, :], packed, preferred_element_type=F32)
            whole = conv + factor * signal[s, b].astype(F32)
            final[b] = (query[b] * whole).astype(BF16)

        out_across = remote(final.at[g], out.at[:, columns(f)], out_send, out_recv, across)
        out_here = pltpu.make_async_copy(final.at[f], out.at[:, columns(f)], out_local)
        finish(g)
        out_across.start()
        finish(f)
        out_here.start()

    with jax.named_scope("drain"):

        @pl.when(jnp.logical_not(holds))
        def _():
            for i in range(count + 1):
                for a in range(2):
                    token_copy(i, a).wait_send()

        @pl.when(holds)
        def _():
            own_copy.wait_send()

        taps_x_copy.wait_send()
        for i in range(count + 1):
            forward_copy(i).wait_send()
        for i in range(count):
            part_copy(i).wait_send()
            across_copy(i).wait_send()
        own_taps_y.wait_send()
        for i in range(2):
            query_copy(i).wait_send()
        for t in range(last):

            @pl.when(t < s)
            def _():
                taps_y_copy(t).wait_send()


        @pl.when(f == 1)
        def _():
            edge_across.wait_send()

        @pl.when(goes_up)
        def _():
            edge_up(1 - f).wait_send()
            for h in range(2):
                query_edge(h).wait_send()

        for t in range(1, seq):

            @pl.when(t > s)
            def _():
                taps_z_copy(t).wait_send()
                for i in range(count):
                    up_copy(i, t).wait_send()
                    cross_copy(i, t).wait_send()

    with jax.named_scope("out"):
        out_across.wait_send()
        out_here.wait()
        arrive(out.at[:, columns(g)], out_recv)


def causal_device(seq, tokens, proj_weight, short_weight, skip_gain, filter_taps):
    rows = tokens.shape[0]
    depth, branches, width = proj_weight.shape
    lanes = width // 2
    step = depth // 2
    forward, inverse = causal_tables(2 * rows)
    count = len(chunk_spans(rows))
    dma = pltpu.SemaphoreType.DMA
    hbm = pl.BlockSpec(memory_space=pl.ANY)
    scratch = [
        ((branches, 2, step, width), BF16),
        (forward.shape, BF16),
        (inverse.shape, BF16),
        (short_weight.shape, F32),
        ((1, width), F32),
        ((rows, depth), BF16),
        ((2, rows, step), BF16),
        ((2, rows, width), BF16),
        ((2, rows, width), BF16),
        ((2, 2, 8, width), F32),
        ((2, 2, 8, width), F32),
        ((2, 8 + rows, width), F32),
        ((2, rows, lanes), BF16),
        ((seq, 2, rows, lanes), BF16),
        ((seq, 2, rows, lanes), BF16),
        ((seq, 4 * rows, lanes), F32),
        ((seq, 2, 2 * rows, lanes), F32),
        ((2, rows, lanes), F32),
        ((2, rows, lanes), BF16),
        ((2, rows, lanes), BF16),
        ((2, 8, lanes), F32),
        ((2, 8, lanes), F32),
        ((8 + 2 * rows, lanes), F32),
        ((2, 2 * rows, lanes), F32),
        ((2, rows, lanes), BF16),
    ]
    sems = [
        (6,),
        (),
        (),
        (count + 1, 2),
        (count + 1, 2),
        (count + 1,),
        (count,),
        (count,),
        (2,),
        (2,),
        (count,),
        (count,),
        (count, seq),
        (seq, count),
        (count, seq),
        (seq, count),
        (),
        (),
        (),
        (seq,),
        (seq,),
        (seq,),
        (seq,),
        (2,),
        (2,),
        (2,),
        (2,),
        (),
        (),
        (),
    ]
    return pl.pallas_call(
        functools.partial(causal_kernel, seq),
        out_shape=pltpu.VMEM((rows, width), BF16),
        in_specs=[hbm] * 7,
        out_specs=pl.BlockSpec(memory_space=pltpu.VMEM),
        scratch_shapes=[pltpu.VMEM(shape, kind) for shape, kind in scratch]
        + [dma(shape) for shape in sems]
        + [pltpu.SemaphoreType.REGULAR] * 2,
        compiler_params=pltpu.CompilerParams(
            collective_id=0, has_side_effects=True, vmem_limit_bytes=60 * 1024 * 1024
        ),
        name="hyena",
    )(
        tokens,
        jnp.transpose(proj_weight, (1, 0, 2)).reshape(branches, 2, step, width),
        short_weight,
        skip_gain.reshape(1, width),
        filter_taps,
        jnp.asarray(forward),
        jnp.asarray(inverse),
    )


def solution(mesh):
    seq = mesh.shape["seq"]
    paired = all(mesh.shape[axis] == 2 for axis in ("grp", "fsdp", "chan"))
    sizes = (mesh.shape["seq"], mesh.shape["fsdp"], mesh.shape["chan"])
    in_specs = (
        P(("grp", "seq", "fsdp"), "chan"),
        P("fsdp", None, "chan"),
        P(None, None, "chan"),
        P("chan"),
        P(("seq", "fsdp"), "chan"),
    )
    out_specs = P(("grp", "seq", "fsdp"), "chan")
    return jax.shard_map(
        functools.partial(causal_device, seq)
        if paired
        else functools.partial(per_device, sizes),
        mesh=mesh,
        in_specs=in_specs,
        out_specs=out_specs,
        check_vma=False,
    )
```

```python
import functools
import math

import jax
import jax.numpy as jnp
import ml_dtypes
import numpy as np
from jax import lax
from jax.experimental import pallas as pl
from jax.experimental.pallas import tpu as pltpu
from jax.sharding import PartitionSpec as P

MESH = pl.DeviceIdType.MESH
BF16 = jnp.bfloat16
F32 = jnp.float32
MOST_CHUNKS = 2
HALVES = 2
EDGE = 16
CHUNK = 64


def phase_pair(rows, cols, period):
    wrapped = (np.arange(rows)[:, None] * np.arange(cols)[None, :]) % period
    phase = wrapped.astype(np.float32) * np.float32(2.0 * math.pi / period)
    return np.cos(phase), np.sin(phase)


def tables(groups, per, rows):
    bf = ml_dtypes.bfloat16
    bins = 2 * groups
    cos, sin = phase_pair(bins, groups, bins)
    eye = np.eye(per, dtype=np.float32)
    first = np.concatenate([np.kron(cos, eye), np.kron(-sin, eye)], axis=0).astype(bf)
    cos, sin = phase_pair(rows, rows, rows)
    ahead = np.block([[cos, -sin], [sin, cos]]).astype(bf)
    behind = np.block([[cos, sin], [-sin, cos]]).astype(bf)
    cos, sin = phase_pair(bins, rows, bins * rows)
    twist = np.stack([np.repeat(cos, per, axis=0), np.repeat(sin, per, axis=0)])
    last = np.ascontiguousarray(first.T)
    return first, last, ahead, behind, twist.astype(np.float32)


def kernel(
    sizes,
    tokens,
    weight,
    short_h,
    gain_h,
    taps_h,
    first_h,
    last_h,
    ahead_h,
    behind_h,
    twist_h,
    out,
    w,
    first,
    last,
    ahead,
    behind,
    twist,
    short,
    gain,
    taps,
    held,
    acc,
    psend,
    precv,
    hrecv,
    query,
    product,
    tsend,
    trecv,
    gsend,
    grecv,
    csend,
    crecv,
    tapspec,
    load_sem,
    tok_send,
    tok_recv,
    fwd_send,
    part_send,
    part_recv,
    halo_send,
    halo_recv,
    a2a_send,
    a2a_recv,
):
    seq, fsdp, chan = sizes
    groups = seq * fsdp
    rows = tokens.shape[0]
    chunks = weight.shape[1]
    lines = rows // HALVES
    depth = chunks * weight.shape[2]
    width = weight.shape[3]
    per = width // groups
    bins = 2 * groups
    step = depth // chunks
    share = fsdp // chan
    s = lax.axis_index("seq")
    f = lax.axis_index("fsdp")
    c = lax.axis_index("chan")
    me = s * fsdp + f

    loads = [
        pltpu.make_async_copy(source, target, load_sem.at[i])
        for i, (source, target) in enumerate(
            [
                (taps_h, taps),
                (weight.at[pl.ds(1, 2)], w.at[pl.ds(1, 2)]),
                (first_h, first),
                (ahead_h, ahead),
                (twist_h, twist),
                (last_h, last),
                (behind_h, behind),
                (short_h, short),
                (gain_h, gain),
                (weight.at[pl.ds(0, 1)], w.at[pl.ds(0, 1)]),
            ]
        )
    ]
    for load in loads:
        load.start()

    barrier = pltpu.get_barrier_semaphore()
    everyone = groups * chan

    def greet(k, carry):
        other = lax.rem(me * chan + c + k, everyone)
        spot = other // chan
        pl.semaphore_signal(
            barrier,
            inc=1,
            device_id={"seq": spot // fsdp, "fsdp": spot % fsdp, "chan": other % chan},
            device_id_type=MESH,
        )
        return carry

    lax.fori_loop(1, everyone, greet, 0, unroll=everyone <= 16)

    @pl.when(me == 0)
    def _():
        hrecv[...] = jnp.zeros_like(hrecv)

    loads[0].wait()
    tsend[...] = jnp.transpose(taps[...].astype(F32)).astype(BF16).reshape(groups, per, rows)
    pl.semaphore_wait(barrier, everyone - 1)

    sibling = lax.rem(c + 1, chan)

    def span(h):
        return pl.ds(h * lines, lines)

    def token_copy(i, h, k, same):
        return pltpu.make_async_remote_copy(
            src_ref=tokens.at[span(h), pl.ds(i * depth + k * step, step)],
            dst_ref=held.at[f, k, span(h)],
            send_sem=tok_send.at[i, h, k],
            recv_sem=tok_recv.at[f, h, k],
            device_id={"fsdp": c * share + i, "chan": sibling if same else k % chan},
            device_id_type=MESH,
        )

    for h, k in [(h, k) for h in range(HALVES) for k in range(chunks)]:
        for i in range(share):
            stays = c * share + i == f

            @pl.when(jnp.logical_not(stays))
            def _():
                token_copy(i, h, k, False).start()

            @pl.when(stays)
            def _():
                token_copy(i, h, k, True).start()
                pltpu.make_async_copy(
                    tokens.at[span(h), pl.ds(i * depth + k * step, step)],
                    held.at[f, k, span(h)],
                    tok_recv.at[f, h, k],
                ).start()

    def exchange_copy(which, source, target, k):
        other = lax.rem(me + k, groups)
        return pltpu.make_async_remote_copy(
            src_ref=source.at[other],
            dst_ref=target.at[me],
            send_sem=a2a_send.at[which, k],
            recv_sem=a2a_recv.at[which, k],
            device_id={"seq": other // fsdp, "fsdp": other % fsdp},
            device_id_type=MESH,
        )

    def exchange_start(which, source, target):
        def go(k, carry):
            exchange_copy(which, source, target, k).start()
            return carry

        lax.fori_loop(1, groups, go, 0, unroll=groups <= 8)
        target[me] = source[me]

    def exchange_wait(which, source, target):
        def go(k, carry):
            exchange_copy(which, source, target, k).wait_recv()
            return carry

        lax.fori_loop(1, groups, go, 0, unroll=groups <= 8)

    def exchange_sent(which, source, target):
        def go(k, carry):
            exchange_copy(which, source, target, k).wait_send()
            return carry

        lax.fori_loop(1, groups, go, 0)


    half = bins * per

    def spectrum(signal):
        a = jnp.dot(first[...], signal, preferred_element_type=F32)
        real_a, imag_a = a[:half], a[half:]
        real_b = (real_a * twist[0] + imag_a * twist[1]).astype(BF16)
        imag_b = (imag_a * twist[0] - real_a * twist[1]).astype(BF16)
        b = jnp.concatenate([real_b, imag_b], axis=1)
        return jnp.dot(b, ahead[...], preferred_element_type=F32).astype(BF16)

    def arrival(spot, h, k):
        block = held.at[spot, k, span(h)]
        pltpu.make_async_copy(block, block, tok_recv.at[spot, h, k]).wait()

    def forward_copy(d, h, t):
        k = t * chan + c
        block = held.at[lax.rem(f + d, fsdp), k, span(h)]
        return pltpu.make_async_remote_copy(
            src_ref=block,
            dst_ref=block,
            send_sem=fwd_send.at[d - 1, h, t],
            recv_sem=tok_recv.at[lax.rem(f + d, fsdp), h, k],
            device_id={"chan": sibling},
            device_id_type=MESH,
        )

    def part_copy(d, j, h):
        return pltpu.make_async_remote_copy(
            src_ref=psend.at[d - 1, j, span(h)],
            dst_ref=precv.at[d - 1, j, span(h)],
            send_sem=part_send.at[d - 1, j, h],
            recv_sem=part_recv.at[d - 1, j, h],
            device_id={"fsdp": lax.rem(f + d, fsdp)},
            device_id_type=MESH,
        )

    phases = ((1, 2), (0, 1))

    def halo_target(d):
        return s * fsdp + lax.rem(f + d, fsdp) + 1

    def halo_copy(d, phase):
        target = jnp.minimum(halo_target(d), groups - 1)
        start, count = phases[phase]
        return pltpu.make_async_remote_copy(
            src_ref=acc.at[d - 1, pl.ds(start, count), pl.ds(rows - 8, 8)],
            dst_ref=hrecv.at[f, pl.ds(start, count)],
            send_sem=halo_send.at[d - 1, phase],
            recv_sem=halo_recv.at[f, phase],
            device_id={"seq": target // fsdp, "fsdp": target % fsdp},
            device_id_type=MESH,
        )

    def halo_remote(d):
        target = halo_target(d)
        return jnp.logical_and(target < groups, target != me)

    def halo_start(d, phase):
        @pl.when(halo_remote(d))
        def _():
            halo_copy(d, phase).start()

        start, count = phases[phase]

        @pl.when(halo_target(d) == me)
        def _():
            hrecv[f, start : start + count] = acc[d - 1, start : start + count, rows - 8 :]

    def halo_wait(phase):
        start, count = phases[phase]
        for h in range(fsdp):
            local = jnp.logical_and(f > 0, f == h)

            @pl.when(jnp.logical_and(me > 0, jnp.logical_not(local)))
            def _():
                block = hrecv.at[h, pl.ds(start, count)]
                pltpu.make_async_copy(block, block, halo_recv.at[h, phase]).wait()

    loads[1].wait()
    for k in range(chunks):
        for h in range(HALVES):
            arrival(f, h, k)
        for j in (1, 2):
            term = jnp.dot(held[f, k], w[j, k], preferred_element_type=F32)
            acc[fsdp - 1, j] = term if k == 0 else acc[fsdp - 1, j] + term
    halo_start(fsdp, 0)

    for d in range(1, fsdp):
        spot = lax.rem(f + d, fsdp)
        for h, t, b in [
            (h, t, b)
            for h in range(HALVES)
            for t in range(chunks // chan)
            for b in range(chan)
        ]:
            k = t * chan + lax.rem(c + b, chan)
            arrival(spot, h, k)
            if b == 0:
                forward_copy(d, h, t).start()
            final = (t + 1) * chan == chunks and b == chan - 1
            at = slice(h * lines, (h + 1) * lines)
            for j in (1, 2):
                term = jnp.dot(held[spot, k, at], w[j, k], preferred_element_type=F32)
                if t > 0 or b > 0:
                    term = acc[d - 1, j, at] + term
                acc[d - 1, j, at] = term
                if final:
                    psend[d - 1, j, at] = term.astype(BF16)
                    part_copy(d, j, h).start()
        halo_start(d, 0)

    for load in loads[2:]:
        load.wait()
    exchange_start(0, tsend, trecv)

    row_ids = lax.broadcasted_iota(jnp.int32, (rows, width), 0)

    def branch(j):
        total = acc[fsdp - 1, j]
        edge = hrecv[0, j]
        for d in range(1, fsdp):
            for h in range(HALVES):
                part_copy(d, j, h).wait_recv()
            total = total + precv[d - 1, j].astype(F32)
            edge = edge + hrecv[d, j]
        now = total.astype(BF16).astype(F32)
        edge = edge.astype(BF16).astype(F32)
        before = edge[7:8]
        earlier = edge[6:7]
        one = jnp.where(row_ids == 0, before, pltpu.roll(now, 1, 0))
        two = jnp.where(
            row_ids == 0, earlier, jnp.where(row_ids == 1, before, pltpu.roll(now, 2, 0))
        )
        return (
            short[0, j : j + 1, :] * now
            + short[1, j : j + 1, :] * one
            + short[2, j : j + 1, :] * two
        )

    halo_wait(0)
    prod = (branch(1) * branch(2)).astype(BF16).astype(F32)
    gsend[...] = jnp.transpose(prod).astype(BF16).reshape(groups, per, rows)
    exchange_start(1, gsend, grecv)
    product[...] = prod * gain[...]

    for d in range(1, fsdp + 1):
        spot = lax.rem(f + d, fsdp)
        term = jnp.dot(held[spot, 0], w[0, 0], preferred_element_type=F32)
        for k in range(1, chunks):
            term += jnp.dot(held[spot, k], w[0, k], preferred_element_type=F32)
        acc[d - 1, 0] = term
        if d < fsdp:
            psend[d - 1, 0] = term.astype(BF16)

    exchange_wait(0, tsend, trecv)
    tapspec[...] = spectrum(trecv[...].reshape(width, rows))
    exchange_wait(1, gsend, grecv)
    for d in range(1, fsdp + 1):
        if d < fsdp:
            for h in range(HALVES):
                part_copy(d, 0, h).start()
        halo_start(d, 1)

    x = spectrum(grecv[...].reshape(width, rows)).astype(F32)
    t = tapspec[...].astype(F32)
    xr, xi = x[:, :rows], x[:, rows:]
    tr, ti = t[:, :rows], t[:, rows:]
    real_z = (xr * tr - xi * ti).astype(BF16)
    imag_z = (xr * ti + xi * tr).astype(BF16)
    z = jnp.concatenate([real_z, imag_z], axis=1)
    v = jnp.dot(z, behind[...], preferred_element_type=F32)
    vr, vi = v[:, :rows], v[:, rows:]
    real_w = (vr * twist[0] - vi * twist[1]).astype(BF16)
    imag_w = (vi * twist[0] + vr * twist[1]).astype(BF16)
    packed = jnp.concatenate([real_w, imag_w], axis=0)
    y = jnp.dot(last[...], packed, preferred_element_type=F32) * (1.0 / (bins * rows))
    csend[...] = y.astype(BF16).reshape(groups, per, rows)
    exchange_start(2, csend, crecv)
    halo_wait(1)
    query[...] = branch(0)
    exchange_wait(2, csend, crecv)
    conv = jnp.transpose(crecv[...].reshape(width, rows).astype(F32))
    out[...] = (query[...] * (conv + product[...])).astype(BF16)

    exchange_sent(0, tsend, trecv)
    exchange_sent(1, gsend, grecv)
    exchange_sent(2, csend, crecv)
    for d in range(1, fsdp + 1):
        for phase in range(2):

            @pl.when(halo_remote(d))
            def _():
                halo_copy(d, phase).wait_send()

    for d in range(1, fsdp):
        for h in range(HALVES):
            for j in range(3):
                part_copy(d, j, h).wait_send()
            for t in range(chunks // chan):
                forward_copy(d, h, t).wait_send()
    for h, k in [(h, k) for h in range(HALVES) for k in range(chunks)]:
        for i in range(share):
            token_copy(i, h, k, False).wait_send()


def per_device(sizes, tokens, proj_weight, short_weight, skip_gain, filter_taps):
    seq, fsdp, chan = sizes
    groups = seq * fsdp
    rows = tokens.shape[0]
    depth, branches, width = proj_weight.shape
    per = width // groups
    chunks = min(MOST_CHUNKS, depth // 128)
    made = tables(groups, per, rows)
    dma = pltpu.SemaphoreType.DMA
    vmem = pl.BlockSpec(memory_space=pltpu.VMEM)
    hbm = pl.BlockSpec(memory_space=pl.ANY)
    half = 2 * groups * per
    return pl.pallas_call(
        functools.partial(kernel, sizes),
        out_shape=jax.ShapeDtypeStruct((rows, width), BF16),
        in_specs=[hbm] * 10,
        out_specs=vmem,
        scratch_shapes=[
            pltpu.VMEM((branches, chunks, depth // chunks, width), BF16),
            pltpu.VMEM(made[0].shape, BF16),
            pltpu.VMEM(made[1].shape, BF16),
            pltpu.VMEM(made[2].shape, BF16),
            pltpu.VMEM(made[3].shape, BF16),
            pltpu.VMEM(made[4].shape, F32),
            pltpu.VMEM(short_weight.shape, F32),
            pltpu.VMEM((1, width), F32),
            pltpu.VMEM((rows, width), BF16),
            pltpu.VMEM((fsdp, chunks, rows, depth // chunks), BF16),
            pltpu.VMEM((fsdp, branches, rows, width), F32),
            pltpu.VMEM((fsdp - 1, branches, rows, width), BF16),
            pltpu.VMEM((fsdp - 1, branches, rows, width), BF16),
            pltpu.VMEM((fsdp, branches, 8, width), F32),
            pltpu.VMEM((rows, width), F32),
            pltpu.VMEM((rows, width), F32),
        ]
        + [pltpu.VMEM((groups, per, rows), BF16)] * 6
        + [
            pltpu.VMEM((half, 2 * rows), BF16),
            dma((10,)),
            dma((fsdp // chan, HALVES, chunks)),
            dma((fsdp, HALVES, chunks)),
            dma((fsdp - 1, HALVES, chunks // chan)),
            dma((fsdp - 1, branches, HALVES)),
            dma((fsdp - 1, branches, HALVES)),
            dma((fsdp, 2)),
            dma((fsdp, 2)),
            dma((3, groups)),
            dma((3, groups)),
        ],
        compiler_params=pltpu.CompilerParams(
            collective_id=0, has_side_effects=True, vmem_limit_bytes=60 * 1024 * 1024
        ),
        name="hyena",
    )(
        tokens,
        jnp.transpose(proj_weight, (1, 0, 2)).reshape(branches, chunks, depth // chunks, width),
        short_weight,
        skip_gain.reshape(1, width),
        filter_taps,
        *[jnp.asarray(table) for table in made],
    )


def causal_tables(rows):
    bf = ml_dtypes.bfloat16
    odd = 2 * np.arange(rows) + 1
    period = 4 * rows

    def angles(times):
        wrapped = (odd[:, None] * times[None, :]) % period
        return wrapped.astype(np.float64) * (2.0 * math.pi / period)

    ahead = angles(np.arange(rows))
    behind = angles(rows + np.arange(rows)).T
    forward = np.concatenate([np.cos(ahead), -np.sin(ahead)], axis=0)
    inverse = np.concatenate([np.cos(behind), -np.sin(behind)], axis=1) / rows
    return forward.astype(bf), inverse.astype(bf)


def chunk_spans(rows):
    head = rows - EDGE
    return [(at, min(at + CHUNK, head)) for at in range(0, head, CHUNK)]


def causal_kernel(
    seq,
    tokens,
    weight,
    short_h,
    gain_h,
    taps_h,
    forward_h,
    inverse_h,
    out,
    w,
    forward,
    inverse,
    short,
    gain,
    own,
    far,
    part_out,
    part_in,
    edge_out,
    edge_in,
    projected,
    halves,
    signal,
    taps,
    tapspec,
    response,
    query,
    query_out,
    query_in,
    query_edge_out,
    query_edge_in,
    mixed,
    result,
    final,
    load_sem,
    own_send,
    own_recv,
    far_send,
    far_recv,
    fwd_send,
    part_send,
    part_recv,
    edge_send,
    edge_recv,
    across_send,
    across_recv,
    up_send,
    up_recv,
    taps_local,
    taps_x_send,
    taps_x_recv,
    taps_z_send,
    taps_z_recv,
    taps_y_send,
    taps_y_recv,
    query_send,
    query_recv,
    query_edge_send,
    query_edge_recv,
    out_send,
    out_recv,
    out_local,
    ready,
    near,
):
    rows = tokens.shape[0]
    width = weight.shape[3]
    depth = weight.shape[2]
    lanes = width // 2
    bins = 2 * rows
    last = seq - 1
    spans = chunk_spans(rows)
    count = len(spans)
    pieces = [(rows - EDGE, rows), *spans]
    made = [*spans[:-1], (spans[-1][0], rows)]
    group = lax.axis_index("grp")
    s = lax.axis_index("seq")
    f = lax.axis_index("fsdp")
    c = lax.axis_index("chan")
    g = 1 - f
    sibling = 1 - c
    holds = c == f
    goes_up = s < last
    across = {"fsdp": g}

    def half_of(value):
        return jnp.where(f == 0, value[:, :lanes], value[:, lanes:])

    def other_half(value):
        return jnp.where(f == 0, value[:, lanes:], value[:, :lanes])

    def rounded(value):
        return value.astype(BF16).astype(F32)

    def columns(h):
        return pl.ds(pl.multiple_of(h * lanes, lanes), lanes)

    def at(span):
        return pl.ds(span[0], span[1] - span[0])

    def remote(source, target, send, recv, device):
        return pltpu.make_async_remote_copy(
            src_ref=source,
            dst_ref=target,
            send_sem=send,
            recv_sem=recv,
            device_id=device,
            device_id_type=MESH,
        )

    def arrive(block, sem):
        pltpu.make_async_copy(block, block, sem).wait()

    own_load = pltpu.make_async_copy(tokens, own, own_recv)

    @pl.when(holds)
    def _():
        own_load.start()

    loads = [
        pltpu.make_async_copy(source, target, load_sem.at[i])
        for i, (source, target) in enumerate(
            [
                (weight.at[pl.ds(1, 2)], w.at[pl.ds(1, 2)]),
                (weight.at[pl.ds(0, 1)], w.at[pl.ds(0, 1)]),
                (forward_h, forward),
                (inverse_h, inverse),
                (short_h, short),
                (gain_h, gain),
            ]
        )
    ]
    for load in loads:
        load.start()
    taps_load = pltpu.make_async_copy(taps_h.at[:, columns(f)], taps.at[s, f], taps_local)
    taps_load.start()
    edge_in[...] = jnp.zeros_like(edge_in)
    query_edge_in[...] = jnp.zeros_like(query_edge_in)

    barrier = pltpu.get_barrier_semaphore()
    beside = {"grp": 1 - group}
    for device in [{"chan": sibling}, across, {"fsdp": g, "chan": sibling}]:
        pl.semaphore_signal(barrier, inc=1, device_id=device, device_id_type=MESH)

    @pl.when(f == 0)
    def _():
        pl.semaphore_signal(barrier, inc=1, device_id=beside, device_id_type=MESH)

    for t in range(seq):
        for h in range(2):

            @pl.when(t > s)
            def _():
                pl.semaphore_signal(
                    barrier, inc=1, device_id={"seq": t, "fsdp": h}, device_id_type=MESH
                )

    pl.semaphore_wait(barrier, 3 + g + 2 * s)

    def token_copy(i, a):
        return remote(
            tokens.at[at(pieces[i]), pl.ds(a * depth, depth)],
            far.at[a, at(pieces[i])],
            far_send,
            far_recv.at[i, a],
            {"fsdp": g, "chan": a},
        )

    own_copy = remote(tokens, own, own_send, own_recv, {"chan": sibling})
    share = pl.ds(pl.multiple_of(group * (rows // 2), rows // 2), rows // 2)
    rest = pl.ds(pl.multiple_of((1 - group) * (rows // 2), rows // 2), rows // 2)
    taps_x_copy = remote(
        taps_h.at[share, columns(g)],
        taps.at[s, f, share],
        taps_x_send,
        taps_x_recv,
        across,
    )

    @pl.when(jnp.logical_not(holds))
    def _():
        for a in range(2):
            token_copy(0, a).start()

    taps_x_copy.start()

    @pl.when(jnp.logical_not(holds))
    def _():
        for a in range(2):
            token_copy(1, a).start()

    @pl.when(holds)
    def _():
        own_copy.start()

    @pl.when(f == 0)
    def _():
        pl.semaphore_signal(near, inc=1, device_id=beside, device_id_type=MESH)

    for t in range(seq):
        for h in range(2):

            @pl.when(t < s)
            def _():
                pl.semaphore_signal(
                    ready, inc=1, device_id={"seq": t, "fsdp": h}, device_id_type=MESH
                )

    def part_copy(i):
        return remote(
            part_out.at[:, at(made[i])],
            part_in.at[:, at(made[i])],
            part_send,
            part_recv.at[i],
            across,
        )

    def query_copy(i):
        return remote(
            query_out.at[i], query_in.at[i], query_send, query_recv, across
        )

    def own_part(j):
        return jnp.dot(own[:, :depth], w[j, 0], preferred_element_type=F32) + jnp.dot(
            own[:, depth:], w[j, 1], preferred_element_type=F32
        )

    def far_part(j, span):
        rows_at = slice(*span)
        return jnp.dot(far[0, rows_at], w[j, 0], preferred_element_type=F32) + jnp.dot(
            far[1, rows_at], w[j, 1], preferred_element_type=F32
        )

    with jax.named_scope("own_rows"):
        arrive(own, own_recv)
        loads[0].wait()
        for j in range(2):
            term = own_part(j + 1)
            part_out[j] = term.astype(BF16)
            edge_out[0, j] = term[rows - 8 :]
        part_copy(0).start()

        @pl.when(f == 0)
        def _():
            edge_in[0] = edge_out[0]

    with jax.named_scope("own_query"):
        for load in loads[1:]:
            load.wait()
        term = own_part(0)
        query[f] = half_of(term)
        query_out[0] = other_half(term).astype(BF16)

        @pl.when(f == 1)
        def _():
            query_edge_out[0] = term[rows - 8 :, :lanes]
            query_edge_out[1] = term[rows - 8 :, lanes:]

    @pl.when(f == 0)
    def _():
        pl.semaphore_wait(near, 1)
        pl.semaphore_signal(near, inc=1, device_id=across, device_id_type=MESH)

    def edge_up(i):
        return remote(
            edge_out.at[i],
            edge_in.at[i],
            edge_send.at[i],
            edge_recv.at[i],
            {"seq": jnp.minimum(s + 1, last), "fsdp": 1},
        )

    edge_across = remote(
        edge_out.at[1], edge_in.at[1], edge_send.at[1], edge_recv.at[1], {"fsdp": 0}
    )

    def query_edge(h):
        return remote(
            query_edge_out.at[h],
            query_edge_in.at[f],
            query_edge_send,
            query_edge_recv,
            {"seq": jnp.minimum(s + 1, last), "fsdp": h},
        )

    def taps_z_copy(t):
        block = taps.at[s, :, share]
        return remote(block, block, taps_z_send, taps_z_recv, {"seq": t})

    def taps_y_copy(n):
        block = taps.at[pl.ds(0, n), :, share]
        return remote(block, block, taps_y_send.at[1], taps_y_recv.at[1], beside)

    own_taps_y = remote(
        taps.at[s, g, share],
        taps.at[s, g, share],
        taps_y_send.at[0],
        taps_y_recv.at[0],
        beside,
    )

    def forward_copy(i):
        block = far.at[c, at(pieces[i])]
        return remote(
            block, block, fwd_send, far_recv.at[i, c], {"chan": sibling}
        )

    def take(i):
        with jax.named_scope("direct"):
            arrive(far.at[c, at(pieces[i])], far_recv.at[i, c])
        forward_copy(i).start()
        arrive(far.at[sibling, at(pieces[i])], far_recv.at[i, sibling])

    with jax.named_scope("edge_rows"):
        take(0)
        for j in range(2):
            term = far_part(j + 1, pieces[0])
            projected[j, 8 + rows - EDGE :] = term
            edge_out[1, j] = term[EDGE - 8 :]

        @pl.when(f == 1)
        def _():
            edge_across.start()

        @pl.when(jnp.logical_not(holds))
        def _():
            for i in range(2, count + 1):
                for a in range(2):
                    token_copy(i, a).start()

        @pl.when(goes_up)
        def _():
            pl.semaphore_wait(ready, 2 * (last - s))

            @pl.when(f == 1)
            def _():
                edge_up(0).start()
                for h in range(2):
                    query_edge(h).start()

        @pl.when(jnp.logical_and(f == 0, goes_up))
        def _():
            edge_up(1).start()
            term = far_part(0, pieces[0])
            query_edge_out[0] = term[EDGE - 8 :, :lanes]
            query_edge_out[1] = term[EDGE - 8 :, lanes:]
            for h in range(2):
                query_edge(h).start()

    with jax.named_scope("taps_up"):
        taps_load.wait()
        arrive(taps.at[s, g, share], taps_x_recv)
        for t in range(1, seq):

            @pl.when(t > s)
            def _():
                taps_z_copy(t).start()

        @pl.when(f == 1)
        def _():
            pl.semaphore_wait(near, 1)

        own_taps_y.start()

    def across_copy(i):
        return remote(
            halves.at[g, at(made[i])],
            signal.at[s, g, at(made[i])],
            across_send,
            across_recv,
            across,
        )

    def up_copy(i, t):
        return remote(
            halves.at[f, at(made[i])],
            signal.at[s, g, at(made[i])],
            up_send,
            up_recv.at[s],
            {"seq": t},
        )

    def cross_copy(i, t):
        return remote(
            halves.at[g, at(made[i])],
            signal.at[s, g, at(made[i])],
            up_send,
            up_recv.at[s],
            {"seq": t, "fsdp": g},
        )

    def cross_start(i, low):
        for t in range(1, seq):

            @pl.when(jnp.logical_and(t > s, (s == 0) if low else (s > 0)))
            def _():
                cross_copy(i, t).start()

    def branch(j, span):
        low, high = span
        now = projected[j, 8 + low : 8 + high]
        one = projected[j, 7 + low : 7 + high]
        two = projected[j, 6 + low : 6 + high]
        return (
            short[0, j + 1 : j + 2, :] * now
            + short[1, j + 1 : j + 2, :] * one
            + short[2, j + 1 : j + 2, :] * two
        )

    def taps_spectrum():
        ids = lax.broadcasted_iota(jnp.int32, (bins, lanes), 0)
        sign = 1.0 - 2.0 * (ids % 2).astype(F32)
        arrive(taps.at[s, g, rest], taps_y_recv.at[0])
        for n in range(1, seq):

            @pl.when(s == n)
            def _():
                arrive(taps.at[pl.ds(0, n), :, rest], taps_y_recv.at[1])

        for d in range(seq):

            @pl.when(d <= s)
            def _():
                spec = jnp.dot(
                    forward[...], taps[d].reshape(bins, lanes), preferred_element_type=F32
                )
                real, imag = spec[:bins], spec[bins:]
                tapspec[d] = spec
                if d == 0:
                    response[0, 0] = sign * imag
                    response[0, 1] = -sign * real
                else:
                    response[d, 0] = tapspec[d - 1, :bins] + sign * imag
                    response[d, 1] = tapspec[d - 1, bins:] - sign * real

    for i in range(count):
        low, high = made[i]
        with jax.named_scope("tokens"):
            take(i + 1)
            if i + 1 < count:
                part_copy(i + 1).start()
        with jax.named_scope("chunk"):
            for j in range(2):
                projected[j, 8 + spans[i][0] : 8 + spans[i][1]] = far_part(j + 1, spans[i])
        if i == 0:
            with jax.named_scope("edges"):

                @pl.when(jnp.logical_and(f == 1, s > 0))
                def _():
                    arrive(edge_in.at[0], edge_recv.at[0])

                @pl.when(jnp.logical_or(f == 0, s > 0))
                def _():
                    arrive(edge_in.at[1], edge_recv.at[1])

                for j in range(2):
                    projected[j, :8] = rounded(edge_in[0, j] + edge_in[1, j])
        with jax.named_scope("partial"):
            part_copy(i).wait_recv()
        with jax.named_scope("product"):
            for j in range(2):
                block = slice(8 + low, 8 + high)
                projected[j, block] = rounded(
                    projected[j, block] + part_in[j, low:high].astype(F32)
                )
            product = (branch(0, made[i]) * branch(1, made[i])).astype(BF16)
            halves[0, low:high] = product[:, :lanes]
            halves[1, low:high] = product[:, lanes:]
            across_copy(i).start()
            for t in range(1, seq):

                @pl.when(t > s)
                def _():
                    up_copy(i, t).start()

            signal[s, g, low:high] = half_of(product)
        cross_start(i, False)
        if i == count - 1:
            query_copy(0).start()
        with jax.named_scope("far_query"):
            term = far_part(0, made[i])
            query[g, low:high] = half_of(term)
            query_out[1, low:high] = other_half(term).astype(BF16)
        if i == 0:
            with jax.named_scope("taps_side"):
                for n in range(1, seq):

                    @pl.when(s == n)
                    def _():
                        arrive(taps.at[pl.ds(0, n), :, share], taps_z_recv)
                        taps_y_copy(n).start()

    def spectrum(j):
        spec = jnp.dot(
            forward[...], signal[j].reshape(bins, lanes), preferred_element_type=F32
        )
        real, imag = spec[:bins], spec[bins:]
        d = s - j
        hr, hi = response[d, 0], response[d, 1]
        return real * hr - imag * hi, real * hi + imag * hr

    query_copy(1).start()
    for i in range(count):
        cross_start(i, True)

    with jax.named_scope("taps_spectra"):
        taps_spectrum()

    with jax.named_scope("earlier_slabs"):
        result[...] = jnp.zeros_like(result)
        for j in range(last):

            @pl.when(j < s)
            def _():
                arrive(signal.at[j], up_recv.at[j])
                real, imag = spectrum(j)
                result[0] += real
                result[1] += imag

    with jax.named_scope("query"):
        arrive(query_in, query_recv)

        @pl.when(s > 0)
        def _():
            arrive(query_edge_in, query_edge_recv)

        mixed[:8] = rounded(query_edge_in[0] + query_edge_in[1])
        other = pl.multiple_of(8 + g * rows, 8)
        mine = pl.multiple_of(8 + f * rows, 8)
        mixed[pl.ds(other, rows)] = rounded(query[g] + query_in[0].astype(F32))
        mixed[pl.ds(mine, rows)] = rounded(query[f] + query_in[1].astype(F32))
        gate = [half_of(short[i, 0:1, :]) for i in range(3)]
        gated = gate[0] * mixed[8 : 8 + bins] + gate[1] * mixed[7 : 7 + bins]
        gated += gate[2] * mixed[6 : 6 + bins]
        query[...] = gated.reshape(2, rows, lanes)

    with jax.named_scope("own_wait"):
        arrive(signal.at[s, f], across_recv)
    with jax.named_scope("own_slab"):
        real, imag = spectrum(s)
        packed = jnp.concatenate([result[0] + real, result[1] + imag], axis=0).astype(BF16)
        factor = half_of(gain[...])

        def finish(b):
            lines = pl.ds(pl.multiple_of(b * rows, rows), rows)
            conv = jnp.dot(inverse[lines, :], packed, preferred_element_type=F32)
            whole = conv + factor * signal[s, b].astype(F32)
            final[b] = (query[b] * whole).astype(BF16)

        out_across = remote(final.at[g], out.at[:, columns(f)], out_send, out_recv, across)
        out_here = pltpu.make_async_copy(final.at[f], out.at[:, columns(f)], out_local)
        finish(g)
        out_across.start()
        finish(f)
        out_here.start()

    with jax.named_scope("drain"):

        @pl.when(jnp.logical_not(holds))
        def _():
            arrive(far, far_send)

        @pl.when(holds)
        def _():
            own_copy.wait_send()

        taps_x_copy.wait_send()
        arrive(far.at[c], fwd_send)
        arrive(part_out, part_send)
        arrive(halves.at[g], across_send)
        arrive(query_out, query_send)
        own_taps_y.wait_send()

        @pl.when(f == 1)
        def _():
            edge_across.wait_send()

        @pl.when(goes_up)
        def _():
            edge_up(1 - f).wait_send()
            arrive(query_edge_out, query_edge_send)

        for n in range(1, seq):

            @pl.when(s == n)
            def _():
                taps_y_copy(n).wait_send()

            @pl.when(last - s == n)
            def _():
                arrive(taps.at[pl.ds(0, n), :, share], taps_z_send)
                arrive(signal.at[pl.ds(0, n)], up_send)

    with jax.named_scope("out"):
        out_across.wait_send()
        out_here.wait()
        arrive(out.at[:, columns(g)], out_recv)


def causal_device(seq, tokens, proj_weight, short_weight, skip_gain, filter_taps):
    rows = tokens.shape[0]
    depth, branches, width = proj_weight.shape
    lanes = width // 2
    step = depth // 2
    forward, inverse = causal_tables(2 * rows)
    count = len(chunk_spans(rows))
    dma = pltpu.SemaphoreType.DMA
    hbm = pl.BlockSpec(memory_space=pl.ANY)
    scratch = [
        ((branches, 2, step, width), BF16),
        (forward.shape, BF16),
        (inverse.shape, BF16),
        (short_weight.shape, F32),
        ((1, width), F32),
        ((rows, depth), BF16),
        ((2, rows, step), BF16),
        ((2, rows, width), BF16),
        ((2, rows, width), BF16),
        ((2, 2, 8, width), F32),
        ((2, 2, 8, width), F32),
        ((2, 8 + rows, width), F32),
        ((2, rows, lanes), BF16),
        ((seq, 2, rows, lanes), BF16),
        ((seq, 2, rows, lanes), BF16),
        ((seq, 4 * rows, lanes), F32),
        ((seq, 2, 2 * rows, lanes), F32),
        ((2, rows, lanes), F32),
        ((2, rows, lanes), BF16),
        ((2, rows, lanes), BF16),
        ((2, 8, lanes), F32),
        ((2, 8, lanes), F32),
        ((8 + 2 * rows, lanes), F32),
        ((2, 2 * rows, lanes), F32),
        ((2, rows, lanes), BF16),
    ]
    sems = [
        (6,),
        (),
        (),
        (),
        (count + 1, 2),
        (),
        (),
        (count,),
        (2,),
        (2,),
        (),
        (),
        (),
        (seq,),
        (),
        (),
        (),
        (),
        (),
        (2,),
        (2,),
        (),
        (),
        (),
        (),
        (),
        (),
        (),
    ]
    return pl.pallas_call(
        functools.partial(causal_kernel, seq),
        out_shape=pltpu.VMEM((rows, width), BF16),
        in_specs=[hbm] * 7,
        out_specs=pl.BlockSpec(memory_space=pltpu.VMEM),
        scratch_shapes=[pltpu.VMEM(shape, kind) for shape, kind in scratch]
        + [dma(shape) for shape in sems]
        + [pltpu.SemaphoreType.REGULAR] * 2,
        compiler_params=pltpu.CompilerParams(
            collective_id=0, has_side_effects=True, vmem_limit_bytes=60 * 1024 * 1024
        ),
        name="hyena",
    )(
        tokens,
        jnp.transpose(proj_weight, (1, 0, 2)).reshape(branches, 2, step, width),
        short_weight,
        skip_gain.reshape(1, width),
        filter_taps,
        jnp.asarray(forward),
        jnp.asarray(inverse),
    )


def solution(mesh):
    seq = mesh.shape["seq"]
    paired = all(mesh.shape[axis] == 2 for axis in ("grp", "fsdp", "chan"))
    sizes = (mesh.shape["seq"], mesh.shape["fsdp"], mesh.shape["chan"])
    in_specs = (
        P(("grp", "seq", "fsdp"), "chan"),
        P("fsdp", None, "chan"),
        P(None, None, "chan"),
        P("chan"),
        P(("seq", "fsdp"), "chan"),
    )
    out_specs = P(("grp", "seq", "fsdp"), "chan")
    return jax.shard_map(
        functools.partial(causal_device, seq)
        if paired
        else functools.partial(per_device, sizes),
        mesh=mesh,
        in_specs=in_specs,
        out_specs=out_specs,
        check_vma=False,
    )
```

```python
import functools
import math

import jax
import jax.numpy as jnp
import ml_dtypes
import numpy as np
from jax import lax
from jax.experimental import pallas as pl
from jax.experimental.pallas import tpu as pltpu
from jax.sharding import PartitionSpec as P

MESH = pl.DeviceIdType.MESH
BF16 = jnp.bfloat16
F32 = jnp.float32
MOST_CHUNKS = 2
HALVES = 2
EDGE = 16
CHUNK = 80


def phase_pair(rows, cols, period):
    wrapped = (np.arange(rows)[:, None] * np.arange(cols)[None, :]) % period
    phase = wrapped.astype(np.float32) * np.float32(2.0 * math.pi / period)
    return np.cos(phase), np.sin(phase)


def tables(groups, per, rows):
    bf = ml_dtypes.bfloat16
    bins = 2 * groups
    cos, sin = phase_pair(bins, groups, bins)
    eye = np.eye(per, dtype=np.float32)
    first = np.concatenate([np.kron(cos, eye), np.kron(-sin, eye)], axis=0).astype(bf)
    cos, sin = phase_pair(rows, rows, rows)
    ahead = np.block([[cos, -sin], [sin, cos]]).astype(bf)
    behind = np.block([[cos, sin], [-sin, cos]]).astype(bf)
    cos, sin = phase_pair(bins, rows, bins * rows)
    twist = np.stack([np.repeat(cos, per, axis=0), np.repeat(sin, per, axis=0)])
    last = np.ascontiguousarray(first.T)
    return first, last, ahead, behind, twist.astype(np.float32)


def kernel(
    sizes,
    tokens,
    weight,
    short_h,
    gain_h,
    taps_h,
    first_h,
    last_h,
    ahead_h,
    behind_h,
    twist_h,
    out,
    w,
    first,
    last,
    ahead,
    behind,
    twist,
    short,
    gain,
    taps,
    held,
    acc,
    psend,
    precv,
    hrecv,
    query,
    product,
    tsend,
    trecv,
    gsend,
    grecv,
    csend,
    crecv,
    tapspec,
    load_sem,
    tok_send,
    tok_recv,
    fwd_send,
    part_send,
    part_recv,
    halo_send,
    halo_recv,
    a2a_send,
    a2a_recv,
):
    seq, fsdp, chan = sizes
    groups = seq * fsdp
    rows = tokens.shape[0]
    chunks = weight.shape[1]
    lines = rows // HALVES
    depth = chunks * weight.shape[2]
    width = weight.shape[3]
    per = width // groups
    bins = 2 * groups
    step = depth // chunks
    share = fsdp // chan
    s = lax.axis_index("seq")
    f = lax.axis_index("fsdp")
    c = lax.axis_index("chan")
    me = s * fsdp + f

    loads = [
        pltpu.make_async_copy(source, target, load_sem.at[i])
        for i, (source, target) in enumerate(
            [
                (taps_h, taps),
                (weight.at[pl.ds(1, 2)], w.at[pl.ds(1, 2)]),
                (first_h, first),
                (ahead_h, ahead),
                (twist_h, twist),
                (last_h, last),
                (behind_h, behind),
                (short_h, short),
                (gain_h, gain),
                (weight.at[pl.ds(0, 1)], w.at[pl.ds(0, 1)]),
            ]
        )
    ]
    for load in loads:
        load.start()

    barrier = pltpu.get_barrier_semaphore()
    everyone = groups * chan

    def greet(k, carry):
        other = lax.rem(me * chan + c + k, everyone)
        spot = other // chan
        pl.semaphore_signal(
            barrier,
            inc=1,
            device_id={"seq": spot // fsdp, "fsdp": spot % fsdp, "chan": other % chan},
            device_id_type=MESH,
        )
        return carry

    lax.fori_loop(1, everyone, greet, 0, unroll=everyone <= 16)

    @pl.when(me == 0)
    def _():
        hrecv[...] = jnp.zeros_like(hrecv)

    loads[0].wait()
    tsend[...] = jnp.transpose(taps[...].astype(F32)).astype(BF16).reshape(groups, per, rows)
    pl.semaphore_wait(barrier, everyone - 1)

    sibling = lax.rem(c + 1, chan)

    def span(h):
        return pl.ds(h * lines, lines)

    def token_copy(i, h, k, same):
        return pltpu.make_async_remote_copy(
            src_ref=tokens.at[span(h), pl.ds(i * depth + k * step, step)],
            dst_ref=held.at[f, k, span(h)],
            send_sem=tok_send.at[i, h, k],
            recv_sem=tok_recv.at[f, h, k],
            device_id={"fsdp": c * share + i, "chan": sibling if same else k % chan},
            device_id_type=MESH,
        )

    for h, k in [(h, k) for h in range(HALVES) for k in range(chunks)]:
        for i in range(share):
            stays = c * share + i == f

            @pl.when(jnp.logical_not(stays))
            def _():
                token_copy(i, h, k, False).start()

            @pl.when(stays)
            def _():
                token_copy(i, h, k, True).start()
                pltpu.make_async_copy(
                    tokens.at[span(h), pl.ds(i * depth + k * step, step)],
                    held.at[f, k, span(h)],
                    tok_recv.at[f, h, k],
                ).start()

    def exchange_copy(which, source, target, k):
        other = lax.rem(me + k, groups)
        return pltpu.make_async_remote_copy(
            src_ref=source.at[other],
            dst_ref=target.at[me],
            send_sem=a2a_send.at[which, k],
            recv_sem=a2a_recv.at[which, k],
            device_id={"seq": other // fsdp, "fsdp": other % fsdp},
            device_id_type=MESH,
        )

    def exchange_start(which, source, target):
        def go(k, carry):
            exchange_copy(which, source, target, k).start()
            return carry

        lax.fori_loop(1, groups, go, 0, unroll=groups <= 8)
        target[me] = source[me]

    def exchange_wait(which, source, target):
        def go(k, carry):
            exchange_copy(which, source, target, k).wait_recv()
            return carry

        lax.fori_loop(1, groups, go, 0, unroll=groups <= 8)

    def exchange_sent(which, source, target):
        def go(k, carry):
            exchange_copy(which, source, target, k).wait_send()
            return carry

        lax.fori_loop(1, groups, go, 0)


    half = bins * per

    def spectrum(signal):
        a = jnp.dot(first[...], signal, preferred_element_type=F32)
        real_a, imag_a = a[:half], a[half:]
        real_b = (real_a * twist[0] + imag_a * twist[1]).astype(BF16)
        imag_b = (imag_a * twist[0] - real_a * twist[1]).astype(BF16)
        b = jnp.concatenate([real_b, imag_b], axis=1)
        return jnp.dot(b, ahead[...], preferred_element_type=F32).astype(BF16)

    def arrival(spot, h, k):
        block = held.at[spot, k, span(h)]
        pltpu.make_async_copy(block, block, tok_recv.at[spot, h, k]).wait()

    def forward_copy(d, h, t):
        k = t * chan + c
        block = held.at[lax.rem(f + d, fsdp), k, span(h)]
        return pltpu.make_async_remote_copy(
            src_ref=block,
            dst_ref=block,
            send_sem=fwd_send.at[d - 1, h, t],
            recv_sem=tok_recv.at[lax.rem(f + d, fsdp), h, k],
            device_id={"chan": sibling},
            device_id_type=MESH,
        )

    def part_copy(d, j, h):
        return pltpu.make_async_remote_copy(
            src_ref=psend.at[d - 1, j, span(h)],
            dst_ref=precv.at[d - 1, j, span(h)],
            send_sem=part_send.at[d - 1, j, h],
            recv_sem=part_recv.at[d - 1, j, h],
            device_id={"fsdp": lax.rem(f + d, fsdp)},
            device_id_type=MESH,
        )

    phases = ((1, 2), (0, 1))

    def halo_target(d):
        return s * fsdp + lax.rem(f + d, fsdp) + 1

    def halo_copy(d, phase):
        target = jnp.minimum(halo_target(d), groups - 1)
        start, count = phases[phase]
        return pltpu.make_async_remote_copy(
            src_ref=acc.at[d - 1, pl.ds(start, count), pl.ds(rows - 8, 8)],
            dst_ref=hrecv.at[f, pl.ds(start, count)],
            send_sem=halo_send.at[d - 1, phase],
            recv_sem=halo_recv.at[f, phase],
            device_id={"seq": target // fsdp, "fsdp": target % fsdp},
            device_id_type=MESH,
        )

    def halo_remote(d):
        target = halo_target(d)
        return jnp.logical_and(target < groups, target != me)

    def halo_start(d, phase):
        @pl.when(halo_remote(d))
        def _():
            halo_copy(d, phase).start()

        start, count = phases[phase]

        @pl.when(halo_target(d) == me)
        def _():
            hrecv[f, start : start + count] = acc[d - 1, start : start + count, rows - 8 :]

    def halo_wait(phase):
        start, count = phases[phase]
        for h in range(fsdp):
            local = jnp.logical_and(f > 0, f == h)

            @pl.when(jnp.logical_and(me > 0, jnp.logical_not(local)))
            def _():
                block = hrecv.at[h, pl.ds(start, count)]
                pltpu.make_async_copy(block, block, halo_recv.at[h, phase]).wait()

    loads[1].wait()
    for k in range(chunks):
        for h in range(HALVES):
            arrival(f, h, k)
        for j in (1, 2):
            term = jnp.dot(held[f, k], w[j, k], preferred_element_type=F32)
            acc[fsdp - 1, j] = term if k == 0 else acc[fsdp - 1, j] + term
    halo_start(fsdp, 0)

    for d in range(1, fsdp):
        spot = lax.rem(f + d, fsdp)
        for h, t, b in [
            (h, t, b)
            for h in range(HALVES)
            for t in range(chunks // chan)
            for b in range(chan)
        ]:
            k = t * chan + lax.rem(c + b, chan)
            arrival(spot, h, k)
            if b == 0:
                forward_copy(d, h, t).start()
            final = (t + 1) * chan == chunks and b == chan - 1
            at = slice(h * lines, (h + 1) * lines)
            for j in (1, 2):
                term = jnp.dot(held[spot, k, at], w[j, k], preferred_element_type=F32)
                if t > 0 or b > 0:
                    term = acc[d - 1, j, at] + term
                acc[d - 1, j, at] = term
                if final:
                    psend[d - 1, j, at] = term.astype(BF16)
                    part_copy(d, j, h).start()
        halo_start(d, 0)

    for load in loads[2:]:
        load.wait()
    exchange_start(0, tsend, trecv)

    row_ids = lax.broadcasted_iota(jnp.int32, (rows, width), 0)

    def branch(j):
        total = acc[fsdp - 1, j]
        edge = hrecv[0, j]
        for d in range(1, fsdp):
            for h in range(HALVES):
                part_copy(d, j, h).wait_recv()
            total = total + precv[d - 1, j].astype(F32)
            edge = edge + hrecv[d, j]
        now = total.astype(BF16).astype(F32)
        edge = edge.astype(BF16).astype(F32)
        before = edge[7:8]
        earlier = edge[6:7]
        one = jnp.where(row_ids == 0, before, pltpu.roll(now, 1, 0))
        two = jnp.where(
            row_ids == 0, earlier, jnp.where(row_ids == 1, before, pltpu.roll(now, 2, 0))
        )
        return (
            short[0, j : j + 1, :] * now
            + short[1, j : j + 1, :] * one
            + short[2, j : j + 1, :] * two
        )

    halo_wait(0)
    prod = (branch(1) * branch(2)).astype(BF16).astype(F32)
    gsend[...] = jnp.transpose(prod).astype(BF16).reshape(groups, per, rows)
    exchange_start(1, gsend, grecv)
    product[...] = prod * gain[...]

    for d in range(1, fsdp + 1):
        spot = lax.rem(f + d, fsdp)
        term = jnp.dot(held[spot, 0], w[0, 0], preferred_element_type=F32)
        for k in range(1, chunks):
            term += jnp.dot(held[spot, k], w[0, k], preferred_element_type=F32)
        acc[d - 1, 0] = term
        if d < fsdp:
            psend[d - 1, 0] = term.astype(BF16)

    exchange_wait(0, tsend, trecv)
    tapspec[...] = spectrum(trecv[...].reshape(width, rows))
    exchange_wait(1, gsend, grecv)
    for d in range(1, fsdp + 1):
        if d < fsdp:
            for h in range(HALVES):
                part_copy(d, 0, h).start()
        halo_start(d, 1)

    x = spectrum(grecv[...].reshape(width, rows)).astype(F32)
    t = tapspec[...].astype(F32)
    xr, xi = x[:, :rows], x[:, rows:]
    tr, ti = t[:, :rows], t[:, rows:]
    real_z = (xr * tr - xi * ti).astype(BF16)
    imag_z = (xr * ti + xi * tr).astype(BF16)
    z = jnp.concatenate([real_z, imag_z], axis=1)
    v = jnp.dot(z, behind[...], preferred_element_type=F32)
    vr, vi = v[:, :rows], v[:, rows:]
    real_w = (vr * twist[0] - vi * twist[1]).astype(BF16)
    imag_w = (vi * twist[0] + vr * twist[1]).astype(BF16)
    packed = jnp.concatenate([real_w, imag_w], axis=0)
    y = jnp.dot(last[...], packed, preferred_element_type=F32) * (1.0 / (bins * rows))
    csend[...] = y.astype(BF16).reshape(groups, per, rows)
    exchange_start(2, csend, crecv)
    halo_wait(1)
    query[...] = branch(0)
    exchange_wait(2, csend, crecv)
    conv = jnp.transpose(crecv[...].reshape(width, rows).astype(F32))
    out[...] = (query[...] * (conv + product[...])).astype(BF16)

    exchange_sent(0, tsend, trecv)
    exchange_sent(1, gsend, grecv)
    exchange_sent(2, csend, crecv)
    for d in range(1, fsdp + 1):
        for phase in range(2):

            @pl.when(halo_remote(d))
            def _():
                halo_copy(d, phase).wait_send()

    for d in range(1, fsdp):
        for h in range(HALVES):
            for j in range(3):
                part_copy(d, j, h).wait_send()
            for t in range(chunks // chan):
                forward_copy(d, h, t).wait_send()
    for h, k in [(h, k) for h in range(HALVES) for k in range(chunks)]:
        for i in range(share):
            token_copy(i, h, k, False).wait_send()


def per_device(sizes, tokens, proj_weight, short_weight, skip_gain, filter_taps):
    seq, fsdp, chan = sizes
    groups = seq * fsdp
    rows = tokens.shape[0]
    depth, branches, width = proj_weight.shape
    per = width // groups
    chunks = min(MOST_CHUNKS, depth // 128)
    made = tables(groups, per, rows)
    dma = pltpu.SemaphoreType.DMA
    vmem = pl.BlockSpec(memory_space=pltpu.VMEM)
    hbm = pl.BlockSpec(memory_space=pl.ANY)
    half = 2 * groups * per
    return pl.pallas_call(
        functools.partial(kernel, sizes),
        out_shape=jax.ShapeDtypeStruct((rows, width), BF16),
        in_specs=[hbm] * 10,
        out_specs=vmem,
        scratch_shapes=[
            pltpu.VMEM((branches, chunks, depth // chunks, width), BF16),
            pltpu.VMEM(made[0].shape, BF16),
            pltpu.VMEM(made[1].shape, BF16),
            pltpu.VMEM(made[2].shape, BF16),
            pltpu.VMEM(made[3].shape, BF16),
            pltpu.VMEM(made[4].shape, F32),
            pltpu.VMEM(short_weight.shape, F32),
            pltpu.VMEM((1, width), F32),
            pltpu.VMEM((rows, width), BF16),
            pltpu.VMEM((fsdp, chunks, rows, depth // chunks), BF16),
            pltpu.VMEM((fsdp, branches, rows, width), F32),
            pltpu.VMEM((fsdp - 1, branches, rows, width), BF16),
            pltpu.VMEM((fsdp - 1, branches, rows, width), BF16),
            pltpu.VMEM((fsdp, branches, 8, width), F32),
            pltpu.VMEM((rows, width), F32),
            pltpu.VMEM((rows, width), F32),
        ]
        + [pltpu.VMEM((groups, per, rows), BF16)] * 6
        + [
            pltpu.VMEM((half, 2 * rows), BF16),
            dma((10,)),
            dma((fsdp // chan, HALVES, chunks)),
            dma((fsdp, HALVES, chunks)),
            dma((fsdp - 1, HALVES, chunks // chan)),
            dma((fsdp - 1, branches, HALVES)),
            dma((fsdp - 1, branches, HALVES)),
            dma((fsdp, 2)),
            dma((fsdp, 2)),
            dma((3, groups)),
            dma((3, groups)),
        ],
        compiler_params=pltpu.CompilerParams(
            collective_id=0, has_side_effects=True, vmem_limit_bytes=60 * 1024 * 1024
        ),
        name="hyena",
    )(
        tokens,
        jnp.transpose(proj_weight, (1, 0, 2)).reshape(branches, chunks, depth // chunks, width),
        short_weight,
        skip_gain.reshape(1, width),
        filter_taps,
        *[jnp.asarray(table) for table in made],
    )


def causal_tables(rows):
    bf = ml_dtypes.bfloat16
    odd = 2 * np.arange(rows) + 1
    period = 4 * rows

    def angles(times):
        wrapped = (odd[:, None] * times[None, :]) % period
        return wrapped.astype(np.float64) * (2.0 * math.pi / period)

    ahead = angles(np.arange(rows))
    behind = angles(rows + np.arange(rows)).T
    forward = np.concatenate([np.cos(ahead), -np.sin(ahead)], axis=0)
    inverse = np.concatenate([np.cos(behind), -np.sin(behind)], axis=1) / rows
    return forward.astype(bf), inverse.astype(bf)


def chunk_spans(rows):
    head = rows - EDGE
    return [(at, min(at + CHUNK, head)) for at in range(0, head, CHUNK)]


def causal_kernel(
    seq,
    tokens,
    weight,
    short_h,
    gain_h,
    taps_h,
    forward_h,
    inverse_h,
    out,
    w,
    forward,
    inverse,
    short,
    gain,
    own,
    far,
    part_out,
    part_in,
    edge_out,
    edge_in,
    projected,
    halves,
    signal,
    taps,
    tapspec,
    response,
    query,
    query_term,
    query_out,
    query_in,
    query_edge_out,
    query_edge_in,
    mixed,
    result,
    final,
    load_sem,
    own_send,
    own_recv,
    far_send,
    far_recv,
    fwd_send,
    part_send,
    part_recv,
    edge_send,
    edge_recv,
    across_send,
    across_recv,
    up_send,
    up_recv,
    taps_local,
    taps_x_send,
    taps_x_recv,
    taps_z_send,
    taps_z_recv,
    taps_y_send,
    taps_y_recv,
    query_send,
    query_recv,
    query_edge_send,
    query_edge_recv,
    out_send,
    out_recv,
    out_local,
    ready,
    near,
):
    rows = tokens.shape[0]
    width = weight.shape[3]
    depth = weight.shape[2]
    lanes = width // 2
    bins = 2 * rows
    last = seq - 1
    spans = chunk_spans(rows)
    count = len(spans)
    pieces = [(rows - EDGE, rows), *spans]
    made = [*spans[:-1], (spans[-1][0], rows)]
    group = lax.axis_index("grp")
    s = lax.axis_index("seq")
    f = lax.axis_index("fsdp")
    c = lax.axis_index("chan")
    g = 1 - f
    sibling = 1 - c
    holds = c == f
    goes_up = s < last
    across = {"fsdp": g}

    def half_of(value):
        return jnp.where(f == 0, value[:, :lanes], value[:, lanes:])

    def other_half(value):
        return jnp.where(f == 0, value[:, lanes:], value[:, :lanes])

    def rounded(value):
        return value.astype(BF16).astype(F32)

    def columns(h):
        return pl.ds(pl.multiple_of(h * lanes, lanes), lanes)

    def at(span):
        return pl.ds(span[0], span[1] - span[0])

    def remote(source, target, send, recv, device):
        return pltpu.make_async_remote_copy(
            src_ref=source,
            dst_ref=target,
            send_sem=send,
            recv_sem=recv,
            device_id=device,
            device_id_type=MESH,
        )

    def arrive(block, sem):
        pltpu.make_async_copy(block, block, sem).wait()

    own_load = pltpu.make_async_copy(tokens, own, own_recv)

    @pl.when(holds)
    def _():
        own_load.start()

    loads = [
        pltpu.make_async_copy(source, target, load_sem.at[i])
        for i, (source, target) in enumerate(
            [
                (weight.at[pl.ds(1, 2)], w.at[pl.ds(1, 2)]),
                (weight.at[pl.ds(0, 1)], w.at[pl.ds(0, 1)]),
                (forward_h, forward),
                (inverse_h, inverse),
                (short_h, short),
                (gain_h, gain),
            ]
        )
    ]
    for load in loads:
        load.start()
    taps_load = pltpu.make_async_copy(taps_h.at[:, columns(f)], taps.at[s, f], taps_local)
    taps_load.start()
    edge_in[...] = jnp.zeros_like(edge_in)
    query_edge_in[...] = jnp.zeros_like(query_edge_in)

    barrier = pltpu.get_barrier_semaphore()
    beside = {"grp": 1 - group}
    for device in [{"chan": sibling}, across, {"fsdp": g, "chan": sibling}]:
        pl.semaphore_signal(barrier, inc=1, device_id=device, device_id_type=MESH)

    @pl.when(f == 0)
    def _():
        pl.semaphore_signal(barrier, inc=1, device_id=beside, device_id_type=MESH)

    for t in range(seq):
        for h in range(2):

            @pl.when(t > s)
            def _():
                pl.semaphore_signal(
                    barrier, inc=1, device_id={"seq": t, "fsdp": h}, device_id_type=MESH
                )

    pl.semaphore_wait(barrier, 3 + g + 2 * s)

    def token_copy(i, a):
        return remote(
            tokens.at[at(pieces[i]), pl.ds(a * depth, depth)],
            far.at[a, at(pieces[i])],
            far_send,
            far_recv.at[i, a],
            {"fsdp": g, "chan": a},
        )

    own_copy = remote(tokens, own, own_send, own_recv, {"chan": sibling})
    share = pl.ds(pl.multiple_of(group * (rows // 2), rows // 2), rows // 2)
    rest = pl.ds(pl.multiple_of((1 - group) * (rows // 2), rows // 2), rows // 2)
    taps_x_copy = remote(
        taps_h.at[share, columns(g)],
        taps.at[s, f, share],
        taps_x_send,
        taps_x_recv,
        across,
    )

    @pl.when(jnp.logical_not(holds))
    def _():
        for a in range(2):
            token_copy(0, a).start()

    taps_x_copy.start()

    @pl.when(jnp.logical_not(holds))
    def _():
        for a in range(2):
            token_copy(1, a).start()

    @pl.when(holds)
    def _():
        own_copy.start()

    @pl.when(f == 0)
    def _():
        pl.semaphore_signal(near, inc=1, device_id=beside, device_id_type=MESH)

    for t in range(seq):
        for h in range(2):

            @pl.when(t < s)
            def _():
                pl.semaphore_signal(
                    ready, inc=1, device_id={"seq": t, "fsdp": h}, device_id_type=MESH
                )

    def part_copy(i):
        return remote(
            part_out.at[:, at(made[i])],
            part_in.at[:, at(made[i])],
            part_send,
            part_recv.at[i],
            across,
        )

    own_query_copy = remote(
        query_out.at[0], query_in.at[0], query_send, query_recv, across
    )

    def query_copy(i):
        return remote(
            query_out.at[1, at(made[i])],
            query_in.at[1, at(made[i])],
            query_send,
            query_recv,
            across,
        )

    def own_part(j):
        return jnp.dot(own[:, :depth], w[j, 0], preferred_element_type=F32) + jnp.dot(
            own[:, depth:], w[j, 1], preferred_element_type=F32
        )

    def far_part(j, span):
        rows_at = slice(*span)
        return jnp.dot(far[0, rows_at], w[j, 0], preferred_element_type=F32) + jnp.dot(
            far[1, rows_at], w[j, 1], preferred_element_type=F32
        )

    with jax.named_scope("own_rows"):
        arrive(own, own_recv)
        loads[0].wait()
        for j in range(2):
            term = own_part(j + 1)
            part_out[j] = term.astype(BF16)
            edge_out[0, j] = term[rows - 8 :]
        part_copy(0).start()

        @pl.when(f == 0)
        def _():
            edge_in[0] = edge_out[0]

    with jax.named_scope("own_query"):
        for load in loads[1:]:
            load.wait()
        term = own_part(0)
        query[f] = half_of(term)
        query_out[0] = other_half(term).astype(BF16)

        @pl.when(f == 1)
        def _():
            query_edge_out[0] = term[rows - 8 :, :lanes]
            query_edge_out[1] = term[rows - 8 :, lanes:]

    @pl.when(f == 0)
    def _():
        pl.semaphore_wait(near, 1)
        pl.semaphore_signal(near, inc=1, device_id=across, device_id_type=MESH)

    def edge_up(i):
        return remote(
            edge_out.at[i],
            edge_in.at[i],
            edge_send.at[i],
            edge_recv.at[i],
            {"seq": jnp.minimum(s + 1, last), "fsdp": 1},
        )

    edge_across = remote(
        edge_out.at[1], edge_in.at[1], edge_send.at[1], edge_recv.at[1], {"fsdp": 0}
    )

    def query_edge(h):
        return remote(
            query_edge_out.at[h],
            query_edge_in.at[f],
            query_edge_send,
            query_edge_recv,
            {"seq": jnp.minimum(s + 1, last), "fsdp": h},
        )

    def taps_z_copy(t):
        block = taps.at[s, :, share]
        return remote(block, block, taps_z_send, taps_z_recv, {"seq": t})

    def taps_y_copy(n):
        block = taps.at[pl.ds(0, n), :, share]
        return remote(block, block, taps_y_send.at[1], taps_y_recv.at[1], beside)

    own_taps_y = remote(
        taps.at[s, g, share],
        taps.at[s, g, share],
        taps_y_send.at[0],
        taps_y_recv.at[0],
        beside,
    )

    def forward_copy(i):
        block = far.at[c, at(pieces[i])]
        return remote(
            block, block, fwd_send, far_recv.at[i, c], {"chan": sibling}
        )

    def half_part(j, a, span):
        return jnp.dot(far[a, slice(*span)], w[j, a], preferred_element_type=F32)

    def take(i):
        with jax.named_scope("direct"):
            arrive(far.at[c, at(pieces[i])], far_recv.at[i, c])
        forward_copy(i).start()

    def take_other(i):
        arrive(far.at[sibling, at(pieces[i])], far_recv.at[i, sibling])

    with jax.named_scope("edge_rows"):
        take(0)
        for j in range(2):
            projected[j, 8 + rows - EDGE :] = half_part(j + 1, c, pieces[0])
        take_other(0)
        for j in range(2):
            term = projected[j, 8 + rows - EDGE :] + half_part(j + 1, sibling, pieces[0])
            projected[j, 8 + rows - EDGE :] = term
            edge_out[1, j] = term[EDGE - 8 :]

        @pl.when(f == 1)
        def _():
            edge_across.start()

        @pl.when(jnp.logical_not(holds))
        def _():
            for i in range(2, count + 1):
                for a in range(2):
                    token_copy(i, a).start()

        @pl.when(goes_up)
        def _():
            pl.semaphore_wait(ready, 2 * (last - s))

            @pl.when(f == 1)
            def _():
                edge_up(0).start()
                for h in range(2):
                    query_edge(h).start()

        @pl.when(jnp.logical_and(f == 0, goes_up))
        def _():
            edge_up(1).start()
            term = far_part(0, pieces[0])
            query_edge_out[0] = term[EDGE - 8 :, :lanes]
            query_edge_out[1] = term[EDGE - 8 :, lanes:]
            for h in range(2):
                query_edge(h).start()

    with jax.named_scope("taps_up"):
        taps_load.wait()
        arrive(taps.at[s, g, share], taps_x_recv)
        for t in range(1, seq):

            @pl.when(t > s)
            def _():
                taps_z_copy(t).start()

        @pl.when(f == 1)
        def _():
            pl.semaphore_wait(near, 1)

        own_taps_y.start()

    def across_copy(i):
        return remote(
            halves.at[g, at(made[i])],
            signal.at[s, g, at(made[i])],
            across_send,
            across_recv,
            across,
        )

    def up_copy(i, t):
        return remote(
            halves.at[f, at(made[i])],
            signal.at[s, g, at(made[i])],
            up_send,
            up_recv.at[s],
            {"seq": t},
        )

    def cross_copy(i, t):
        return remote(
            halves.at[g, at(made[i])],
            signal.at[s, g, at(made[i])],
            up_send,
            up_recv.at[s],
            {"seq": t, "fsdp": g},
        )

    def cross_start(i, low):
        for t in range(1, seq):

            @pl.when(jnp.logical_and(t > s, (s == 0) if low else (s > 0)))
            def _():
                cross_copy(i, t).start()

    def branch(j, span):
        low, high = span
        now = projected[j, 8 + low : 8 + high]
        one = projected[j, 7 + low : 7 + high]
        two = projected[j, 6 + low : 6 + high]
        return (
            short[0, j + 1 : j + 2, :] * now
            + short[1, j + 1 : j + 2, :] * one
            + short[2, j + 1 : j + 2, :] * two
        )

    def taps_spectrum():
        ids = lax.broadcasted_iota(jnp.int32, (bins, lanes), 0)
        sign = 1.0 - 2.0 * (ids % 2).astype(F32)
        arrive(taps.at[s, g, rest], taps_y_recv.at[0])
        for n in range(1, seq):

            @pl.when(s == n)
            def _():
                arrive(taps.at[pl.ds(0, n), :, rest], taps_y_recv.at[1])

        for d in range(seq):

            @pl.when(d <= s)
            def _():
                spec = jnp.dot(
                    forward[...], taps[d].reshape(bins, lanes), preferred_element_type=F32
                )
                real, imag = spec[:bins], spec[bins:]
                tapspec[d] = spec
                if d == 0:
                    response[0, 0] = sign * imag
                    response[0, 1] = -sign * real
                else:
                    response[d, 0] = tapspec[d - 1, :bins] + sign * imag
                    response[d, 1] = tapspec[d - 1, bins:] - sign * real

    for i in range(count):
        low, high = made[i]
        final_chunk = i == count - 1
        with jax.named_scope("tokens"):
            take(i + 1)
            if final_chunk:
                own_query_copy.start()
                for r in range(i):
                    query_copy(r).start()
                    cross_start(r, True)
            lines = slice(8 + spans[i][0], 8 + spans[i][1])
            for j in range(2):
                projected[j, lines] = half_part(j + 1, c, spans[i])
            if final_chunk:
                query_term[low:high] = half_part(0, c, made[i])
            take_other(i + 1)
            if not final_chunk:
                part_copy(i + 1).start()
        with jax.named_scope("chunk"):
            for j in range(2):
                projected[j, lines] += half_part(j + 1, sibling, spans[i])
        if i == 0:
            with jax.named_scope("edges"):

                @pl.when(jnp.logical_and(f == 1, s > 0))
                def _():
                    arrive(edge_in.at[0], edge_recv.at[0])

                @pl.when(jnp.logical_or(f == 0, s > 0))
                def _():
                    arrive(edge_in.at[1], edge_recv.at[1])

                for j in range(2):
                    projected[j, :8] = rounded(edge_in[0, j] + edge_in[1, j])
        with jax.named_scope("partial"):
            part_copy(i).wait_recv()
        with jax.named_scope("product"):
            for j in range(2):
                block = slice(8 + low, 8 + high)
                projected[j, block] = rounded(
                    projected[j, block] + part_in[j, low:high].astype(F32)
                )
            product = (branch(0, made[i]) * branch(1, made[i])).astype(BF16)
            halves[0, low:high] = product[:, :lanes]
            halves[1, low:high] = product[:, lanes:]
            across_copy(i).start()
            for t in range(1, seq):

                @pl.when(t > s)
                def _():
                    up_copy(i, t).start()

            signal[s, g, low:high] = half_of(product)
        cross_start(i, False)
        if final_chunk:
            cross_start(i, True)
        with jax.named_scope("far_query"):
            if final_chunk:
                term = query_term[low:high] + half_part(0, sibling, made[i])
            else:
                term = far_part(0, made[i])
            query[g, low:high] = half_of(term)
            query_out[1, low:high] = other_half(term).astype(BF16)
            if final_chunk:
                query_copy(i).start()
        if i == 0:
            with jax.named_scope("taps_side"):
                for n in range(1, seq):

                    @pl.when(s == n)
                    def _():
                        arrive(taps.at[pl.ds(0, n), :, share], taps_z_recv)
                        taps_y_copy(n).start()

    def spectrum(j):
        spec = jnp.dot(
            forward[...], signal[j].reshape(bins, lanes), preferred_element_type=F32
        )
        real, imag = spec[:bins], spec[bins:]
        d = s - j
        hr, hi = response[d, 0], response[d, 1]
        return real * hr - imag * hi, real * hi + imag * hr

    with jax.named_scope("taps_spectra"):
        taps_spectrum()

    with jax.named_scope("earlier_slabs"):
        result[...] = jnp.zeros_like(result)
        for j in range(last):

            @pl.when(j < s)
            def _():
                arrive(signal.at[j], up_recv.at[j])
                real, imag = spectrum(j)
                result[0] += real
                result[1] += imag

    with jax.named_scope("query"):
        arrive(query_in, query_recv)

        @pl.when(s > 0)
        def _():
            arrive(query_edge_in, query_edge_recv)

        mixed[:8] = rounded(query_edge_in[0] + query_edge_in[1])
        other = pl.multiple_of(8 + g * rows, 8)
        mine = pl.multiple_of(8 + f * rows, 8)
        mixed[pl.ds(other, rows)] = rounded(query[g] + query_in[0].astype(F32))
        mixed[pl.ds(mine, rows)] = rounded(query[f] + query_in[1].astype(F32))
        gate = [half_of(short[i, 0:1, :]) for i in range(3)]
        gated = gate[0] * mixed[8 : 8 + bins] + gate[1] * mixed[7 : 7 + bins]
        gated += gate[2] * mixed[6 : 6 + bins]
        query[...] = gated.reshape(2, rows, lanes)

    with jax.named_scope("own_wait"):
        arrive(signal.at[s, f], across_recv)
    with jax.named_scope("own_slab"):
        real, imag = spectrum(s)
        packed = jnp.concatenate([result[0] + real, result[1] + imag], axis=0).astype(BF16)
        factor = half_of(gain[...])

        def finish(b):
            lines = pl.ds(pl.multiple_of(b * rows, rows), rows)
            conv = jnp.dot(inverse[lines, :], packed, preferred_element_type=F32)
            whole = conv + factor * signal[s, b].astype(F32)
            final[b] = (query[b] * whole).astype(BF16)

        out_across = remote(final.at[g], out.at[:, columns(f)], out_send, out_recv, across)
        out_here = pltpu.make_async_copy(final.at[f], out.at[:, columns(f)], out_local)
        finish(g)
        out_across.start()
        finish(f)
        out_here.start()

    with jax.named_scope("drain"):

        @pl.when(jnp.logical_not(holds))
        def _():
            arrive(far, far_send)

        @pl.when(holds)
        def _():
            own_copy.wait_send()

        taps_x_copy.wait_send()
        arrive(far.at[c], fwd_send)
        arrive(part_out, part_send)
        arrive(halves.at[g], across_send)
        arrive(query_out, query_send)
        own_taps_y.wait_send()

        @pl.when(f == 1)
        def _():
            edge_across.wait_send()

        @pl.when(goes_up)
        def _():
            edge_up(1 - f).wait_send()
            arrive(query_edge_out, query_edge_send)

        for n in range(1, seq):

            @pl.when(s == n)
            def _():
                taps_y_copy(n).wait_send()

            @pl.when(last - s == n)
            def _():
                arrive(taps.at[pl.ds(0, n), :, share], taps_z_send)
                arrive(signal.at[pl.ds(0, n)], up_send)

    with jax.named_scope("out"):
        out_across.wait_send()
        out_here.wait()
        arrive(out.at[:, columns(g)], out_recv)


def causal_device(seq, tokens, proj_weight, short_weight, skip_gain, filter_taps):
    rows = tokens.shape[0]
    depth, branches, width = proj_weight.shape
    lanes = width // 2
    step = depth // 2
    forward, inverse = causal_tables(2 * rows)
    count = len(chunk_spans(rows))
    dma = pltpu.SemaphoreType.DMA
    hbm = pl.BlockSpec(memory_space=pl.ANY)
    scratch = [
        ((branches, 2, step, width), BF16),
        (forward.shape, BF16),
        (inverse.shape, BF16),
        (short_weight.shape, F32),
        ((1, width), F32),
        ((rows, depth), BF16),
        ((2, rows, step), BF16),
        ((2, rows, width), BF16),
        ((2, rows, width), BF16),
        ((2, 2, 8, width), F32),
        ((2, 2, 8, width), F32),
        ((2, 8 + rows, width), F32),
        ((2, rows, lanes), BF16),
        ((seq, 2, rows, lanes), BF16),
        ((seq, 2, rows, lanes), BF16),
        ((seq, 4 * rows, lanes), F32),
        ((seq, 2, 2 * rows, lanes), F32),
        ((2, rows, lanes), F32),
        ((rows, width), F32),
        ((2, rows, lanes), BF16),
        ((2, rows, lanes), BF16),
        ((2, 8, lanes), F32),
        ((2, 8, lanes), F32),
        ((8 + 2 * rows, lanes), F32),
        ((2, 2 * rows, lanes), F32),
        ((2, rows, lanes), BF16),
    ]
    sems = [
        (6,),
        (),
        (),
        (),
        (count + 1, 2),
        (),
        (),
        (count,),
        (2,),
        (2,),
        (),
        (),
        (),
        (seq,),
        (),
        (),
        (),
        (),
        (),
        (2,),
        (2,),
        (),
        (),
        (),
        (),
        (),
        (),
        (),
    ]
    return pl.pallas_call(
        functools.partial(causal_kernel, seq),
        out_shape=pltpu.VMEM((rows, width), BF16),
        in_specs=[hbm] * 7,
        out_specs=pl.BlockSpec(memory_space=pltpu.VMEM),
        scratch_shapes=[pltpu.VMEM(shape, kind) for shape, kind in scratch]
        + [dma(shape) for shape in sems]
        + [pltpu.SemaphoreType.REGULAR] * 2,
        compiler_params=pltpu.CompilerParams(
            collective_id=0, has_side_effects=True, vmem_limit_bytes=60 * 1024 * 1024
        ),
        name="hyena",
    )(
        tokens,
        jnp.transpose(proj_weight, (1, 0, 2)).reshape(branches, 2, step, width),
        short_weight,
        skip_gain.reshape(1, width),
        filter_taps,
        jnp.asarray(forward),
        jnp.asarray(inverse),
    )


def solution(mesh):
    seq = mesh.shape["seq"]
    paired = all(mesh.shape[axis] == 2 for axis in ("grp", "fsdp", "chan"))
    sizes = (mesh.shape["seq"], mesh.shape["fsdp"], mesh.shape["chan"])
    in_specs = (
        P(("grp", "seq", "fsdp"), "chan"),
        P("fsdp", None, "chan"),
        P(None, None, "chan"),
        P("chan"),
        P(("seq", "fsdp"), "chan"),
    )
    out_specs = P(("grp", "seq", "fsdp"), "chan")
    return jax.shard_map(
        functools.partial(causal_device, seq)
        if paired
        else functools.partial(per_device, sizes),
        mesh=mesh,
        in_specs=in_specs,
        out_specs=out_specs,
        check_vma=False,
    )
```

```python
import functools
import math

import jax
import jax.numpy as jnp
import ml_dtypes
import numpy as np
from jax import lax
from jax.experimental import pallas as pl
from jax.experimental.pallas import tpu as pltpu
from jax.sharding import PartitionSpec as P

MESH = pl.DeviceIdType.MESH
BF16 = jnp.bfloat16
F32 = jnp.float32
MOST_CHUNKS = 2
HALVES = 2
EDGE = 16
CHUNK = 80
REACH = 2


def phase_pair(rows, cols, period):
    wrapped = (np.arange(rows)[:, None] * np.arange(cols)[None, :]) % period
    phase = wrapped.astype(np.float32) * np.float32(2.0 * math.pi / period)
    return np.cos(phase), np.sin(phase)


def tables(groups, per, rows):
    bf = ml_dtypes.bfloat16
    bins = 2 * groups
    cos, sin = phase_pair(bins, groups, bins)
    eye = np.eye(per, dtype=np.float32)
    first = np.concatenate([np.kron(cos, eye), np.kron(-sin, eye)], axis=0).astype(bf)
    cos, sin = phase_pair(rows, rows, rows)
    ahead = np.block([[cos, -sin], [sin, cos]]).astype(bf)
    behind = np.block([[cos, sin], [-sin, cos]]).astype(bf)
    cos, sin = phase_pair(bins, rows, bins * rows)
    twist = np.stack([np.repeat(cos, per, axis=0), np.repeat(sin, per, axis=0)])
    last = np.ascontiguousarray(first.T)
    return first, last, ahead, behind, twist.astype(np.float32)


def kernel(
    sizes,
    tokens,
    weight,
    short_h,
    gain_h,
    taps_h,
    first_h,
    last_h,
    ahead_h,
    behind_h,
    twist_h,
    out,
    w,
    first,
    last,
    ahead,
    behind,
    twist,
    short,
    gain,
    taps,
    held,
    acc,
    psend,
    precv,
    hrecv,
    query,
    product,
    tsend,
    trecv,
    gsend,
    grecv,
    csend,
    crecv,
    tapspec,
    load_sem,
    tok_send,
    tok_recv,
    fwd_send,
    part_send,
    part_recv,
    halo_send,
    halo_recv,
    a2a_send,
    a2a_recv,
):
    seq, fsdp, chan = sizes
    groups = seq * fsdp
    rows = tokens.shape[0]
    chunks = weight.shape[1]
    lines = rows // HALVES
    depth = chunks * weight.shape[2]
    width = weight.shape[3]
    per = width // groups
    bins = 2 * groups
    step = depth // chunks
    share = fsdp // chan
    s = lax.axis_index("seq")
    f = lax.axis_index("fsdp")
    c = lax.axis_index("chan")
    me = s * fsdp + f

    loads = [
        pltpu.make_async_copy(source, target, load_sem.at[i])
        for i, (source, target) in enumerate(
            [
                (taps_h, taps),
                (weight.at[pl.ds(1, 2)], w.at[pl.ds(1, 2)]),
                (first_h, first),
                (ahead_h, ahead),
                (twist_h, twist),
                (last_h, last),
                (behind_h, behind),
                (short_h, short),
                (gain_h, gain),
                (weight.at[pl.ds(0, 1)], w.at[pl.ds(0, 1)]),
            ]
        )
    ]
    for load in loads:
        load.start()

    barrier = pltpu.get_barrier_semaphore()
    everyone = groups * chan

    def greet(k, carry):
        other = lax.rem(me * chan + c + k, everyone)
        spot = other // chan
        pl.semaphore_signal(
            barrier,
            inc=1,
            device_id={"seq": spot // fsdp, "fsdp": spot % fsdp, "chan": other % chan},
            device_id_type=MESH,
        )
        return carry

    lax.fori_loop(1, everyone, greet, 0, unroll=everyone <= 16)

    @pl.when(me == 0)
    def _():
        hrecv[...] = jnp.zeros_like(hrecv)

    loads[0].wait()
    tsend[...] = jnp.transpose(taps[...].astype(F32)).astype(BF16).reshape(groups, per, rows)
    pl.semaphore_wait(barrier, everyone - 1)

    sibling = lax.rem(c + 1, chan)

    def span(h):
        return pl.ds(h * lines, lines)

    def token_copy(i, h, k, same):
        return pltpu.make_async_remote_copy(
            src_ref=tokens.at[span(h), pl.ds(i * depth + k * step, step)],
            dst_ref=held.at[f, k, span(h)],
            send_sem=tok_send.at[i, h, k],
            recv_sem=tok_recv.at[f, h, k],
            device_id={"fsdp": c * share + i, "chan": sibling if same else k % chan},
            device_id_type=MESH,
        )

    for h, k in [(h, k) for h in range(HALVES) for k in range(chunks)]:
        for i in range(share):
            stays = c * share + i == f

            @pl.when(jnp.logical_not(stays))
            def _():
                token_copy(i, h, k, False).start()

            @pl.when(stays)
            def _():
                token_copy(i, h, k, True).start()
                pltpu.make_async_copy(
                    tokens.at[span(h), pl.ds(i * depth + k * step, step)],
                    held.at[f, k, span(h)],
                    tok_recv.at[f, h, k],
                ).start()

    def exchange_copy(which, source, target, k):
        other = lax.rem(me + k, groups)
        return pltpu.make_async_remote_copy(
            src_ref=source.at[other],
            dst_ref=target.at[me],
            send_sem=a2a_send.at[which, k],
            recv_sem=a2a_recv.at[which, k],
            device_id={"seq": other // fsdp, "fsdp": other % fsdp},
            device_id_type=MESH,
        )

    def exchange_start(which, source, target):
        def go(k, carry):
            exchange_copy(which, source, target, k).start()
            return carry

        lax.fori_loop(1, groups, go, 0, unroll=groups <= 8)
        target[me] = source[me]

    def exchange_wait(which, source, target):
        def go(k, carry):
            exchange_copy(which, source, target, k).wait_recv()
            return carry

        lax.fori_loop(1, groups, go, 0, unroll=groups <= 8)

    def exchange_sent(which, source, target):
        def go(k, carry):
            exchange_copy(which, source, target, k).wait_send()
            return carry

        lax.fori_loop(1, groups, go, 0)


    half = bins * per

    def spectrum(signal):
        a = jnp.dot(first[...], signal, preferred_element_type=F32)
        real_a, imag_a = a[:half], a[half:]
        real_b = (real_a * twist[0] + imag_a * twist[1]).astype(BF16)
        imag_b = (imag_a * twist[0] - real_a * twist[1]).astype(BF16)
        b = jnp.concatenate([real_b, imag_b], axis=1)
        return jnp.dot(b, ahead[...], preferred_element_type=F32).astype(BF16)

    def arrival(spot, h, k):
        block = held.at[spot, k, span(h)]
        pltpu.make_async_copy(block, block, tok_recv.at[spot, h, k]).wait()

    def forward_copy(d, h, t):
        k = t * chan + c
        block = held.at[lax.rem(f + d, fsdp), k, span(h)]
        return pltpu.make_async_remote_copy(
            src_ref=block,
            dst_ref=block,
            send_sem=fwd_send.at[d - 1, h, t],
            recv_sem=tok_recv.at[lax.rem(f + d, fsdp), h, k],
            device_id={"chan": sibling},
            device_id_type=MESH,
        )

    def part_copy(d, j, h):
        return pltpu.make_async_remote_copy(
            src_ref=psend.at[d - 1, j, span(h)],
            dst_ref=precv.at[d - 1, j, span(h)],
            send_sem=part_send.at[d - 1, j, h],
            recv_sem=part_recv.at[d - 1, j, h],
            device_id={"fsdp": lax.rem(f + d, fsdp)},
            device_id_type=MESH,
        )

    phases = ((1, 2), (0, 1))

    def halo_target(d):
        return s * fsdp + lax.rem(f + d, fsdp) + 1

    def halo_copy(d, phase):
        target = jnp.minimum(halo_target(d), groups - 1)
        start, count = phases[phase]
        return pltpu.make_async_remote_copy(
            src_ref=acc.at[d - 1, pl.ds(start, count), pl.ds(rows - 8, 8)],
            dst_ref=hrecv.at[f, pl.ds(start, count)],
            send_sem=halo_send.at[d - 1, phase],
            recv_sem=halo_recv.at[f, phase],
            device_id={"seq": target // fsdp, "fsdp": target % fsdp},
            device_id_type=MESH,
        )

    def halo_remote(d):
        target = halo_target(d)
        return jnp.logical_and(target < groups, target != me)

    def halo_start(d, phase):
        @pl.when(halo_remote(d))
        def _():
            halo_copy(d, phase).start()

        start, count = phases[phase]

        @pl.when(halo_target(d) == me)
        def _():
            hrecv[f, start : start + count] = acc[d - 1, start : start + count, rows - 8 :]

    def halo_wait(phase):
        start, count = phases[phase]
        for h in range(fsdp):
            local = jnp.logical_and(f > 0, f == h)

            @pl.when(jnp.logical_and(me > 0, jnp.logical_not(local)))
            def _():
                block = hrecv.at[h, pl.ds(start, count)]
                pltpu.make_async_copy(block, block, halo_recv.at[h, phase]).wait()

    loads[1].wait()
    for k in range(chunks):
        for h in range(HALVES):
            arrival(f, h, k)
        for j in (1, 2):
            term = jnp.dot(held[f, k], w[j, k], preferred_element_type=F32)
            acc[fsdp - 1, j] = term if k == 0 else acc[fsdp - 1, j] + term
    halo_start(fsdp, 0)

    for d in range(1, fsdp):
        spot = lax.rem(f + d, fsdp)
        for h, t, b in [
            (h, t, b)
            for h in range(HALVES)
            for t in range(chunks // chan)
            for b in range(chan)
        ]:
            k = t * chan + lax.rem(c + b, chan)
            arrival(spot, h, k)
            if b == 0:
                forward_copy(d, h, t).start()
            final = (t + 1) * chan == chunks and b == chan - 1
            at = slice(h * lines, (h + 1) * lines)
            for j in (1, 2):
                term = jnp.dot(held[spot, k, at], w[j, k], preferred_element_type=F32)
                if t > 0 or b > 0:
                    term = acc[d - 1, j, at] + term
                acc[d - 1, j, at] = term
                if final:
                    psend[d - 1, j, at] = term.astype(BF16)
                    part_copy(d, j, h).start()
        halo_start(d, 0)

    for load in loads[2:]:
        load.wait()
    exchange_start(0, tsend, trecv)

    row_ids = lax.broadcasted_iota(jnp.int32, (rows, width), 0)

    def branch(j):
        total = acc[fsdp - 1, j]
        edge = hrecv[0, j]
        for d in range(1, fsdp):
            for h in range(HALVES):
                part_copy(d, j, h).wait_recv()
            total = total + precv[d - 1, j].astype(F32)
            edge = edge + hrecv[d, j]
        now = total.astype(BF16).astype(F32)
        edge = edge.astype(BF16).astype(F32)
        before = edge[7:8]
        earlier = edge[6:7]
        one = jnp.where(row_ids == 0, before, pltpu.roll(now, 1, 0))
        two = jnp.where(
            row_ids == 0, earlier, jnp.where(row_ids == 1, before, pltpu.roll(now, 2, 0))
        )
        return (
            short[0, j : j + 1, :] * now
            + short[1, j : j + 1, :] * one
            + short[2, j : j + 1, :] * two
        )

    halo_wait(0)
    prod = (branch(1) * branch(2)).astype(BF16).astype(F32)
    gsend[...] = jnp.transpose(prod).astype(BF16).reshape(groups, per, rows)
    exchange_start(1, gsend, grecv)
    product[...] = prod * gain[...]

    for d in range(1, fsdp + 1):
        spot = lax.rem(f + d, fsdp)
        term = jnp.dot(held[spot, 0], w[0, 0], preferred_element_type=F32)
        for k in range(1, chunks):
            term += jnp.dot(held[spot, k], w[0, k], preferred_element_type=F32)
        acc[d - 1, 0] = term
        if d < fsdp:
            psend[d - 1, 0] = term.astype(BF16)

    exchange_wait(0, tsend, trecv)
    tapspec[...] = spectrum(trecv[...].reshape(width, rows))
    exchange_wait(1, gsend, grecv)
    for d in range(1, fsdp + 1):
        if d < fsdp:
            for h in range(HALVES):
                part_copy(d, 0, h).start()
        halo_start(d, 1)

    x = spectrum(grecv[...].reshape(width, rows)).astype(F32)
    t = tapspec[...].astype(F32)
    xr, xi = x[:, :rows], x[:, rows:]
    tr, ti = t[:, :rows], t[:, rows:]
    real_z = (xr * tr - xi * ti).astype(BF16)
    imag_z = (xr * ti + xi * tr).astype(BF16)
    z = jnp.concatenate([real_z, imag_z], axis=1)
    v = jnp.dot(z, behind[...], preferred_element_type=F32)
    vr, vi = v[:, :rows], v[:, rows:]
    real_w = (vr * twist[0] - vi * twist[1]).astype(BF16)
    imag_w = (vi * twist[0] + vr * twist[1]).astype(BF16)
    packed = jnp.concatenate([real_w, imag_w], axis=0)
    y = jnp.dot(last[...], packed, preferred_element_type=F32) * (1.0 / (bins * rows))
    csend[...] = y.astype(BF16).reshape(groups, per, rows)
    exchange_start(2, csend, crecv)
    halo_wait(1)
    query[...] = branch(0)
    exchange_wait(2, csend, crecv)
    conv = jnp.transpose(crecv[...].reshape(width, rows).astype(F32))
    out[...] = (query[...] * (conv + product[...])).astype(BF16)

    exchange_sent(0, tsend, trecv)
    exchange_sent(1, gsend, grecv)
    exchange_sent(2, csend, crecv)
    for d in range(1, fsdp + 1):
        for phase in range(2):

            @pl.when(halo_remote(d))
            def _():
                halo_copy(d, phase).wait_send()

    for d in range(1, fsdp):
        for h in range(HALVES):
            for j in range(3):
                part_copy(d, j, h).wait_send()
            for t in range(chunks // chan):
                forward_copy(d, h, t).wait_send()
    for h, k in [(h, k) for h in range(HALVES) for k in range(chunks)]:
        for i in range(share):
            token_copy(i, h, k, False).wait_send()


def per_device(sizes, tokens, proj_weight, short_weight, skip_gain, filter_taps):
    seq, fsdp, chan = sizes
    groups = seq * fsdp
    rows = tokens.shape[0]
    depth, branches, width = proj_weight.shape
    per = width // groups
    chunks = min(MOST_CHUNKS, depth // 128)
    made = tables(groups, per, rows)
    dma = pltpu.SemaphoreType.DMA
    vmem = pl.BlockSpec(memory_space=pltpu.VMEM)
    hbm = pl.BlockSpec(memory_space=pl.ANY)
    half = 2 * groups * per
    return pl.pallas_call(
        functools.partial(kernel, sizes),
        out_shape=jax.ShapeDtypeStruct((rows, width), BF16),
        in_specs=[hbm] * 10,
        out_specs=vmem,
        scratch_shapes=[
            pltpu.VMEM((branches, chunks, depth // chunks, width), BF16),
            pltpu.VMEM(made[0].shape, BF16),
            pltpu.VMEM(made[1].shape, BF16),
            pltpu.VMEM(made[2].shape, BF16),
            pltpu.VMEM(made[3].shape, BF16),
            pltpu.VMEM(made[4].shape, F32),
            pltpu.VMEM(short_weight.shape, F32),
            pltpu.VMEM((1, width), F32),
            pltpu.VMEM((rows, width), BF16),
            pltpu.VMEM((fsdp, chunks, rows, depth // chunks), BF16),
            pltpu.VMEM((fsdp, branches, rows, width), F32),
            pltpu.VMEM((fsdp - 1, branches, rows, width), BF16),
            pltpu.VMEM((fsdp - 1, branches, rows, width), BF16),
            pltpu.VMEM((fsdp, branches, 8, width), F32),
            pltpu.VMEM((rows, width), F32),
            pltpu.VMEM((rows, width), F32),
        ]
        + [pltpu.VMEM((groups, per, rows), BF16)] * 6
        + [
            pltpu.VMEM((half, 2 * rows), BF16),
            dma((10,)),
            dma((fsdp // chan, HALVES, chunks)),
            dma((fsdp, HALVES, chunks)),
            dma((fsdp - 1, HALVES, chunks // chan)),
            dma((fsdp - 1, branches, HALVES)),
            dma((fsdp - 1, branches, HALVES)),
            dma((fsdp, 2)),
            dma((fsdp, 2)),
            dma((3, groups)),
            dma((3, groups)),
        ],
        compiler_params=pltpu.CompilerParams(
            collective_id=0, has_side_effects=True, vmem_limit_bytes=60 * 1024 * 1024
        ),
        name="hyena",
    )(
        tokens,
        jnp.transpose(proj_weight, (1, 0, 2)).reshape(branches, chunks, depth // chunks, width),
        short_weight,
        skip_gain.reshape(1, width),
        filter_taps,
        *[jnp.asarray(table) for table in made],
    )


def causal_tables(rows):
    bf = ml_dtypes.bfloat16
    odd = 2 * np.arange(rows) + 1
    period = 4 * rows

    def angles(times):
        wrapped = (odd[:, None] * times[None, :]) % period
        return wrapped.astype(np.float64) * (2.0 * math.pi / period)

    ahead = angles(np.arange(rows))
    behind = angles(rows + np.arange(rows)).T
    pair = [np.cos(behind) / rows, -np.sin(behind) / rows]
    return np.stack([np.cos(ahead), -np.sin(ahead), *pair]).astype(bf)


def chunk_spans(rows):
    head = rows - EDGE
    return [(at, min(at + CHUNK, head)) for at in range(0, head, CHUNK)]


def causal_kernel(
    seq,
    tokens,
    weight,
    short_h,
    gain_h,
    taps_h,
    table_h,
    out,
    w,
    table,
    short,
    gain,
    own,
    far,
    part_out,
    part_in,
    edge_out,
    edge_in,
    projected,
    halves,
    signal,
    taps,
    tapspec,
    response,
    query,
    query_term,
    query_out,
    query_in,
    query_edge_out,
    query_edge_in,
    mixed,
    result,
    packed,
    final,
    load_sem,
    own_send,
    own_recv,
    far_send,
    far_recv,
    fwd_send,
    part_send,
    part_recv,
    edge_send,
    edge_recv,
    across_send,
    across_recv,
    up_send,
    up_recv,
    taps_local,
    taps_x_send,
    taps_x_recv,
    taps_z_send,
    taps_z_recv,
    taps_y_send,
    taps_y_recv,
    query_send,
    query_recv,
    query_edge_send,
    query_edge_recv,
    out_send,
    out_recv,
    ready,
    near,
):
    rows = tokens.shape[0]
    width = weight.shape[3]
    depth = weight.shape[2]
    lanes = width // 2
    bins = 2 * rows
    last = seq - 1
    spans = chunk_spans(rows)
    count = len(spans)
    pieces = [(rows - EDGE, rows), *spans]
    made = [*spans[:-1], (spans[-1][0], rows)]
    group = lax.axis_index("grp")
    s = lax.axis_index("seq")
    f = lax.axis_index("fsdp")
    c = lax.axis_index("chan")
    g = 1 - f
    sibling = 1 - c
    holds = c == f
    goes_up = s < last
    across = {"fsdp": g}

    def half_of(value):
        return jnp.where(f == 0, value[:, :lanes], value[:, lanes:])

    def other_half(value):
        return jnp.where(f == 0, value[:, lanes:], value[:, :lanes])

    def rounded(value):
        return value.astype(BF16).astype(F32)

    def columns(h):
        return pl.ds(pl.multiple_of(h * lanes, lanes), lanes)

    def at(span):
        return pl.ds(span[0], span[1] - span[0])

    def remote(source, target, send, recv, device):
        return pltpu.make_async_remote_copy(
            src_ref=source,
            dst_ref=target,
            send_sem=send,
            recv_sem=recv,
            device_id=device,
            device_id_type=MESH,
        )

    def arrive(block, sem):
        pltpu.make_async_copy(block, block, sem).wait()

    own_load = pltpu.make_async_copy(tokens, own, own_recv)

    @pl.when(holds)
    def _():
        own_load.start()

    loads = [
        pltpu.make_async_copy(source, target, load_sem.at[i])
        for i, (source, target) in enumerate(
            [
                (weight.at[pl.ds(1, 2)], w.at[pl.ds(1, 2)]),
                (weight.at[pl.ds(0, 1)], w.at[pl.ds(0, 1)]),
                (table_h, table),
                (short_h, short),
                (gain_h, gain),
            ]
        )
    ]
    for load in loads:
        load.start()
    taps_load = pltpu.make_async_copy(taps_h.at[:, columns(f)], taps.at[s, f], taps_local)
    taps_load.start()
    edge_in[...] = jnp.zeros_like(edge_in)
    query_edge_in[...] = jnp.zeros_like(query_edge_in)

    barrier = pltpu.get_barrier_semaphore()
    beside = {"grp": 1 - group}
    for device in [{"chan": sibling}, across, {"fsdp": g, "chan": sibling}]:
        pl.semaphore_signal(barrier, inc=1, device_id=device, device_id_type=MESH)

    @pl.when(f == 0)
    def _():
        pl.semaphore_signal(barrier, inc=1, device_id=beside, device_id_type=MESH)

    for t in range(seq):
        for h in range(2):

            @pl.when(t > s)
            def _():
                pl.semaphore_signal(
                    barrier, inc=1, device_id={"seq": t, "fsdp": h}, device_id_type=MESH
                )

    pl.semaphore_wait(barrier, 3 + g + 2 * s)

    def token_copy(i, a):
        return remote(
            tokens.at[at(pieces[i]), pl.ds(a * depth, depth)],
            far.at[a, at(pieces[i])],
            far_send,
            far_recv.at[i, a],
            {"fsdp": g, "chan": a},
        )

    own_copy = remote(tokens, own, own_send, own_recv, {"chan": sibling})
    share = pl.ds(pl.multiple_of(group * (rows // 2), rows // 2), rows // 2)
    rest = pl.ds(pl.multiple_of((1 - group) * (rows // 2), rows // 2), rows // 2)
    taps_x_copy = remote(
        taps_h.at[share, columns(g)],
        taps.at[s, f, share],
        taps_x_send,
        taps_x_recv,
        across,
    )

    @pl.when(jnp.logical_not(holds))
    def _():
        for a in range(2):
            token_copy(0, a).start()

    taps_x_copy.start()

    @pl.when(jnp.logical_not(holds))
    def _():
        for a in range(2):
            token_copy(1, a).start()

    @pl.when(holds)
    def _():
        own_copy.start()

    @pl.when(f == 0)
    def _():
        pl.semaphore_signal(near, inc=1, device_id=beside, device_id_type=MESH)

    for t in range(seq):
        for h in range(2):

            @pl.when(t < s)
            def _():
                pl.semaphore_signal(
                    ready, inc=1, device_id={"seq": t, "fsdp": h}, device_id_type=MESH
                )

    def part_copy(i):
        return remote(
            part_out.at[:, at(made[i])],
            part_in.at[:, at(made[i])],
            part_send,
            part_recv.at[i],
            across,
        )

    own_query_copy = remote(
        query_out.at[0], query_in.at[0], query_send, query_recv, across
    )

    def query_copy(i):
        return remote(
            query_out.at[1, at(made[i])],
            query_in.at[1, at(made[i])],
            query_send,
            query_recv,
            across,
        )

    def own_part(j):
        return jnp.dot(own[:, :depth], w[j, 0], preferred_element_type=F32) + jnp.dot(
            own[:, depth:], w[j, 1], preferred_element_type=F32
        )

    def far_part(j, span):
        rows_at = slice(*span)
        return jnp.dot(far[0, rows_at], w[j, 0], preferred_element_type=F32) + jnp.dot(
            far[1, rows_at], w[j, 1], preferred_element_type=F32
        )

    with jax.named_scope("own_rows"):
        arrive(own, own_recv)
        loads[0].wait()
        for j in range(2):
            term = own_part(j + 1)
            part_out[j] = term.astype(BF16)
            edge_out[0, j] = term[rows - 8 :]
        part_copy(0).start()

        @pl.when(f == 0)
        def _():
            edge_in[0] = edge_out[0]

    with jax.named_scope("own_query"):
        for load in loads[1:]:
            load.wait()
        term = own_part(0)
        query[f] = half_of(term)
        query_out[0] = other_half(term).astype(BF16)

        @pl.when(f == 1)
        def _():
            query_edge_out[0] = term[rows - 8 :, :lanes]
            query_edge_out[1] = term[rows - 8 :, lanes:]

    @pl.when(f == 0)
    def _():
        pl.semaphore_wait(near, 1)
        pl.semaphore_signal(near, inc=1, device_id=across, device_id_type=MESH)

    def edge_up(i):
        return remote(
            edge_out.at[i],
            edge_in.at[i],
            edge_send.at[i],
            edge_recv.at[i],
            {"seq": jnp.minimum(s + 1, last), "fsdp": 1},
        )

    edge_across = remote(
        edge_out.at[1], edge_in.at[1], edge_send.at[1], edge_recv.at[1], {"fsdp": 0}
    )

    def query_edge(h):
        return remote(
            query_edge_out.at[h],
            query_edge_in.at[f],
            query_edge_send,
            query_edge_recv,
            {"seq": jnp.minimum(s + 1, last), "fsdp": h},
        )

    def taps_z_copy(t):
        block = taps.at[s, :, share]
        return remote(block, block, taps_z_send, taps_z_recv, {"seq": t})

    def taps_y_copy(n):
        block = taps.at[pl.ds(0, n), :, share]
        return remote(block, block, taps_y_send.at[1], taps_y_recv.at[1], beside)

    own_taps_y = remote(
        taps.at[s, g, share],
        taps.at[s, g, share],
        taps_y_send.at[0],
        taps_y_recv.at[0],
        beside,
    )

    def forward_copy(i):
        block = far.at[c, at(pieces[i])]
        return remote(
            block, block, fwd_send, far_recv.at[i, c], {"chan": sibling}
        )

    def half_part(j, a, span):
        return jnp.dot(far[a, slice(*span)], w[j, a], preferred_element_type=F32)

    def take(i):
        with jax.named_scope("direct"):
            arrive(far.at[c, at(pieces[i])], far_recv.at[i, c])
        forward_copy(i).start()

    def take_other(i):
        arrive(far.at[sibling, at(pieces[i])], far_recv.at[i, sibling])

    with jax.named_scope("edge_rows"):
        take(0)
        for j in range(2):
            projected[j, 8 + rows - EDGE :] = half_part(j + 1, c, pieces[0])
        @pl.when(goes_up)
        def _():
            pl.semaphore_wait(ready, 2 * (last - s))

            @pl.when(f == 1)
            def _():
                edge_up(0).start()
                for h in range(2):
                    query_edge(h).start()

        with jax.named_scope("taps_up"):
            taps_load.wait()
            arrive(taps.at[s, g, share], taps_x_recv)
            for t in range(1, seq):

                @pl.when(t > s)
                def _():
                    taps_z_copy(t).start()

            @pl.when(f == 1)
            def _():
                pl.semaphore_wait(near, 1)

            own_taps_y.start()

        take_other(0)
        for j in range(2):
            term = projected[j, 8 + rows - EDGE :] + half_part(j + 1, sibling, pieces[0])
            projected[j, 8 + rows - EDGE :] = term
            edge_out[1, j] = term[EDGE - 8 :]

        @pl.when(f == 1)
        def _():
            edge_across.start()

        @pl.when(jnp.logical_not(holds))
        def _():
            for i in range(2, count + 1):
                for a in range(2):
                    token_copy(i, a).start()

        @pl.when(jnp.logical_and(f == 0, goes_up))
        def _():
            edge_up(1).start()
            term = far_part(0, pieces[0])
            query_edge_out[0] = term[EDGE - 8 :, :lanes]
            query_edge_out[1] = term[EDGE - 8 :, lanes:]
            for h in range(2):
                query_edge(h).start()

    def across_copy(i):
        return remote(
            halves.at[g, at(made[i])],
            signal.at[s, g, at(made[i])],
            across_send,
            across_recv,
            across,
        )

    def up_copy(i, t):
        return remote(
            halves.at[f, at(made[i])],
            signal.at[s, g, at(made[i])],
            up_send.at[i],
            up_recv.at[s, i],
            {"seq": t},
        )

    def cross_copy(i, t):
        return remote(
            halves.at[g, at(made[i])],
            signal.at[s, g, at(made[i])],
            up_send.at[i],
            up_recv.at[s, i],
            {"seq": t, "fsdp": g},
        )

    def direct_to(i, t):
        reach = seq if i == count - 1 else REACH
        return jnp.logical_and(t > s, t <= s + reach)

    def relayed(j):
        return jnp.logical_and(j + REACH <= s, goes_up)

    def relays():
        for j in range(seq - 1 - REACH):

            @pl.when(relayed(j))
            def _():
                for i in range(count - 1):
                    arrive(signal.at[j, :, at(made[i])], up_recv.at[j, i])
                    relay_copy(i, j).start()

    def cross_start(i, low):
        for t in range(1, seq):

            @pl.when(jnp.logical_and(direct_to(i, t), (s == 0) if low else (s > 0)))
            def _():
                cross_copy(i, t).start()

    def relay_copy(i, j):
        block = signal.at[j, :, at(made[i])]
        return remote(block, block, up_send.at[i], up_recv.at[j, i], {"seq": s + 1})

    def branch(j, span):
        low, high = span
        now = projected[j, 8 + low : 8 + high]
        one = projected[j, 7 + low : 7 + high]
        two = projected[j, 6 + low : 6 + high]
        return (
            short[0, j + 1 : j + 2, :] * now
            + short[1, j + 1 : j + 2, :] * one
            + short[2, j + 1 : j + 2, :] * two
        )

    def transform(values):
        whole = table[:2].reshape(2 * bins, bins)
        return jnp.dot(whole, values, preferred_element_type=F32)

    def taps_spectrum():
        ids = lax.broadcasted_iota(jnp.int32, (bins, lanes), 0)
        sign = 1.0 - 2.0 * (ids % 2).astype(F32)
        arrive(taps.at[s, g, rest], taps_y_recv.at[0])
        for n in range(1, seq):

            @pl.when(s == n)
            def _():
                arrive(taps.at[pl.ds(0, n), :, rest], taps_y_recv.at[1])

        for d in range(seq):

            @pl.when(d <= s)
            def _():
                spec = transform(taps[d].reshape(bins, lanes))
                real, imag = spec[:bins], spec[bins:]
                tapspec[d] = spec
                if d == 0:
                    response[0, 0] = sign * imag
                    response[0, 1] = -sign * real
                else:
                    response[d, 0] = tapspec[d - 1, :bins] + sign * imag
                    response[d, 1] = tapspec[d - 1, bins:] - sign * real

    for i in range(count):
        low, high = made[i]
        final_chunk = i == count - 1
        with jax.named_scope("tokens"):
            take(i + 1)
            if final_chunk:
                own_query_copy.start()
                for r in range(i):
                    query_copy(r).start()
                    cross_start(r, True)
            lines = slice(8 + spans[i][0], 8 + spans[i][1])
            for j in range(2):
                projected[j, lines] = half_part(j + 1, c, spans[i])
            if final_chunk:
                query_term[low:high] = half_part(0, c, made[i])
            if i == 0:
                with jax.named_scope("taps_side"):
                    for n in range(1, seq):

                        @pl.when(s == n)
                        def _():
                            arrive(taps.at[pl.ds(0, n), :, share], taps_z_recv)
                            taps_y_copy(n).start()

            take_other(i + 1)
            if not final_chunk:
                part_copy(i + 1).start()
        with jax.named_scope("chunk"):
            for j in range(2):
                projected[j, lines] += half_part(j + 1, sibling, spans[i])
        if i == 0:
            with jax.named_scope("edges"):

                @pl.when(jnp.logical_and(f == 1, s > 0))
                def _():
                    arrive(edge_in.at[0], edge_recv.at[0])

                @pl.when(jnp.logical_or(f == 0, s > 0))
                def _():
                    arrive(edge_in.at[1], edge_recv.at[1])

                for j in range(2):
                    projected[j, :8] = rounded(edge_in[0, j] + edge_in[1, j])
        with jax.named_scope("partial"):
            part_copy(i).wait_recv()
        with jax.named_scope("product"):
            for j in range(2):
                block = slice(8 + low, 8 + high)
                projected[j, block] = rounded(
                    projected[j, block] + part_in[j, low:high].astype(F32)
                )
            product = (branch(0, made[i]) * branch(1, made[i])).astype(BF16)
            halves[0, low:high] = product[:, :lanes]
            halves[1, low:high] = product[:, lanes:]
            across_copy(i).start()
            signal[s, g, low:high] = half_of(product)
            cross_start(i, False)
            for t in range(1, seq):

                @pl.when(direct_to(i, t))
                def _():
                    up_copy(i, t).start()

        if final_chunk:
            cross_start(i, True)
            relays()
        with jax.named_scope("far_query"):
            if final_chunk:
                term = query_term[low:high] + half_part(0, sibling, made[i])
            else:
                term = far_part(0, made[i])
            query[g, low:high] = half_of(term)
            query_out[1, low:high] = other_half(term).astype(BF16)
            if final_chunk:
                query_copy(i).start()
    def spectrum(j, d):
        spec = transform(signal[j].reshape(bins, lanes))
        real, imag = spec[:bins], spec[bins:]
        hr, hi = response[d, 0], response[d, 1]
        return real * hr - imag * hi, real * hi + imag * hr

    with jax.named_scope("taps_spectra"):
        taps_spectrum()

    with jax.named_scope("earlier_slabs"):
        result[...] = jnp.zeros_like(result)
        for d in range(1, seq):

            @pl.when(d <= s)
            def _():
                j = s - d

                @pl.when(jnp.logical_not(relayed(j)))
                def _():
                    for i in range(count - 1):
                        arrive(signal.at[j, :, at(made[i])], up_recv.at[j, i])

                arrive(signal.at[j, :, at(made[-1])], up_recv.at[j, count - 1])
                real, imag = spectrum(j, d)
                result[0] += real
                result[1] += imag

    with jax.named_scope("own_wait"):
        arrive(signal.at[s, f], across_recv)
    with jax.named_scope("own_slab"):
        real, imag = spectrum(s, 0)
        packed[0] = (result[0] + real).astype(BF16)
        packed[1] = (result[1] + imag).astype(BF16)

    with jax.named_scope("query"):
        arrive(query_in, query_recv)

        @pl.when(s > 0)
        def _():
            arrive(query_edge_in, query_edge_recv)

        mixed[:8] = rounded(query_edge_in[0] + query_edge_in[1])
        other = pl.multiple_of(8 + g * rows, 8)
        mine = pl.multiple_of(8 + f * rows, 8)
        mixed[pl.ds(other, rows)] = rounded(query[g] + query_in[0].astype(F32))
        mixed[pl.ds(mine, rows)] = rounded(query[f] + query_in[1].astype(F32))
        gate = [half_of(short[i, 0:1, :]) for i in range(3)]
        gated = gate[0] * mixed[8 : 8 + bins] + gate[1] * mixed[7 : 7 + bins]
        gated += gate[2] * mixed[6 : 6 + bins]
        query[...] = gated.reshape(2, rows, lanes)

    with jax.named_scope("finish"):
        factor = half_of(gain[...])

        def finish(b):
            lines = pl.ds(pl.multiple_of(b * rows, rows), rows)
            conv = jnp.dot(table[2, lines], packed[0], preferred_element_type=F32)
            conv += jnp.dot(table[3, lines], packed[1], preferred_element_type=F32)
            whole = conv + factor * signal[s, b].astype(F32)
            return (query[b] * whole).astype(BF16)

        out_across = remote(final, out.at[:, columns(f)], out_send, out_recv, across)
        final[...] = finish(g)
        out_across.start()
        out[:, columns(f)] = finish(f)

    with jax.named_scope("drain"):

        @pl.when(jnp.logical_not(holds))
        def _():
            arrive(far, far_send)

        @pl.when(holds)
        def _():
            own_copy.wait_send()

        taps_x_copy.wait_send()
        arrive(far.at[c], fwd_send)
        arrive(part_out, part_send)
        arrive(halves.at[g], across_send)
        arrive(query_out, query_send)
        own_taps_y.wait_send()

        @pl.when(f == 1)
        def _():
            edge_across.wait_send()

        @pl.when(goes_up)
        def _():
            edge_up(1 - f).wait_send()
            arrive(query_edge_out, query_edge_send)

        for n in range(1, seq):

            @pl.when(s == n)
            def _():
                taps_y_copy(n).wait_send()

            @pl.when(last - s == n)
            def _():
                sent = min(REACH, n) + max(last - n + 1 - REACH, 0)
                arrive(taps.at[pl.ds(0, n), :, share], taps_z_send)
                for i in range(count - 1):
                    arrive(signal.at[pl.ds(0, sent), :, at(made[i])], up_send.at[i])
                arrive(signal.at[pl.ds(0, n), :, at(made[-1])], up_send.at[count - 1])

    with jax.named_scope("out"):
        out_across.wait_send()
        arrive(out.at[:, columns(g)], out_recv)


def causal_device(seq, tokens, proj_weight, short_weight, skip_gain, filter_taps):
    rows = tokens.shape[0]
    depth, branches, width = proj_weight.shape
    lanes = width // 2
    step = depth // 2
    table = causal_tables(2 * rows)
    count = len(chunk_spans(rows))
    dma = pltpu.SemaphoreType.DMA
    hbm = pl.BlockSpec(memory_space=pl.ANY)
    scratch = [
        ((branches, 2, step, width), BF16),
        (table.shape, BF16),
        (short_weight.shape, F32),
        ((1, width), F32),
        ((rows, depth), BF16),
        ((2, rows, step), BF16),
        ((2, rows, width), BF16),
        ((2, rows, width), BF16),
        ((2, 2, 8, width), F32),
        ((2, 2, 8, width), F32),
        ((2, 8 + rows, width), F32),
        ((2, rows, lanes), BF16),
        ((seq, 2, rows, lanes), BF16),
        ((seq, 2, rows, lanes), BF16),
        ((seq, 4 * rows, lanes), F32),
        ((seq, 2, 2 * rows, lanes), F32),
        ((2, rows, lanes), F32),
        ((rows, width), F32),
        ((2, rows, lanes), BF16),
        ((2, rows, lanes), BF16),
        ((2, 8, lanes), F32),
        ((2, 8, lanes), F32),
        ((8 + 2 * rows, lanes), F32),
        ((2, 2 * rows, lanes), F32),
        ((2, 2 * rows, lanes), BF16),
        ((rows, lanes), BF16),
    ]
    sems = [
        (5,),
        (),
        (),
        (),
        (count + 1, 2),
        (),
        (),
        (count,),
        (2,),
        (2,),
        (),
        (),
        (count,),
        (seq, count),
        (),
        (),
        (),
        (),
        (),
        (2,),
        (2,),
        (),
        (),
        (),
        (),
        (),
        (),
    ]
    return pl.pallas_call(
        functools.partial(causal_kernel, seq),
        out_shape=pltpu.VMEM((rows, width), BF16),
        in_specs=[hbm] * 6,
        out_specs=pl.BlockSpec(memory_space=pltpu.VMEM),
        scratch_shapes=[pltpu.VMEM(shape, kind) for shape, kind in scratch]
        + [dma(shape) for shape in sems]
        + [pltpu.SemaphoreType.REGULAR] * 2,
        compiler_params=pltpu.CompilerParams(
            collective_id=0, has_side_effects=True, vmem_limit_bytes=60 * 1024 * 1024
        ),
        name="hyena",
    )(
        tokens,
        jnp.transpose(proj_weight, (1, 0, 2)).reshape(branches, 2, step, width),
        short_weight,
        skip_gain.reshape(1, width),
        filter_taps,
        jnp.asarray(table),
    )


def solution(mesh):
    seq = mesh.shape["seq"]
    paired = all(mesh.shape[axis] == 2 for axis in ("grp", "fsdp", "chan"))
    sizes = (mesh.shape["seq"], mesh.shape["fsdp"], mesh.shape["chan"])
    in_specs = (
        P(("grp", "seq", "fsdp"), "chan"),
        P("fsdp", None, "chan"),
        P(None, None, "chan"),
        P("chan"),
        P(("seq", "fsdp"), "chan"),
    )
    out_specs = P(("grp", "seq", "fsdp"), "chan")
    return jax.shard_map(
        functools.partial(causal_device, seq)
        if paired
        else functools.partial(per_device, sizes),
        mesh=mesh,
        in_specs=in_specs,
        out_specs=out_specs,
        check_vma=False,
    )
```

```python
import functools
import math

import jax
import jax.numpy as jnp
import ml_dtypes
import numpy as np
from jax import lax
from jax.experimental import pallas as pl
from jax.experimental.pallas import tpu as pltpu
from jax.sharding import PartitionSpec as P

MESH = pl.DeviceIdType.MESH
BF16 = jnp.bfloat16
F32 = jnp.float32
MOST_CHUNKS = 2
HALVES = 2
EDGE = 16
CHUNK = 80
REACH = 2


def phase_pair(rows, cols, period):
    wrapped = (np.arange(rows)[:, None] * np.arange(cols)[None, :]) % period
    phase = wrapped.astype(np.float32) * np.float32(2.0 * math.pi / period)
    return np.cos(phase), np.sin(phase)


def tables(groups, per, rows):
    bf = ml_dtypes.bfloat16
    bins = 2 * groups
    cos, sin = phase_pair(bins, groups, bins)
    eye = np.eye(per, dtype=np.float32)
    first = np.concatenate([np.kron(cos, eye), np.kron(-sin, eye)], axis=0).astype(bf)
    cos, sin = phase_pair(rows, rows, rows)
    ahead = np.block([[cos, -sin], [sin, cos]]).astype(bf)
    behind = np.block([[cos, sin], [-sin, cos]]).astype(bf)
    cos, sin = phase_pair(bins, rows, bins * rows)
    twist = np.stack([np.repeat(cos, per, axis=0), np.repeat(sin, per, axis=0)])
    last = np.ascontiguousarray(first.T)
    return first, last, ahead, behind, twist.astype(np.float32)


def kernel(
    sizes,
    tokens,
    weight,
    short_h,
    gain_h,
    taps_h,
    first_h,
    last_h,
    ahead_h,
    behind_h,
    twist_h,
    out,
    w,
    first,
    last,
    ahead,
    behind,
    twist,
    short,
    gain,
    taps,
    held,
    acc,
    psend,
    precv,
    hrecv,
    query,
    product,
    tsend,
    trecv,
    gsend,
    grecv,
    csend,
    crecv,
    tapspec,
    load_sem,
    tok_send,
    tok_recv,
    fwd_send,
    part_send,
    part_recv,
    halo_send,
    halo_recv,
    a2a_send,
    a2a_recv,
):
    seq, fsdp, chan = sizes
    groups = seq * fsdp
    rows = tokens.shape[0]
    chunks = weight.shape[1]
    lines = rows // HALVES
    depth = chunks * weight.shape[2]
    width = weight.shape[3]
    per = width // groups
    bins = 2 * groups
    step = depth // chunks
    share = fsdp // chan
    s = lax.axis_index("seq")
    f = lax.axis_index("fsdp")
    c = lax.axis_index("chan")
    me = s * fsdp + f

    loads = [
        pltpu.make_async_copy(source, target, load_sem.at[i])
        for i, (source, target) in enumerate(
            [
                (taps_h, taps),
                (weight.at[pl.ds(1, 2)], w.at[pl.ds(1, 2)]),
                (first_h, first),
                (ahead_h, ahead),
                (twist_h, twist),
                (last_h, last),
                (behind_h, behind),
                (short_h, short),
                (gain_h, gain),
                (weight.at[pl.ds(0, 1)], w.at[pl.ds(0, 1)]),
            ]
        )
    ]
    for load in loads:
        load.start()

    barrier = pltpu.get_barrier_semaphore()
    everyone = groups * chan

    def greet(k, carry):
        other = lax.rem(me * chan + c + k, everyone)
        spot = other // chan
        pl.semaphore_signal(
            barrier,
            inc=1,
            device_id={"seq": spot // fsdp, "fsdp": spot % fsdp, "chan": other % chan},
            device_id_type=MESH,
        )
        return carry

    lax.fori_loop(1, everyone, greet, 0, unroll=everyone <= 16)

    @pl.when(me == 0)
    def _():
        hrecv[...] = jnp.zeros_like(hrecv)

    loads[0].wait()
    tsend[...] = jnp.transpose(taps[...].astype(F32)).astype(BF16).reshape(groups, per, rows)
    pl.semaphore_wait(barrier, everyone - 1)

    sibling = lax.rem(c + 1, chan)

    def span(h):
        return pl.ds(h * lines, lines)

    def token_copy(i, h, k, same):
        return pltpu.make_async_remote_copy(
            src_ref=tokens.at[span(h), pl.ds(i * depth + k * step, step)],
            dst_ref=held.at[f, k, span(h)],
            send_sem=tok_send.at[i, h, k],
            recv_sem=tok_recv.at[f, h, k],
            device_id={"fsdp": c * share + i, "chan": sibling if same else k % chan},
            device_id_type=MESH,
        )

    for h, k in [(h, k) for h in range(HALVES) for k in range(chunks)]:
        for i in range(share):
            stays = c * share + i == f

            @pl.when(jnp.logical_not(stays))
            def _():
                token_copy(i, h, k, False).start()

            @pl.when(stays)
            def _():
                token_copy(i, h, k, True).start()
                pltpu.make_async_copy(
                    tokens.at[span(h), pl.ds(i * depth + k * step, step)],
                    held.at[f, k, span(h)],
                    tok_recv.at[f, h, k],
                ).start()

    def exchange_copy(which, source, target, k):
        other = lax.rem(me + k, groups)
        return pltpu.make_async_remote_copy(
            src_ref=source.at[other],
            dst_ref=target.at[me],
            send_sem=a2a_send.at[which, k],
            recv_sem=a2a_recv.at[which, k],
            device_id={"seq": other // fsdp, "fsdp": other % fsdp},
            device_id_type=MESH,
        )

    def exchange_start(which, source, target):
        def go(k, carry):
            exchange_copy(which, source, target, k).start()
            return carry

        lax.fori_loop(1, groups, go, 0, unroll=groups <= 8)
        target[me] = source[me]

    def exchange_wait(which, source, target):
        def go(k, carry):
            exchange_copy(which, source, target, k).wait_recv()
            return carry

        lax.fori_loop(1, groups, go, 0, unroll=groups <= 8)

    def exchange_sent(which, source, target):
        def go(k, carry):
            exchange_copy(which, source, target, k).wait_send()
            return carry

        lax.fori_loop(1, groups, go, 0)


    half = bins * per

    def spectrum(signal):
        a = jnp.dot(first[...], signal, preferred_element_type=F32)
        real_a, imag_a = a[:half], a[half:]
        real_b = (real_a * twist[0] + imag_a * twist[1]).astype(BF16)
        imag_b = (imag_a * twist[0] - real_a * twist[1]).astype(BF16)
        b = jnp.concatenate([real_b, imag_b], axis=1)
        return jnp.dot(b, ahead[...], preferred_element_type=F32).astype(BF16)

    def arrival(spot, h, k):
        block = held.at[spot, k, span(h)]
        pltpu.make_async_copy(block, block, tok_recv.at[spot, h, k]).wait()

    def forward_copy(d, h, t):
        k = t * chan + c
        block = held.at[lax.rem(f + d, fsdp), k, span(h)]
        return pltpu.make_async_remote_copy(
            src_ref=block,
            dst_ref=block,
            send_sem=fwd_send.at[d - 1, h, t],
            recv_sem=tok_recv.at[lax.rem(f + d, fsdp), h, k],
            device_id={"chan": sibling},
            device_id_type=MESH,
        )

    def part_copy(d, j, h):
        return pltpu.make_async_remote_copy(
            src_ref=psend.at[d - 1, j, span(h)],
            dst_ref=precv.at[d - 1, j, span(h)],
            send_sem=part_send.at[d - 1, j, h],
            recv_sem=part_recv.at[d - 1, j, h],
            device_id={"fsdp": lax.rem(f + d, fsdp)},
            device_id_type=MESH,
        )

    phases = ((1, 2), (0, 1))

    def halo_target(d):
        return s * fsdp + lax.rem(f + d, fsdp) + 1

    def halo_copy(d, phase):
        target = jnp.minimum(halo_target(d), groups - 1)
        start, count = phases[phase]
        return pltpu.make_async_remote_copy(
            src_ref=acc.at[d - 1, pl.ds(start, count), pl.ds(rows - 8, 8)],
            dst_ref=hrecv.at[f, pl.ds(start, count)],
            send_sem=halo_send.at[d - 1, phase],
            recv_sem=halo_recv.at[f, phase],
            device_id={"seq": target // fsdp, "fsdp": target % fsdp},
            device_id_type=MESH,
        )

    def halo_remote(d):
        target = halo_target(d)
        return jnp.logical_and(target < groups, target != me)

    def halo_start(d, phase):
        @pl.when(halo_remote(d))
        def _():
            halo_copy(d, phase).start()

        start, count = phases[phase]

        @pl.when(halo_target(d) == me)
        def _():
            hrecv[f, start : start + count] = acc[d - 1, start : start + count, rows - 8 :]

    def halo_wait(phase):
        start, count = phases[phase]
        for h in range(fsdp):
            local = jnp.logical_and(f > 0, f == h)

            @pl.when(jnp.logical_and(me > 0, jnp.logical_not(local)))
            def _():
                block = hrecv.at[h, pl.ds(start, count)]
                pltpu.make_async_copy(block, block, halo_recv.at[h, phase]).wait()

    loads[1].wait()
    for k in range(chunks):
        for h in range(HALVES):
            arrival(f, h, k)
        for j in (1, 2):
            term = jnp.dot(held[f, k], w[j, k], preferred_element_type=F32)
            acc[fsdp - 1, j] = term if k == 0 else acc[fsdp - 1, j] + term
    halo_start(fsdp, 0)

    for d in range(1, fsdp):
        spot = lax.rem(f + d, fsdp)
        for h, t, b in [
            (h, t, b)
            for h in range(HALVES)
            for t in range(chunks // chan)
            for b in range(chan)
        ]:
            k = t * chan + lax.rem(c + b, chan)
            arrival(spot, h, k)
            if b == 0:
                forward_copy(d, h, t).start()
            final = (t + 1) * chan == chunks and b == chan - 1
            at = slice(h * lines, (h + 1) * lines)
            for j in (1, 2):
                term = jnp.dot(held[spot, k, at], w[j, k], preferred_element_type=F32)
                if t > 0 or b > 0:
                    term = acc[d - 1, j, at] + term
                acc[d - 1, j, at] = term
                if final:
                    psend[d - 1, j, at] = term.astype(BF16)
                    part_copy(d, j, h).start()
        halo_start(d, 0)

    for load in loads[2:]:
        load.wait()
    exchange_start(0, tsend, trecv)

    row_ids = lax.broadcasted_iota(jnp.int32, (rows, width), 0)

    def branch(j):
        total = acc[fsdp - 1, j]
        edge = hrecv[0, j]
        for d in range(1, fsdp):
            for h in range(HALVES):
                part_copy(d, j, h).wait_recv()
            total = total + precv[d - 1, j].astype(F32)
            edge = edge + hrecv[d, j]
        now = total.astype(BF16).astype(F32)
        edge = edge.astype(BF16).astype(F32)
        before = edge[7:8]
        earlier = edge[6:7]
        one = jnp.where(row_ids == 0, before, pltpu.roll(now, 1, 0))
        two = jnp.where(
            row_ids == 0, earlier, jnp.where(row_ids == 1, before, pltpu.roll(now, 2, 0))
        )
        return (
            short[0, j : j + 1, :] * now
            + short[1, j : j + 1, :] * one
            + short[2, j : j + 1, :] * two
        )

    halo_wait(0)
    prod = (branch(1) * branch(2)).astype(BF16).astype(F32)
    gsend[...] = jnp.transpose(prod).astype(BF16).reshape(groups, per, rows)
    exchange_start(1, gsend, grecv)
    product[...] = prod * gain[...]

    for d in range(1, fsdp + 1):
        spot = lax.rem(f + d, fsdp)
        term = jnp.dot(held[spot, 0], w[0, 0], preferred_element_type=F32)
        for k in range(1, chunks):
            term += jnp.dot(held[spot, k], w[0, k], preferred_element_type=F32)
        acc[d - 1, 0] = term
        if d < fsdp:
            psend[d - 1, 0] = term.astype(BF16)

    exchange_wait(0, tsend, trecv)
    tapspec[...] = spectrum(trecv[...].reshape(width, rows))
    exchange_wait(1, gsend, grecv)
    for d in range(1, fsdp + 1):
        if d < fsdp:
            for h in range(HALVES):
                part_copy(d, 0, h).start()
        halo_start(d, 1)

    x = spectrum(grecv[...].reshape(width, rows)).astype(F32)
    t = tapspec[...].astype(F32)
    xr, xi = x[:, :rows], x[:, rows:]
    tr, ti = t[:, :rows], t[:, rows:]
    real_z = (xr * tr - xi * ti).astype(BF16)
    imag_z = (xr * ti + xi * tr).astype(BF16)
    z = jnp.concatenate([real_z, imag_z], axis=1)
    v = jnp.dot(z, behind[...], preferred_element_type=F32)
    vr, vi = v[:, :rows], v[:, rows:]
    real_w = (vr * twist[0] - vi * twist[1]).astype(BF16)
    imag_w = (vi * twist[0] + vr * twist[1]).astype(BF16)
    packed = jnp.concatenate([real_w, imag_w], axis=0)
    y = jnp.dot(last[...], packed, preferred_element_type=F32) * (1.0 / (bins * rows))
    csend[...] = y.astype(BF16).reshape(groups, per, rows)
    exchange_start(2, csend, crecv)
    halo_wait(1)
    query[...] = branch(0)
    exchange_wait(2, csend, crecv)
    conv = jnp.transpose(crecv[...].reshape(width, rows).astype(F32))
    out[...] = (query[...] * (conv + product[...])).astype(BF16)

    exchange_sent(0, tsend, trecv)
    exchange_sent(1, gsend, grecv)
    exchange_sent(2, csend, crecv)
    for d in range(1, fsdp + 1):
        for phase in range(2):

            @pl.when(halo_remote(d))
            def _():
                halo_copy(d, phase).wait_send()

    for d in range(1, fsdp):
        for h in range(HALVES):
            for j in range(3):
                part_copy(d, j, h).wait_send()
            for t in range(chunks // chan):
                forward_copy(d, h, t).wait_send()
    for h, k in [(h, k) for h in range(HALVES) for k in range(chunks)]:
        for i in range(share):
            token_copy(i, h, k, False).wait_send()


def per_device(sizes, tokens, proj_weight, short_weight, skip_gain, filter_taps):
    seq, fsdp, chan = sizes
    groups = seq * fsdp
    rows = tokens.shape[0]
    depth, branches, width = proj_weight.shape
    per = width // groups
    chunks = min(MOST_CHUNKS, depth // 128)
    made = tables(groups, per, rows)
    dma = pltpu.SemaphoreType.DMA
    vmem = pl.BlockSpec(memory_space=pltpu.VMEM)
    hbm = pl.BlockSpec(memory_space=pl.ANY)
    half = 2 * groups * per
    return pl.pallas_call(
        functools.partial(kernel, sizes),
        out_shape=jax.ShapeDtypeStruct((rows, width), BF16),
        in_specs=[hbm] * 10,
        out_specs=vmem,
        scratch_shapes=[
            pltpu.VMEM((branches, chunks, depth // chunks, width), BF16),
            pltpu.VMEM(made[0].shape, BF16),
            pltpu.VMEM(made[1].shape, BF16),
            pltpu.VMEM(made[2].shape, BF16),
            pltpu.VMEM(made[3].shape, BF16),
            pltpu.VMEM(made[4].shape, F32),
            pltpu.VMEM(short_weight.shape, F32),
            pltpu.VMEM((1, width), F32),
            pltpu.VMEM((rows, width), BF16),
            pltpu.VMEM((fsdp, chunks, rows, depth // chunks), BF16),
            pltpu.VMEM((fsdp, branches, rows, width), F32),
            pltpu.VMEM((fsdp - 1, branches, rows, width), BF16),
            pltpu.VMEM((fsdp - 1, branches, rows, width), BF16),
            pltpu.VMEM((fsdp, branches, 8, width), F32),
            pltpu.VMEM((rows, width), F32),
            pltpu.VMEM((rows, width), F32),
        ]
        + [pltpu.VMEM((groups, per, rows), BF16)] * 6
        + [
            pltpu.VMEM((half, 2 * rows), BF16),
            dma((10,)),
            dma((fsdp // chan, HALVES, chunks)),
            dma((fsdp, HALVES, chunks)),
            dma((fsdp - 1, HALVES, chunks // chan)),
            dma((fsdp - 1, branches, HALVES)),
            dma((fsdp - 1, branches, HALVES)),
            dma((fsdp, 2)),
            dma((fsdp, 2)),
            dma((3, groups)),
            dma((3, groups)),
        ],
        compiler_params=pltpu.CompilerParams(
            collective_id=0, has_side_effects=True, vmem_limit_bytes=60 * 1024 * 1024
        ),
        name="hyena",
    )(
        tokens,
        jnp.transpose(proj_weight, (1, 0, 2)).reshape(branches, chunks, depth // chunks, width),
        short_weight,
        skip_gain.reshape(1, width),
        filter_taps,
        *[jnp.asarray(table) for table in made],
    )


def causal_tables(rows):
    bf = ml_dtypes.bfloat16
    odd = 2 * np.arange(rows) + 1
    period = 4 * rows

    def angles(times):
        wrapped = (odd[:, None] * times[None, :]) % period
        return wrapped.astype(np.float64) * (2.0 * math.pi / period)

    ahead = angles(np.arange(rows))
    behind = angles(rows + np.arange(rows)).T
    pair = [np.cos(behind) / rows, -np.sin(behind) / rows]
    return np.stack([np.cos(ahead), -np.sin(ahead), *pair]).astype(bf)


def chunk_spans(rows):
    head = rows - EDGE
    return [(at, min(at + CHUNK, head)) for at in range(0, head, CHUNK)]


def causal_kernel(
    seq,
    tokens,
    weight,
    short_h,
    gain_h,
    taps_h,
    table_h,
    out,
    w,
    table,
    short,
    gain,
    own,
    far,
    part_out,
    part_in,
    edge_out,
    edge_in,
    projected,
    halves,
    signal,
    taps,
    tapspec,
    response,
    query,
    query_term,
    query_out,
    query_in,
    query_edge_out,
    query_edge_in,
    mixed,
    result,
    packed,
    final,
    query_near,
    short_near,
    load_sem,
    own_send,
    own_recv,
    far_recv,
    fwd_send,
    part_send,
    part_recv,
    edge_send,
    edge_recv,
    across_send,
    across_recv,
    up_send,
    up_recv,
    taps_local,
    taps_x_send,
    taps_x_recv,
    taps_z_send,
    taps_z_recv,
    taps_y_send,
    taps_y_recv,
    query_send,
    query_recv,
    query_edge_send,
    query_edge_recv,
    out_send,
    out_recv,
    query_aside_send,
    query_aside_recv,
    short_send,
    short_recv,
    gain_send,
    gain_recv,
    taps_local_send,
    ready,
    near,
):
    rows = tokens.shape[0]
    width = weight.shape[3]
    depth = weight.shape[2]
    lanes = width // 2
    bins = 2 * rows
    last = seq - 1
    spans = chunk_spans(rows)
    count = len(spans)
    pieces = [(rows - EDGE, rows), *spans]
    made = [*spans[:-1], (spans[-1][0], rows)]
    group = lax.axis_index("grp")
    s = lax.axis_index("seq")
    f = lax.axis_index("fsdp")
    c = lax.axis_index("chan")
    g = 1 - f
    sibling = 1 - c
    holds = c == f
    goes_up = s < last
    across = {"fsdp": g}
    aside = {"chan": sibling}
    diagonal = {"fsdp": g, "chan": sibling}

    def half_of(value):
        return jnp.where(f == 0, value[:, :lanes], value[:, lanes:])

    def other_half(value):
        return jnp.where(f == 0, value[:, lanes:], value[:, :lanes])

    def rounded(value):
        return value.astype(BF16).astype(F32)

    def columns(h):
        return pl.ds(pl.multiple_of(h * lanes, lanes), lanes)

    def at(span):
        return pl.ds(span[0], span[1] - span[0])

    def remote(source, target, send, recv, device):
        return pltpu.make_async_remote_copy(
            src_ref=source,
            dst_ref=target,
            send_sem=send,
            recv_sem=recv,
            device_id=device,
            device_id_type=MESH,
        )

    def arrive(block, sem):
        pltpu.make_async_copy(block, block, sem).wait()

    own_load = pltpu.make_async_copy(tokens, own, own_recv)

    @pl.when(holds)
    def _():
        own_load.start()

    loads = [
        pltpu.make_async_copy(source, target, load_sem.at[i])
        for i, (source, target) in enumerate(
            [
                (weight.at[pl.ds(1, 2)], w.at[pl.ds(1, 2)]),
                (weight.at[pl.ds(0, 1)], w.at[pl.ds(0, 1)]),
                (table_h, table),
                (short_h, short),
            ]
        )
    ]
    for load in loads:
        load.start()
    edge_in[...] = jnp.zeros_like(edge_in)
    query_edge_in[...] = jnp.zeros_like(query_edge_in)

    def member(t, h):
        return {"seq": t, "fsdp": h // 2, "chan": h % 2}

    barrier = pltpu.get_barrier_semaphore()
    beside = {"grp": 1 - group}
    for device in [{"chan": sibling}, across, {"fsdp": g, "chan": sibling}]:
        pl.semaphore_signal(barrier, inc=1, device_id=device, device_id_type=MESH)

    @pl.when(f == 0)
    def _():
        pl.semaphore_signal(barrier, inc=1, device_id=beside, device_id_type=MESH)

    for t in range(seq):
        for h in range(4):

            @pl.when(t > s)
            def _():
                pl.semaphore_signal(
                    barrier, inc=1, device_id=member(t, h), device_id_type=MESH
                )

    pl.semaphore_wait(barrier, 3 + g + 4 * s)

    def token_copy(i, a):
        return remote(
            tokens.at[at(pieces[i]), pl.ds(a * depth, depth)],
            far.at[a, at(pieces[i])],
            own_send,
            far_recv.at[i, a],
            {"fsdp": g, "chan": a},
        )

    own_copy = remote(tokens, own, own_send, own_recv, aside)
    short_copy = remote(short_h, short_near, short_send, short_recv, aside)
    gain_copy = remote(gain_h, gain, gain_send, gain_recv, aside)
    taps_aside = remote(
        taps_h.at[:, columns(f)], taps.at[s, f], taps_local_send, taps_local, aside
    )
    share = pl.ds(pl.multiple_of(group * (rows // 2), rows // 2), rows // 2)
    rest = pl.ds(pl.multiple_of((1 - group) * (rows // 2), rows // 2), rows // 2)
    taps_x_copy = remote(
        taps_h.at[share, columns(g)],
        taps.at[s, f, share],
        taps_x_send,
        taps_x_recv,
        diagonal,
    )

    @pl.when(jnp.logical_not(holds))
    def _():
        for a in range(2):
            token_copy(0, a).start()

    taps_x_copy.start()

    @pl.when(jnp.logical_not(holds))
    def _():
        for a in range(2):
            token_copy(1, a).start()

    @pl.when(holds)
    def _():
        own_copy.start()

    taps_aside.start()
    short_copy.start()
    gain_copy.start()

    @pl.when(f == 0)
    def _():
        pl.semaphore_signal(near, inc=1, device_id=beside, device_id_type=MESH)

    for t in range(seq):
        for h in range(4):

            @pl.when(t < s)
            def _():
                pl.semaphore_signal(
                    ready, inc=1, device_id=member(t, h), device_id_type=MESH
                )

    def part_copy(i):
        return remote(
            part_out.at[:, at(made[i])],
            part_in.at[:, at(made[i])],
            part_send,
            part_recv.at[i],
            across,
        )

    own_query_copy = remote(
        query_out.at[0], query_in.at[0], query_send, query_recv, diagonal
    )

    def query_copy(i):
        return remote(
            query_out.at[1, at(made[i])],
            query_in.at[1, at(made[i])],
            query_send,
            query_recv,
            diagonal,
        )

    def query_aside(block):
        return remote(
            query.at[block],
            query_near.at[block],
            query_aside_send,
            query_aside_recv,
            aside,
        )

    def own_part(j):
        return jnp.dot(own[:, :depth], w[j, 0], preferred_element_type=F32) + jnp.dot(
            own[:, depth:], w[j, 1], preferred_element_type=F32
        )

    def far_part(j, span):
        rows_at = slice(*span)
        return jnp.dot(far[0, rows_at], w[j, 0], preferred_element_type=F32) + jnp.dot(
            far[1, rows_at], w[j, 1], preferred_element_type=F32
        )

    with jax.named_scope("own_rows"):
        arrive(own, own_recv)
        loads[0].wait()
        for j in range(2):
            term = own_part(j + 1)
            part_out[j] = term.astype(BF16)
            edge_out[0, j] = term[rows - 8 :]
        part_copy(0).start()

        @pl.when(f == 0)
        def _():
            edge_in[0] = edge_out[0]

    with jax.named_scope("own_query"):
        for load in loads[1:]:
            load.wait()
        term = own_part(0)
        query[f] = half_of(term)
        query_aside(f).start()
        query_out[0] = other_half(term).astype(BF16)

        @pl.when(f == 1)
        def _():
            query_edge_out[0] = term[rows - 8 :, :lanes]
            query_edge_out[1] = term[rows - 8 :, lanes:]

    @pl.when(f == 0)
    def _():
        pl.semaphore_wait(near, 1)
        pl.semaphore_signal(near, inc=1, device_id=across, device_id_type=MESH)

    def edge_up(i):
        return remote(
            edge_out.at[i],
            edge_in.at[i],
            edge_send,
            edge_recv,
            {"seq": jnp.minimum(s + 1, last), "fsdp": 1},
        )

    edge_across = remote(
        edge_out.at[1], edge_in.at[1], edge_send, edge_recv, {"fsdp": 0}
    )

    def query_edge(h):
        return remote(
            query_edge_out.at[h],
            query_edge_in.at[f],
            query_edge_send,
            query_edge_recv,
            {"seq": jnp.minimum(s + 1, last), "fsdp": h, "chan": sibling},
        )

    def taps_z_copy(t):
        block = taps.at[s, :, share]
        return remote(block, block, taps_z_send, taps_z_recv, {"seq": t})

    def taps_y_copy(n):
        block = taps.at[pl.ds(0, n), :, share]
        return remote(block, block, taps_y_send.at[1], taps_y_recv.at[1], beside)

    own_taps_y = remote(
        taps.at[s, g, share],
        taps.at[s, g, share],
        taps_y_send.at[0],
        taps_y_recv.at[0],
        beside,
    )

    def forward_copy(i):
        block = far.at[c, at(pieces[i])]
        return remote(
            block, block, fwd_send, far_recv.at[i, c], {"chan": sibling}
        )

    def half_part(j, a, span):
        return jnp.dot(far[a, slice(*span)], w[j, a], preferred_element_type=F32)

    def take(i):
        with jax.named_scope("direct"):
            arrive(far.at[c, at(pieces[i])], far_recv.at[i, c])
        forward_copy(i).start()

    def take_other(i):
        arrive(far.at[sibling, at(pieces[i])], far_recv.at[i, sibling])

    with jax.named_scope("edge_rows"):
        take(0)
        for j in range(2):
            projected[j, 8 + rows - EDGE :] = half_part(j + 1, c, pieces[0])
        @pl.when(goes_up)
        def _():
            pl.semaphore_wait(ready, 4 * (last - s))

            @pl.when(f == 1)
            def _():
                edge_up(0).start()
                for h in range(2):
                    query_edge(h).start()

        with jax.named_scope("taps_up"):
            arrive(taps.at[s, f], taps_local)
            arrive(taps.at[s, g, share], taps_x_recv)
            for t in range(1, seq):

                @pl.when(t > s)
                def _():
                    taps_z_copy(t).start()

            @pl.when(f == 1)
            def _():
                pl.semaphore_wait(near, 1)

            own_taps_y.start()

        take_other(0)
        for j in range(2):
            term = projected[j, 8 + rows - EDGE :] + half_part(j + 1, sibling, pieces[0])
            projected[j, 8 + rows - EDGE :] = term
            edge_out[1, j] = term[EDGE - 8 :]

        @pl.when(f == 1)
        def _():
            edge_across.start()

        @pl.when(jnp.logical_not(holds))
        def _():
            for i in range(2, count + 1):
                for a in range(2):
                    token_copy(i, a).start()

        @pl.when(jnp.logical_and(f == 0, goes_up))
        def _():
            edge_up(1).start()
            term = far_part(0, pieces[0])
            query_edge_out[0] = term[EDGE - 8 :, :lanes]
            query_edge_out[1] = term[EDGE - 8 :, lanes:]
            for h in range(2):
                query_edge(h).start()

    def across_copy(i):
        return remote(
            halves.at[g, at(made[i])],
            signal.at[s, g, at(made[i])],
            across_send,
            across_recv,
            diagonal,
        )

    def aside_copy(i):
        return remote(
            halves.at[f, at(made[i])],
            signal.at[s, g, at(made[i])],
            across_send,
            across_recv,
            aside,
        )

    def up_copy(i, t):
        return remote(
            halves.at[f, at(made[i])],
            signal.at[s, g, at(made[i])],
            up_send.at[i],
            up_recv.at[s, i],
            {"seq": t, "chan": sibling},
        )

    def cross_copy(i, t):
        return remote(
            halves.at[g, at(made[i])],
            signal.at[s, g, at(made[i])],
            up_send.at[i],
            up_recv.at[s, i],
            {"seq": t, "fsdp": g, "chan": sibling},
        )

    def direct_to(i, t):
        reach = seq if i == count - 1 else REACH
        return jnp.logical_and(t > s, t <= s + reach)

    def relayed(j):
        return jnp.logical_and(j + REACH <= s, goes_up)

    def relays():
        for j in range(seq - 1 - REACH):

            @pl.when(relayed(j))
            def _():
                for i in range(count - 1):
                    arrive(signal.at[j, :, at(made[i])], up_recv.at[j, i])
                    relay_copy(i, j).start()

    def cross_start(i, low):
        for t in range(1, seq):

            @pl.when(jnp.logical_and(direct_to(i, t), (s == 0) if low else (s > 0)))
            def _():
                cross_copy(i, t).start()

    def relay_copy(i, j):
        block = signal.at[j, :, at(made[i])]
        return remote(block, block, up_send.at[i], up_recv.at[j, i], {"seq": s + 1})

    def branch(j, span):
        low, high = span
        now = projected[j, 8 + low : 8 + high]
        one = projected[j, 7 + low : 7 + high]
        two = projected[j, 6 + low : 6 + high]
        return (
            short[0, j + 1 : j + 2, :] * now
            + short[1, j + 1 : j + 2, :] * one
            + short[2, j + 1 : j + 2, :] * two
        )

    def transform(values):
        whole = table[:2].reshape(2 * bins, bins)
        return jnp.dot(whole, values, preferred_element_type=F32)

    def taps_spectrum():
        ids = lax.broadcasted_iota(jnp.int32, (bins, lanes), 0)
        sign = 1.0 - 2.0 * (ids % 2).astype(F32)
        arrive(taps.at[s, g, rest], taps_y_recv.at[0])
        for n in range(1, seq):

            @pl.when(s == n)
            def _():
                arrive(taps.at[pl.ds(0, n), :, rest], taps_y_recv.at[1])

        for d in range(seq):

            @pl.when(d <= s)
            def _():
                spec = transform(taps[d].reshape(bins, lanes))
                real, imag = spec[:bins], spec[bins:]
                tapspec[d] = spec
                if d == 0:
                    response[0, 0] = sign * imag
                    response[0, 1] = -sign * real
                else:
                    response[d, 0] = tapspec[d - 1, :bins] + sign * imag
                    response[d, 1] = tapspec[d - 1, bins:] - sign * real

    for i in range(count):
        low, high = made[i]
        final_chunk = i == count - 1
        with jax.named_scope("tokens"):
            take(i + 1)
            if final_chunk:
                own_query_copy.start()
                for r in range(i):
                    query_copy(r).start()
                    cross_start(r, True)
            lines = slice(8 + spans[i][0], 8 + spans[i][1])
            for j in range(2):
                projected[j, lines] = half_part(j + 1, c, spans[i])
            if final_chunk:
                query_term[low:high] = half_part(0, c, made[i])
            if i == 0:
                with jax.named_scope("taps_side"):
                    for n in range(1, seq):

                        @pl.when(s == n)
                        def _():
                            arrive(taps.at[pl.ds(0, n), :, share], taps_z_recv)
                            taps_y_copy(n).start()

            take_other(i + 1)
            if not final_chunk:
                part_copy(i + 1).start()
        with jax.named_scope("chunk"):
            for j in range(2):
                projected[j, lines] += half_part(j + 1, sibling, spans[i])
        if i == 0:
            with jax.named_scope("edges"):

                @pl.when(jnp.logical_and(f == 1, s > 0))
                def _():
                    arrive(edge_in, edge_recv)

                @pl.when(f == 0)
                def _():
                    arrive(edge_in.at[1], edge_recv)

                for j in range(2):
                    projected[j, :8] = rounded(edge_in[0, j] + edge_in[1, j])
        with jax.named_scope("partial"):
            part_copy(i).wait_recv()
        with jax.named_scope("product"):
            for j in range(2):
                block = slice(8 + low, 8 + high)
                projected[j, block] = rounded(
                    projected[j, block] + part_in[j, low:high].astype(F32)
                )
            product = (branch(0, made[i]) * branch(1, made[i])).astype(BF16)
            halves[0, low:high] = product[:, :lanes]
            halves[1, low:high] = product[:, lanes:]
            across_copy(i).start()
            aside_copy(i).start()
            cross_start(i, False)
            for t in range(1, seq):

                @pl.when(direct_to(i, t))
                def _():
                    up_copy(i, t).start()

        if final_chunk:
            cross_start(i, True)
            relays()
        with jax.named_scope("far_query"):
            if final_chunk:
                term = query_term[low:high] + half_part(0, sibling, made[i])
            else:
                term = far_part(0, made[i])
            query[g, low:high] = half_of(term)
            query_aside((g, at(made[i]))).start()
            query_out[1, low:high] = other_half(term).astype(BF16)
            if final_chunk:
                query_copy(i).start()
    def spectrum(j, d):
        spec = transform(signal[j].reshape(bins, lanes))
        real, imag = spec[:bins], spec[bins:]
        hr, hi = response[d, 0], response[d, 1]
        return real * hr - imag * hi, real * hi + imag * hr

    with jax.named_scope("taps_spectra"):
        taps_spectrum()

    with jax.named_scope("earlier_slabs"):
        result[...] = jnp.zeros_like(result)
        for d in range(1, seq):

            @pl.when(d <= s)
            def _():
                j = s - d

                @pl.when(jnp.logical_not(relayed(j)))
                def _():
                    for i in range(count - 1):
                        arrive(signal.at[j, :, at(made[i])], up_recv.at[j, i])

                arrive(signal.at[j, :, at(made[-1])], up_recv.at[j, count - 1])
                real, imag = spectrum(j, d)
                result[0] += real
                result[1] += imag

    arrive(short_near, short_recv)
    arrive(gain, gain_recv)
    with jax.named_scope("own_wait"):
        arrive(signal.at[s], across_recv)
    with jax.named_scope("own_slab"):
        real, imag = spectrum(s, 0)
        packed[0] = (result[0] + real).astype(BF16)
        packed[1] = (result[1] + imag).astype(BF16)

    with jax.named_scope("query"):
        arrive(query_in, query_recv)
        arrive(query_near, query_aside_recv)

        @pl.when(s > 0)
        def _():
            arrive(query_edge_in, query_edge_recv)

        mixed[:8] = rounded(query_edge_in[0] + query_edge_in[1])
        other = pl.multiple_of(8 + g * rows, 8)
        mine = pl.multiple_of(8 + f * rows, 8)
        mixed[pl.ds(other, rows)] = rounded(query_near[g] + query_in[0].astype(F32))
        mixed[pl.ds(mine, rows)] = rounded(query_near[f] + query_in[1].astype(F32))
        gate = [half_of(short_near[i, 0:1, :]) for i in range(3)]
        gated = gate[0] * mixed[8 : 8 + bins] + gate[1] * mixed[7 : 7 + bins]
        gated += gate[2] * mixed[6 : 6 + bins]
        query_near[...] = gated.reshape(2, rows, lanes)

    with jax.named_scope("finish"):
        factor = half_of(gain[...])

        def finish(b):
            lines = pl.ds(pl.multiple_of(b * rows, rows), rows)
            conv = jnp.dot(table[2, lines], packed[0], preferred_element_type=F32)
            conv += jnp.dot(table[3, lines], packed[1], preferred_element_type=F32)
            whole = conv + factor * signal[s, b].astype(F32)
            return (query_near[b] * whole).astype(BF16)

        landing = out.at[:, columns(f)]
        out_across = remote(final.at[0], landing, out_send, out_recv, diagonal)
        out_aside = remote(final.at[1], landing, out_send, out_recv, aside)
        final[0] = finish(g)
        out_across.start()
        final[1] = finish(f)
        out_aside.start()

    with jax.named_scope("drain"):

        @pl.when(jnp.logical_not(holds))
        def _():
            arrive(far, own_send)

        @pl.when(holds)
        def _():
            own_copy.wait_send()

        taps_x_copy.wait_send()
        arrive(far.at[c], fwd_send)
        arrive(part_out, part_send)
        arrive(halves, across_send)
        arrive(query, query_aside_send)
        short_copy.wait_send()
        gain_copy.wait_send()
        taps_aside.wait_send()
        arrive(query_out, query_send)
        own_taps_y.wait_send()

        @pl.when(jnp.logical_and(f == 1, goes_up))
        def _():
            arrive(edge_out, edge_send)

        @pl.when(f != jnp.where(goes_up, 1, 0))
        def _():
            arrive(edge_out.at[1], edge_send)

        @pl.when(goes_up)
        def _():
            arrive(query_edge_out, query_edge_send)

        for n in range(1, seq):

            @pl.when(s == n)
            def _():
                taps_y_copy(n).wait_send()

            @pl.when(last - s == n)
            def _():
                sent = min(REACH, n) + max(last - n + 1 - REACH, 0)
                arrive(taps.at[pl.ds(0, n), :, share], taps_z_send)
                for i in range(count - 1):
                    arrive(signal.at[pl.ds(0, sent), :, at(made[i])], up_send.at[i])
                arrive(signal.at[pl.ds(0, n), :, at(made[-1])], up_send.at[count - 1])

    with jax.named_scope("out"):
        arrive(final, out_send)
        arrive(out, out_recv)


def causal_device(seq, tokens, proj_weight, short_weight, skip_gain, filter_taps):
    rows = tokens.shape[0]
    depth, branches, width = proj_weight.shape
    lanes = width // 2
    step = depth // 2
    table = causal_tables(2 * rows)
    count = len(chunk_spans(rows))
    dma = pltpu.SemaphoreType.DMA
    hbm = pl.BlockSpec(memory_space=pl.ANY)
    scratch = [
        ((branches, 2, step, width), BF16),
        (table.shape, BF16),
        (short_weight.shape, F32),
        ((1, width), F32),
        ((rows, depth), BF16),
        ((2, rows, step), BF16),
        ((2, rows, width), BF16),
        ((2, rows, width), BF16),
        ((2, 2, 8, width), F32),
        ((2, 2, 8, width), F32),
        ((2, 8 + rows, width), F32),
        ((2, rows, lanes), BF16),
        ((seq, 2, rows, lanes), BF16),
        ((seq, 2, rows, lanes), BF16),
        ((seq, 4 * rows, lanes), F32),
        ((seq, 2, 2 * rows, lanes), F32),
        ((2, rows, lanes), F32),
        ((rows, width), F32),
        ((2, rows, lanes), BF16),
        ((2, rows, lanes), BF16),
        ((2, 8, lanes), F32),
        ((2, 8, lanes), F32),
        ((8 + 2 * rows, lanes), F32),
        ((2, 2 * rows, lanes), F32),
        ((2, 2 * rows, lanes), BF16),
        ((2, rows, lanes), BF16),
        ((2, rows, lanes), F32),
        (short_weight.shape, F32),
    ]
    sems = [
        (4,),
        (),
        (),
        (count + 1, 2),
        (),
        (),
        (count,),
        (),
        (),
        (),
        (),
        (count,),
        (max(seq - 1, 1), count),
        (),
        (),
        (),
        (),
        (),
        (2,),
        (2,),
        (),
        (),
        (),
        (),
        (),
        (),
        (),
        (),
        (),
        (),
        (),
        (),
        (),
    ]
    return pl.pallas_call(
        functools.partial(causal_kernel, seq),
        out_shape=pltpu.VMEM((rows, width), BF16),
        in_specs=[hbm] * 6,
        out_specs=pl.BlockSpec(memory_space=pltpu.VMEM),
        scratch_shapes=[pltpu.VMEM(shape, kind) for shape, kind in scratch]
        + [dma(shape) for shape in sems]
        + [pltpu.SemaphoreType.REGULAR] * 2,
        compiler_params=pltpu.CompilerParams(
            collective_id=0, has_side_effects=True, vmem_limit_bytes=60 * 1024 * 1024
        ),
        name="hyena",
    )(
        tokens,
        jnp.transpose(proj_weight, (1, 0, 2)).reshape(branches, 2, step, width),
        short_weight,
        skip_gain.reshape(1, width),
        filter_taps,
        jnp.asarray(table),
    )


def solution(mesh):
    seq = mesh.shape["seq"]
    paired = all(mesh.shape[axis] == 2 for axis in ("grp", "fsdp", "chan"))
    sizes = (mesh.shape["seq"], mesh.shape["fsdp"], mesh.shape["chan"])
    in_specs = (
        P(("grp", "seq", "fsdp"), "chan"),
        P("fsdp", None, "chan"),
        P(None, None, "chan"),
        P("chan"),
        P(("seq", "fsdp"), "chan"),
    )
    out_specs = P(("grp", "seq", "fsdp"), "chan")
    return jax.shard_map(
        functools.partial(causal_device, seq)
        if paired
        else functools.partial(per_device, sizes),
        mesh=mesh,
        in_specs=in_specs,
        out_specs=out_specs,
        check_vma=False,
    )
```

```python
import functools
import math

import jax
import jax.numpy as jnp
import ml_dtypes
import numpy as np
from jax import lax
from jax.experimental import pallas as pl
from jax.experimental.pallas import tpu as pltpu
from jax.sharding import PartitionSpec as P

MESH = pl.DeviceIdType.MESH
BF16 = jnp.bfloat16
F32 = jnp.float32
MOST_CHUNKS = 2
HALVES = 2
EDGE = 16
CHUNK = 80


def phase_pair(rows, cols, period):
    wrapped = (np.arange(rows)[:, None] * np.arange(cols)[None, :]) % period
    phase = wrapped.astype(np.float32) * np.float32(2.0 * math.pi / period)
    return np.cos(phase), np.sin(phase)


def tables(groups, per, rows):
    bf = ml_dtypes.bfloat16
    bins = 2 * groups
    cos, sin = phase_pair(bins, groups, bins)
    eye = np.eye(per, dtype=np.float32)
    first = np.concatenate([np.kron(cos, eye), np.kron(-sin, eye)], axis=0).astype(bf)
    cos, sin = phase_pair(rows, rows, rows)
    ahead = np.block([[cos, -sin], [sin, cos]]).astype(bf)
    behind = np.block([[cos, sin], [-sin, cos]]).astype(bf)
    cos, sin = phase_pair(bins, rows, bins * rows)
    twist = np.stack([np.repeat(cos, per, axis=0), np.repeat(sin, per, axis=0)])
    last = np.ascontiguousarray(first.T)
    return first, last, ahead, behind, twist.astype(np.float32)


def kernel(
    sizes,
    tokens,
    weight,
    short_h,
    gain_h,
    taps_h,
    first_h,
    last_h,
    ahead_h,
    behind_h,
    twist_h,
    out,
    w,
    first,
    last,
    ahead,
    behind,
    twist,
    short,
    gain,
    taps,
    held,
    acc,
    psend,
    precv,
    hrecv,
    query,
    product,
    tsend,
    trecv,
    gsend,
    grecv,
    csend,
    crecv,
    tapspec,
    load_sem,
    tok_send,
    tok_recv,
    fwd_send,
    part_send,
    part_recv,
    halo_send,
    halo_recv,
    a2a_send,
    a2a_recv,
):
    seq, fsdp, chan = sizes
    groups = seq * fsdp
    rows = tokens.shape[0]
    chunks = weight.shape[1]
    lines = rows // HALVES
    depth = chunks * weight.shape[2]
    width = weight.shape[3]
    per = width // groups
    bins = 2 * groups
    step = depth // chunks
    share = fsdp // chan
    s = lax.axis_index("seq")
    f = lax.axis_index("fsdp")
    c = lax.axis_index("chan")
    me = s * fsdp + f

    loads = [
        pltpu.make_async_copy(source, target, load_sem.at[i])
        for i, (source, target) in enumerate(
            [
                (taps_h, taps),
                (weight.at[pl.ds(1, 2)], w.at[pl.ds(1, 2)]),
                (first_h, first),
                (ahead_h, ahead),
                (twist_h, twist),
                (last_h, last),
                (behind_h, behind),
                (short_h, short),
                (gain_h, gain),
                (weight.at[pl.ds(0, 1)], w.at[pl.ds(0, 1)]),
            ]
        )
    ]
    for load in loads:
        load.start()

    barrier = pltpu.get_barrier_semaphore()
    everyone = groups * chan

    def greet(k, carry):
        other = lax.rem(me * chan + c + k, everyone)
        spot = other // chan
        pl.semaphore_signal(
            barrier,
            inc=1,
            device_id={"seq": spot // fsdp, "fsdp": spot % fsdp, "chan": other % chan},
            device_id_type=MESH,
        )
        return carry

    lax.fori_loop(1, everyone, greet, 0, unroll=everyone <= 16)

    @pl.when(me == 0)
    def _():
        hrecv[...] = jnp.zeros_like(hrecv)

    loads[0].wait()
    tsend[...] = jnp.transpose(taps[...].astype(F32)).astype(BF16).reshape(groups, per, rows)
    pl.semaphore_wait(barrier, everyone - 1)

    sibling = lax.rem(c + 1, chan)

    def span(h):
        return pl.ds(h * lines, lines)

    def token_copy(i, h, k, same):
        return pltpu.make_async_remote_copy(
            src_ref=tokens.at[span(h), pl.ds(i * depth + k * step, step)],
            dst_ref=held.at[f, k, span(h)],
            send_sem=tok_send.at[i, h, k],
            recv_sem=tok_recv.at[f, h, k],
            device_id={"fsdp": c * share + i, "chan": sibling if same else k % chan},
            device_id_type=MESH,
        )

    for h, k in [(h, k) for h in range(HALVES) for k in range(chunks)]:
        for i in range(share):
            stays = c * share + i == f

            @pl.when(jnp.logical_not(stays))
            def _():
                token_copy(i, h, k, False).start()

            @pl.when(stays)
            def _():
                token_copy(i, h, k, True).start()
                pltpu.make_async_copy(
                    tokens.at[span(h), pl.ds(i * depth + k * step, step)],
                    held.at[f, k, span(h)],
                    tok_recv.at[f, h, k],
                ).start()

    def exchange_copy(which, source, target, k):
        other = lax.rem(me + k, groups)
        return pltpu.make_async_remote_copy(
            src_ref=source.at[other],
            dst_ref=target.at[me],
            send_sem=a2a_send.at[which, k],
            recv_sem=a2a_recv.at[which, k],
            device_id={"seq": other // fsdp, "fsdp": other % fsdp},
            device_id_type=MESH,
        )

    def exchange_start(which, source, target):
        def go(k, carry):
            exchange_copy(which, source, target, k).start()
            return carry

        lax.fori_loop(1, groups, go, 0, unroll=groups <= 8)
        target[me] = source[me]

    def exchange_wait(which, source, target):
        def go(k, carry):
            exchange_copy(which, source, target, k).wait_recv()
            return carry

        lax.fori_loop(1, groups, go, 0, unroll=groups <= 8)

    def exchange_sent(which, source, target):
        def go(k, carry):
            exchange_copy(which, source, target, k).wait_send()
            return carry

        lax.fori_loop(1, groups, go, 0)


    half = bins * per

    def spectrum(signal):
        a = jnp.dot(first[...], signal, preferred_element_type=F32)
        real_a, imag_a = a[:half], a[half:]
        real_b = (real_a * twist[0] + imag_a * twist[1]).astype(BF16)
        imag_b = (imag_a * twist[0] - real_a * twist[1]).astype(BF16)
        b = jnp.concatenate([real_b, imag_b], axis=1)
        return jnp.dot(b, ahead[...], preferred_element_type=F32).astype(BF16)

    def arrival(spot, h, k):
        block = held.at[spot, k, span(h)]
        pltpu.make_async_copy(block, block, tok_recv.at[spot, h, k]).wait()

    def forward_copy(d, h, t):
        k = t * chan + c
        block = held.at[lax.rem(f + d, fsdp), k, span(h)]
        return pltpu.make_async_remote_copy(
            src_ref=block,
            dst_ref=block,
            send_sem=fwd_send.at[d - 1, h, t],
            recv_sem=tok_recv.at[lax.rem(f + d, fsdp), h, k],
            device_id={"chan": sibling},
            device_id_type=MESH,
        )

    def part_copy(d, j, h):
        return pltpu.make_async_remote_copy(
            src_ref=psend.at[d - 1, j, span(h)],
            dst_ref=precv.at[d - 1, j, span(h)],
            send_sem=part_send.at[d - 1, j, h],
            recv_sem=part_recv.at[d - 1, j, h],
            device_id={"fsdp": lax.rem(f + d, fsdp)},
            device_id_type=MESH,
        )

    phases = ((1, 2), (0, 1))

    def halo_target(d):
        return s * fsdp + lax.rem(f + d, fsdp) + 1

    def halo_copy(d, phase):
        target = jnp.minimum(halo_target(d), groups - 1)
        start, count = phases[phase]
        return pltpu.make_async_remote_copy(
            src_ref=acc.at[d - 1, pl.ds(start, count), pl.ds(rows - 8, 8)],
            dst_ref=hrecv.at[f, pl.ds(start, count)],
            send_sem=halo_send.at[d - 1, phase],
            recv_sem=halo_recv.at[f, phase],
            device_id={"seq": target // fsdp, "fsdp": target % fsdp},
            device_id_type=MESH,
        )

    def halo_remote(d):
        target = halo_target(d)
        return jnp.logical_and(target < groups, target != me)

    def halo_start(d, phase):
        @pl.when(halo_remote(d))
        def _():
            halo_copy(d, phase).start()

        start, count = phases[phase]

        @pl.when(halo_target(d) == me)
        def _():
            hrecv[f, start : start + count] = acc[d - 1, start : start + count, rows - 8 :]

    def halo_wait(phase):
        start, count = phases[phase]
        for h in range(fsdp):
            local = jnp.logical_and(f > 0, f == h)

            @pl.when(jnp.logical_and(me > 0, jnp.logical_not(local)))
            def _():
                block = hrecv.at[h, pl.ds(start, count)]
                pltpu.make_async_copy(block, block, halo_recv.at[h, phase]).wait()

    loads[1].wait()
    for k in range(chunks):
        for h in range(HALVES):
            arrival(f, h, k)
        for j in (1, 2):
            term = jnp.dot(held[f, k], w[j, k], preferred_element_type=F32)
            acc[fsdp - 1, j] = term if k == 0 else acc[fsdp - 1, j] + term
    halo_start(fsdp, 0)

    for d in range(1, fsdp):
        spot = lax.rem(f + d, fsdp)
        for h, t, b in [
            (h, t, b)
            for h in range(HALVES)
            for t in range(chunks // chan)
            for b in range(chan)
        ]:
            k = t * chan + lax.rem(c + b, chan)
            arrival(spot, h, k)
            if b == 0:
                forward_copy(d, h, t).start()
            final = (t + 1) * chan == chunks and b == chan - 1
            at = slice(h * lines, (h + 1) * lines)
            for j in (1, 2):
                term = jnp.dot(held[spot, k, at], w[j, k], preferred_element_type=F32)
                if t > 0 or b > 0:
                    term = acc[d - 1, j, at] + term
                acc[d - 1, j, at] = term
                if final:
                    psend[d - 1, j, at] = term.astype(BF16)
                    part_copy(d, j, h).start()
        halo_start(d, 0)

    for load in loads[2:]:
        load.wait()
    exchange_start(0, tsend, trecv)

    row_ids = lax.broadcasted_iota(jnp.int32, (rows, width), 0)

    def branch(j):
        total = acc[fsdp - 1, j]
        edge = hrecv[0, j]
        for d in range(1, fsdp):
            for h in range(HALVES):
                part_copy(d, j, h).wait_recv()
            total = total + precv[d - 1, j].astype(F32)
            edge = edge + hrecv[d, j]
        now = total.astype(BF16).astype(F32)
        edge = edge.astype(BF16).astype(F32)
        before = edge[7:8]
        earlier = edge[6:7]
        one = jnp.where(row_ids == 0, before, pltpu.roll(now, 1, 0))
        two = jnp.where(
            row_ids == 0, earlier, jnp.where(row_ids == 1, before, pltpu.roll(now, 2, 0))
        )
        return (
            short[0, j : j + 1, :] * now
            + short[1, j : j + 1, :] * one
            + short[2, j : j + 1, :] * two
        )

    halo_wait(0)
    prod = (branch(1) * branch(2)).astype(BF16).astype(F32)
    gsend[...] = jnp.transpose(prod).astype(BF16).reshape(groups, per, rows)
    exchange_start(1, gsend, grecv)
    product[...] = prod * gain[...]

    for d in range(1, fsdp + 1):
        spot = lax.rem(f + d, fsdp)
        term = jnp.dot(held[spot, 0], w[0, 0], preferred_element_type=F32)
        for k in range(1, chunks):
            term += jnp.dot(held[spot, k], w[0, k], preferred_element_type=F32)
        acc[d - 1, 0] = term
        if d < fsdp:
            psend[d - 1, 0] = term.astype(BF16)

    exchange_wait(0, tsend, trecv)
    tapspec[...] = spectrum(trecv[...].reshape(width, rows))
    exchange_wait(1, gsend, grecv)
    for d in range(1, fsdp + 1):
        if d < fsdp:
            for h in range(HALVES):
                part_copy(d, 0, h).start()
        halo_start(d, 1)

    x = spectrum(grecv[...].reshape(width, rows)).astype(F32)
    t = tapspec[...].astype(F32)
    xr, xi = x[:, :rows], x[:, rows:]
    tr, ti = t[:, :rows], t[:, rows:]
    real_z = (xr * tr - xi * ti).astype(BF16)
    imag_z = (xr * ti + xi * tr).astype(BF16)
    z = jnp.concatenate([real_z, imag_z], axis=1)
    v = jnp.dot(z, behind[...], preferred_element_type=F32)
    vr, vi = v[:, :rows], v[:, rows:]
    real_w = (vr * twist[0] - vi * twist[1]).astype(BF16)
    imag_w = (vi * twist[0] + vr * twist[1]).astype(BF16)
    packed = jnp.concatenate([real_w, imag_w], axis=0)
    y = jnp.dot(last[...], packed, preferred_element_type=F32) * (1.0 / (bins * rows))
    csend[...] = y.astype(BF16).reshape(groups, per, rows)
    exchange_start(2, csend, crecv)
    halo_wait(1)
    query[...] = branch(0)
    exchange_wait(2, csend, crecv)
    conv = jnp.transpose(crecv[...].reshape(width, rows).astype(F32))
    out[...] = (query[...] * (conv + product[...])).astype(BF16)

    exchange_sent(0, tsend, trecv)
    exchange_sent(1, gsend, grecv)
    exchange_sent(2, csend, crecv)
    for d in range(1, fsdp + 1):
        for phase in range(2):

            @pl.when(halo_remote(d))
            def _():
                halo_copy(d, phase).wait_send()

    for d in range(1, fsdp):
        for h in range(HALVES):
            for j in range(3):
                part_copy(d, j, h).wait_send()
            for t in range(chunks // chan):
                forward_copy(d, h, t).wait_send()
    for h, k in [(h, k) for h in range(HALVES) for k in range(chunks)]:
        for i in range(share):
            token_copy(i, h, k, False).wait_send()


def per_device(sizes, tokens, proj_weight, short_weight, skip_gain, filter_taps):
    seq, fsdp, chan = sizes
    groups = seq * fsdp
    rows = tokens.shape[0]
    depth, branches, width = proj_weight.shape
    per = width // groups
    chunks = min(MOST_CHUNKS, depth // 128)
    made = tables(groups, per, rows)
    dma = pltpu.SemaphoreType.DMA
    vmem = pl.BlockSpec(memory_space=pltpu.VMEM)
    hbm = pl.BlockSpec(memory_space=pl.ANY)
    half = 2 * groups * per
    return pl.pallas_call(
        functools.partial(kernel, sizes),
        out_shape=jax.ShapeDtypeStruct((rows, width), BF16),
        in_specs=[hbm] * 10,
        out_specs=vmem,
        scratch_shapes=[
            pltpu.VMEM((branches, chunks, depth // chunks, width), BF16),
            pltpu.VMEM(made[0].shape, BF16),
            pltpu.VMEM(made[1].shape, BF16),
            pltpu.VMEM(made[2].shape, BF16),
            pltpu.VMEM(made[3].shape, BF16),
            pltpu.VMEM(made[4].shape, F32),
            pltpu.VMEM(short_weight.shape, F32),
            pltpu.VMEM((1, width), F32),
            pltpu.VMEM((rows, width), BF16),
            pltpu.VMEM((fsdp, chunks, rows, depth // chunks), BF16),
            pltpu.VMEM((fsdp, branches, rows, width), F32),
            pltpu.VMEM((fsdp - 1, branches, rows, width), BF16),
            pltpu.VMEM((fsdp - 1, branches, rows, width), BF16),
            pltpu.VMEM((fsdp, branches, 8, width), F32),
            pltpu.VMEM((rows, width), F32),
            pltpu.VMEM((rows, width), F32),
        ]
        + [pltpu.VMEM((groups, per, rows), BF16)] * 6
        + [
            pltpu.VMEM((half, 2 * rows), BF16),
            dma((10,)),
            dma((fsdp // chan, HALVES, chunks)),
            dma((fsdp, HALVES, chunks)),
            dma((fsdp - 1, HALVES, chunks // chan)),
            dma((fsdp - 1, branches, HALVES)),
            dma((fsdp - 1, branches, HALVES)),
            dma((fsdp, 2)),
            dma((fsdp, 2)),
            dma((3, groups)),
            dma((3, groups)),
        ],
        compiler_params=pltpu.CompilerParams(
            collective_id=0, has_side_effects=True, vmem_limit_bytes=60 * 1024 * 1024
        ),
        name="hyena",
    )(
        tokens,
        jnp.transpose(proj_weight, (1, 0, 2)).reshape(branches, chunks, depth // chunks, width),
        short_weight,
        skip_gain.reshape(1, width),
        filter_taps,
        *[jnp.asarray(table) for table in made],
    )


def causal_tables(rows):
    bf = ml_dtypes.bfloat16
    odd = 2 * np.arange(rows) + 1
    period = 4 * rows

    def angles(times):
        wrapped = (odd[:, None] * times[None, :]) % period
        return wrapped.astype(np.float64) * (2.0 * math.pi / period)

    ahead = angles(np.arange(rows))
    behind = angles(rows + np.arange(rows)).T
    pair = [np.cos(behind) / rows, -np.sin(behind) / rows]
    return np.stack([np.cos(ahead), -np.sin(ahead), *pair]).astype(bf)


def chunk_spans(rows):
    head = rows - EDGE
    return [(at, min(at + CHUNK, head)) for at in range(0, head, CHUNK)]


def causal_kernel(
    seq,
    tokens,
    weight,
    short_h,
    gain_h,
    taps_h,
    table_h,
    out,
    w,
    table,
    short,
    gain,
    own,
    far,
    part_out,
    part_in,
    edge_out,
    edge_in,
    projected,
    halves,
    signal,
    taps,
    tapspec,
    response,
    query,
    query_term,
    query_out,
    query_in,
    query_edge_out,
    query_edge_in,
    mixed,
    result,
    packed,
    final,
    query_near,
    short_near,
    load_sem,
    own_send,
    own_recv,
    far_recv,
    fwd_send,
    part_send,
    part_recv,
    edge_send,
    edge_recv,
    across_send,
    across_recv,
    up_send,
    up_recv,
    taps_local,
    taps_x_send,
    taps_x_recv,
    taps_z_send,
    taps_z_recv,
    taps_y_send,
    taps_y_recv,
    query_send,
    query_recv,
    query_edge_send,
    query_edge_recv,
    out_send,
    out_recv,
    query_aside_send,
    query_aside_recv,
    short_send,
    short_recv,
    gain_send,
    gain_recv,
    taps_local_send,
    ready,
    near,
):
    rows = tokens.shape[0]
    width = weight.shape[3]
    depth = weight.shape[2]
    lanes = width // 2
    bins = 2 * rows
    last = seq - 1
    spans = chunk_spans(rows)
    count = len(spans)
    pieces = [(rows - EDGE, rows), *spans]
    made = [*spans[:-1], (spans[-1][0], rows)]
    group = lax.axis_index("grp")
    s = lax.axis_index("seq")
    f = lax.axis_index("fsdp")
    c = lax.axis_index("chan")
    g = 1 - f
    sibling = 1 - c
    holds = c == f
    goes_up = s < last
    across = {"fsdp": g}
    aside = {"chan": sibling}
    diagonal = {"fsdp": g, "chan": sibling}

    def half_of(value):
        return jnp.where(f == 0, value[:, :lanes], value[:, lanes:])

    def other_half(value):
        return jnp.where(f == 0, value[:, lanes:], value[:, :lanes])

    def rounded(value):
        return value.astype(BF16).astype(F32)

    def columns(h):
        return pl.ds(pl.multiple_of(h * lanes, lanes), lanes)

    def at(span):
        return pl.ds(span[0], span[1] - span[0])

    def remote(source, target, send, recv, device):
        return pltpu.make_async_remote_copy(
            src_ref=source,
            dst_ref=target,
            send_sem=send,
            recv_sem=recv,
            device_id=device,
            device_id_type=MESH,
        )

    def arrive(block, sem):
        pltpu.make_async_copy(block, block, sem).wait()

    own_load = pltpu.make_async_copy(tokens, own, own_recv)

    @pl.when(holds)
    def _():
        own_load.start()

    loads = [
        pltpu.make_async_copy(source, target, load_sem.at[i])
        for i, (source, target) in enumerate(
            [
                (weight.at[pl.ds(1, 2)], w.at[pl.ds(1, 2)]),
                (weight.at[pl.ds(0, 1)], w.at[pl.ds(0, 1)]),
                (table_h, table),
                (short_h, short),
            ]
        )
    ]
    for load in loads:
        load.start()
    edge_in[...] = jnp.zeros_like(edge_in)
    query_edge_in[...] = jnp.zeros_like(query_edge_in)

    def member(t, h):
        return {"seq": t, "fsdp": h // 2, "chan": h % 2}

    barrier = pltpu.get_barrier_semaphore()
    beside = {"grp": 1 - group}
    for device in [{"chan": sibling}, across, {"fsdp": g, "chan": sibling}]:
        pl.semaphore_signal(barrier, inc=1, device_id=device, device_id_type=MESH)

    @pl.when(f == 0)
    def _():
        pl.semaphore_signal(barrier, inc=1, device_id=beside, device_id_type=MESH)

    for t in range(seq):
        for h in range(4):

            @pl.when(t > s)
            def _():
                pl.semaphore_signal(
                    barrier, inc=1, device_id=member(t, h), device_id_type=MESH
                )

    pl.semaphore_wait(barrier, 3 + g + 4 * s)

    def token_copy(i, a):
        return remote(
            tokens.at[at(pieces[i]), pl.ds(a * depth, depth)],
            far.at[a, at(pieces[i])],
            own_send,
            far_recv.at[i, a],
            {"fsdp": g, "chan": a},
        )

    own_copy = remote(tokens, own, own_send, own_recv, aside)
    short_copy = remote(short_h, short_near, short_send, short_recv, aside)
    gain_copy = remote(gain_h, gain, gain_send, gain_recv, aside)
    taps_aside = remote(
        taps_h.at[:, columns(f)], taps.at[s, f], taps_local_send, taps_local, aside
    )
    share = pl.ds(pl.multiple_of(group * (rows // 2), rows // 2), rows // 2)
    rest = pl.ds(pl.multiple_of((1 - group) * (rows // 2), rows // 2), rows // 2)
    taps_x_copy = remote(
        taps_h.at[share, columns(g)],
        taps.at[s, f, share],
        taps_x_send,
        taps_x_recv,
        diagonal,
    )

    @pl.when(jnp.logical_not(holds))
    def _():
        for a in range(2):
            token_copy(0, a).start()

    taps_x_copy.start()

    @pl.when(jnp.logical_not(holds))
    def _():
        for a in range(2):
            token_copy(1, a).start()

    @pl.when(holds)
    def _():
        own_copy.start()

    taps_aside.start()
    short_copy.start()
    gain_copy.start()

    @pl.when(f == 0)
    def _():
        pl.semaphore_signal(near, inc=1, device_id=beside, device_id_type=MESH)

    for t in range(seq):
        for h in range(4):

            @pl.when(t < s)
            def _():
                pl.semaphore_signal(
                    ready, inc=1, device_id=member(t, h), device_id_type=MESH
                )

    def part_copy(i):
        return remote(
            part_out.at[:, at(made[i])],
            part_in.at[:, at(made[i])],
            part_send,
            part_recv.at[i],
            across,
        )

    own_query_copy = remote(
        query_out.at[0], query_in.at[0], query_send, query_recv, diagonal
    )

    def query_copy(i):
        return remote(
            query_out.at[1, at(made[i])],
            query_in.at[1, at(made[i])],
            query_send,
            query_recv,
            diagonal,
        )

    def query_aside(block):
        return remote(
            query.at[block],
            query_near.at[block],
            query_aside_send,
            query_aside_recv,
            aside,
        )

    def own_part(j):
        return jnp.dot(own[:, :depth], w[j, 0], preferred_element_type=F32) + jnp.dot(
            own[:, depth:], w[j, 1], preferred_element_type=F32
        )

    def far_part(j, span):
        rows_at = slice(*span)
        return jnp.dot(far[0, rows_at], w[j, 0], preferred_element_type=F32) + jnp.dot(
            far[1, rows_at], w[j, 1], preferred_element_type=F32
        )

    with jax.named_scope("own_rows"):
        arrive(own, own_recv)
        loads[0].wait()
        for j in range(2):
            term = own_part(j + 1)
            part_out[j] = term.astype(BF16)
            edge_out[0, j] = term[rows - 8 :]
        part_copy(0).start()

        @pl.when(f == 0)
        def _():
            edge_in[0] = edge_out[0]

    with jax.named_scope("own_query"):
        for load in loads[1:]:
            load.wait()
        term = own_part(0)
        query[f] = half_of(term)
        query_aside(f).start()
        query_out[0] = other_half(term).astype(BF16)

        @pl.when(f == 1)
        def _():
            query_edge_out[0] = term[rows - 8 :, :lanes]
            query_edge_out[1] = term[rows - 8 :, lanes:]

    @pl.when(f == 0)
    def _():
        pl.semaphore_wait(near, 1)
        pl.semaphore_signal(near, inc=1, device_id=across, device_id_type=MESH)

    def edge_up(i):
        return remote(
            edge_out.at[i],
            edge_in.at[i],
            edge_send,
            edge_recv,
            {"seq": jnp.minimum(s + 1, last), "fsdp": 1},
        )

    edge_across = remote(
        edge_out.at[1], edge_in.at[1], edge_send, edge_recv, {"fsdp": 0}
    )

    def query_edge(h):
        return remote(
            query_edge_out.at[h],
            query_edge_in.at[f],
            query_edge_send,
            query_edge_recv,
            {"seq": jnp.minimum(s + 1, last), "fsdp": h, "chan": sibling},
        )

    def taps_z_copy(t):
        block = taps.at[s, :, share]
        return remote(block, block, taps_z_send, taps_z_recv, {"seq": t})

    def taps_y_copy(n):
        block = taps.at[pl.ds(0, n), :, share]
        return remote(block, block, taps_y_send.at[1], taps_y_recv.at[1], beside)

    own_taps_y = remote(
        taps.at[s, g, share],
        taps.at[s, g, share],
        taps_y_send.at[0],
        taps_y_recv.at[0],
        beside,
    )

    def forward_copy(i):
        block = far.at[c, at(pieces[i])]
        return remote(
            block, block, fwd_send, far_recv.at[i, c], {"chan": sibling}
        )

    def half_part(j, a, span):
        return jnp.dot(far[a, slice(*span)], w[j, a], preferred_element_type=F32)

    def take(i):
        with jax.named_scope("direct"):
            arrive(far.at[c, at(pieces[i])], far_recv.at[i, c])
        forward_copy(i).start()

    def take_other(i):
        arrive(far.at[sibling, at(pieces[i])], far_recv.at[i, sibling])

    with jax.named_scope("edge_rows"):
        take(0)
        for j in range(2):
            projected[j, 8 + rows - EDGE :] = half_part(j + 1, c, pieces[0])
        @pl.when(goes_up)
        def _():
            pl.semaphore_wait(ready, 4 * (last - s))

            @pl.when(f == 1)
            def _():
                edge_up(0).start()
                for h in range(2):
                    query_edge(h).start()

        with jax.named_scope("taps_up"):
            arrive(taps.at[s, f], taps_local)
            arrive(taps.at[s, g, share], taps_x_recv)
            for t in range(1, seq):

                @pl.when(t > s)
                def _():
                    taps_z_copy(t).start()

            @pl.when(f == 1)
            def _():
                pl.semaphore_wait(near, 1)

            own_taps_y.start()

        take_other(0)
        for j in range(2):
            term = projected[j, 8 + rows - EDGE :] + half_part(j + 1, sibling, pieces[0])
            projected[j, 8 + rows - EDGE :] = term
            edge_out[1, j] = term[EDGE - 8 :]

        @pl.when(f == 1)
        def _():
            edge_across.start()

        @pl.when(jnp.logical_not(holds))
        def _():
            for i in range(2, count + 1):
                for a in range(2):
                    token_copy(i, a).start()

        @pl.when(jnp.logical_and(f == 0, goes_up))
        def _():
            edge_up(1).start()
            term = far_part(0, pieces[0])
            query_edge_out[0] = term[EDGE - 8 :, :lanes]
            query_edge_out[1] = term[EDGE - 8 :, lanes:]
            for h in range(2):
                query_edge(h).start()

    def across_copy(i):
        return remote(
            halves.at[g, at(made[i])],
            signal.at[s, g, at(made[i])],
            across_send,
            across_recv,
            diagonal,
        )

    def aside_copy(i):
        return remote(
            halves.at[f, at(made[i])],
            signal.at[s, g, at(made[i])],
            across_send,
            across_recv,
            aside,
        )

    def up_copy(i, t):
        return remote(
            halves.at[f, at(made[i])],
            signal.at[s, g, at(made[i])],
            up_send,
            up_recv.at[s],
            {"seq": t, "chan": sibling},
        )

    def cross_copy(i, t):
        return remote(
            halves.at[g, at(made[i])],
            signal.at[s, g, at(made[i])],
            up_send,
            up_recv.at[s],
            {"seq": t, "fsdp": g, "chan": sibling},
        )

    def cross_start(i, low):
        for t in range(1, seq):

            @pl.when(jnp.logical_and(t > s, (s == 0) if low else (s > 0)))
            def _():
                cross_copy(i, t).start()

    def branch(j, span):
        low, high = span
        now = projected[j, 8 + low : 8 + high]
        one = projected[j, 7 + low : 7 + high]
        two = projected[j, 6 + low : 6 + high]
        return (
            short[0, j + 1 : j + 2, :] * now
            + short[1, j + 1 : j + 2, :] * one
            + short[2, j + 1 : j + 2, :] * two
        )

    def transform(values):
        whole = table[:2].reshape(2 * bins, bins)
        return jnp.dot(whole, values, preferred_element_type=F32)

    def taps_spectrum():
        ids = lax.broadcasted_iota(jnp.int32, (bins, lanes), 0)
        sign = 1.0 - 2.0 * (ids % 2).astype(F32)
        arrive(taps.at[s, g, rest], taps_y_recv.at[0])
        for n in range(1, seq):

            @pl.when(s == n)
            def _():
                arrive(taps.at[pl.ds(0, n), :, rest], taps_y_recv.at[1])

        for d in range(seq):

            @pl.when(d <= s)
            def _():
                spec = transform(taps[d].reshape(bins, lanes))
                real, imag = spec[:bins], spec[bins:]
                tapspec[d] = spec
                if d == 0:
                    response[0, 0] = sign * imag
                    response[0, 1] = -sign * real
                else:
                    response[d, 0] = tapspec[d - 1, :bins] + sign * imag
                    response[d, 1] = tapspec[d - 1, bins:] - sign * real

    for i in range(count):
        low, high = made[i]
        final_chunk = i == count - 1
        with jax.named_scope("tokens"):
            take(i + 1)
            if final_chunk:
                own_query_copy.start()
                for r in range(i):
                    query_copy(r).start()
                    cross_start(r, True)
            lines = slice(8 + spans[i][0], 8 + spans[i][1])
            for j in range(2):
                projected[j, lines] = half_part(j + 1, c, spans[i])
            if final_chunk:
                query_term[low:high] = half_part(0, c, made[i])
            if i == 0:
                with jax.named_scope("taps_side"):
                    for n in range(1, seq):

                        @pl.when(s == n)
                        def _():
                            arrive(taps.at[pl.ds(0, n), :, share], taps_z_recv)
                            taps_y_copy(n).start()

            take_other(i + 1)
            if not final_chunk:
                part_copy(i + 1).start()
        with jax.named_scope("chunk"):
            for j in range(2):
                projected[j, lines] += half_part(j + 1, sibling, spans[i])
        if i == 0:
            with jax.named_scope("edges"):

                @pl.when(jnp.logical_and(f == 1, s > 0))
                def _():
                    arrive(edge_in, edge_recv)

                @pl.when(f == 0)
                def _():
                    arrive(edge_in.at[1], edge_recv)

                for j in range(2):
                    projected[j, :8] = rounded(edge_in[0, j] + edge_in[1, j])
        with jax.named_scope("partial"):
            part_copy(i).wait_recv()
        with jax.named_scope("product"):
            for j in range(2):
                block = slice(8 + low, 8 + high)
                projected[j, block] = rounded(
                    projected[j, block] + part_in[j, low:high].astype(F32)
                )
            product = (branch(0, made[i]) * branch(1, made[i])).astype(BF16)
            halves[0, low:high] = product[:, :lanes]
            halves[1, low:high] = product[:, lanes:]
            across_copy(i).start()
            aside_copy(i).start()
            cross_start(i, False)
            for t in range(1, seq):

                @pl.when(t > s)
                def _():
                    up_copy(i, t).start()

        if final_chunk:
            cross_start(i, True)
        with jax.named_scope("far_query"):
            if final_chunk:
                term = query_term[low:high] + half_part(0, sibling, made[i])
            else:
                term = far_part(0, made[i])
            query[g, low:high] = half_of(term)
            query_aside((g, at(made[i]))).start()
            query_out[1, low:high] = other_half(term).astype(BF16)
            if final_chunk:
                query_copy(i).start()
    def spectrum(j, d):
        spec = transform(signal[j].reshape(bins, lanes))
        real, imag = spec[:bins], spec[bins:]
        hr, hi = response[d, 0], response[d, 1]
        return real * hr - imag * hi, real * hi + imag * hr

    with jax.named_scope("taps_spectra"):
        taps_spectrum()

    with jax.named_scope("earlier_slabs"):
        result[...] = jnp.zeros_like(result)
        for j in range(last - 1):

            @pl.when(j < s - 1)
            def _():
                arrive(signal.at[j], up_recv.at[j])
                real, imag = spectrum(j, s - j)
                result[0] += real
                result[1] += imag

    arrive(short_near, short_recv)
    arrive(gain, gain_recv)
    with jax.named_scope("own_wait"):
        arrive(signal.at[s], across_recv)
    with jax.named_scope("own_slab"):
        real, imag = spectrum(s, 0)
        result[0] += real
        result[1] += imag

    with jax.named_scope("slab_before"):

        @pl.when(s == 0)
        def _():
            packed[...] = result[...].astype(BF16)

        @pl.when(s > 0)
        def _():
            arrive(signal.at[s - 1], up_recv.at[s - 1])
            real, imag = spectrum(s - 1, 1)
            packed[0] = (result[0] + real).astype(BF16)
            packed[1] = (result[1] + imag).astype(BF16)

    with jax.named_scope("query"):
        arrive(query_in, query_recv)
        arrive(query_near, query_aside_recv)

        @pl.when(s > 0)
        def _():
            arrive(query_edge_in, query_edge_recv)

        mixed[:8] = rounded(query_edge_in[0] + query_edge_in[1])
        other = pl.multiple_of(8 + g * rows, 8)
        mine = pl.multiple_of(8 + f * rows, 8)
        mixed[pl.ds(other, rows)] = rounded(query_near[g] + query_in[0].astype(F32))
        mixed[pl.ds(mine, rows)] = rounded(query_near[f] + query_in[1].astype(F32))
        gate = [half_of(short_near[i, 0:1, :]) for i in range(3)]
        gated = gate[0] * mixed[8 : 8 + bins] + gate[1] * mixed[7 : 7 + bins]
        gated += gate[2] * mixed[6 : 6 + bins]
        query_near[...] = gated.reshape(2, rows, lanes)

    with jax.named_scope("finish"):
        factor = half_of(gain[...])

        def finish(b):
            lines = pl.ds(pl.multiple_of(b * rows, rows), rows)
            conv = jnp.dot(table[2, lines], packed[0], preferred_element_type=F32)
            conv += jnp.dot(table[3, lines], packed[1], preferred_element_type=F32)
            whole = conv + factor * signal[s, b].astype(F32)
            return (query_near[b] * whole).astype(BF16)

        landing = out.at[:, columns(f)]
        out_across = remote(final.at[0], landing, out_send, out_recv, diagonal)
        out_aside = remote(final.at[1], landing, out_send, out_recv, aside)
        final[0] = finish(g)
        out_across.start()
        final[1] = finish(f)
        out_aside.start()

    with jax.named_scope("drain"):

        @pl.when(jnp.logical_not(holds))
        def _():
            arrive(far, own_send)

        @pl.when(holds)
        def _():
            own_copy.wait_send()

        taps_x_copy.wait_send()
        arrive(far.at[c], fwd_send)
        arrive(part_out, part_send)
        arrive(halves, across_send)
        arrive(query, query_aside_send)
        short_copy.wait_send()
        gain_copy.wait_send()
        taps_aside.wait_send()
        arrive(query_out, query_send)
        own_taps_y.wait_send()

        @pl.when(jnp.logical_and(f == 1, goes_up))
        def _():
            arrive(edge_out, edge_send)

        @pl.when(f != jnp.where(goes_up, 1, 0))
        def _():
            arrive(edge_out.at[1], edge_send)

        @pl.when(goes_up)
        def _():
            arrive(query_edge_out, query_edge_send)

        for n in range(1, seq):

            @pl.when(s == n)
            def _():
                taps_y_copy(n).wait_send()

            @pl.when(last - s == n)
            def _():
                arrive(taps.at[pl.ds(0, n), :, share], taps_z_send)
                arrive(signal.at[pl.ds(0, n)], up_send)

    with jax.named_scope("out"):
        arrive(final, out_send)
        arrive(out, out_recv)


def causal_device(seq, tokens, proj_weight, short_weight, skip_gain, filter_taps):
    rows = tokens.shape[0]
    depth, branches, width = proj_weight.shape
    lanes = width // 2
    step = depth // 2
    table = causal_tables(2 * rows)
    count = len(chunk_spans(rows))
    dma = pltpu.SemaphoreType.DMA
    hbm = pl.BlockSpec(memory_space=pl.ANY)
    scratch = [
        ((branches, 2, step, width), BF16),
        (table.shape, BF16),
        (short_weight.shape, F32),
        ((1, width), F32),
        ((rows, depth), BF16),
        ((2, rows, step), BF16),
        ((2, rows, width), BF16),
        ((2, rows, width), BF16),
        ((2, 2, 8, width), F32),
        ((2, 2, 8, width), F32),
        ((2, 8 + rows, width), F32),
        ((2, rows, lanes), BF16),
        ((seq, 2, rows, lanes), BF16),
        ((seq, 2, rows, lanes), BF16),
        ((seq, 4 * rows, lanes), F32),
        ((seq, 2, 2 * rows, lanes), F32),
        ((2, rows, lanes), F32),
        ((rows, width), F32),
        ((2, rows, lanes), BF16),
        ((2, rows, lanes), BF16),
        ((2, 8, lanes), F32),
        ((2, 8, lanes), F32),
        ((8 + 2 * rows, lanes), F32),
        ((2, 2 * rows, lanes), F32),
        ((2, 2 * rows, lanes), BF16),
        ((2, rows, lanes), BF16),
        ((2, rows, lanes), F32),
        (short_weight.shape, F32),
    ]
    sems = [
        (4,),
        (),
        (),
        (count + 1, 2),
        (),
        (),
        (count,),
        (),
        (),
        (),
        (),
        (),
        (max(seq - 1, 1),),
        (),
        (),
        (),
        (),
        (),
        (2,),
        (2,),
        (),
        (),
        (),
        (),
        (),
        (),
        (),
        (),
        (),
        (),
        (),
        (),
        (),
    ]
    return pl.pallas_call(
        functools.partial(causal_kernel, seq),
        out_shape=pltpu.VMEM((rows, width), BF16),
        in_specs=[hbm] * 6,
        out_specs=pl.BlockSpec(memory_space=pltpu.VMEM),
        scratch_shapes=[pltpu.VMEM(shape, kind) for shape, kind in scratch]
        + [dma(shape) for shape in sems]
        + [pltpu.SemaphoreType.REGULAR] * 2,
        compiler_params=pltpu.CompilerParams(
            collective_id=0, has_side_effects=True, vmem_limit_bytes=60 * 1024 * 1024
        ),
        name="hyena",
    )(
        tokens,
        jnp.transpose(proj_weight, (1, 0, 2)).reshape(branches, 2, step, width),
        short_weight,
        skip_gain.reshape(1, width),
        filter_taps,
        jnp.asarray(table),
    )


def solution(mesh):
    seq = mesh.shape["seq"]
    paired = all(mesh.shape[axis] == 2 for axis in ("grp", "fsdp", "chan"))
    sizes = (mesh.shape["seq"], mesh.shape["fsdp"], mesh.shape["chan"])
    in_specs = (
        P(("grp", "seq", "fsdp"), "chan"),
        P("fsdp", None, "chan"),
        P(None, None, "chan"),
        P("chan"),
        P(("seq", "fsdp"), "chan"),
    )
    out_specs = P(("grp", "seq", "fsdp"), "chan")
    return jax.shard_map(
        functools.partial(causal_device, seq)
        if paired
        else functools.partial(per_device, sizes),
        mesh=mesh,
        in_specs=in_specs,
        out_specs=out_specs,
        check_vma=False,
    )
```

```python
import functools
import math

import jax
import jax.numpy as jnp
import ml_dtypes
import numpy as np
from jax import lax
from jax.experimental import pallas as pl
from jax.experimental.pallas import tpu as pltpu
from jax.sharding import PartitionSpec as P

MESH = pl.DeviceIdType.MESH
BF16 = jnp.bfloat16
F32 = jnp.float32
MOST_CHUNKS = 2
HALVES = 2
EDGE = 16
CHUNK = 80


def phase_pair(rows, cols, period):
    wrapped = (np.arange(rows)[:, None] * np.arange(cols)[None, :]) % period
    phase = wrapped.astype(np.float32) * np.float32(2.0 * math.pi / period)
    return np.cos(phase), np.sin(phase)


def tables(groups, per, rows):
    bf = ml_dtypes.bfloat16
    bins = 2 * groups
    cos, sin = phase_pair(bins, groups, bins)
    eye = np.eye(per, dtype=np.float32)
    first = np.concatenate([np.kron(cos, eye), np.kron(-sin, eye)], axis=0).astype(bf)
    cos, sin = phase_pair(rows, rows, rows)
    ahead = np.block([[cos, -sin], [sin, cos]]).astype(bf)
    behind = np.block([[cos, sin], [-sin, cos]]).astype(bf)
    cos, sin = phase_pair(bins, rows, bins * rows)
    twist = np.stack([np.repeat(cos, per, axis=0), np.repeat(sin, per, axis=0)])
    last = np.ascontiguousarray(first.T)
    return first, last, ahead, behind, twist.astype(np.float32)


def kernel(
    sizes,
    tokens,
    weight,
    short_h,
    gain_h,
    taps_h,
    first_h,
    last_h,
    ahead_h,
    behind_h,
    twist_h,
    out,
    w,
    first,
    last,
    ahead,
    behind,
    twist,
    short,
    gain,
    taps,
    held,
    acc,
    psend,
    precv,
    hrecv,
    query,
    product,
    tsend,
    trecv,
    gsend,
    grecv,
    csend,
    crecv,
    tapspec,
    load_sem,
    tok_send,
    tok_recv,
    fwd_send,
    part_send,
    part_recv,
    halo_send,
    halo_recv,
    a2a_send,
    a2a_recv,
):
    seq, fsdp, chan = sizes
    groups = seq * fsdp
    rows = tokens.shape[0]
    chunks = weight.shape[1]
    lines = rows // HALVES
    depth = chunks * weight.shape[2]
    width = weight.shape[3]
    per = width // groups
    bins = 2 * groups
    step = depth // chunks
    share = fsdp // chan
    s = lax.axis_index("seq")
    f = lax.axis_index("fsdp")
    c = lax.axis_index("chan")
    me = s * fsdp + f

    loads = [
        pltpu.make_async_copy(source, target, load_sem.at[i])
        for i, (source, target) in enumerate(
            [
                (taps_h, taps),
                (weight.at[pl.ds(1, 2)], w.at[pl.ds(1, 2)]),
                (first_h, first),
                (ahead_h, ahead),
                (twist_h, twist),
                (last_h, last),
                (behind_h, behind),
                (short_h, short),
                (gain_h, gain),
                (weight.at[pl.ds(0, 1)], w.at[pl.ds(0, 1)]),
            ]
        )
    ]
    for load in loads:
        load.start()

    barrier = pltpu.get_barrier_semaphore()
    everyone = groups * chan

    def greet(k, carry):
        other = lax.rem(me * chan + c + k, everyone)
        spot = other // chan
        pl.semaphore_signal(
            barrier,
            inc=1,
            device_id={"seq": spot // fsdp, "fsdp": spot % fsdp, "chan": other % chan},
            device_id_type=MESH,
        )
        return carry

    lax.fori_loop(1, everyone, greet, 0, unroll=everyone <= 16)

    @pl.when(me == 0)
    def _():
        hrecv[...] = jnp.zeros_like(hrecv)

    loads[0].wait()
    tsend[...] = jnp.transpose(taps[...].astype(F32)).astype(BF16).reshape(groups, per, rows)
    pl.semaphore_wait(barrier, everyone - 1)

    sibling = lax.rem(c + 1, chan)

    def span(h):
        return pl.ds(h * lines, lines)

    def token_copy(i, h, k, same):
        return pltpu.make_async_remote_copy(
            src_ref=tokens.at[span(h), pl.ds(i * depth + k * step, step)],
            dst_ref=held.at[f, k, span(h)],
            send_sem=tok_send.at[i, h, k],
            recv_sem=tok_recv.at[f, h, k],
            device_id={"fsdp": c * share + i, "chan": sibling if same else k % chan},
            device_id_type=MESH,
        )

    for h, k in [(h, k) for h in range(HALVES) for k in range(chunks)]:
        for i in range(share):
            stays = c * share + i == f

            @pl.when(jnp.logical_not(stays))
            def _():
                token_copy(i, h, k, False).start()

            @pl.when(stays)
            def _():
                token_copy(i, h, k, True).start()
                pltpu.make_async_copy(
                    tokens.at[span(h), pl.ds(i * depth + k * step, step)],
                    held.at[f, k, span(h)],
                    tok_recv.at[f, h, k],
                ).start()

    def exchange_copy(which, source, target, k):
        other = lax.rem(me + k, groups)
        return pltpu.make_async_remote_copy(
            src_ref=source.at[other],
            dst_ref=target.at[me],
            send_sem=a2a_send.at[which, k],
            recv_sem=a2a_recv.at[which, k],
            device_id={"seq": other // fsdp, "fsdp": other % fsdp},
            device_id_type=MESH,
        )

    def exchange_start(which, source, target):
        def go(k, carry):
            exchange_copy(which, source, target, k).start()
            return carry

        lax.fori_loop(1, groups, go, 0, unroll=groups <= 8)
        target[me] = source[me]

    def exchange_wait(which, source, target):
        def go(k, carry):
            exchange_copy(which, source, target, k).wait_recv()
            return carry

        lax.fori_loop(1, groups, go, 0, unroll=groups <= 8)

    def exchange_sent(which, source, target):
        def go(k, carry):
            exchange_copy(which, source, target, k).wait_send()
            return carry

        lax.fori_loop(1, groups, go, 0)


    half = bins * per

    def spectrum(signal):
        a = jnp.dot(first[...], signal, preferred_element_type=F32)
        real_a, imag_a = a[:half], a[half:]
        real_b = (real_a * twist[0] + imag_a * twist[1]).astype(BF16)
        imag_b = (imag_a * twist[0] - real_a * twist[1]).astype(BF16)
        b = jnp.concatenate([real_b, imag_b], axis=1)
        return jnp.dot(b, ahead[...], preferred_element_type=F32).astype(BF16)

    def arrival(spot, h, k):
        block = held.at[spot, k, span(h)]
        pltpu.make_async_copy(block, block, tok_recv.at[spot, h, k]).wait()

    def forward_copy(d, h, t):
        k = t * chan + c
        block = held.at[lax.rem(f + d, fsdp), k, span(h)]
        return pltpu.make_async_remote_copy(
            src_ref=block,
            dst_ref=block,
            send_sem=fwd_send.at[d - 1, h, t],
            recv_sem=tok_recv.at[lax.rem(f + d, fsdp), h, k],
            device_id={"chan": sibling},
            device_id_type=MESH,
        )

    def part_copy(d, j, h):
        return pltpu.make_async_remote_copy(
            src_ref=psend.at[d - 1, j, span(h)],
            dst_ref=precv.at[d - 1, j, span(h)],
            send_sem=part_send.at[d - 1, j, h],
            recv_sem=part_recv.at[d - 1, j, h],
            device_id={"fsdp": lax.rem(f + d, fsdp)},
            device_id_type=MESH,
        )

    phases = ((1, 2), (0, 1))

    def halo_target(d):
        return s * fsdp + lax.rem(f + d, fsdp) + 1

    def halo_copy(d, phase):
        target = jnp.minimum(halo_target(d), groups - 1)
        start, count = phases[phase]
        return pltpu.make_async_remote_copy(
            src_ref=acc.at[d - 1, pl.ds(start, count), pl.ds(rows - 8, 8)],
            dst_ref=hrecv.at[f, pl.ds(start, count)],
            send_sem=halo_send.at[d - 1, phase],
            recv_sem=halo_recv.at[f, phase],
            device_id={"seq": target // fsdp, "fsdp": target % fsdp},
            device_id_type=MESH,
        )

    def halo_remote(d):
        target = halo_target(d)
        return jnp.logical_and(target < groups, target != me)

    def halo_start(d, phase):
        @pl.when(halo_remote(d))
        def _():
            halo_copy(d, phase).start()

        start, count = phases[phase]

        @pl.when(halo_target(d) == me)
        def _():
            hrecv[f, start : start + count] = acc[d - 1, start : start + count, rows - 8 :]

    def halo_wait(phase):
        start, count = phases[phase]
        for h in range(fsdp):
            local = jnp.logical_and(f > 0, f == h)

            @pl.when(jnp.logical_and(me > 0, jnp.logical_not(local)))
            def _():
                block = hrecv.at[h, pl.ds(start, count)]
                pltpu.make_async_copy(block, block, halo_recv.at[h, phase]).wait()

    loads[1].wait()
    for k in range(chunks):
        for h in range(HALVES):
            arrival(f, h, k)
        for j in (1, 2):
            term = jnp.dot(held[f, k], w[j, k], preferred_element_type=F32)
            acc[fsdp - 1, j] = term if k == 0 else acc[fsdp - 1, j] + term
    halo_start(fsdp, 0)

    for d in range(1, fsdp):
        spot = lax.rem(f + d, fsdp)
        for h, t, b in [
            (h, t, b)
            for h in range(HALVES)
            for t in range(chunks // chan)
            for b in range(chan)
        ]:
            k = t * chan + lax.rem(c + b, chan)
            arrival(spot, h, k)
            if b == 0:
                forward_copy(d, h, t).start()
            final = (t + 1) * chan == chunks and b == chan - 1
            at = slice(h * lines, (h + 1) * lines)
            for j in (1, 2):
                term = jnp.dot(held[spot, k, at], w[j, k], preferred_element_type=F32)
                if t > 0 or b > 0:
                    term = acc[d - 1, j, at] + term
                acc[d - 1, j, at] = term
                if final:
                    psend[d - 1, j, at] = term.astype(BF16)
                    part_copy(d, j, h).start()
        halo_start(d, 0)

    for load in loads[2:]:
        load.wait()
    exchange_start(0, tsend, trecv)

    row_ids = lax.broadcasted_iota(jnp.int32, (rows, width), 0)

    def branch(j):
        total = acc[fsdp - 1, j]
        edge = hrecv[0, j]
        for d in range(1, fsdp):
            for h in range(HALVES):
                part_copy(d, j, h).wait_recv()
            total = total + precv[d - 1, j].astype(F32)
            edge = edge + hrecv[d, j]
        now = total.astype(BF16).astype(F32)
        edge = edge.astype(BF16).astype(F32)
        before = edge[7:8]
        earlier = edge[6:7]
        one = jnp.where(row_ids == 0, before, pltpu.roll(now, 1, 0))
        two = jnp.where(
            row_ids == 0, earlier, jnp.where(row_ids == 1, before, pltpu.roll(now, 2, 0))
        )
        return (
            short[0, j : j + 1, :] * now
            + short[1, j : j + 1, :] * one
            + short[2, j : j + 1, :] * two
        )

    halo_wait(0)
    prod = (branch(1) * branch(2)).astype(BF16).astype(F32)
    gsend[...] = jnp.transpose(prod).astype(BF16).reshape(groups, per, rows)
    exchange_start(1, gsend, grecv)
    product[...] = prod * gain[...]

    for d in range(1, fsdp + 1):
        spot = lax.rem(f + d, fsdp)
        term = jnp.dot(held[spot, 0], w[0, 0], preferred_element_type=F32)
        for k in range(1, chunks):
            term += jnp.dot(held[spot, k], w[0, k], preferred_element_type=F32)
        acc[d - 1, 0] = term
        if d < fsdp:
            psend[d - 1, 0] = term.astype(BF16)

    exchange_wait(0, tsend, trecv)
    tapspec[...] = spectrum(trecv[...].reshape(width, rows))
    exchange_wait(1, gsend, grecv)
    for d in range(1, fsdp + 1):
        if d < fsdp:
            for h in range(HALVES):
                part_copy(d, 0, h).start()
        halo_start(d, 1)

    x = spectrum(grecv[...].reshape(width, rows)).astype(F32)
    t = tapspec[...].astype(F32)
    xr, xi = x[:, :rows], x[:, rows:]
    tr, ti = t[:, :rows], t[:, rows:]
    real_z = (xr * tr - xi * ti).astype(BF16)
    imag_z = (xr * ti + xi * tr).astype(BF16)
    z = jnp.concatenate([real_z, imag_z], axis=1)
    v = jnp.dot(z, behind[...], preferred_element_type=F32)
    vr, vi = v[:, :rows], v[:, rows:]
    real_w = (vr * twist[0] - vi * twist[1]).astype(BF16)
    imag_w = (vi * twist[0] + vr * twist[1]).astype(BF16)
    packed = jnp.concatenate([real_w, imag_w], axis=0)
    y = jnp.dot(last[...], packed, preferred_element_type=F32) * (1.0 / (bins * rows))
    csend[...] = y.astype(BF16).reshape(groups, per, rows)
    exchange_start(2, csend, crecv)
    halo_wait(1)
    query[...] = branch(0)
    exchange_wait(2, csend, crecv)
    conv = jnp.transpose(crecv[...].reshape(width, rows).astype(F32))
    out[...] = (query[...] * (conv + product[...])).astype(BF16)

    exchange_sent(0, tsend, trecv)
    exchange_sent(1, gsend, grecv)
    exchange_sent(2, csend, crecv)
    for d in range(1, fsdp + 1):
        for phase in range(2):

            @pl.when(halo_remote(d))
            def _():
                halo_copy(d, phase).wait_send()

    for d in range(1, fsdp):
        for h in range(HALVES):
            for j in range(3):
                part_copy(d, j, h).wait_send()
            for t in range(chunks // chan):
                forward_copy(d, h, t).wait_send()
    for h, k in [(h, k) for h in range(HALVES) for k in range(chunks)]:
        for i in range(share):
            token_copy(i, h, k, False).wait_send()


def per_device(sizes, tokens, proj_weight, short_weight, skip_gain, filter_taps):
    seq, fsdp, chan = sizes
    groups = seq * fsdp
    rows = tokens.shape[0]
    depth, branches, width = proj_weight.shape
    per = width // groups
    chunks = min(MOST_CHUNKS, depth // 128)
    made = tables(groups, per, rows)
    dma = pltpu.SemaphoreType.DMA
    vmem = pl.BlockSpec(memory_space=pltpu.VMEM)
    hbm = pl.BlockSpec(memory_space=pl.ANY)
    half = 2 * groups * per
    return pl.pallas_call(
        functools.partial(kernel, sizes),
        out_shape=jax.ShapeDtypeStruct((rows, width), BF16),
        in_specs=[hbm] * 10,
        out_specs=vmem,
        scratch_shapes=[
            pltpu.VMEM((branches, chunks, depth // chunks, width), BF16),
            pltpu.VMEM(made[0].shape, BF16),
            pltpu.VMEM(made[1].shape, BF16),
            pltpu.VMEM(made[2].shape, BF16),
            pltpu.VMEM(made[3].shape, BF16),
            pltpu.VMEM(made[4].shape, F32),
            pltpu.VMEM(short_weight.shape, F32),
            pltpu.VMEM((1, width), F32),
            pltpu.VMEM((rows, width), BF16),
            pltpu.VMEM((fsdp, chunks, rows, depth // chunks), BF16),
            pltpu.VMEM((fsdp, branches, rows, width), F32),
            pltpu.VMEM((fsdp - 1, branches, rows, width), BF16),
            pltpu.VMEM((fsdp - 1, branches, rows, width), BF16),
            pltpu.VMEM((fsdp, branches, 8, width), F32),
            pltpu.VMEM((rows, width), F32),
            pltpu.VMEM((rows, width), F32),
        ]
        + [pltpu.VMEM((groups, per, rows), BF16)] * 6
        + [
            pltpu.VMEM((half, 2 * rows), BF16),
            dma((10,)),
            dma((fsdp // chan, HALVES, chunks)),
            dma((fsdp, HALVES, chunks)),
            dma((fsdp - 1, HALVES, chunks // chan)),
            dma((fsdp - 1, branches, HALVES)),
            dma((fsdp - 1, branches, HALVES)),
            dma((fsdp, 2)),
            dma((fsdp, 2)),
            dma((3, groups)),
            dma((3, groups)),
        ],
        compiler_params=pltpu.CompilerParams(
            collective_id=0, has_side_effects=True, vmem_limit_bytes=60 * 1024 * 1024
        ),
        name="hyena",
    )(
        tokens,
        jnp.transpose(proj_weight, (1, 0, 2)).reshape(branches, chunks, depth // chunks, width),
        short_weight,
        skip_gain.reshape(1, width),
        filter_taps,
        *[jnp.asarray(table) for table in made],
    )


def causal_tables(rows):
    bf = ml_dtypes.bfloat16
    odd = 2 * np.arange(rows) + 1
    period = 4 * rows

    def angles(times):
        wrapped = (odd[:, None] * times[None, :]) % period
        return wrapped.astype(np.float64) * (2.0 * math.pi / period)

    ahead = angles(np.arange(rows))
    behind = angles(rows + np.arange(rows)).T
    pair = [np.cos(behind) / rows, -np.sin(behind) / rows]
    return np.stack([np.cos(ahead), -np.sin(ahead), *pair]).astype(bf)


def chunk_spans(rows):
    head = rows - EDGE
    return [(at, min(at + CHUNK, head)) for at in range(0, head, CHUNK)]


def causal_kernel(
    seq,
    tokens,
    weight,
    short_h,
    gain_h,
    taps_h,
    table_h,
    out,
    w,
    table,
    short,
    gain,
    own,
    far,
    part_out,
    part_in,
    edge_out,
    edge_in,
    projected,
    halves,
    signal,
    taps,
    tapspec,
    response,
    query,
    query_term,
    query_out,
    query_in,
    query_edge_out,
    query_edge_in,
    mixed,
    result,
    packed,
    final,
    query_near,
    short_near,
    load_sem,
    own_send,
    own_recv,
    far_recv,
    fwd_send,
    part_send,
    part_recv,
    edge_send,
    edge_recv,
    across_send,
    across_recv,
    up_send,
    up_recv,
    taps_local,
    taps_x_send,
    taps_x_recv,
    taps_z_send,
    taps_z_recv,
    taps_y_send,
    taps_y_recv,
    query_send,
    query_recv,
    query_edge_send,
    query_edge_recv,
    out_send,
    out_recv,
    query_aside_send,
    query_aside_recv,
    short_send,
    short_recv,
    gain_send,
    gain_recv,
    taps_local_send,
    ready,
    near,
):
    rows = tokens.shape[0]
    width = weight.shape[3]
    depth = weight.shape[2]
    lanes = width // 2
    bins = 2 * rows
    last = seq - 1
    spans = chunk_spans(rows)
    count = len(spans)
    pieces = [(rows - EDGE, rows), *spans]
    made = [*spans[:-1], (spans[-1][0], rows)]
    group = lax.axis_index("grp")
    s = lax.axis_index("seq")
    f = lax.axis_index("fsdp")
    c = lax.axis_index("chan")
    g = 1 - f
    sibling = 1 - c
    holds = c == f
    goes_up = s < last
    across = {"fsdp": g}
    aside = {"chan": sibling}
    diagonal = {"fsdp": g, "chan": sibling}

    def half_of(value):
        return jnp.where(f == 0, value[:, :lanes], value[:, lanes:])

    def other_half(value):
        return jnp.where(f == 0, value[:, lanes:], value[:, :lanes])

    def rounded(value):
        return value.astype(BF16).astype(F32)

    def columns(h):
        return pl.ds(pl.multiple_of(h * lanes, lanes), lanes)

    def at(span):
        return pl.ds(span[0], span[1] - span[0])

    def remote(source, target, send, recv, device):
        return pltpu.make_async_remote_copy(
            src_ref=source,
            dst_ref=target,
            send_sem=send,
            recv_sem=recv,
            device_id=device,
            device_id_type=MESH,
        )

    def arrive(block, sem):
        pltpu.make_async_copy(block, block, sem).wait()

    own_load = pltpu.make_async_copy(tokens, own, own_recv)

    @pl.when(holds)
    def _():
        own_load.start()

    loads = [
        pltpu.make_async_copy(source, target, load_sem.at[i])
        for i, (source, target) in enumerate(
            [
                (weight.at[pl.ds(1, 2)], w.at[pl.ds(1, 2)]),
                (weight.at[pl.ds(0, 1)], w.at[pl.ds(0, 1)]),
                (table_h, table),
                (short_h, short),
            ]
        )
    ]
    for load in loads:
        load.start()
    edge_in[...] = jnp.zeros_like(edge_in)
    query_edge_in[...] = jnp.zeros_like(query_edge_in)

    def member(t, h):
        return {"seq": t, "fsdp": h // 2, "chan": h % 2}

    barrier = pltpu.get_barrier_semaphore()
    beside = {"grp": 1 - group}
    for device in [{"chan": sibling}, across, {"fsdp": g, "chan": sibling}]:
        pl.semaphore_signal(barrier, inc=1, device_id=device, device_id_type=MESH)

    @pl.when(f == 0)
    def _():
        pl.semaphore_signal(barrier, inc=1, device_id=beside, device_id_type=MESH)

    for t in range(seq):
        for h in range(4):

            @pl.when(t > s)
            def _():
                pl.semaphore_signal(
                    barrier, inc=1, device_id=member(t, h), device_id_type=MESH
                )

    pl.semaphore_wait(barrier, 3 + g + 4 * s)

    def token_copy(i, a):
        return remote(
            tokens.at[at(pieces[i]), pl.ds(a * depth, depth)],
            far.at[a, at(pieces[i])],
            own_send,
            far_recv.at[i, a],
            {"fsdp": g, "chan": a},
        )

    own_copy = remote(tokens, own, own_send, own_recv, aside)
    short_copy = remote(short_h, short_near, short_send, short_recv, aside)
    gain_copy = remote(gain_h, gain, gain_send, gain_recv, aside)
    taps_aside = remote(
        taps_h.at[:, columns(f)], taps.at[s, f], taps_local_send, taps_local, aside
    )
    share = pl.ds(pl.multiple_of(group * (rows // 2), rows // 2), rows // 2)
    rest = pl.ds(pl.multiple_of((1 - group) * (rows // 2), rows // 2), rows // 2)
    taps_x_copy = remote(
        taps_h.at[share, columns(g)],
        taps.at[s, f, share],
        taps_x_send,
        taps_x_recv,
        diagonal,
    )

    @pl.when(jnp.logical_not(holds))
    def _():
        for a in range(2):
            token_copy(0, a).start()

    taps_x_copy.start()

    @pl.when(jnp.logical_not(holds))
    def _():
        for a in range(2):
            token_copy(1, a).start()

    @pl.when(holds)
    def _():
        own_copy.start()

    taps_aside.start()
    short_copy.start()
    gain_copy.start()

    @pl.when(f == 0)
    def _():
        pl.semaphore_signal(near, inc=1, device_id=beside, device_id_type=MESH)

    for t in range(seq):
        for h in range(4):

            @pl.when(t < s)
            def _():
                pl.semaphore_signal(
                    ready, inc=1, device_id=member(t, h), device_id_type=MESH
                )

    def part_copy(i):
        return remote(
            part_out.at[:, at(made[i])],
            part_in.at[:, at(made[i])],
            part_send,
            part_recv.at[i],
            across,
        )

    own_query_copy = remote(
        query_out.at[0], query_in.at[0], query_send, query_recv, diagonal
    )

    def query_copy(i):
        return remote(
            query_out.at[1, at(made[i])],
            query_in.at[1, at(made[i])],
            query_send,
            query_recv,
            diagonal,
        )

    def query_aside(block):
        return remote(
            query.at[block],
            query_near.at[block],
            query_aside_send,
            query_aside_recv,
            aside,
        )

    def own_part(j):
        return jnp.dot(own[:, :depth], w[j, 0], preferred_element_type=F32) + jnp.dot(
            own[:, depth:], w[j, 1], preferred_element_type=F32
        )

    def far_part(j, span):
        rows_at = slice(*span)
        return jnp.dot(far[0, rows_at], w[j, 0], preferred_element_type=F32) + jnp.dot(
            far[1, rows_at], w[j, 1], preferred_element_type=F32
        )

    with jax.named_scope("own_rows"):
        arrive(own, own_recv)
        loads[0].wait()
        for j in range(2):
            term = own_part(j + 1)
            part_out[j] = term.astype(BF16)
            edge_out[0, j] = term[rows - 8 :]
        part_copy(0).start()

        @pl.when(f == 0)
        def _():
            edge_in[0] = edge_out[0]

    with jax.named_scope("own_query"):
        for load in loads[1:]:
            load.wait()
        term = own_part(0)
        query[f] = half_of(term)
        query_aside(f).start()
        query_out[0] = other_half(term).astype(BF16)

        @pl.when(f == 1)
        def _():
            query_edge_out[0] = term[rows - 8 :, :lanes]
            query_edge_out[1] = term[rows - 8 :, lanes:]

    @pl.when(f == 0)
    def _():
        pl.semaphore_wait(near, 1)
        pl.semaphore_signal(near, inc=1, device_id=across, device_id_type=MESH)

    def edge_up(i):
        return remote(
            edge_out.at[i],
            edge_in.at[i],
            edge_send,
            edge_recv,
            {"seq": jnp.minimum(s + 1, last), "fsdp": 1},
        )

    edge_across = remote(
        edge_out.at[1], edge_in.at[1], edge_send, edge_recv, {"fsdp": 0}
    )

    def query_edge(h):
        return remote(
            query_edge_out.at[h],
            query_edge_in.at[f],
            query_edge_send,
            query_edge_recv,
            {"seq": jnp.minimum(s + 1, last), "fsdp": h, "chan": sibling},
        )

    def taps_z_copy(t):
        block = taps.at[s, :, share]
        return remote(block, block, taps_z_send, taps_z_recv, {"seq": t})

    def taps_y_copy(n):
        block = taps.at[pl.ds(0, n), :, share]
        return remote(block, block, taps_y_send.at[1], taps_y_recv.at[1], beside)

    own_taps_y = remote(
        taps.at[s, g, share],
        taps.at[s, g, share],
        taps_y_send.at[0],
        taps_y_recv.at[0],
        beside,
    )

    def forward_copy(i):
        block = far.at[c, at(pieces[i])]
        return remote(
            block, block, fwd_send, far_recv.at[i, c], {"chan": sibling}
        )

    def half_part(j, a, span):
        return jnp.dot(far[a, slice(*span)], w[j, a], preferred_element_type=F32)

    def take(i):
        with jax.named_scope("direct"):
            arrive(far.at[c, at(pieces[i])], far_recv.at[i, c])
        forward_copy(i).start()

    def take_other(i):
        arrive(far.at[sibling, at(pieces[i])], far_recv.at[i, sibling])

    with jax.named_scope("edge_rows"):
        take(0)
        for j in range(2):
            projected[j, 8 + rows - EDGE :] = half_part(j + 1, c, pieces[0])
        @pl.when(goes_up)
        def _():
            pl.semaphore_wait(ready, 4 * (last - s))

            @pl.when(f == 1)
            def _():
                edge_up(0).start()
                for h in range(2):
                    query_edge(h).start()

        with jax.named_scope("taps_up"):
            arrive(taps.at[s, f], taps_local)
            arrive(taps.at[s, g, share], taps_x_recv)
            for t in range(1, seq):

                @pl.when(t > s)
                def _():
                    taps_z_copy(t).start()

            @pl.when(f == 1)
            def _():
                pl.semaphore_wait(near, 1)

            own_taps_y.start()

        take_other(0)
        for j in range(2):
            term = projected[j, 8 + rows - EDGE :] + half_part(j + 1, sibling, pieces[0])
            projected[j, 8 + rows - EDGE :] = term
            edge_out[1, j] = term[EDGE - 8 :]

        @pl.when(f == 1)
        def _():
            edge_across.start()

        @pl.when(jnp.logical_not(holds))
        def _():
            for i in range(2, count + 1):
                for a in range(2):
                    token_copy(i, a).start()

        @pl.when(jnp.logical_and(f == 0, goes_up))
        def _():
            edge_up(1).start()
            term = far_part(0, pieces[0])
            query_edge_out[0] = term[EDGE - 8 :, :lanes]
            query_edge_out[1] = term[EDGE - 8 :, lanes:]
            for h in range(2):
                query_edge(h).start()

    def across_copy(i):
        return remote(
            halves.at[g, at(made[i])],
            signal.at[s, g, at(made[i])],
            across_send,
            across_recv,
            diagonal,
        )

    def aside_copy(i):
        return remote(
            halves.at[f, at(made[i])],
            signal.at[s, g, at(made[i])],
            across_send,
            across_recv,
            aside,
        )

    def up_copy(i, t):
        return remote(
            halves.at[f, at(made[i])],
            signal.at[s, g, at(made[i])],
            up_send,
            up_recv.at[s],
            {"seq": t, "chan": sibling},
        )

    def cross_copy(i, t):
        return remote(
            halves.at[g, at(made[i])],
            signal.at[s, g, at(made[i])],
            up_send,
            up_recv.at[s],
            {"seq": t, "fsdp": g, "chan": sibling},
        )

    def cross_start(i, low):
        for t in range(1, seq):

            @pl.when(jnp.logical_and(t > s, (s == 0) if low else (s > 0)))
            def _():
                cross_copy(i, t).start()

    def query_early(now):
        @pl.when(now)
        def _():
            own_query_copy.start()
            for i in range(count - 1):
                query_copy(i).start()

    def branch(j, span):
        low, high = span
        now = projected[j, 8 + low : 8 + high]
        one = projected[j, 7 + low : 7 + high]
        two = projected[j, 6 + low : 6 + high]
        return (
            short[0, j + 1 : j + 2, :] * now
            + short[1, j + 1 : j + 2, :] * one
            + short[2, j + 1 : j + 2, :] * two
        )

    def transform(values):
        whole = table[:2].reshape(2 * bins, bins)
        return jnp.dot(whole, values, preferred_element_type=F32)

    def taps_spectrum():
        ids = lax.broadcasted_iota(jnp.int32, (bins, lanes), 0)
        sign = 1.0 - 2.0 * (ids % 2).astype(F32)
        arrive(taps.at[s, g, rest], taps_y_recv.at[0])
        for n in range(1, seq):

            @pl.when(s == n)
            def _():
                arrive(taps.at[pl.ds(0, n), :, rest], taps_y_recv.at[1])

        for d in range(seq):

            @pl.when(d <= s)
            def _():
                spec = transform(taps[d].reshape(bins, lanes))
                real, imag = spec[:bins], spec[bins:]
                tapspec[d] = spec
                if d == 0:
                    response[0, 0] = sign * imag
                    response[0, 1] = -sign * real
                else:
                    response[d, 0] = tapspec[d - 1, :bins] + sign * imag
                    response[d, 1] = tapspec[d - 1, bins:] - sign * real

    for i in range(count):
        low, high = made[i]
        final_chunk = i == count - 1
        with jax.named_scope("tokens"):
            take(i + 1)
            if final_chunk:
                query_early(s == 0)
                for r in range(i):
                    cross_start(r, True)
            lines = slice(8 + spans[i][0], 8 + spans[i][1])
            for j in range(2):
                projected[j, lines] = half_part(j + 1, c, spans[i])
            if final_chunk:
                query_term[low:high] = half_part(0, c, made[i])
            if i == 0:
                with jax.named_scope("taps_side"):
                    for n in range(1, seq):

                        @pl.when(s == n)
                        def _():
                            arrive(taps.at[pl.ds(0, n), :, share], taps_z_recv)
                            taps_y_copy(n).start()

            take_other(i + 1)
            if not final_chunk:
                part_copy(i + 1).start()
        with jax.named_scope("chunk"):
            for j in range(2):
                projected[j, lines] += half_part(j + 1, sibling, spans[i])
        if i == 0:
            with jax.named_scope("edges"):

                @pl.when(jnp.logical_and(f == 1, s > 0))
                def _():
                    arrive(edge_in, edge_recv)

                @pl.when(f == 0)
                def _():
                    arrive(edge_in.at[1], edge_recv)

                for j in range(2):
                    projected[j, :8] = rounded(edge_in[0, j] + edge_in[1, j])
        with jax.named_scope("partial"):
            part_copy(i).wait_recv()
        with jax.named_scope("product"):
            for j in range(2):
                block = slice(8 + low, 8 + high)
                projected[j, block] = rounded(
                    projected[j, block] + part_in[j, low:high].astype(F32)
                )
            product = (branch(0, made[i]) * branch(1, made[i])).astype(BF16)
            halves[0, low:high] = product[:, :lanes]
            halves[1, low:high] = product[:, lanes:]
            across_copy(i).start()
            aside_copy(i).start()
            cross_start(i, False)
            for t in range(1, seq):

                @pl.when(t > s)
                def _():
                    up_copy(i, t).start()

        if final_chunk:
            cross_start(i, True)
            query_early(s > 0)
        with jax.named_scope("far_query"):
            if final_chunk:
                term = query_term[low:high] + half_part(0, sibling, made[i])
            else:
                term = far_part(0, made[i])
            query[g, low:high] = half_of(term)
            query_aside((g, at(made[i]))).start()
            query_out[1, low:high] = other_half(term).astype(BF16)
            if final_chunk:
                query_copy(i).start()
    def spectrum(j, d):
        spec = transform(signal[j].reshape(bins, lanes))
        real, imag = spec[:bins], spec[bins:]
        hr, hi = response[d, 0], response[d, 1]
        return real * hr - imag * hi, real * hi + imag * hr

    with jax.named_scope("taps_spectra"):
        taps_spectrum()

    with jax.named_scope("earlier_slabs"):
        result[...] = jnp.zeros_like(result)
        for j in range(last - 1):

            @pl.when(j < s - 1)
            def _():
                arrive(signal.at[j], up_recv.at[j])
                real, imag = spectrum(j, s - j)
                result[0] += real
                result[1] += imag

    arrive(short_near, short_recv)
    arrive(gain, gain_recv)
    with jax.named_scope("own_wait"):
        arrive(signal.at[s], across_recv)
    with jax.named_scope("own_slab"):
        real, imag = spectrum(s, 0)
        result[0] += real
        result[1] += imag

    with jax.named_scope("slab_before"):

        @pl.when(s == 0)
        def _():
            packed[...] = result[...].astype(BF16)

        @pl.when(s > 0)
        def _():
            arrive(signal.at[s - 1], up_recv.at[s - 1])
            real, imag = spectrum(s - 1, 1)
            packed[0] = (result[0] + real).astype(BF16)
            packed[1] = (result[1] + imag).astype(BF16)

    with jax.named_scope("query"):
        arrive(query_in, query_recv)
        arrive(query_near, query_aside_recv)

        @pl.when(s > 0)
        def _():
            arrive(query_edge_in, query_edge_recv)

        mixed[:8] = rounded(query_edge_in[0] + query_edge_in[1])
        other = pl.multiple_of(8 + g * rows, 8)
        mine = pl.multiple_of(8 + f * rows, 8)
        mixed[pl.ds(other, rows)] = rounded(query_near[g] + query_in[0].astype(F32))
        mixed[pl.ds(mine, rows)] = rounded(query_near[f] + query_in[1].astype(F32))
        gate = [half_of(short_near[i, 0:1, :]) for i in range(3)]
        gated = gate[0] * mixed[8 : 8 + bins] + gate[1] * mixed[7 : 7 + bins]
        gated += gate[2] * mixed[6 : 6 + bins]
        query_near[...] = gated.reshape(2, rows, lanes)

    with jax.named_scope("finish"):
        factor = half_of(gain[...])

        def finish(b):
            lines = pl.ds(pl.multiple_of(b * rows, rows), rows)
            conv = jnp.dot(table[2, lines], packed[0], preferred_element_type=F32)
            conv += jnp.dot(table[3, lines], packed[1], preferred_element_type=F32)
            whole = conv + factor * signal[s, b].astype(F32)
            return (query_near[b] * whole).astype(BF16)

        landing = out.at[:, columns(f)]
        out_across = remote(final.at[0], landing, out_send, out_recv, diagonal)
        out_aside = remote(final.at[1], landing, out_send, out_recv, aside)
        final[0] = finish(g)
        out_across.start()
        final[1] = finish(f)
        out_aside.start()

    with jax.named_scope("drain"):

        @pl.when(jnp.logical_not(holds))
        def _():
            arrive(far, own_send)

        @pl.when(holds)
        def _():
            own_copy.wait_send()

        taps_x_copy.wait_send()
        arrive(far.at[c], fwd_send)
        arrive(part_out, part_send)
        arrive(halves, across_send)
        arrive(query, query_aside_send)
        short_copy.wait_send()
        gain_copy.wait_send()
        taps_aside.wait_send()
        arrive(query_out, query_send)
        own_taps_y.wait_send()

        @pl.when(jnp.logical_and(f == 1, goes_up))
        def _():
            arrive(edge_out, edge_send)

        @pl.when(f != jnp.where(goes_up, 1, 0))
        def _():
            arrive(edge_out.at[1], edge_send)

        @pl.when(goes_up)
        def _():
            arrive(query_edge_out, query_edge_send)

        for n in range(1, seq):

            @pl.when(s == n)
            def _():
                taps_y_copy(n).wait_send()

            @pl.when(last - s == n)
            def _():
                arrive(taps.at[pl.ds(0, n), :, share], taps_z_send)
                arrive(signal.at[pl.ds(0, n)], up_send)

    with jax.named_scope("out"):
        arrive(final, out_send)
        arrive(out, out_recv)


def causal_device(seq, tokens, proj_weight, short_weight, skip_gain, filter_taps):
    rows = tokens.shape[0]
    depth, branches, width = proj_weight.shape
    lanes = width // 2
    step = depth // 2
    table = causal_tables(2 * rows)
    count = len(chunk_spans(rows))
    dma = pltpu.SemaphoreType.DMA
    hbm = pl.BlockSpec(memory_space=pl.ANY)
    scratch = [
        ((branches, 2, step, width), BF16),
        (table.shape, BF16),
        (short_weight.shape, F32),
        ((1, width), F32),
        ((rows, depth), BF16),
        ((2, rows, step), BF16),
        ((2, rows, width), BF16),
        ((2, rows, width), BF16),
        ((2, 2, 8, width), F32),
        ((2, 2, 8, width), F32),
        ((2, 8 + rows, width), F32),
        ((2, rows, lanes), BF16),
        ((seq, 2, rows, lanes), BF16),
        ((seq, 2, rows, lanes), BF16),
        ((seq, 4 * rows, lanes), F32),
        ((seq, 2, 2 * rows, lanes), F32),
        ((2, rows, lanes), F32),
        ((rows, width), F32),
        ((2, rows, lanes), BF16),
        ((2, rows, lanes), BF16),
        ((2, 8, lanes), F32),
        ((2, 8, lanes), F32),
        ((8 + 2 * rows, lanes), F32),
        ((2, 2 * rows, lanes), F32),
        ((2, 2 * rows, lanes), BF16),
        ((2, rows, lanes), BF16),
        ((2, rows, lanes), F32),
        (short_weight.shape, F32),
    ]
    sems = [
        (4,),
        (),
        (),
        (count + 1, 2),
        (),
        (),
        (count,),
        (),
        (),
        (),
        (),
        (),
        (max(seq - 1, 1),),
        (),
        (),
        (),
        (),
        (),
        (2,),
        (2,),
        (),
        (),
        (),
        (),
        (),
        (),
        (),
        (),
        (),
        (),
        (),
        (),
        (),
    ]
    return pl.pallas_call(
        functools.partial(causal_kernel, seq),
        out_shape=pltpu.VMEM((rows, width), BF16),
        in_specs=[hbm] * 6,
        out_specs=pl.BlockSpec(memory_space=pltpu.VMEM),
        scratch_shapes=[pltpu.VMEM(shape, kind) for shape, kind in scratch]
        + [dma(shape) for shape in sems]
        + [pltpu.SemaphoreType.REGULAR] * 2,
        compiler_params=pltpu.CompilerParams(
            collective_id=0, has_side_effects=True, vmem_limit_bytes=60 * 1024 * 1024
        ),
        name="hyena",
    )(
        tokens,
        jnp.transpose(proj_weight, (1, 0, 2)).reshape(branches, 2, step, width),
        short_weight,
        skip_gain.reshape(1, width),
        filter_taps,
        jnp.asarray(table),
    )


def solution(mesh):
    seq = mesh.shape["seq"]
    paired = all(mesh.shape[axis] == 2 for axis in ("grp", "fsdp", "chan"))
    sizes = (mesh.shape["seq"], mesh.shape["fsdp"], mesh.shape["chan"])
    in_specs = (
        P(("grp", "seq", "fsdp"), "chan"),
        P("fsdp", None, "chan"),
        P(None, None, "chan"),
        P("chan"),
        P(("seq", "fsdp"), "chan"),
    )
    out_specs = P(("grp", "seq", "fsdp"), "chan")
    return jax.shard_map(
        functools.partial(causal_device, seq)
        if paired
        else functools.partial(per_device, sizes),
        mesh=mesh,
        in_specs=in_specs,
        out_specs=out_specs,
        check_vma=False,
    )
```

```python
import functools
import math

import jax
import jax.numpy as jnp
import ml_dtypes
import numpy as np
from jax import lax
from jax.experimental import pallas as pl
from jax.experimental.pallas import tpu as pltpu
from jax.sharding import PartitionSpec as P

MESH = pl.DeviceIdType.MESH
BF16 = jnp.bfloat16
F32 = jnp.float32
MOST_CHUNKS = 2
HALVES = 2
EDGE = 16
CHUNK = 80


def phase_pair(rows, cols, period):
    wrapped = (np.arange(rows)[:, None] * np.arange(cols)[None, :]) % period
    phase = wrapped.astype(np.float32) * np.float32(2.0 * math.pi / period)
    return np.cos(phase), np.sin(phase)


def tables(groups, per, rows):
    bf = ml_dtypes.bfloat16
    bins = 2 * groups
    cos, sin = phase_pair(bins, groups, bins)
    eye = np.eye(per, dtype=np.float32)
    first = np.concatenate([np.kron(cos, eye), np.kron(-sin, eye)], axis=0).astype(bf)
    cos, sin = phase_pair(rows, rows, rows)
    ahead = np.block([[cos, -sin], [sin, cos]]).astype(bf)
    behind = np.block([[cos, sin], [-sin, cos]]).astype(bf)
    cos, sin = phase_pair(bins, rows, bins * rows)
    twist = np.stack([np.repeat(cos, per, axis=0), np.repeat(sin, per, axis=0)])
    last = np.ascontiguousarray(first.T)
    return first, last, ahead, behind, twist.astype(np.float32)


def kernel(
    sizes,
    tokens,
    weight,
    short_h,
    gain_h,
    taps_h,
    first_h,
    last_h,
    ahead_h,
    behind_h,
    twist_h,
    out,
    w,
    first,
    last,
    ahead,
    behind,
    twist,
    short,
    gain,
    taps,
    held,
    acc,
    psend,
    precv,
    hrecv,
    query,
    product,
    tsend,
    trecv,
    gsend,
    grecv,
    csend,
    crecv,
    tapspec,
    load_sem,
    tok_send,
    tok_recv,
    fwd_send,
    part_send,
    part_recv,
    halo_send,
    halo_recv,
    a2a_send,
    a2a_recv,
):
    seq, fsdp, chan = sizes
    groups = seq * fsdp
    rows = tokens.shape[0]
    chunks = weight.shape[1]
    lines = rows // HALVES
    depth = chunks * weight.shape[2]
    width = weight.shape[3]
    per = width // groups
    bins = 2 * groups
    step = depth // chunks
    share = fsdp // chan
    s = lax.axis_index("seq")
    f = lax.axis_index("fsdp")
    c = lax.axis_index("chan")
    me = s * fsdp + f

    loads = [
        pltpu.make_async_copy(source, target, load_sem.at[i])
        for i, (source, target) in enumerate(
            [
                (taps_h, taps),
                (weight.at[pl.ds(1, 2)], w.at[pl.ds(1, 2)]),
                (first_h, first),
                (ahead_h, ahead),
                (twist_h, twist),
                (last_h, last),
                (behind_h, behind),
                (short_h, short),
                (gain_h, gain),
                (weight.at[pl.ds(0, 1)], w.at[pl.ds(0, 1)]),
            ]
        )
    ]
    for load in loads:
        load.start()

    barrier = pltpu.get_barrier_semaphore()
    everyone = groups * chan

    def greet(k, carry):
        other = lax.rem(me * chan + c + k, everyone)
        spot = other // chan
        pl.semaphore_signal(
            barrier,
            inc=1,
            device_id={"seq": spot // fsdp, "fsdp": spot % fsdp, "chan": other % chan},
            device_id_type=MESH,
        )
        return carry

    lax.fori_loop(1, everyone, greet, 0, unroll=everyone <= 16)

    @pl.when(me == 0)
    def _():
        hrecv[...] = jnp.zeros_like(hrecv)

    loads[0].wait()
    tsend[...] = jnp.transpose(taps[...].astype(F32)).astype(BF16).reshape(groups, per, rows)
    pl.semaphore_wait(barrier, everyone - 1)

    sibling = lax.rem(c + 1, chan)

    def span(h):
        return pl.ds(h * lines, lines)

    def token_copy(i, h, k, same):
        return pltpu.make_async_remote_copy(
            src_ref=tokens.at[span(h), pl.ds(i * depth + k * step, step)],
            dst_ref=held.at[f, k, span(h)],
            send_sem=tok_send.at[i, h, k],
            recv_sem=tok_recv.at[f, h, k],
            device_id={"fsdp": c * share + i, "chan": sibling if same else k % chan},
            device_id_type=MESH,
        )

    for h, k in [(h, k) for h in range(HALVES) for k in range(chunks)]:
        for i in range(share):
            stays = c * share + i == f

            @pl.when(jnp.logical_not(stays))
            def _():
                token_copy(i, h, k, False).start()

            @pl.when(stays)
            def _():
                token_copy(i, h, k, True).start()
                pltpu.make_async_copy(
                    tokens.at[span(h), pl.ds(i * depth + k * step, step)],
                    held.at[f, k, span(h)],
                    tok_recv.at[f, h, k],
                ).start()

    def exchange_copy(which, source, target, k):
        other = lax.rem(me + k, groups)
        return pltpu.make_async_remote_copy(
            src_ref=source.at[other],
            dst_ref=target.at[me],
            send_sem=a2a_send.at[which, k],
            recv_sem=a2a_recv.at[which, k],
            device_id={"seq": other // fsdp, "fsdp": other % fsdp},
            device_id_type=MESH,
        )

    def exchange_start(which, source, target):
        def go(k, carry):
            exchange_copy(which, source, target, k).start()
            return carry

        lax.fori_loop(1, groups, go, 0, unroll=groups <= 8)
        target[me] = source[me]

    def exchange_wait(which, source, target):
        def go(k, carry):
            exchange_copy(which, source, target, k).wait_recv()
            return carry

        lax.fori_loop(1, groups, go, 0, unroll=groups <= 8)

    def exchange_sent(which, source, target):
        def go(k, carry):
            exchange_copy(which, source, target, k).wait_send()
            return carry

        lax.fori_loop(1, groups, go, 0)


    half = bins * per

    def spectrum(signal):
        a = jnp.dot(first[...], signal, preferred_element_type=F32)
        real_a, imag_a = a[:half], a[half:]
        real_b = (real_a * twist[0] + imag_a * twist[1]).astype(BF16)
        imag_b = (imag_a * twist[0] - real_a * twist[1]).astype(BF16)
        b = jnp.concatenate([real_b, imag_b], axis=1)
        return jnp.dot(b, ahead[...], preferred_element_type=F32).astype(BF16)

    def arrival(spot, h, k):
        block = held.at[spot, k, span(h)]
        pltpu.make_async_copy(block, block, tok_recv.at[spot, h, k]).wait()

    def forward_copy(d, h, t):
        k = t * chan + c
        block = held.at[lax.rem(f + d, fsdp), k, span(h)]
        return pltpu.make_async_remote_copy(
            src_ref=block,
            dst_ref=block,
            send_sem=fwd_send.at[d - 1, h, t],
            recv_sem=tok_recv.at[lax.rem(f + d, fsdp), h, k],
            device_id={"chan": sibling},
            device_id_type=MESH,
        )

    def part_copy(d, j, h):
        return pltpu.make_async_remote_copy(
            src_ref=psend.at[d - 1, j, span(h)],
            dst_ref=precv.at[d - 1, j, span(h)],
            send_sem=part_send.at[d - 1, j, h],
            recv_sem=part_recv.at[d - 1, j, h],
            device_id={"fsdp": lax.rem(f + d, fsdp)},
            device_id_type=MESH,
        )

    phases = ((1, 2), (0, 1))

    def halo_target(d):
        return s * fsdp + lax.rem(f + d, fsdp) + 1

    def halo_copy(d, phase):
        target = jnp.minimum(halo_target(d), groups - 1)
        start, count = phases[phase]
        return pltpu.make_async_remote_copy(
            src_ref=acc.at[d - 1, pl.ds(start, count), pl.ds(rows - 8, 8)],
            dst_ref=hrecv.at[f, pl.ds(start, count)],
            send_sem=halo_send.at[d - 1, phase],
            recv_sem=halo_recv.at[f, phase],
            device_id={"seq": target // fsdp, "fsdp": target % fsdp},
            device_id_type=MESH,
        )

    def halo_remote(d):
        target = halo_target(d)
        return jnp.logical_and(target < groups, target != me)

    def halo_start(d, phase):
        @pl.when(halo_remote(d))
        def _():
            halo_copy(d, phase).start()

        start, count = phases[phase]

        @pl.when(halo_target(d) == me)
        def _():
            hrecv[f, start : start + count] = acc[d - 1, start : start + count, rows - 8 :]

    def halo_wait(phase):
        start, count = phases[phase]
        for h in range(fsdp):
            local = jnp.logical_and(f > 0, f == h)

            @pl.when(jnp.logical_and(me > 0, jnp.logical_not(local)))
            def _():
                block = hrecv.at[h, pl.ds(start, count)]
                pltpu.make_async_copy(block, block, halo_recv.at[h, phase]).wait()

    loads[1].wait()
    for k in range(chunks):
        for h in range(HALVES):
            arrival(f, h, k)
        for j in (1, 2):
            term = jnp.dot(held[f, k], w[j, k], preferred_element_type=F32)
            acc[fsdp - 1, j] = term if k == 0 else acc[fsdp - 1, j] + term
    halo_start(fsdp, 0)

    for d in range(1, fsdp):
        spot = lax.rem(f + d, fsdp)
        for h, t, b in [
            (h, t, b)
            for h in range(HALVES)
            for t in range(chunks // chan)
            for b in range(chan)
        ]:
            k = t * chan + lax.rem(c + b, chan)
            arrival(spot, h, k)
            if b == 0:
                forward_copy(d, h, t).start()
            final = (t + 1) * chan == chunks and b == chan - 1
            at = slice(h * lines, (h + 1) * lines)
            for j in (1, 2):
                term = jnp.dot(held[spot, k, at], w[j, k], preferred_element_type=F32)
                if t > 0 or b > 0:
                    term = acc[d - 1, j, at] + term
                acc[d - 1, j, at] = term
                if final:
                    psend[d - 1, j, at] = term.astype(BF16)
                    part_copy(d, j, h).start()
        halo_start(d, 0)

    for load in loads[2:]:
        load.wait()
    exchange_start(0, tsend, trecv)

    row_ids = lax.broadcasted_iota(jnp.int32, (rows, width), 0)

    def branch(j):
        total = acc[fsdp - 1, j]
        edge = hrecv[0, j]
        for d in range(1, fsdp):
            for h in range(HALVES):
                part_copy(d, j, h).wait_recv()
            total = total + precv[d - 1, j].astype(F32)
            edge = edge + hrecv[d, j]
        now = total.astype(BF16).astype(F32)
        edge = edge.astype(BF16).astype(F32)
        before = edge[7:8]
        earlier = edge[6:7]
        one = jnp.where(row_ids == 0, before, pltpu.roll(now, 1, 0))
        two = jnp.where(
            row_ids == 0, earlier, jnp.where(row_ids == 1, before, pltpu.roll(now, 2, 0))
        )
        return (
            short[0, j : j + 1, :] * now
            + short[1, j : j + 1, :] * one
            + short[2, j : j + 1, :] * two
        )

    halo_wait(0)
    prod = (branch(1) * branch(2)).astype(BF16).astype(F32)
    gsend[...] = jnp.transpose(prod).astype(BF16).reshape(groups, per, rows)
    exchange_start(1, gsend, grecv)
    product[...] = prod * gain[...]

    for d in range(1, fsdp + 1):
        spot = lax.rem(f + d, fsdp)
        term = jnp.dot(held[spot, 0], w[0, 0], preferred_element_type=F32)
        for k in range(1, chunks):
            term += jnp.dot(held[spot, k], w[0, k], preferred_element_type=F32)
        acc[d - 1, 0] = term
        if d < fsdp:
            psend[d - 1, 0] = term.astype(BF16)

    exchange_wait(0, tsend, trecv)
    tapspec[...] = spectrum(trecv[...].reshape(width, rows))
    exchange_wait(1, gsend, grecv)
    for d in range(1, fsdp + 1):
        if d < fsdp:
            for h in range(HALVES):
                part_copy(d, 0, h).start()
        halo_start(d, 1)

    x = spectrum(grecv[...].reshape(width, rows)).astype(F32)
    t = tapspec[...].astype(F32)
    xr, xi = x[:, :rows], x[:, rows:]
    tr, ti = t[:, :rows], t[:, rows:]
    real_z = (xr * tr - xi * ti).astype(BF16)
    imag_z = (xr * ti + xi * tr).astype(BF16)
    z = jnp.concatenate([real_z, imag_z], axis=1)
    v = jnp.dot(z, behind[...], preferred_element_type=F32)
    vr, vi = v[:, :rows], v[:, rows:]
    real_w = (vr * twist[0] - vi * twist[1]).astype(BF16)
    imag_w = (vi * twist[0] + vr * twist[1]).astype(BF16)
    packed = jnp.concatenate([real_w, imag_w], axis=0)
    y = jnp.dot(last[...], packed, preferred_element_type=F32) * (1.0 / (bins * rows))
    csend[...] = y.astype(BF16).reshape(groups, per, rows)
    exchange_start(2, csend, crecv)
    halo_wait(1)
    query[...] = branch(0)
    exchange_wait(2, csend, crecv)
    conv = jnp.transpose(crecv[...].reshape(width, rows).astype(F32))
    out[...] = (query[...] * (conv + product[...])).astype(BF16)

    exchange_sent(0, tsend, trecv)
    exchange_sent(1, gsend, grecv)
    exchange_sent(2, csend, crecv)
    for d in range(1, fsdp + 1):
        for phase in range(2):

            @pl.when(halo_remote(d))
            def _():
                halo_copy(d, phase).wait_send()

    for d in range(1, fsdp):
        for h in range(HALVES):
            for j in range(3):
                part_copy(d, j, h).wait_send()
            for t in range(chunks // chan):
                forward_copy(d, h, t).wait_send()
    for h, k in [(h, k) for h in range(HALVES) for k in range(chunks)]:
        for i in range(share):
            token_copy(i, h, k, False).wait_send()


def per_device(sizes, tokens, proj_weight, short_weight, skip_gain, filter_taps):
    seq, fsdp, chan = sizes
    groups = seq * fsdp
    rows = tokens.shape[0]
    depth, branches, width = proj_weight.shape
    per = width // groups
    chunks = min(MOST_CHUNKS, depth // 128)
    made = tables(groups, per, rows)
    dma = pltpu.SemaphoreType.DMA
    vmem = pl.BlockSpec(memory_space=pltpu.VMEM)
    hbm = pl.BlockSpec(memory_space=pl.ANY)
    half = 2 * groups * per
    return pl.pallas_call(
        functools.partial(kernel, sizes),
        out_shape=jax.ShapeDtypeStruct((rows, width), BF16),
        in_specs=[hbm] * 10,
        out_specs=vmem,
        scratch_shapes=[
            pltpu.VMEM((branches, chunks, depth // chunks, width), BF16),
            pltpu.VMEM(made[0].shape, BF16),
            pltpu.VMEM(made[1].shape, BF16),
            pltpu.VMEM(made[2].shape, BF16),
            pltpu.VMEM(made[3].shape, BF16),
            pltpu.VMEM(made[4].shape, F32),
            pltpu.VMEM(short_weight.shape, F32),
            pltpu.VMEM((1, width), F32),
            pltpu.VMEM((rows, width), BF16),
            pltpu.VMEM((fsdp, chunks, rows, depth // chunks), BF16),
            pltpu.VMEM((fsdp, branches, rows, width), F32),
            pltpu.VMEM((fsdp - 1, branches, rows, width), BF16),
            pltpu.VMEM((fsdp - 1, branches, rows, width), BF16),
            pltpu.VMEM((fsdp, branches, 8, width), F32),
            pltpu.VMEM((rows, width), F32),
            pltpu.VMEM((rows, width), F32),
        ]
        + [pltpu.VMEM((groups, per, rows), BF16)] * 6
        + [
            pltpu.VMEM((half, 2 * rows), BF16),
            dma((10,)),
            dma((fsdp // chan, HALVES, chunks)),
            dma((fsdp, HALVES, chunks)),
            dma((fsdp - 1, HALVES, chunks // chan)),
            dma((fsdp - 1, branches, HALVES)),
            dma((fsdp - 1, branches, HALVES)),
            dma((fsdp, 2)),
            dma((fsdp, 2)),
            dma((3, groups)),
            dma((3, groups)),
        ],
        compiler_params=pltpu.CompilerParams(
            collective_id=0, has_side_effects=True, vmem_limit_bytes=60 * 1024 * 1024
        ),
        name="hyena",
    )(
        tokens,
        jnp.transpose(proj_weight, (1, 0, 2)).reshape(branches, chunks, depth // chunks, width),
        short_weight,
        skip_gain.reshape(1, width),
        filter_taps,
        *[jnp.asarray(table) for table in made],
    )


def causal_tables(rows):
    bf = ml_dtypes.bfloat16
    odd = 2 * np.arange(rows) + 1
    period = 4 * rows

    def angles(times):
        wrapped = (odd[:, None] * times[None, :]) % period
        return wrapped.astype(np.float64) * (2.0 * math.pi / period)

    ahead = angles(np.arange(rows))
    behind = angles(rows + np.arange(rows)).T
    pair = [np.cos(behind) / rows, -np.sin(behind) / rows]
    return np.stack([np.cos(ahead), -np.sin(ahead), *pair]).astype(bf)


def chunk_spans(rows):
    head = rows - EDGE
    return [(at, min(at + CHUNK, head)) for at in range(0, head, CHUNK)]


def causal_kernel(
    seq,
    tokens,
    weight,
    short_h,
    gain_h,
    taps_h,
    table_h,
    out,
    w,
    table,
    short,
    gain,
    own,
    far,
    part_out,
    part_in,
    edge_out,
    edge_in,
    projected,
    halves,
    signal,
    taps,
    tapspec,
    response,
    query,
    query_term,
    query_out,
    query_in,
    query_edge_out,
    query_edge_in,
    mixed,
    result,
    packed,
    final,
    query_near,
    short_near,
    load_sem,
    own_send,
    own_recv,
    far_recv,
    fwd_send,
    part_send,
    part_recv,
    edge_send,
    edge_recv,
    across_send,
    across_recv,
    up_send,
    up_recv,
    taps_local,
    taps_x_send,
    taps_x_recv,
    taps_z_send,
    taps_z_recv,
    taps_y_send,
    taps_y_recv,
    query_send,
    query_recv,
    query_edge_send,
    query_edge_recv,
    out_send,
    out_recv,
    query_aside_send,
    query_aside_recv,
    short_send,
    short_recv,
    gain_send,
    gain_recv,
    taps_local_send,
    ready,
    near,
):
    rows = tokens.shape[0]
    width = weight.shape[3]
    depth = weight.shape[2]
    lanes = width // 2
    bins = 2 * rows
    last = seq - 1
    spans = chunk_spans(rows)
    count = len(spans)
    pieces = [(rows - EDGE, rows), *spans]
    made = [*spans[:-1], (spans[-1][0], rows)]
    group = lax.axis_index("grp")
    s = lax.axis_index("seq")
    f = lax.axis_index("fsdp")
    c = lax.axis_index("chan")
    g = 1 - f
    sibling = 1 - c
    holds = c == f
    goes_up = s < last
    across = {"fsdp": g}
    aside = {"chan": sibling}
    diagonal = {"fsdp": g, "chan": sibling}

    def half_of(value):
        return jnp.where(f == 0, value[:, :lanes], value[:, lanes:])

    def other_half(value):
        return jnp.where(f == 0, value[:, lanes:], value[:, :lanes])

    def rounded(value):
        return value.astype(BF16).astype(F32)

    def columns(h):
        return pl.ds(pl.multiple_of(h * lanes, lanes), lanes)

    def at(span):
        return pl.ds(span[0], span[1] - span[0])

    def remote(source, target, send, recv, device):
        return pltpu.make_async_remote_copy(
            src_ref=source,
            dst_ref=target,
            send_sem=send,
            recv_sem=recv,
            device_id=device,
            device_id_type=MESH,
        )

    def arrive(block, sem):
        pltpu.make_async_copy(block, block, sem).wait()

    own_load = pltpu.make_async_copy(tokens, own, own_recv)

    @pl.when(holds)
    def _():
        own_load.start()

    loads = [
        pltpu.make_async_copy(source, target, load_sem.at[i])
        for i, (source, target) in enumerate(
            [
                (weight.at[pl.ds(1, 2)], w.at[pl.ds(1, 2)]),
                (weight.at[pl.ds(0, 1)], w.at[pl.ds(0, 1)]),
                (table_h, table),
                (short_h, short),
            ]
        )
    ]
    for load in loads:
        load.start()
    edge_in[...] = jnp.zeros_like(edge_in)
    query_edge_in[...] = jnp.zeros_like(query_edge_in)

    def member(t, h):
        return {"seq": t, "fsdp": h // 2, "chan": h % 2}

    barrier = pltpu.get_barrier_semaphore()
    beside = {"grp": 1 - group}
    for device in [{"chan": sibling}, across, {"fsdp": g, "chan": sibling}]:
        pl.semaphore_signal(barrier, inc=1, device_id=device, device_id_type=MESH)

    @pl.when(f == 0)
    def _():
        pl.semaphore_signal(barrier, inc=1, device_id=beside, device_id_type=MESH)

    for t in range(seq):
        for h in range(4):

            @pl.when(t > s)
            def _():
                pl.semaphore_signal(
                    barrier, inc=1, device_id=member(t, h), device_id_type=MESH
                )

    pl.semaphore_wait(barrier, 3 + g + 4 * s)

    def token_copy(i, a):
        return remote(
            tokens.at[at(pieces[i]), pl.ds(a * depth, depth)],
            far.at[a, at(pieces[i])],
            own_send,
            far_recv.at[i, a],
            {"fsdp": g, "chan": a},
        )

    own_copy = remote(tokens, own, own_send, own_recv, aside)
    short_copy = remote(short_h, short_near, short_send, short_recv, aside)
    gain_copy = remote(gain_h, gain, gain_send, gain_recv, aside)
    taps_aside = remote(
        taps_h.at[:, columns(f)], taps.at[s, f], taps_local_send, taps_local, aside
    )
    share = pl.ds(pl.multiple_of(group * (rows // 2), rows // 2), rows // 2)
    rest = pl.ds(pl.multiple_of((1 - group) * (rows // 2), rows // 2), rows // 2)
    taps_x_copy = remote(
        taps_h.at[share, columns(g)],
        taps.at[s, f, share],
        taps_x_send,
        taps_x_recv,
        diagonal,
    )

    @pl.when(jnp.logical_not(holds))
    def _():
        for a in range(2):
            token_copy(0, a).start()

    taps_x_copy.start()

    @pl.when(jnp.logical_not(holds))
    def _():
        for a in range(2):
            token_copy(1, a).start()

    @pl.when(holds)
    def _():
        own_copy.start()

    taps_aside.start()
    short_copy.start()
    gain_copy.start()

    @pl.when(f == 0)
    def _():
        pl.semaphore_signal(near, inc=1, device_id=beside, device_id_type=MESH)

    for t in range(seq):
        for h in range(4):

            @pl.when(t < s)
            def _():
                pl.semaphore_signal(
                    ready, inc=1, device_id=member(t, h), device_id_type=MESH
                )

    def part_copy(i):
        return remote(
            part_out.at[:, at(made[i])],
            part_in.at[:, at(made[i])],
            part_send,
            part_recv.at[i],
            across,
        )

    own_query_copy = remote(
        query_out.at[0], query_in.at[0], query_send, query_recv, diagonal
    )

    def query_copy(i):
        return remote(
            query_out.at[1, at(made[i])],
            query_in.at[1, at(made[i])],
            query_send,
            query_recv,
            diagonal,
        )

    def query_aside(block):
        return remote(
            query.at[block],
            query_near.at[block],
            query_aside_send,
            query_aside_recv,
            aside,
        )

    def own_part(j):
        return jnp.dot(own[:, :depth], w[j, 0], preferred_element_type=F32) + jnp.dot(
            own[:, depth:], w[j, 1], preferred_element_type=F32
        )

    def far_part(j, span):
        rows_at = slice(*span)
        return jnp.dot(far[0, rows_at], w[j, 0], preferred_element_type=F32) + jnp.dot(
            far[1, rows_at], w[j, 1], preferred_element_type=F32
        )

    with jax.named_scope("own_rows"):
        arrive(own, own_recv)
        loads[0].wait()
        for j in range(2):
            term = own_part(j + 1)
            part_out[j] = term.astype(BF16)
            edge_out[0, j] = term[rows - 8 :]
        part_copy(0).start()

        @pl.when(f == 0)
        def _():
            edge_in[0] = edge_out[0]

    with jax.named_scope("own_query"):
        for load in loads[1:]:
            load.wait()
        term = own_part(0)
        query[f] = half_of(term)
        query_aside(f).start()
        query_out[0] = other_half(term).astype(BF16)

        @pl.when(f == 1)
        def _():
            query_edge_out[0] = term[rows - 8 :, :lanes]
            query_edge_out[1] = term[rows - 8 :, lanes:]

    @pl.when(f == 0)
    def _():
        pl.semaphore_wait(near, 1)
        pl.semaphore_signal(near, inc=1, device_id=across, device_id_type=MESH)

    def edge_up(i):
        return remote(
            edge_out.at[i],
            edge_in.at[i],
            edge_send,
            edge_recv,
            {"seq": jnp.minimum(s + 1, last), "fsdp": 1},
        )

    edge_across = remote(
        edge_out.at[1], edge_in.at[1], edge_send, edge_recv, {"fsdp": 0}
    )

    def query_edge(h):
        return remote(
            query_edge_out.at[h],
            query_edge_in.at[f],
            query_edge_send,
            query_edge_recv,
            {"seq": jnp.minimum(s + 1, last), "fsdp": h, "chan": sibling},
        )

    def taps_z_copy(t):
        block = taps.at[s, :, share]
        return remote(block, block, taps_z_send, taps_z_recv, {"seq": t})

    def taps_y_copy(n):
        block = taps.at[pl.ds(0, n), :, share]
        return remote(block, block, taps_y_send.at[1], taps_y_recv.at[1], beside)

    own_taps_y = remote(
        taps.at[s, g, share],
        taps.at[s, g, share],
        taps_y_send.at[0],
        taps_y_recv.at[0],
        beside,
    )

    def forward_copy(i):
        block = far.at[c, at(pieces[i])]
        return remote(
            block, block, fwd_send, far_recv.at[i, c], {"chan": sibling}
        )

    def half_part(j, a, span):
        return jnp.dot(far[a, slice(*span)], w[j, a], preferred_element_type=F32)

    def take(i):
        with jax.named_scope("direct"):
            arrive(far.at[c, at(pieces[i])], far_recv.at[i, c])
        forward_copy(i).start()

    def take_other(i):
        arrive(far.at[sibling, at(pieces[i])], far_recv.at[i, sibling])

    with jax.named_scope("edge_rows"):
        take(0)
        for j in range(2):
            projected[j, 8 + rows - EDGE :] = half_part(j + 1, c, pieces[0])
        @pl.when(goes_up)
        def _():
            pl.semaphore_wait(ready, 4 * (last - s))

            @pl.when(f == 1)
            def _():
                edge_up(0).start()
                for h in range(2):
                    query_edge(h).start()

        with jax.named_scope("taps_up"):
            arrive(taps.at[s, f], taps_local)
            arrive(taps.at[s, g, share], taps_x_recv)
            for t in range(1, seq):

                @pl.when(t > s)
                def _():
                    taps_z_copy(t).start()

            @pl.when(f == 1)
            def _():
                pl.semaphore_wait(near, 1)

            own_taps_y.start()

        take_other(0)
        for j in range(2):
            term = projected[j, 8 + rows - EDGE :] + half_part(j + 1, sibling, pieces[0])
            projected[j, 8 + rows - EDGE :] = term
            edge_out[1, j] = term[EDGE - 8 :]

        @pl.when(f == 1)
        def _():
            edge_across.start()

        @pl.when(jnp.logical_not(holds))
        def _():
            for i in range(2, count + 1):
                for a in range(2):
                    token_copy(i, a).start()

        @pl.when(jnp.logical_and(f == 0, goes_up))
        def _():
            edge_up(1).start()
            term = far_part(0, pieces[0])
            query_edge_out[0] = term[EDGE - 8 :, :lanes]
            query_edge_out[1] = term[EDGE - 8 :, lanes:]
            for h in range(2):
                query_edge(h).start()

    def across_copy(i):
        return remote(
            halves.at[g, at(made[i])],
            signal.at[s, g, at(made[i])],
            across_send,
            across_recv,
            diagonal,
        )

    def aside_copy(i):
        return remote(
            halves.at[f, at(made[i])],
            signal.at[s, g, at(made[i])],
            across_send,
            across_recv,
            aside,
        )

    def up_copy(i, t):
        return remote(
            halves.at[f, at(made[i])],
            signal.at[s, g, at(made[i])],
            up_send,
            up_recv.at[s],
            {"seq": t, "chan": sibling},
        )

    def cross_copy(i, t):
        return remote(
            halves.at[g, at(made[i])],
            signal.at[s, g, at(made[i])],
            up_send,
            up_recv.at[s],
            {"seq": t, "fsdp": g, "chan": sibling},
        )

    def cross_start(i, low):
        for t in range(1, seq):

            @pl.when(jnp.logical_and(t > s, (s == 0) if low else (s > 0)))
            def _():
                cross_copy(i, t).start()

    def query_early(now):
        @pl.when(now)
        def _():
            own_query_copy.start()
            for i in range(count - 1):
                query_copy(i).start()

    def branch(j, span):
        low, high = span
        now = projected[j, 8 + low : 8 + high]
        one = projected[j, 7 + low : 7 + high]
        two = projected[j, 6 + low : 6 + high]
        return (
            short[0, j + 1 : j + 2, :] * now
            + short[1, j + 1 : j + 2, :] * one
            + short[2, j + 1 : j + 2, :] * two
        )

    def transform(values):
        whole = table[:2].reshape(2 * bins, bins)
        return jnp.dot(whole, values, preferred_element_type=F32)

    def taps_spectrum():
        ids = lax.broadcasted_iota(jnp.int32, (bins, lanes), 0)
        sign = 1.0 - 2.0 * (ids % 2).astype(F32)
        arrive(taps.at[s, g, rest], taps_y_recv.at[0])
        for n in range(1, seq):

            @pl.when(s == n)
            def _():
                arrive(taps.at[pl.ds(0, n), :, rest], taps_y_recv.at[1])

        for d in range(seq):

            @pl.when(d <= s)
            def _():
                spec = transform(taps[d].reshape(bins, lanes))
                real, imag = spec[:bins], spec[bins:]
                tapspec[d] = spec
                if d == 0:
                    response[0, 0] = sign * imag
                    response[0, 1] = -sign * real
                else:
                    response[d, 0] = tapspec[d - 1, :bins] + sign * imag
                    response[d, 1] = tapspec[d - 1, bins:] - sign * real

    for i in range(count):
        low, high = made[i]
        final_chunk = i == count - 1
        with jax.named_scope("tokens"):
            take(i + 1)
            if final_chunk:
                query_early(s < last)
                for r in range(i):
                    cross_start(r, True)
            lines = slice(8 + spans[i][0], 8 + spans[i][1])
            for j in range(2):
                projected[j, lines] = half_part(j + 1, c, spans[i])
            if final_chunk:
                query_term[low:high] = half_part(0, c, made[i])
            if i == 0:
                with jax.named_scope("taps_side"):
                    for n in range(1, seq):

                        @pl.when(s == n)
                        def _():
                            arrive(taps.at[pl.ds(0, n), :, share], taps_z_recv)
                            taps_y_copy(n).start()

            take_other(i + 1)
            if not final_chunk:
                part_copy(i + 1).start()
        with jax.named_scope("chunk"):
            for j in range(2):
                projected[j, lines] += half_part(j + 1, sibling, spans[i])
        if i == 0:
            with jax.named_scope("edges"):

                @pl.when(jnp.logical_and(f == 1, s > 0))
                def _():
                    arrive(edge_in, edge_recv)

                @pl.when(f == 0)
                def _():
                    arrive(edge_in.at[1], edge_recv)

                for j in range(2):
                    projected[j, :8] = rounded(edge_in[0, j] + edge_in[1, j])
        with jax.named_scope("partial"):
            part_copy(i).wait_recv()
        with jax.named_scope("product"):
            for j in range(2):
                block = slice(8 + low, 8 + high)
                projected[j, block] = rounded(
                    projected[j, block] + part_in[j, low:high].astype(F32)
                )
            product = (branch(0, made[i]) * branch(1, made[i])).astype(BF16)
            halves[0, low:high] = product[:, :lanes]
            halves[1, low:high] = product[:, lanes:]
            across_copy(i).start()
            aside_copy(i).start()
            cross_start(i, False)
            for t in range(1, seq):

                @pl.when(t > s)
                def _():
                    up_copy(i, t).start()

        if final_chunk:
            cross_start(i, True)
            query_early(s == last)
        with jax.named_scope("far_query"):
            if final_chunk:
                term = query_term[low:high] + half_part(0, sibling, made[i])
            else:
                term = far_part(0, made[i])
            query[g, low:high] = half_of(term)
            query_aside((g, at(made[i]))).start()
            query_out[1, low:high] = other_half(term).astype(BF16)
            if final_chunk:
                query_copy(i).start()
    def spectrum(j, d):
        spec = transform(signal[j].reshape(bins, lanes))
        real, imag = spec[:bins], spec[bins:]
        hr, hi = response[d, 0], response[d, 1]
        return real * hr - imag * hi, real * hi + imag * hr

    with jax.named_scope("taps_spectra"):
        taps_spectrum()

    with jax.named_scope("earlier_slabs"):
        result[...] = jnp.zeros_like(result)
        for j in range(last - 1):

            @pl.when(j < s - 1)
            def _():
                arrive(signal.at[j], up_recv.at[j])
                real, imag = spectrum(j, s - j)
                result[0] += real
                result[1] += imag

    arrive(short_near, short_recv)
    arrive(gain, gain_recv)
    with jax.named_scope("own_wait"):
        arrive(signal.at[s], across_recv)
    with jax.named_scope("own_slab"):
        real, imag = spectrum(s, 0)
        result[0] += real
        result[1] += imag

    with jax.named_scope("slab_before"):

        @pl.when(s == 0)
        def _():
            packed[...] = result[...].astype(BF16)

        @pl.when(s > 0)
        def _():
            arrive(signal.at[s - 1], up_recv.at[s - 1])
            real, imag = spectrum(s - 1, 1)
            packed[0] = (result[0] + real).astype(BF16)
            packed[1] = (result[1] + imag).astype(BF16)

    with jax.named_scope("query"):
        arrive(query_in, query_recv)
        arrive(query_near, query_aside_recv)

        @pl.when(s > 0)
        def _():
            arrive(query_edge_in, query_edge_recv)

        mixed[:8] = rounded(query_edge_in[0] + query_edge_in[1])
        other = pl.multiple_of(8 + g * rows, 8)
        mine = pl.multiple_of(8 + f * rows, 8)
        mixed[pl.ds(other, rows)] = rounded(query_near[g] + query_in[0].astype(F32))
        mixed[pl.ds(mine, rows)] = rounded(query_near[f] + query_in[1].astype(F32))
        gate = [half_of(short_near[i, 0:1, :]) for i in range(3)]
        gated = gate[0] * mixed[8 : 8 + bins] + gate[1] * mixed[7 : 7 + bins]
        gated += gate[2] * mixed[6 : 6 + bins]
        query_near[...] = gated.reshape(2, rows, lanes)

    with jax.named_scope("finish"):
        factor = half_of(gain[...])

        def finish(b):
            lines = pl.ds(pl.multiple_of(b * rows, rows), rows)
            conv = jnp.dot(table[2, lines], packed[0], preferred_element_type=F32)
            conv += jnp.dot(table[3, lines], packed[1], preferred_element_type=F32)
            whole = conv + factor * signal[s, b].astype(F32)
            return (query_near[b] * whole).astype(BF16)

        landing = out.at[:, columns(f)]
        out_across = remote(final.at[0], landing, out_send, out_recv, diagonal)
        out_aside = remote(final.at[1], landing, out_send, out_recv, aside)
        final[0] = finish(g)
        out_across.start()
        final[1] = finish(f)
        out_aside.start()

    with jax.named_scope("drain"):

        @pl.when(jnp.logical_not(holds))
        def _():
            arrive(far, own_send)

        @pl.when(holds)
        def _():
            own_copy.wait_send()

        taps_x_copy.wait_send()
        arrive(far.at[c], fwd_send)
        arrive(part_out, part_send)
        arrive(halves, across_send)
        arrive(query, query_aside_send)
        short_copy.wait_send()
        gain_copy.wait_send()
        taps_aside.wait_send()
        arrive(query_out, query_send)
        own_taps_y.wait_send()

        @pl.when(jnp.logical_and(f == 1, goes_up))
        def _():
            arrive(edge_out, edge_send)

        @pl.when(f != jnp.where(goes_up, 1, 0))
        def _():
            arrive(edge_out.at[1], edge_send)

        @pl.when(goes_up)
        def _():
            arrive(query_edge_out, query_edge_send)

        for n in range(1, seq):

            @pl.when(s == n)
            def _():
                taps_y_copy(n).wait_send()

            @pl.when(last - s == n)
            def _():
                arrive(taps.at[pl.ds(0, n), :, share], taps_z_send)
                arrive(signal.at[pl.ds(0, n)], up_send)

    with jax.named_scope("out"):
        arrive(final, out_send)
        arrive(out, out_recv)


def causal_device(seq, tokens, proj_weight, short_weight, skip_gain, filter_taps):
    rows = tokens.shape[0]
    depth, branches, width = proj_weight.shape
    lanes = width // 2
    step = depth // 2
    table = causal_tables(2 * rows)
    count = len(chunk_spans(rows))
    dma = pltpu.SemaphoreType.DMA
    hbm = pl.BlockSpec(memory_space=pl.ANY)
    scratch = [
        ((branches, 2, step, width), BF16),
        (table.shape, BF16),
        (short_weight.shape, F32),
        ((1, width), F32),
        ((rows, depth), BF16),
        ((2, rows, step), BF16),
        ((2, rows, width), BF16),
        ((2, rows, width), BF16),
        ((2, 2, 8, width), F32),
        ((2, 2, 8, width), F32),
        ((2, 8 + rows, width), F32),
        ((2, rows, lanes), BF16),
        ((seq, 2, rows, lanes), BF16),
        ((seq, 2, rows, lanes), BF16),
        ((seq, 4 * rows, lanes), F32),
        ((seq, 2, 2 * rows, lanes), F32),
        ((2, rows, lanes), F32),
        ((rows, width), F32),
        ((2, rows, lanes), BF16),
        ((2, rows, lanes), BF16),
        ((2, 8, lanes), F32),
        ((2, 8, lanes), F32),
        ((8 + 2 * rows, lanes), F32),
        ((2, 2 * rows, lanes), F32),
        ((2, 2 * rows, lanes), BF16),
        ((2, rows, lanes), BF16),
        ((2, rows, lanes), F32),
        (short_weight.shape, F32),
    ]
    sems = [
        (4,),
        (),
        (),
        (count + 1, 2),
        (),
        (),
        (count,),
        (),
        (),
        (),
        (),
        (),
        (max(seq - 1, 1),),
        (),
        (),
        (),
        (),
        (),
        (2,),
        (2,),
        (),
        (),
        (),
        (),
        (),
        (),
        (),
        (),
        (),
        (),
        (),
        (),
        (),
    ]
    return pl.pallas_call(
        functools.partial(causal_kernel, seq),
        out_shape=pltpu.VMEM((rows, width), BF16),
        in_specs=[hbm] * 6,
        out_specs=pl.BlockSpec(memory_space=pltpu.VMEM),
        scratch_shapes=[pltpu.VMEM(shape, kind) for shape, kind in scratch]
        + [dma(shape) for shape in sems]
        + [pltpu.SemaphoreType.REGULAR] * 2,
        compiler_params=pltpu.CompilerParams(
            collective_id=0, has_side_effects=True, vmem_limit_bytes=60 * 1024 * 1024
        ),
        name="hyena",
    )(
        tokens,
        jnp.transpose(proj_weight, (1, 0, 2)).reshape(branches, 2, step, width),
        short_weight,
        skip_gain.reshape(1, width),
        filter_taps,
        jnp.asarray(table),
    )


def solution(mesh):
    seq = mesh.shape["seq"]
    paired = all(mesh.shape[axis] == 2 for axis in ("grp", "fsdp", "chan"))
    sizes = (mesh.shape["seq"], mesh.shape["fsdp"], mesh.shape["chan"])
    in_specs = (
        P(("grp", "seq", "fsdp"), "chan"),
        P("fsdp", None, "chan"),
        P(None, None, "chan"),
        P("chan"),
        P(("seq", "fsdp"), "chan"),
    )
    out_specs = P(("grp", "seq", "fsdp"), "chan")
    return jax.shard_map(
        functools.partial(causal_device, seq)
        if paired
        else functools.partial(per_device, sizes),
        mesh=mesh,
        in_specs=in_specs,
        out_specs=out_specs,
        check_vma=False,
    )
```

```python
import functools
import math

import jax
import jax.numpy as jnp
import ml_dtypes
import numpy as np
from jax import lax
from jax.experimental import pallas as pl
from jax.experimental.pallas import tpu as pltpu
from jax.sharding import PartitionSpec as P

MESH = pl.DeviceIdType.MESH
BF16 = jnp.bfloat16
F32 = jnp.float32
MOST_CHUNKS = 2
HALVES = 2
EDGE = 16
CHUNK = 80


def phase_pair(rows, cols, period):
    wrapped = (np.arange(rows)[:, None] * np.arange(cols)[None, :]) % period
    phase = wrapped.astype(np.float32) * np.float32(2.0 * math.pi / period)
    return np.cos(phase), np.sin(phase)


def tables(groups, per, rows):
    bf = ml_dtypes.bfloat16
    bins = 2 * groups
    cos, sin = phase_pair(bins, groups, bins)
    eye = np.eye(per, dtype=np.float32)
    first = np.concatenate([np.kron(cos, eye), np.kron(-sin, eye)], axis=0).astype(bf)
    cos, sin = phase_pair(rows, rows, rows)
    ahead = np.block([[cos, -sin], [sin, cos]]).astype(bf)
    behind = np.block([[cos, sin], [-sin, cos]]).astype(bf)
    cos, sin = phase_pair(bins, rows, bins * rows)
    twist = np.stack([np.repeat(cos, per, axis=0), np.repeat(sin, per, axis=0)])
    last = np.ascontiguousarray(first.T)
    return first, last, ahead, behind, twist.astype(np.float32)


def kernel(
    sizes,
    tokens,
    weight,
    short_h,
    gain_h,
    taps_h,
    first_h,
    last_h,
    ahead_h,
    behind_h,
    twist_h,
    out,
    w,
    first,
    last,
    ahead,
    behind,
    twist,
    short,
    gain,
    taps,
    held,
    acc,
    psend,
    precv,
    hrecv,
    query,
    product,
    tsend,
    trecv,
    gsend,
    grecv,
    csend,
    crecv,
    tapspec,
    load_sem,
    tok_send,
    tok_recv,
    fwd_send,
    part_send,
    part_recv,
    halo_send,
    halo_recv,
    a2a_send,
    a2a_recv,
):
    seq, fsdp, chan = sizes
    groups = seq * fsdp
    rows = tokens.shape[0]
    chunks = weight.shape[1]
    lines = rows // HALVES
    depth = chunks * weight.shape[2]
    width = weight.shape[3]
    per = width // groups
    bins = 2 * groups
    step = depth // chunks
    share = fsdp // chan
    s = lax.axis_index("seq")
    f = lax.axis_index("fsdp")
    c = lax.axis_index("chan")
    me = s * fsdp + f

    loads = [
        pltpu.make_async_copy(source, target, load_sem.at[i])
        for i, (source, target) in enumerate(
            [
                (taps_h, taps),
                (weight.at[pl.ds(1, 2)], w.at[pl.ds(1, 2)]),
                (first_h, first),
                (ahead_h, ahead),
                (twist_h, twist),
                (last_h, last),
                (behind_h, behind),
                (short_h, short),
                (gain_h, gain),
                (weight.at[pl.ds(0, 1)], w.at[pl.ds(0, 1)]),
            ]
        )
    ]
    for load in loads:
        load.start()

    barrier = pltpu.get_barrier_semaphore()
    everyone = groups * chan

    def greet(k, carry):
        other = lax.rem(me * chan + c + k, everyone)
        spot = other // chan
        pl.semaphore_signal(
            barrier,
            inc=1,
            device_id={"seq": spot // fsdp, "fsdp": spot % fsdp, "chan": other % chan},
            device_id_type=MESH,
        )
        return carry

    lax.fori_loop(1, everyone, greet, 0, unroll=everyone <= 16)

    @pl.when(me == 0)
    def _():
        hrecv[...] = jnp.zeros_like(hrecv)

    loads[0].wait()
    tsend[...] = jnp.transpose(taps[...].astype(F32)).astype(BF16).reshape(groups, per, rows)
    pl.semaphore_wait(barrier, everyone - 1)

    sibling = lax.rem(c + 1, chan)

    def span(h):
        return pl.ds(h * lines, lines)

    def token_copy(i, h, k, same):
        return pltpu.make_async_remote_copy(
            src_ref=tokens.at[span(h), pl.ds(i * depth + k * step, step)],
            dst_ref=held.at[f, k, span(h)],
            send_sem=tok_send.at[i, h, k],
            recv_sem=tok_recv.at[f, h, k],
            device_id={"fsdp": c * share + i, "chan": sibling if same else k % chan},
            device_id_type=MESH,
        )

    for h, k in [(h, k) for h in range(HALVES) for k in range(chunks)]:
        for i in range(share):
            stays = c * share + i == f

            @pl.when(jnp.logical_not(stays))
            def _():
                token_copy(i, h, k, False).start()

            @pl.when(stays)
            def _():
                token_copy(i, h, k, True).start()
                pltpu.make_async_copy(
                    tokens.at[span(h), pl.ds(i * depth + k * step, step)],
                    held.at[f, k, span(h)],
                    tok_recv.at[f, h, k],
                ).start()

    def exchange_copy(which, source, target, k):
        other = lax.rem(me + k, groups)
        return pltpu.make_async_remote_copy(
            src_ref=source.at[other],
            dst_ref=target.at[me],
            send_sem=a2a_send.at[which, k],
            recv_sem=a2a_recv.at[which, k],
            device_id={"seq": other // fsdp, "fsdp": other % fsdp},
            device_id_type=MESH,
        )

    def exchange_start(which, source, target):
        def go(k, carry):
            exchange_copy(which, source, target, k).start()
            return carry

        lax.fori_loop(1, groups, go, 0, unroll=groups <= 8)
        target[me] = source[me]

    def exchange_wait(which, source, target):
        def go(k, carry):
            exchange_copy(which, source, target, k).wait_recv()
            return carry

        lax.fori_loop(1, groups, go, 0, unroll=groups <= 8)

    def exchange_sent(which, source, target):
        def go(k, carry):
            exchange_copy(which, source, target, k).wait_send()
            return carry

        lax.fori_loop(1, groups, go, 0)


    half = bins * per

    def spectrum(signal):
        a = jnp.dot(first[...], signal, preferred_element_type=F32)
        real_a, imag_a = a[:half], a[half:]
        real_b = (real_a * twist[0] + imag_a * twist[1]).astype(BF16)
        imag_b = (imag_a * twist[0] - real_a * twist[1]).astype(BF16)
        b = jnp.concatenate([real_b, imag_b], axis=1)
        return jnp.dot(b, ahead[...], preferred_element_type=F32).astype(BF16)

    def arrival(spot, h, k):
        block = held.at[spot, k, span(h)]
        pltpu.make_async_copy(block, block, tok_recv.at[spot, h, k]).wait()

    def forward_copy(d, h, t):
        k = t * chan + c
        block = held.at[lax.rem(f + d, fsdp), k, span(h)]
        return pltpu.make_async_remote_copy(
            src_ref=block,
            dst_ref=block,
            send_sem=fwd_send.at[d - 1, h, t],
            recv_sem=tok_recv.at[lax.rem(f + d, fsdp), h, k],
            device_id={"chan": sibling},
            device_id_type=MESH,
        )

    def part_copy(d, j, h):
        return pltpu.make_async_remote_copy(
            src_ref=psend.at[d - 1, j, span(h)],
            dst_ref=precv.at[d - 1, j, span(h)],
            send_sem=part_send.at[d - 1, j, h],
            recv_sem=part_recv.at[d - 1, j, h],
            device_id={"fsdp": lax.rem(f + d, fsdp)},
            device_id_type=MESH,
        )

    phases = ((1, 2), (0, 1))

    def halo_target(d):
        return s * fsdp + lax.rem(f + d, fsdp) + 1

    def halo_copy(d, phase):
        target = jnp.minimum(halo_target(d), groups - 1)
        start, count = phases[phase]
        return pltpu.make_async_remote_copy(
            src_ref=acc.at[d - 1, pl.ds(start, count), pl.ds(rows - 8, 8)],
            dst_ref=hrecv.at[f, pl.ds(start, count)],
            send_sem=halo_send.at[d - 1, phase],
            recv_sem=halo_recv.at[f, phase],
            device_id={"seq": target // fsdp, "fsdp": target % fsdp},
            device_id_type=MESH,
        )

    def halo_remote(d):
        target = halo_target(d)
        return jnp.logical_and(target < groups, target != me)

    def halo_start(d, phase):
        @pl.when(halo_remote(d))
        def _():
            halo_copy(d, phase).start()

        start, count = phases[phase]

        @pl.when(halo_target(d) == me)
        def _():
            hrecv[f, start : start + count] = acc[d - 1, start : start + count, rows - 8 :]

    def halo_wait(phase):
        start, count = phases[phase]
        for h in range(fsdp):
            local = jnp.logical_and(f > 0, f == h)

            @pl.when(jnp.logical_and(me > 0, jnp.logical_not(local)))
            def _():
                block = hrecv.at[h, pl.ds(start, count)]
                pltpu.make_async_copy(block, block, halo_recv.at[h, phase]).wait()

    loads[1].wait()
    for k in range(chunks):
        for h in range(HALVES):
            arrival(f, h, k)
        for j in (1, 2):
            term = jnp.dot(held[f, k], w[j, k], preferred_element_type=F32)
            acc[fsdp - 1, j] = term if k == 0 else acc[fsdp - 1, j] + term
    halo_start(fsdp, 0)

    for d in range(1, fsdp):
        spot = lax.rem(f + d, fsdp)
        for h, t, b in [
            (h, t, b)
            for h in range(HALVES)
            for t in range(chunks // chan)
            for b in range(chan)
        ]:
            k = t * chan + lax.rem(c + b, chan)
            arrival(spot, h, k)
            if b == 0:
                forward_copy(d, h, t).start()
            final = (t + 1) * chan == chunks and b == chan - 1
            at = slice(h * lines, (h + 1) * lines)
            for j in (1, 2):
                term = jnp.dot(held[spot, k, at], w[j, k], preferred_element_type=F32)
                if t > 0 or b > 0:
                    term = acc[d - 1, j, at] + term
                acc[d - 1, j, at] = term
                if final:
                    psend[d - 1, j, at] = term.astype(BF16)
                    part_copy(d, j, h).start()
        halo_start(d, 0)

    for load in loads[2:]:
        load.wait()
    exchange_start(0, tsend, trecv)

    row_ids = lax.broadcasted_iota(jnp.int32, (rows, width), 0)

    def branch(j):
        total = acc[fsdp - 1, j]
        edge = hrecv[0, j]
        for d in range(1, fsdp):
            for h in range(HALVES):
                part_copy(d, j, h).wait_recv()
            total = total + precv[d - 1, j].astype(F32)
            edge = edge + hrecv[d, j]
        now = total.astype(BF16).astype(F32)
        edge = edge.astype(BF16).astype(F32)
        before = edge[7:8]
        earlier = edge[6:7]
        one = jnp.where(row_ids == 0, before, pltpu.roll(now, 1, 0))
        two = jnp.where(
            row_ids == 0, earlier, jnp.where(row_ids == 1, before, pltpu.roll(now, 2, 0))
        )
        return (
            short[0, j : j + 1, :] * now
            + short[1, j : j + 1, :] * one
            + short[2, j : j + 1, :] * two
        )

    halo_wait(0)
    prod = (branch(1) * branch(2)).astype(BF16).astype(F32)
    gsend[...] = jnp.transpose(prod).astype(BF16).reshape(groups, per, rows)
    exchange_start(1, gsend, grecv)
    product[...] = prod * gain[...]

    for d in range(1, fsdp + 1):
        spot = lax.rem(f + d, fsdp)
        term = jnp.dot(held[spot, 0], w[0, 0], preferred_element_type=F32)
        for k in range(1, chunks):
            term += jnp.dot(held[spot, k], w[0, k], preferred_element_type=F32)
        acc[d - 1, 0] = term
        if d < fsdp:
            psend[d - 1, 0] = term.astype(BF16)

    exchange_wait(0, tsend, trecv)
    tapspec[...] = spectrum(trecv[...].reshape(width, rows))
    exchange_wait(1, gsend, grecv)
    for d in range(1, fsdp + 1):
        if d < fsdp:
            for h in range(HALVES):
                part_copy(d, 0, h).start()
        halo_start(d, 1)

    x = spectrum(grecv[...].reshape(width, rows)).astype(F32)
    t = tapspec[...].astype(F32)
    xr, xi = x[:, :rows], x[:, rows:]
    tr, ti = t[:, :rows], t[:, rows:]
    real_z = (xr * tr - xi * ti).astype(BF16)
    imag_z = (xr * ti + xi * tr).astype(BF16)
    z = jnp.concatenate([real_z, imag_z], axis=1)
    v = jnp.dot(z, behind[...], preferred_element_type=F32)
    vr, vi = v[:, :rows], v[:, rows:]
    real_w = (vr * twist[0] - vi * twist[1]).astype(BF16)
    imag_w = (vi * twist[0] + vr * twist[1]).astype(BF16)
    packed = jnp.concatenate([real_w, imag_w], axis=0)
    y = jnp.dot(last[...], packed, preferred_element_type=F32) * (1.0 / (bins * rows))
    csend[...] = y.astype(BF16).reshape(groups, per, rows)
    exchange_start(2, csend, crecv)
    halo_wait(1)
    query[...] = branch(0)
    exchange_wait(2, csend, crecv)
    conv = jnp.transpose(crecv[...].reshape(width, rows).astype(F32))
    out[...] = (query[...] * (conv + product[...])).astype(BF16)

    exchange_sent(0, tsend, trecv)
    exchange_sent(1, gsend, grecv)
    exchange_sent(2, csend, crecv)
    for d in range(1, fsdp + 1):
        for phase in range(2):

            @pl.when(halo_remote(d))
            def _():
                halo_copy(d, phase).wait_send()

    for d in range(1, fsdp):
        for h in range(HALVES):
            for j in range(3):
                part_copy(d, j, h).wait_send()
            for t in range(chunks // chan):
                forward_copy(d, h, t).wait_send()
    for h, k in [(h, k) for h in range(HALVES) for k in range(chunks)]:
        for i in range(share):
            token_copy(i, h, k, False).wait_send()


def per_device(sizes, tokens, proj_weight, short_weight, skip_gain, filter_taps):
    seq, fsdp, chan = sizes
    groups = seq * fsdp
    rows = tokens.shape[0]
    depth, branches, width = proj_weight.shape
    per = width // groups
    chunks = min(MOST_CHUNKS, depth // 128)
    made = tables(groups, per, rows)
    dma = pltpu.SemaphoreType.DMA
    vmem = pl.BlockSpec(memory_space=pltpu.VMEM)
    hbm = pl.BlockSpec(memory_space=pl.ANY)
    half = 2 * groups * per
    return pl.pallas_call(
        functools.partial(kernel, sizes),
        out_shape=jax.ShapeDtypeStruct((rows, width), BF16),
        in_specs=[hbm] * 10,
        out_specs=vmem,
        scratch_shapes=[
            pltpu.VMEM((branches, chunks, depth // chunks, width), BF16),
            pltpu.VMEM(made[0].shape, BF16),
            pltpu.VMEM(made[1].shape, BF16),
            pltpu.VMEM(made[2].shape, BF16),
            pltpu.VMEM(made[3].shape, BF16),
            pltpu.VMEM(made[4].shape, F32),
            pltpu.VMEM(short_weight.shape, F32),
            pltpu.VMEM((1, width), F32),
            pltpu.VMEM((rows, width), BF16),
            pltpu.VMEM((fsdp, chunks, rows, depth // chunks), BF16),
            pltpu.VMEM((fsdp, branches, rows, width), F32),
            pltpu.VMEM((fsdp - 1, branches, rows, width), BF16),
            pltpu.VMEM((fsdp - 1, branches, rows, width), BF16),
            pltpu.VMEM((fsdp, branches, 8, width), F32),
            pltpu.VMEM((rows, width), F32),
            pltpu.VMEM((rows, width), F32),
        ]
        + [pltpu.VMEM((groups, per, rows), BF16)] * 6
        + [
            pltpu.VMEM((half, 2 * rows), BF16),
            dma((10,)),
            dma((fsdp // chan, HALVES, chunks)),
            dma((fsdp, HALVES, chunks)),
            dma((fsdp - 1, HALVES, chunks // chan)),
            dma((fsdp - 1, branches, HALVES)),
            dma((fsdp - 1, branches, HALVES)),
            dma((fsdp, 2)),
            dma((fsdp, 2)),
            dma((3, groups)),
            dma((3, groups)),
        ],
        compiler_params=pltpu.CompilerParams(
            collective_id=0, has_side_effects=True, vmem_limit_bytes=60 * 1024 * 1024
        ),
        name="hyena",
    )(
        tokens,
        jnp.transpose(proj_weight, (1, 0, 2)).reshape(branches, chunks, depth // chunks, width),
        short_weight,
        skip_gain.reshape(1, width),
        filter_taps,
        *[jnp.asarray(table) for table in made],
    )


def causal_tables(rows):
    bf = ml_dtypes.bfloat16
    odd = 2 * np.arange(rows) + 1
    period = 4 * rows

    def angles(times):
        wrapped = (odd[:, None] * times[None, :]) % period
        return wrapped.astype(np.float64) * (2.0 * math.pi / period)

    ahead = angles(np.arange(rows))
    behind = angles(rows + np.arange(rows)).T
    pair = [np.cos(behind) / rows, -np.sin(behind) / rows]
    return np.stack([np.cos(ahead), -np.sin(ahead), *pair]).astype(bf)


def chunk_spans(rows):
    head = rows - EDGE
    return [(at, min(at + CHUNK, head)) for at in range(0, head, CHUNK)]


def causal_kernel(
    seq,
    tokens,
    weight,
    short_h,
    gain_h,
    taps_h,
    table_h,
    out,
    w,
    table,
    short,
    gain,
    own,
    far,
    part_out,
    part_in,
    edge_out,
    edge_in,
    projected,
    halves,
    signal,
    taps,
    tapspec,
    response,
    query,
    query_term,
    query_out,
    query_in,
    query_edge_out,
    query_edge_in,
    mixed,
    result,
    packed,
    final,
    query_near,
    short_near,
    load_sem,
    own_send,
    own_recv,
    far_recv,
    fwd_send,
    part_send,
    part_recv,
    edge_send,
    edge_recv,
    across_send,
    across_recv,
    up_send,
    up_recv,
    taps_local,
    taps_x_send,
    taps_x_recv,
    taps_z_send,
    taps_z_recv,
    taps_y_send,
    taps_y_recv,
    query_send,
    query_recv,
    query_edge_send,
    query_edge_recv,
    out_send,
    out_recv,
    query_aside_send,
    query_aside_recv,
    short_send,
    short_recv,
    gain_send,
    gain_recv,
    taps_local_send,
    ready,
    near,
):
    rows = tokens.shape[0]
    width = weight.shape[3]
    depth = weight.shape[2]
    lanes = width // 2
    bins = 2 * rows
    last = seq - 1
    spans = chunk_spans(rows)
    count = len(spans)
    pieces = [(rows - EDGE, rows), *spans]
    made = [*spans[:-1], (spans[-1][0], rows)]
    group = lax.axis_index("grp")
    s = lax.axis_index("seq")
    f = lax.axis_index("fsdp")
    c = lax.axis_index("chan")
    g = 1 - f
    sibling = 1 - c
    holds = c == f
    goes_up = s < last
    across = {"fsdp": g}
    aside = {"chan": sibling}
    diagonal = {"fsdp": g, "chan": sibling}

    def half_of(value):
        return jnp.where(f == 0, value[:, :lanes], value[:, lanes:])

    def other_half(value):
        return jnp.where(f == 0, value[:, lanes:], value[:, :lanes])

    def rounded(value):
        return value.astype(BF16).astype(F32)

    def columns(h):
        return pl.ds(pl.multiple_of(h * lanes, lanes), lanes)

    def at(span):
        return pl.ds(span[0], span[1] - span[0])

    def remote(source, target, send, recv, device):
        return pltpu.make_async_remote_copy(
            src_ref=source,
            dst_ref=target,
            send_sem=send,
            recv_sem=recv,
            device_id=device,
            device_id_type=MESH,
        )

    def arrive(block, sem):
        pltpu.make_async_copy(block, block, sem).wait()

    own_load = pltpu.make_async_copy(tokens, own, own_recv)

    @pl.when(holds)
    def _():
        own_load.start()

    loads = [
        pltpu.make_async_copy(source, target, load_sem.at[i])
        for i, (source, target) in enumerate(
            [
                (weight.at[pl.ds(1, 2)], w.at[pl.ds(1, 2)]),
                (weight.at[pl.ds(0, 1)], w.at[pl.ds(0, 1)]),
                (table_h, table),
                (short_h, short),
            ]
        )
    ]
    for load in loads:
        load.start()
    edge_in[...] = jnp.zeros_like(edge_in)
    query_edge_in[...] = jnp.zeros_like(query_edge_in)

    def member(t, h):
        return {"seq": t, "fsdp": h // 2, "chan": h % 2}

    barrier = pltpu.get_barrier_semaphore()
    beside = {"grp": 1 - group}
    for device in [{"chan": sibling}, across, {"fsdp": g, "chan": sibling}]:
        pl.semaphore_signal(barrier, inc=1, device_id=device, device_id_type=MESH)

    @pl.when(f == 0)
    def _():
        pl.semaphore_signal(barrier, inc=1, device_id=beside, device_id_type=MESH)

    for t in range(seq):
        for h in range(4):

            @pl.when(t > s)
            def _():
                pl.semaphore_signal(
                    barrier, inc=1, device_id=member(t, h), device_id_type=MESH
                )

    pl.semaphore_wait(barrier, 3 + g + 4 * s)

    def token_copy(i, a):
        return remote(
            tokens.at[at(pieces[i]), pl.ds(a * depth, depth)],
            far.at[a, at(pieces[i])],
            own_send,
            far_recv.at[i, a],
            {"fsdp": g, "chan": a},
        )

    own_copy = remote(tokens, own, own_send, own_recv, aside)
    short_copy = remote(short_h, short_near, short_send, short_recv, aside)
    gain_copy = remote(gain_h, gain, gain_send, gain_recv, aside)
    taps_aside = remote(
        taps_h.at[:, columns(f)], taps.at[s, f], taps_local_send, taps_local, aside
    )
    share = pl.ds(pl.multiple_of(group * (rows // 2), rows // 2), rows // 2)
    rest = pl.ds(pl.multiple_of((1 - group) * (rows // 2), rows // 2), rows // 2)
    taps_x_copy = remote(
        taps_h.at[share, columns(g)],
        taps.at[s, f, share],
        taps_x_send,
        taps_x_recv,
        diagonal,
    )

    @pl.when(jnp.logical_not(holds))
    def _():
        for a in range(2):
            token_copy(0, a).start()

    taps_x_copy.start()

    @pl.when(jnp.logical_not(holds))
    def _():
        for a in range(2):
            token_copy(1, a).start()

    @pl.when(holds)
    def _():
        own_copy.start()

    taps_aside.start()
    short_copy.start()
    gain_copy.start()

    @pl.when(f == 0)
    def _():
        pl.semaphore_signal(near, inc=1, device_id=beside, device_id_type=MESH)

    for t in range(seq):
        for h in range(4):

            @pl.when(t < s)
            def _():
                pl.semaphore_signal(
                    ready, inc=1, device_id=member(t, h), device_id_type=MESH
                )

    def part_copy(i):
        return remote(
            part_out.at[:, at(made[i])],
            part_in.at[:, at(made[i])],
            part_send,
            part_recv.at[i],
            across,
        )

    own_query_copy = remote(
        query_out.at[0], query_in.at[0], query_send, query_recv, diagonal
    )

    def query_copy(i):
        return remote(
            query_out.at[1, at(made[i])],
            query_in.at[1, at(made[i])],
            query_send,
            query_recv,
            diagonal,
        )

    def query_aside(block):
        return remote(
            query.at[block],
            query_near.at[block],
            query_aside_send,
            query_aside_recv,
            aside,
        )

    def own_part(j):
        return jnp.dot(own[:, :depth], w[j, 0], preferred_element_type=F32) + jnp.dot(
            own[:, depth:], w[j, 1], preferred_element_type=F32
        )

    def far_part(j, span):
        rows_at = slice(*span)
        return jnp.dot(far[0, rows_at], w[j, 0], preferred_element_type=F32) + jnp.dot(
            far[1, rows_at], w[j, 1], preferred_element_type=F32
        )

    with jax.named_scope("own_rows"):
        arrive(own, own_recv)
        loads[0].wait()
        for j in range(2):
            term = own_part(j + 1)
            part_out[j] = term.astype(BF16)
            edge_out[0, j] = term[rows - 8 :]
        part_copy(0).start()

        @pl.when(f == 0)
        def _():
            edge_in[0] = edge_out[0]

    with jax.named_scope("own_query"):
        for load in loads[1:]:
            load.wait()
        term = own_part(0)
        query[f] = half_of(term)
        query_aside(f).start()
        query_out[0] = other_half(term).astype(BF16)

        @pl.when(f == 1)
        def _():
            query_edge_out[0] = term[rows - 8 :, :lanes]
            query_edge_out[1] = term[rows - 8 :, lanes:]

    @pl.when(f == 0)
    def _():
        pl.semaphore_wait(near, 1)
        pl.semaphore_signal(near, inc=1, device_id=across, device_id_type=MESH)

    def edge_up(i):
        return remote(
            edge_out.at[i],
            edge_in.at[i],
            edge_send,
            edge_recv,
            {"seq": jnp.minimum(s + 1, last), "fsdp": 1},
        )

    edge_across = remote(
        edge_out.at[1], edge_in.at[1], edge_send, edge_recv, {"fsdp": 0}
    )

    def query_edge(h):
        return remote(
            query_edge_out.at[h],
            query_edge_in.at[f],
            query_edge_send,
            query_edge_recv,
            {"seq": jnp.minimum(s + 1, last), "fsdp": h, "chan": sibling},
        )

    def taps_z_copy(t):
        block = taps.at[s, :, share]
        return remote(block, block, taps_z_send, taps_z_recv, {"seq": t})

    def taps_y_copy(n):
        block = taps.at[pl.ds(0, n), :, share]
        return remote(block, block, taps_y_send.at[1], taps_y_recv.at[1], beside)

    own_taps_y = remote(
        taps.at[s, g, share],
        taps.at[s, g, share],
        taps_y_send.at[0],
        taps_y_recv.at[0],
        beside,
    )

    def forward_copy(i):
        block = far.at[c, at(pieces[i])]
        return remote(
            block, block, fwd_send, far_recv.at[i, c], {"chan": sibling}
        )

    def half_part(j, a, span):
        return jnp.dot(far[a, slice(*span)], w[j, a], preferred_element_type=F32)

    def take(i):
        with jax.named_scope("direct"):
            arrive(far.at[c, at(pieces[i])], far_recv.at[i, c])
        forward_copy(i).start()

    def take_other(i):
        arrive(far.at[sibling, at(pieces[i])], far_recv.at[i, sibling])

    with jax.named_scope("edge_rows"):
        take(0)
        for j in range(2):
            projected[j, 8 + rows - EDGE :] = half_part(j + 1, c, pieces[0])
        @pl.when(goes_up)
        def _():
            pl.semaphore_wait(ready, 4 * (last - s))

            @pl.when(f == 1)
            def _():
                edge_up(0).start()
                for h in range(2):
                    query_edge(h).start()

        with jax.named_scope("taps_up"):
            arrive(taps.at[s, f], taps_local)
            arrive(taps.at[s, g, share], taps_x_recv)
            for t in range(1, seq):

                @pl.when(t > s)
                def _():
                    taps_z_copy(t).start()

            @pl.when(f == 1)
            def _():
                pl.semaphore_wait(near, 1)

            own_taps_y.start()

        take_other(0)
        for j in range(2):
            term = projected[j, 8 + rows - EDGE :] + half_part(j + 1, sibling, pieces[0])
            projected[j, 8 + rows - EDGE :] = term
            edge_out[1, j] = term[EDGE - 8 :]

        @pl.when(f == 1)
        def _():
            edge_across.start()

        @pl.when(jnp.logical_not(holds))
        def _():
            for i in range(2, count + 1):
                for a in range(2):
                    token_copy(i, a).start()

        @pl.when(jnp.logical_and(f == 0, goes_up))
        def _():
            edge_up(1).start()
            term = far_part(0, pieces[0])
            query_edge_out[0] = term[EDGE - 8 :, :lanes]
            query_edge_out[1] = term[EDGE - 8 :, lanes:]
            for h in range(2):
                query_edge(h).start()

    def across_copy(i):
        return remote(
            halves.at[g, at(made[i])],
            signal.at[s, g, at(made[i])],
            across_send,
            across_recv,
            diagonal,
        )

    def aside_copy(i):
        return remote(
            halves.at[f, at(made[i])],
            signal.at[s, g, at(made[i])],
            across_send,
            across_recv,
            aside,
        )

    def up_copy(i, t):
        return remote(
            halves.at[f, at(made[i])],
            signal.at[s, g, at(made[i])],
            up_send,
            up_recv.at[s],
            {"seq": t, "chan": sibling},
        )

    def cross_copy(i, t):
        return remote(
            halves.at[g, at(made[i])],
            signal.at[s, g, at(made[i])],
            up_send,
            up_recv.at[s],
            {"seq": t, "fsdp": g, "chan": sibling},
        )

    def cross_start(i, low):
        for t in range(1, seq):

            @pl.when(jnp.logical_and(t > s, (s == 0) if low else (s > 0)))
            def _():
                cross_copy(i, t).start()

    def query_early(now):
        @pl.when(now)
        def _():
            own_query_copy.start()
            for i in range(count - 1):
                query_copy(i).start()

    def branch(j, span):
        low, high = span
        now = projected[j, 8 + low : 8 + high]
        one = projected[j, 7 + low : 7 + high]
        two = projected[j, 6 + low : 6 + high]
        return (
            short[0, j + 1 : j + 2, :] * now
            + short[1, j + 1 : j + 2, :] * one
            + short[2, j + 1 : j + 2, :] * two
        )

    def transform(values):
        whole = table[:2].reshape(2 * bins, bins)
        return jnp.dot(whole, values, preferred_element_type=F32)

    def taps_spectrum():
        ids = lax.broadcasted_iota(jnp.int32, (bins, lanes), 0)
        sign = 1.0 - 2.0 * (ids % 2).astype(F32)
        arrive(taps.at[s, g, rest], taps_y_recv.at[0])
        for n in range(1, seq):

            @pl.when(s == n)
            def _():
                arrive(taps.at[pl.ds(0, n), :, rest], taps_y_recv.at[1])

        for d in range(seq):

            @pl.when(d <= s)
            def _():
                spec = transform(taps[d].reshape(bins, lanes))
                real, imag = spec[:bins], spec[bins:]
                tapspec[d] = spec
                if d == 0:
                    response[0, 0] = sign * imag
                    response[0, 1] = -sign * real
                else:
                    response[d, 0] = tapspec[d - 1, :bins] + sign * imag
                    response[d, 1] = tapspec[d - 1, bins:] - sign * real

    for i in range(count):
        low, high = made[i]
        final_chunk = i == count - 1
        with jax.named_scope("tokens"):
            take(i + 1)
            if final_chunk:
                query_early(s == 0)
                for r in range(i):
                    cross_start(r, True)
            lines = slice(8 + spans[i][0], 8 + spans[i][1])
            for j in range(2):
                projected[j, lines] = half_part(j + 1, c, spans[i])
            if final_chunk:
                query_term[low:high] = half_part(0, c, made[i])
            if i == 0:
                with jax.named_scope("taps_side"):
                    for n in range(1, seq):

                        @pl.when(s == n)
                        def _():
                            arrive(taps.at[pl.ds(0, n), :, share], taps_z_recv)
                            taps_y_copy(n).start()

            take_other(i + 1)
            if not final_chunk:
                part_copy(i + 1).start()
        with jax.named_scope("chunk"):
            for j in range(2):
                projected[j, lines] += half_part(j + 1, sibling, spans[i])
        if i == 0:
            with jax.named_scope("edges"):

                @pl.when(jnp.logical_and(f == 1, s > 0))
                def _():
                    arrive(edge_in, edge_recv)

                @pl.when(f == 0)
                def _():
                    arrive(edge_in.at[1], edge_recv)

                for j in range(2):
                    projected[j, :8] = rounded(edge_in[0, j] + edge_in[1, j])
        with jax.named_scope("partial"):
            part_copy(i).wait_recv()
        with jax.named_scope("product"):
            for j in range(2):
                block = slice(8 + low, 8 + high)
                projected[j, block] = rounded(
                    projected[j, block] + part_in[j, low:high].astype(F32)
                )
            product = (branch(0, made[i]) * branch(1, made[i])).astype(BF16)
            halves[0, low:high] = product[:, :lanes]
            halves[1, low:high] = product[:, lanes:]
            across_copy(i).start()
            aside_copy(i).start()
            cross_start(i, False)
            for t in range(1, seq):

                @pl.when(t > s)
                def _():
                    up_copy(i, t).start()

        if final_chunk:
            cross_start(i, True)
            query_early(s > 0)
        with jax.named_scope("far_query"):
            if final_chunk:
                term = query_term[low:high] + half_part(0, sibling, made[i])
            else:
                term = far_part(0, made[i])
            query[g, low:high] = half_of(term)
            query_aside((g, at(made[i]))).start()
            query_out[1, low:high] = other_half(term).astype(BF16)
            if final_chunk:
                query_copy(i).start()
    def spectrum(j, d):
        spec = transform(signal[j].reshape(bins, lanes))
        real, imag = spec[:bins], spec[bins:]
        hr, hi = response[d, 0], response[d, 1]
        return real * hr - imag * hi, real * hi + imag * hr

    with jax.named_scope("taps_spectra"):
        taps_spectrum()

    with jax.named_scope("earlier_slabs"):
        result[...] = jnp.zeros_like(result)
        for j in range(last - 1):

            @pl.when(j < s - 1)
            def _():
                arrive(signal.at[j], up_recv.at[j])
                real, imag = spectrum(j, s - j)
                result[0] += real
                result[1] += imag

    arrive(short_near, short_recv)
    arrive(gain, gain_recv)
    with jax.named_scope("own_wait"):
        arrive(signal.at[s], across_recv)
    with jax.named_scope("own_slab"):

        @pl.when(s == 0)
        def _():
            real, imag = spectrum(s, 0)
            packed[0] = real.astype(BF16)
            packed[1] = imag.astype(BF16)

        @pl.when(s > 0)
        def _():
            arrive(signal.at[s - 1], up_recv.at[s - 1])
            pair = [signal[s].reshape(bins, lanes), signal[s - 1].reshape(bins, lanes)]
            spec = transform(jnp.concatenate(pair, axis=1))
            real, imag = result[0], result[1]
            for d in range(2):
                side = slice(d * lanes, (d + 1) * lanes)
                hr, hi = response[d, 0], response[d, 1]
                real += spec[:bins, side] * hr - spec[bins:, side] * hi
                imag += spec[:bins, side] * hi + spec[bins:, side] * hr
            packed[0] = real.astype(BF16)
            packed[1] = imag.astype(BF16)

    with jax.named_scope("query"):
        arrive(query_in, query_recv)
        arrive(query_near, query_aside_recv)

        @pl.when(s > 0)
        def _():
            arrive(query_edge_in, query_edge_recv)

        mixed[:8] = rounded(query_edge_in[0] + query_edge_in[1])
        other = pl.multiple_of(8 + g * rows, 8)
        mine = pl.multiple_of(8 + f * rows, 8)
        mixed[pl.ds(other, rows)] = rounded(query_near[g] + query_in[0].astype(F32))
        mixed[pl.ds(mine, rows)] = rounded(query_near[f] + query_in[1].astype(F32))
        gate = [half_of(short_near[i, 0:1, :]) for i in range(3)]
        gated = gate[0] * mixed[8 : 8 + bins] + gate[1] * mixed[7 : 7 + bins]
        gated += gate[2] * mixed[6 : 6 + bins]
        query_near[...] = gated.reshape(2, rows, lanes)

    with jax.named_scope("finish"):
        factor = half_of(gain[...])

        def finish(b):
            lines = pl.ds(pl.multiple_of(b * rows, rows), rows)
            conv = jnp.dot(table[2, lines], packed[0], preferred_element_type=F32)
            conv += jnp.dot(table[3, lines], packed[1], preferred_element_type=F32)
            whole = conv + factor * signal[s, b].astype(F32)
            return (query_near[b] * whole).astype(BF16)

        landing = out.at[:, columns(f)]
        out_across = remote(final.at[0], landing, out_send, out_recv, diagonal)
        out_aside = remote(final.at[1], landing, out_send, out_recv, aside)
        final[0] = finish(g)
        out_across.start()
        final[1] = finish(f)
        out_aside.start()

    with jax.named_scope("drain"):

        @pl.when(jnp.logical_not(holds))
        def _():
            arrive(far, own_send)

        @pl.when(holds)
        def _():
            own_copy.wait_send()

        taps_x_copy.wait_send()
        arrive(far.at[c], fwd_send)
        arrive(part_out, part_send)
        arrive(halves, across_send)
        arrive(query, query_aside_send)
        short_copy.wait_send()
        gain_copy.wait_send()
        taps_aside.wait_send()
        arrive(query_out, query_send)
        own_taps_y.wait_send()

        @pl.when(jnp.logical_and(f == 1, goes_up))
        def _():
            arrive(edge_out, edge_send)

        @pl.when(f != jnp.where(goes_up, 1, 0))
        def _():
            arrive(edge_out.at[1], edge_send)

        @pl.when(goes_up)
        def _():
            arrive(query_edge_out, query_edge_send)

        for n in range(1, seq):

            @pl.when(s == n)
            def _():
                taps_y_copy(n).wait_send()

            @pl.when(last - s == n)
            def _():
                arrive(taps.at[pl.ds(0, n), :, share], taps_z_send)
                arrive(signal.at[pl.ds(0, n)], up_send)

    with jax.named_scope("out"):
        arrive(final, out_send)
        arrive(out, out_recv)


def causal_device(seq, tokens, proj_weight, short_weight, skip_gain, filter_taps):
    rows = tokens.shape[0]
    depth, branches, width = proj_weight.shape
    lanes = width // 2
    step = depth // 2
    table = causal_tables(2 * rows)
    count = len(chunk_spans(rows))
    dma = pltpu.SemaphoreType.DMA
    hbm = pl.BlockSpec(memory_space=pl.ANY)
    scratch = [
        ((branches, 2, step, width), BF16),
        (table.shape, BF16),
        (short_weight.shape, F32),
        ((1, width), F32),
        ((rows, depth), BF16),
        ((2, rows, step), BF16),
        ((2, rows, width), BF16),
        ((2, rows, width), BF16),
        ((2, 2, 8, width), F32),
        ((2, 2, 8, width), F32),
        ((2, 8 + rows, width), F32),
        ((2, rows, lanes), BF16),
        ((seq, 2, rows, lanes), BF16),
        ((seq, 2, rows, lanes), BF16),
        ((seq, 4 * rows, lanes), F32),
        ((seq, 2, 2 * rows, lanes), F32),
        ((2, rows, lanes), F32),
        ((rows, width), F32),
        ((2, rows, lanes), BF16),
        ((2, rows, lanes), BF16),
        ((2, 8, lanes), F32),
        ((2, 8, lanes), F32),
        ((8 + 2 * rows, lanes), F32),
        ((2, 2 * rows, lanes), F32),
        ((2, 2 * rows, lanes), BF16),
        ((2, rows, lanes), BF16),
        ((2, rows, lanes), F32),
        (short_weight.shape, F32),
    ]
    sems = [
        (4,),
        (),
        (),
        (count + 1, 2),
        (),
        (),
        (count,),
        (),
        (),
        (),
        (),
        (),
        (max(seq - 1, 1),),
        (),
        (),
        (),
        (),
        (),
        (2,),
        (2,),
        (),
        (),
        (),
        (),
        (),
        (),
        (),
        (),
        (),
        (),
        (),
        (),
        (),
    ]
    return pl.pallas_call(
        functools.partial(causal_kernel, seq),
        out_shape=pltpu.VMEM((rows, width), BF16),
        in_specs=[hbm] * 6,
        out_specs=pl.BlockSpec(memory_space=pltpu.VMEM),
        scratch_shapes=[pltpu.VMEM(shape, kind) for shape, kind in scratch]
        + [dma(shape) for shape in sems]
        + [pltpu.SemaphoreType.REGULAR] * 2,
        compiler_params=pltpu.CompilerParams(
            collective_id=0, has_side_effects=True, vmem_limit_bytes=60 * 1024 * 1024
        ),
        name="hyena",
    )(
        tokens,
        jnp.transpose(proj_weight, (1, 0, 2)).reshape(branches, 2, step, width),
        short_weight,
        skip_gain.reshape(1, width),
        filter_taps,
        jnp.asarray(table),
    )


def solution(mesh):
    seq = mesh.shape["seq"]
    paired = all(mesh.shape[axis] == 2 for axis in ("grp", "fsdp", "chan"))
    sizes = (mesh.shape["seq"], mesh.shape["fsdp"], mesh.shape["chan"])
    in_specs = (
        P(("grp", "seq", "fsdp"), "chan"),
        P("fsdp", None, "chan"),
        P(None, None, "chan"),
        P("chan"),
        P(("seq", "fsdp"), "chan"),
    )
    out_specs = P(("grp", "seq", "fsdp"), "chan")
    return jax.shard_map(
        functools.partial(causal_device, seq)
        if paired
        else functools.partial(per_device, sizes),
        mesh=mesh,
        in_specs=in_specs,
        out_specs=out_specs,
        check_vma=False,
    )
```
